32 devices in a mesh: dp: 8 (over z, x), tensor: 4 (over y, core).
Axes of the slice: x: 2, y: 2, z: 4, core: 2. Of those that a mesh axis runs over, the one named last changes fastest.
Arguments:
- block_in: bfloat16 [2048, 8, 1024], P('tensor', 'dp'), may hold values from -6 to 6
- lengths: int32 [8, 8], P('dp'), may hold values from 1 to 2041, as said below
- qkv_weight: bfloat16 [1024, 3, 1024], P(None, None, 'tensor'), may hold values from -0.1875 to 0.1875
- out_weight: bfloat16 [1024, 1024], P('tensor'), may hold values from -0.1875 to 0.1875
- up_weight: bfloat16 [1024, 4096], P(None, 'tensor'), may hold values from -0.1875 to 0.1875
- down_weight: bfloat16 [4096, 1024], P('tensor'), may hold values from -0.09375 to 0.09375
- norm_gain: float32 [4, 1024], replicated, may hold values from 0.25 to 1.75
- norm_bias: float32 [4, 1024], replicated, may hold values from -2 to 2
- cotangent: bfloat16 [2048, 8, 1024], P('tensor', 'dp'), may hold values from -6 to 6
Outputs:
- block_out: bfloat16 [2048, 8, 1024], P('tensor', 'dp')
- input_grad: float32 [2048, 8, 1024], P('tensor', 'dp')
- qkv_grad: float32 [1024, 3, 1024], P(None, None, 'tensor')
- out_grad: float32 [1024, 1024], P('tensor')
- up_grad: float32 [1024, 4096], P(None, 'tensor')
- down_grad: float32 [4096, 1024], P('tensor')
- gain_grad: float32 [4, 1024], replicated
- bias_grad: float32 [4, 1024], replicated
The draws below stay inside these ranges and needn't reach their ends.
Inputs may be any that keep to these rules, and one draw needn't show every extreme that they name: The 8 lengths of a row sum to 2048; one document of each row is longer than all others of the row together.
All inputs are finite; a program needn't handle non-finite values.
Results may differ from the reference program's by a relative error of at most 0.015.
Values may be sent and summed in bfloat16 or wider, within the bound.
A program may use at most 192 MiB of HBM per device.

```python
import jax
import jax.numpy as jnp
from jax import lax

D = 1024
HEADS = 16
HD = 64
FF = 4096
SEQ = 2048
NDOC = 8
ROWS = 8
N_TENSOR = 4


def draw_lengths(key, part):
    first_key, second_key, third_key = jax.random.split(jax.random.fold_in(key, 11), 3)
    short_most = SEQ // (N_TENSOR * NDOC)
    shorts = jax.random.randint(first_key, (ROWS, NDOC), 1, short_most + 1)
    single_row = jax.random.randint(third_key, (), 0, ROWS)
    shorts = jnp.where((jnp.arange(ROWS) == single_row)[:, None], 1, shorts)
    longest = jax.random.randint(second_key, (ROWS,), 0, NDOC)
    picked = jnp.arange(NDOC)[None, :] == longest[:, None]
    others = jnp.sum(jnp.where(picked, 0, shorts), axis=1)
    return jnp.where(picked, (SEQ - others)[:, None], shorts).astype(jnp.int32)


def levels(stream_key, dims, cuts, low, high):
    loudness = 1.0
    for dim, blocks in cuts:
        steps = jax.random.uniform(jax.random.fold_in(jax.random.fold_in(stream_key, 6), dim), (blocks,), jnp.float32, low / len(cuts), high / len(cuts))
        loudness = loudness * jnp.repeat(jnp.exp(steps), dims[dim] // blocks).reshape((-1,) + (1,) * (len(dims) - 1 - dim))
    return loudness


def normal_values(rng, dims, scale, limit, cuts=(), held_as=jnp.bfloat16):
    entries = jax.random.normal(rng, dims, jnp.float32) * scale
    if len(cuts) > 0:
        entries = levels(rng, dims, cuts, -0.22, 0.18) * entries
    return jnp.clip(entries, min=-limit, max=limit).astype(held_as)


def setup_inputs(seed: int = 0) -> dict:
    arg_keys = jax.random.split(jax.random.key(seed), 10)
    return {
        "block_in": normal_values(arg_keys[0], (SEQ, ROWS, D), 1.0, 6.0, ((0, 4), (1, 8))),
        "lengths": draw_lengths(jax.random.fold_in(arg_keys[9], 71), 0),
        "qkv_weight": normal_values(arg_keys[2], (D, 3, D), D ** -0.5, 0.1875, ((2, 4),)),
        "out_weight": normal_values(arg_keys[3], (D, D), D ** -0.5, 0.1875, ((0, 4),)),
        "up_weight": normal_values(arg_keys[4], (D, FF), D ** -0.5, 0.1875, ((1, 4),)),
        "down_weight": normal_values(arg_keys[5], (FF, D), FF ** -0.5, 0.09375, ((0, 4),)),
        "norm_gain": jnp.clip(1.0 + 0.15 * jax.random.normal(arg_keys[6], (4, D), jnp.float32), 0.25, 1.75),
        "norm_bias": normal_values(arg_keys[7], (4, D), 0.3, 2.0, (), jnp.float32),
        "cotangent": normal_values(arg_keys[8], (SEQ, ROWS, D), 1.0, 6.0, ((0, 4), (1, 8))),
    }


HIGHEST_PRECISION = lax.Precision.HIGHEST
EPSILON = 1e-05
ROPE_BASE = 10000.0

@jax.custom_vjp
def low(v):
    return lax.optimization_barrier(v.astype(jnp.bfloat16)).astype(jnp.float32)

@jax.custom_vjp
def low_back(v):
    return v

def low_keep(v):
    return (low(v), None)

def low_pass(kept, grad):
    return (grad,)

def back_keep(v):
    return (v, None)

def back_low(kept, grad):
    return (low(grad),)
low.defvjp(low_keep, low_pass)
low_back.defvjp(back_keep, back_low)

def layer_norm(values, gain, shift):
    centre = values - lax.optimization_barrier(jnp.mean(values, axis=-1, keepdims=True))
    spread = lax.optimization_barrier(jnp.mean(centre * centre, axis=-1, keepdims=True))
    return centre * lax.rsqrt(spread + EPSILON) * gain + shift

def doc_layout(lengths, length_total):
    finish = jnp.cumsum(lengths, axis=1)
    begin = finish - lengths
    places = jnp.arange(length_total, dtype=jnp.int32)
    segment = lax.optimization_barrier(jnp.sum((places[:, None, None] >= finish[None, :, :]).astype(jnp.int32), axis=2))
    picked = segment[:, :, None] == jnp.arange(lengths.shape[1], dtype=jnp.int32)[None, None, :]
    position = places[:, None] - lax.optimization_barrier(jnp.sum(jnp.where(picked, begin[None, :, :], 0), axis=2))
    return (segment, position)

def rope_tables(position, head_size):
    half_size = head_size // 2
    inverse = ROPE_BASE ** (-jnp.arange(half_size, dtype=jnp.float32) * 2.0 / head_size)
    angles = position.astype(jnp.float32)[..., None] * inverse
    return (jnp.cos(angles), jnp.sin(angles))

def rotate(values, cosine, sine):
    half_size = values.shape[-1] // 2
    first = values[..., :half_size]
    second = values[..., half_size:]
    return jnp.concatenate([first * cosine - second * sine, second * cosine + first * sine], axis=-1)

def row_forward(row_values, w_qkv, w_out, w_up, w_down, gains, shifts, segment, cosine, sine):
    length_total = row_values.shape[0]
    attn_norm = low(layer_norm(row_values, gains[0], shifts[0]))
    project = low_back(jnp.dot(attn_norm, w_qkv.reshape(D, 3 * D), precision=HIGHEST_PRECISION))
    project = project.reshape(length_total, 3, HEADS, HD)
    queries = low(rotate(project[:, 0], cosine, sine))
    keys = low(rotate(project[:, 1], cosine, sine))
    values = low(project[:, 2])
    block_rows = min(512, length_total)
    blocks = length_total // block_rows
    places = jnp.arange(length_total, dtype=jnp.int32)

    def attend_block(pieces):
        query_block, segment_block, place_block = pieces
        scores = jnp.einsum('qhd,khd->hqk', query_block, keys, precision=HIGHEST_PRECISION) * HD ** (-0.5)
        scores = low_back(scores)
        visible = (segment_block[:, None] == segment[None, :]) & (places[None, :] <= place_block[:, None])
        scores = jnp.where(visible[None], scores, -1e+30)
        top_score = lax.optimization_barrier(jnp.max(scores, axis=-1, keepdims=True))
        weights_exp = jnp.exp(scores - top_score)
        probs = weights_exp / lax.optimization_barrier(jnp.sum(weights_exp, axis=-1, keepdims=True))
        return jnp.einsum('hqk,khd->qhd', low(probs), values, precision=HIGHEST_PRECISION)
    mixed = lax.map(jax.checkpoint(attend_block), (queries.reshape(blocks, block_rows, HEADS, HD), segment.reshape(blocks, block_rows), places.reshape(blocks, block_rows)))
    heads_out = low_back(low(mixed.reshape(length_total, D)))
    attn_proj = low_back(jnp.dot(heads_out, w_out, precision=HIGHEST_PRECISION))
    middle = row_values + layer_norm(attn_proj, gains[1], shifts[1])
    mlp_norm = low(layer_norm(middle, gains[2], shifts[2]))
    upward = low_back(jnp.dot(mlp_norm, w_up, precision=HIGHEST_PRECISION))
    hidden = low(jax.nn.gelu(upward))
    mlp_proj = low_back(jnp.dot(hidden, w_down, precision=HIGHEST_PRECISION))
    return middle + layer_norm(mlp_proj, gains[3], shifts[3])

def reference(block_in, lengths, qkv_weight, out_weight, up_weight, down_weight, norm_gain, norm_bias, cotangent):
    weights_full = (qkv_weight.astype(jnp.float32), out_weight.astype(jnp.float32), up_weight.astype(jnp.float32), down_weight.astype(jnp.float32), norm_gain.astype(jnp.float32), norm_bias.astype(jnp.float32))
    rows_in = jnp.swapaxes(block_in.astype(jnp.float32), 0, 1)
    rows_cot = jnp.swapaxes(cotangent.astype(jnp.float32), 0, 1)

    def one_row(totals, pieces):
        row_in, row_cot, row_lengths = pieces
        segment, position = doc_layout(row_lengths[None, :], SEQ)
        cosine, sine = rope_tables(position[:, 0], HD)
        cosine = cosine[:, None, :]
        sine = sine[:, None, :]

        def forward(row_values, w_qkv, w_out, w_up, w_down, gains, shifts):
            return row_forward(row_values, w_qkv, w_out, w_up, w_down, gains, shifts, segment[:, 0], cosine, sine)
        result, pull = jax.vjp(forward, row_in, *weights_full)
        grads = pull(row_cot)
        totals = jax.tree.map(jnp.add, totals, tuple(grads[1:]))
        return (totals, (result, grads[0]))
    start_totals = tuple((jnp.zeros(weight.shape, jnp.float32) for weight in weights_full))
    totals, (results, input_rows) = lax.scan(one_row, start_totals, (rows_in, rows_cot, lengths))
    block_out = jnp.swapaxes(results, 0, 1).astype(jnp.bfloat16)
    input_grad = jnp.swapaxes(input_rows, 0, 1)
    return (block_out, input_grad, totals[0], totals[1], totals[2], totals[3], totals[4], totals[5])
```

```python
import functools

import jax
import jax.numpy as jnp
from jax import lax
from jax.experimental import pallas as pl
from jax.experimental.pallas import tpu as pltpu
from jax.sharding import PartitionSpec as P

HD = 64
PAIR = 128
EPSILON = 1e-05
ROPE_BASE = 10000.0
NEG = -1e30
BF = jnp.bfloat16
F32 = jnp.float32
NT = (((1,), (1,)), ((), ()))
NN = (((1,), (0,)), ((), ()))
TN = (((0,), (0,)), ((), ()))


def dot(a, b, dims=NN):
    return lax.dot_general(a, b, dims, preferred_element_type=F32)


def layer_norm(values, gain, shift):
    centre = values - jnp.mean(values, axis=-1, keepdims=True)
    spread = jnp.mean(centre * centre, axis=-1, keepdims=True)
    return centre * lax.rsqrt(spread + EPSILON) * gain + shift


def swap(value, axis, offset):
    size = lax.axis_size(axis)
    return lax.ppermute(value, axis, [(i, i ^ offset) for i in range(size)])


def gather_tensor(value):
    parts = [value]
    size = lax.axis_size("tensor")
    step = size // 2
    found = {0: value}
    while step >= 1:
        for place in sorted(found):
            found[place ^ step] = swap(found[place], "tensor", step)
        step //= 2
    parts = [found[d] for d in range(size)]
    return parts


def reduce_scatter_tensor(parts):
    size = lax.axis_size("tensor")
    terms = {d: parts[d] for d in range(size)}
    step = 1
    while step < size:
        kept = {}
        for d in sorted(terms):
            if d & step == 0:
                got = swap(terms[d ^ step].astype(BF), "tensor", step)
                kept[d] = terms[d].astype(F32) + got.astype(F32)
        terms = kept
        step *= 2
    return terms[0]


def tree_sum(parts):
    parts = [part.astype(F32) for part in parts]
    while len(parts) > 1:
        parts = [parts[i] + parts[i + 1] for i in range(0, len(parts), 2)]
    return parts[0]


def sum_all(value):
    for axis in ("tensor", "dp"):
        size = lax.axis_size(axis)
        value = tree_sum([value] + [swap(value, axis, d) for d in range(1, size)])
    return value


def in_order(parts, index):
    size = len(parts)
    step = 1
    while step < size:
        flip = (index & step) != 0
        parts = [jnp.where(flip, parts[d ^ step], parts[d]) for d in range(size)]
        step *= 2
    return parts


def reduce_dp(partial, direct):
    size = lax.axis_size("dp")
    index = lax.axis_index("dp")
    rows = partial.shape[0]
    shift = 0
    if not direct:
        half = rows // 2
        bit = index & 1
        there = lax.dynamic_slice_in_dim(partial, (1 - bit) * half, half, 0).astype(BF)
        here = lax.dynamic_slice_in_dim(partial, bit * half, half, 0)
        got = swap(there, "dp", 1)
        partial = (here.astype(F32) + got.astype(F32)).astype(BF)
        rows, shift = half, 1
    group = size >> shift
    place = index >> shift
    piece = rows // group
    parts = [lax.dynamic_slice_in_dim(partial, place * piece, piece, 0)]
    for d in range(1, group):
        part = lax.dynamic_slice_in_dim(partial, (place ^ d) * piece, piece, 0).astype(BF)
        parts.append(swap(part, "dp", d << shift))
    total = tree_sum(parts).astype(BF)
    parts = [total] + [swap(total, "dp", d << shift) for d in range(1, group)]
    full = jnp.concatenate(in_order(parts, place), axis=0)
    if not direct:
        got = swap(full, "dp", 1)
        flip = (index & 1) != 0
        full = jnp.concatenate([jnp.where(flip, got, full), jnp.where(flip, full, got)], axis=0)
    return full.astype(F32)


def turn(values, cosine, signed_sine):
    lane = lax.broadcasted_iota(jnp.int32, values.shape, 1)
    other = jnp.where(lane % HD < HD // 2, pltpu.roll(values, PAIR - HD // 2, 1), pltpu.roll(values, HD // 2, 1))
    return values * cosine + other * signed_sine


def qkv_kernel(pairs, place_ref, x_ref, w_ref, cos_ref, sin_ref, out_ref):
    x = x_ref[...]
    for part in range(3):
        project = dot(x, w_ref[part])
        for pair in range(pairs):
            piece = project[:, pair * PAIR : (pair + 1) * PAIR]
            if part < 2:
                piece = turn(piece, cos_ref[...], sin_ref[...])
            out_ref[part * pairs + pair] = piece.astype(BF)


def project_qkv(place, tokens, weight, cosine, sine, block):
    length, width = tokens.shape
    columns = weight.shape[2]
    pairs = columns // PAIR
    real = lambda d, place: (d ^ place[0], 0)
    return pl.pallas_call(
        functools.partial(qkv_kernel, pairs),
        out_shape=jax.ShapeDtypeStruct((3 * pairs, length, PAIR), BF),
        grid_spec=pltpu.PrefetchScalarGridSpec(
            num_scalar_prefetch=1,
            grid=(length // block,),
            in_specs=[
                pl.BlockSpec((block, width), lambda d, place: (d, 0)),
                pl.BlockSpec((3, width, columns), lambda d, place: (0, 0, 0)),
                pl.BlockSpec((block, PAIR), real),
                pl.BlockSpec((block, PAIR), real),
            ],
            out_specs=pl.BlockSpec((3 * pairs, block, PAIR), lambda d, place: (0, d, 0)),
        ),
        compiler_params=pltpu.CompilerParams(vmem_limit_bytes=40 << 20),
        cost_estimate=pl.CostEstimate(flops=2 * length * width * 3 * columns, bytes_accessed=2 * length * width, transcendentals=0),
        name="project_qkv",
    )(place, tokens, weight, cosine, sine)


def head_mask(shape, head):
    lane = lax.broadcasted_iota(jnp.int32, shape, 1)
    return lane // HD == head


def forward_kernel(block, place_ref, q_ref, k_ref, v_ref, start_ref, out_ref, log_ref, scores_ref):
    mine = place_ref[0]
    row_block = pl.program_id(0) ^ mine
    queries = q_ref[...] * HD**-0.5
    start = start_ref[...]
    mixed = None
    for head in range(PAIR // HD):
        mask = head_mask(queries.shape, head)
        query = jnp.where(mask, queries, jnp.zeros_like(queries))

        def score(j, top, last):
            keys = k_ref[pl.ds(pl.multiple_of((j ^ mine) * block, block), block), :]
            s = dot(query, keys, NT)
            column = lax.broadcasted_iota(jnp.int32, s.shape, 1)
            visible = column >= start - j * block
            if last:
                visible &= column <= lax.broadcasted_iota(jnp.int32, s.shape, 0)
            s = jnp.where(visible, s, NEG)
            scores_ref[j] = s
            for c in range(0, block, 128):
                top = jnp.maximum(top, s[:, c : c + 128])
            return top

        top = jnp.full((block, 128), NEG, F32)
        top = lax.fori_loop(0, row_block, lambda j, top: score(j, top, False), top)
        top = score(row_block, top, True)
        top = jnp.max(top, axis=1, keepdims=True)

        def mix(j, carry):
            total, acc = carry
            weights = jnp.exp(scores_ref[j] - top)
            for c in range(0, block, 128):
                total = total + weights[:, c : c + 128]
            values = v_ref[pl.ds(pl.multiple_of((j ^ mine) * block, block), block), :]
            return total, acc + dot(weights.astype(BF), values)

        total, acc = lax.fori_loop(
            0, row_block + 1, mix, (jnp.zeros((block, 128), F32), jnp.zeros((block, PAIR), F32))
        )
        total = jnp.sum(total, axis=1, keepdims=True)
        acc = acc / total
        mixed = acc if mixed is None else jnp.where(mask, acc, mixed)
        logs = jnp.broadcast_to(top + jnp.log(total), (block, 128))
        log_ref[head : head + 1, :] = jnp.transpose(logs)[0:1, :]
    out_ref[...] = mixed.astype(BF)


def attend_forward(place, qkv, pair, starts, block):
    pairs3, length, _ = qkv.shape
    pairs = pairs3 // 3
    blocks = length // block
    return pl.pallas_call(
        functools.partial(forward_kernel, block),
        out_shape=(
            jax.ShapeDtypeStruct((length, PAIR), BF),
            jax.ShapeDtypeStruct((8, length), F32),
        ),
        grid_spec=pltpu.PrefetchScalarGridSpec(
            num_scalar_prefetch=1,
            grid=(blocks,),
            in_specs=[
                pl.BlockSpec((None, block, PAIR), lambda d, place: (pair, d, 0)),
                pl.BlockSpec((None, length, PAIR), lambda d, place: (pairs + pair, 0, 0)),
                pl.BlockSpec((None, length, PAIR), lambda d, place: (2 * pairs + pair, 0, 0)),
                pl.BlockSpec((block, 1), lambda d, place: (d ^ place[0], 0)),
            ],
            out_specs=(
                pl.BlockSpec((block, PAIR), lambda d, place: (d, 0)),
                pl.BlockSpec((8, block), lambda d, place: (0, d)),
            ),
            scratch_shapes=[pltpu.VMEM((blocks, block, block), F32)],
        ),
        compiler_params=pltpu.CompilerParams(vmem_limit_bytes=40 << 20),
        cost_estimate=pl.CostEstimate(flops=20 * length * length * PAIR, bytes_accessed=4 * length * PAIR * 2, transcendentals=length * length),
        name="attend_forward",
    )(place, qkv, qkv, qkv, starts)


def backward_kernel(
    block, blocks, place_ref, q_ref, k_ref, v_ref, do_ref, o_ref, log_ref, start_ref, cos_ref, sin_ref, out_ref, dq_ref, inner_ref
):
    mine = place_ref[0]
    step = pl.program_id(0)
    key_block = step ^ mine
    heads = PAIR // HD

    @pl.when(step == 0)
    def _():
        dq_ref[...] = jnp.zeros_like(dq_ref)
        for b in range(blocks):
            rows = pl.ds(b * block, block)
            product = do_ref[rows, :].astype(F32) * o_ref[rows, :].astype(F32)
            high = product.astype(BF)
            low = (product - high.astype(F32)).astype(BF)
            for head in range(heads):
                ones = head_mask((16, PAIR), head).astype(F32).astype(BF)
                inner = dot(ones, high, NT) + dot(ones, low, NT)
                inner_ref[head : head + 1, rows] = inner[0:1, :]

    here = pl.ds(pl.multiple_of(step * block, block), block)
    keys = k_ref[here, :]
    values = v_ref[here, :]
    dk = jnp.zeros((block, PAIR), F32)
    dv = jnp.zeros((block, PAIR), F32)
    for head in range(heads):
        mask = head_mask(keys.shape, head)
        key = jnp.where(mask, keys * HD**-0.5, jnp.zeros_like(keys))
        value = jnp.where(mask, values, jnp.zeros_like(values))

        def one(i, carry, first):
            dk, dv = carry
            rows = pl.ds(pl.multiple_of((i ^ mine) * block, block), block)
            real = pl.ds(pl.multiple_of(i * block, block), block)
            query = q_ref[rows, :]
            grad = do_ref[rows, :]
            s = dot(key, query, NT)
            row = lax.broadcasted_iota(jnp.int32, s.shape, 0)
            visible = row >= start_ref[0:1, real] - key_block * block
            if first:
                visible &= row <= lax.broadcasted_iota(jnp.int32, s.shape, 1)
            probs = jnp.where(visible, jnp.exp(s - log_ref[head : head + 1, rows]), 0.0)
            grad_probs = dot(value, grad, NT)
            ds = (probs * (grad_probs - inner_ref[head : head + 1, rows])).astype(BF)
            zero = jnp.zeros_like(query)
            dv = dv + dot(probs.astype(BF), jnp.where(mask, grad, zero))
            dk = dk + dot(ds, jnp.where(mask, query, zero))
            dq_ref[rows, :] += dot(ds, key, TN)
            return dk, dv

        dk, dv = one(key_block, (dk, dv), True)
        dk, dv = lax.fori_loop(key_block + 1, blocks, lambda i, carry: one(i, carry, False), (dk, dv))
    real = pl.ds(pl.multiple_of(key_block * block, block), block)
    out_ref[1, here, :] = turn(dk * HD**-0.5, cos_ref[real, :], -sin_ref[real, :]).astype(BF)
    out_ref[2, here, :] = dv.astype(BF)

    @pl.when(step == blocks - 1)
    def _():
        for b in range(blocks):
            rows = pl.ds(b * block, block)
            real = pl.ds(pl.multiple_of((b ^ mine) * block, block), block)
            out_ref[0, rows, :] = turn(dq_ref[rows, :], cos_ref[real, :], -sin_ref[real, :]).astype(BF)


def attend_backward(place, qkv, pair, grad_heads, heads_out, logs, start_row, cosine, sine, block):
    pairs3, length, _ = qkv.shape
    pairs = pairs3 // 3
    blocks = length // block
    whole = lambda d, place: (0, 0)
    return pl.pallas_call(
        functools.partial(backward_kernel, block, blocks),
        out_shape=jax.ShapeDtypeStruct((3, length, PAIR), BF),
        grid_spec=pltpu.PrefetchScalarGridSpec(
            num_scalar_prefetch=1,
            grid=(blocks,),
            in_specs=[
                pl.BlockSpec((None, length, PAIR), lambda d, place: (pair, 0, 0)),
                pl.BlockSpec((None, length, PAIR), lambda d, place: (pairs + pair, 0, 0)),
                pl.BlockSpec((None, length, PAIR), lambda d, place: (2 * pairs + pair, 0, 0)),
                pl.BlockSpec((length, PAIR), whole),
                pl.BlockSpec((length, PAIR), whole),
                pl.BlockSpec((8, length), whole),
                pl.BlockSpec((1, length), whole),
                pl.BlockSpec((length, PAIR), whole),
                pl.BlockSpec((length, PAIR), whole),
            ],
            out_specs=pl.BlockSpec((3, length, PAIR), lambda d, place: (0, 0, 0)),
            scratch_shapes=[pltpu.VMEM((length, PAIR), F32), pltpu.VMEM((8, length), F32)],
        ),
        compiler_params=pltpu.CompilerParams(vmem_limit_bytes=40 << 20),
        cost_estimate=pl.CostEstimate(flops=50 * length * length * PAIR, bytes_accessed=8 * length * PAIR * 2, transcendentals=length * length),
        name="attend_backward",
    )(place, qkv, qkv, qkv, grad_heads, heads_out, logs, start_row, cosine, sine)


def body(block_in, lengths, qkv_weight, out_weight, up_weight, down_weight, norm_gain, norm_bias, cotangent):
    block, row_count, width = block_in.shape
    assert row_count == 1
    ranks = lax.axis_size("tensor")
    length = block * ranks
    local = out_weight.shape[0]
    pairs = local // PAIR
    mine = lax.axis_index("tensor")
    place = mine.astype(jnp.int32).reshape(1)

    residual_in = block_in.reshape(block, width).astype(F32)
    attn_norm, attn_norm_pull = jax.vjp(layer_norm, residual_in, norm_gain[0], norm_bias[0])
    attn_low = attn_norm.astype(BF)
    attn_parts = gather_tensor(attn_low)

    out_late, up_late, down_late, _ = lax.optimization_barrier((out_weight, up_weight, down_weight, attn_parts[ranks // 2]))
    up_parts = gather_tensor(up_late)
    out_parts = gather_tensor(out_late)
    down_parts = gather_tensor(down_late)

    finish = jnp.cumsum(lengths[0])
    begin = finish - lengths[0]
    places = jnp.arange(length, dtype=jnp.int32)
    segment = jnp.sum((places[:, None] >= finish[None, :]).astype(jnp.int32), axis=1)
    picked = segment[:, None] == jnp.arange(lengths.shape[1], dtype=jnp.int32)[None, :]
    starts = jnp.sum(jnp.where(picked, begin[None, :], 0), axis=1)
    position = (places - starts).astype(F32)
    lanes = jnp.arange(PAIR, dtype=jnp.int32)
    inverse = ROPE_BASE ** (-(lanes % (HD // 2)).astype(F32) * 2.0 / HD)
    angles = position[:, None] * inverse
    cosine = jnp.cos(angles)
    sine = jnp.sin(angles) * jnp.where(lanes % HD < HD // 2, -1.0, 1.0).astype(F32)
    start_column = starts.reshape(length, 1)
    start_row = starts.reshape(1, length)

    attn_full = jnp.concatenate(attn_parts, axis=0)
    qkv_swapped = jnp.transpose(qkv_weight, (1, 0, 2))
    qkv = project_qkv(place, attn_full, qkv_swapped, cosine, sine, block)

    heads_parts = [[] for _ in range(ranks)]
    heads_mixed, logs = [], []
    for pair in range(pairs):
        mixed, log_total = attend_forward(place, qkv, pair, start_column, block)
        heads_mixed.append(mixed)
        logs.append(log_total)
        for d in range(ranks):
            piece = mixed[d * block : (d + 1) * block]
            heads_parts[d].append(piece if d == 0 else swap(piece, "tensor", d))
    heads_local = jnp.concatenate([piece for parts in heads_parts for piece in parts], axis=1)

    out_full = jnp.concatenate(out_parts, axis=0)
    attn_proj = dot(heads_local, out_full)
    attn_branch, attn_branch_pull = jax.vjp(layer_norm, attn_proj, norm_gain[1], norm_bias[1])
    middle = residual_in + attn_branch
    mlp_norm, mlp_norm_pull = jax.vjp(layer_norm, middle, norm_gain[2], norm_bias[2])
    mlp_low = mlp_norm.astype(BF)
    mlp_parts = gather_tensor(mlp_low)

    upward = [dot(mlp_low, part) for part in up_parts]
    hidden, gelu_pull = jax.vjp(jax.nn.gelu, upward[0])
    pulls, mlp_proj = [], 0.0
    for d in range(ranks):
        hidden, pull = jax.vjp(jax.nn.gelu, upward[d])
        pulls.append(pull)
        mlp_proj = mlp_proj + dot(hidden.astype(BF), down_parts[d])
    mlp_branch, mlp_branch_pull = jax.vjp(layer_norm, mlp_proj, norm_gain[3], norm_bias[3])
    block_out = (middle + mlp_branch).astype(BF)

    grad_rows = cotangent.reshape(block, width).astype(F32)
    grad_mlp_proj, gain_three, shift_three = mlp_branch_pull(grad_rows)
    grad_mlp_low = grad_mlp_proj.astype(BF)
    grad_mlp_parts = gather_tensor(grad_mlp_low)
    grad_mlp_norm = 0.0
    for d in range(ranks):
        grad_hidden = dot(grad_mlp_low, down_parts[d], NT)
        grad_upward = pulls[d](grad_hidden)[0].astype(BF)
        grad_mlp_norm = grad_mlp_norm + dot(grad_upward, up_parts[d], NT)
    grad_from_norm, gain_two, shift_two = mlp_norm_pull(grad_mlp_norm)
    grad_middle = grad_rows + grad_from_norm
    grad_attn_proj, gain_one, shift_one = attn_branch_pull(grad_middle)
    grad_attn_low = grad_attn_proj.astype(BF)
    grad_heads = dot(grad_attn_low, out_full, NT).astype(BF)

    mlp_full = jnp.concatenate(mlp_parts, axis=0)
    grad_mlp_full = jnp.concatenate(grad_mlp_parts, axis=0)
    upward_own = dot(mlp_full, up_weight)
    hidden_own, gelu_own_pull = jax.vjp(jax.nn.gelu, upward_own)
    grad_hidden_own = dot(grad_mlp_full, down_weight, NT)
    grad_upward_own = gelu_own_pull(grad_hidden_own)[0].astype(BF)
    down_grad = reduce_dp(dot(hidden_own.astype(BF), grad_mlp_full, TN), False)
    up_grad = reduce_dp(dot(mlp_full, grad_upward_own, TN), False)

    out_partial = dot(heads_local, grad_attn_low, TN)
    out_terms = [out_partial[d * local : (d + 1) * local] for d in range(ranks)]
    out_grad = reduce_dp(reduce_scatter_tensor(out_terms), False)

    grad_project, qkv_grads = [], []
    for pair in range(pairs):
        parts = []
        for d in range(ranks):
            column = d * local + pair * PAIR
            piece = grad_heads[:, column : column + PAIR]
            parts.append(piece if d == 0 else swap(piece, "tensor", d))
        got = jnp.concatenate(parts, axis=0)
        grads = attend_backward(place, qkv, pair, got, heads_mixed[pair], logs[pair], start_row, cosine, sine, block)
        grad_project += [grads[c] for c in range(3)]
        wide = jnp.concatenate([grads[c] for c in range(3)], axis=1)
        qkv_grads.append(reduce_dp(dot(attn_full, wide, TN), pair == pairs - 1))
    order = [pair * 3 + c for c in range(3) for pair in range(pairs)]
    grad_wide = jnp.concatenate([grad_project[i] for i in order], axis=1)
    qkv_flat = qkv_weight.reshape(width, 3 * local)
    terms = [
        dot(grad_wide[d * block : (d + 1) * block], qkv_flat, NT) for d in range(ranks)
    ]
    grad_attn_norm = reduce_scatter_tensor(terms)
    grad_from_first, gain_zero, shift_zero = attn_norm_pull(grad_attn_norm)
    input_grad = grad_middle + grad_from_first

    late = sum_all(jnp.stack([gain_zero, shift_zero]))
    early = sum_all(jnp.stack([gain_one, gain_two, gain_three, shift_one, shift_two, shift_three]))
    gain_grad = jnp.concatenate([late[0:1], early[0:3]], axis=0)
    bias_grad = jnp.concatenate([late[1:2], early[3:6]], axis=0)
    qkv_grad = jnp.stack(
        [jnp.concatenate([g[:, c * PAIR : (c + 1) * PAIR] for g in qkv_grads], axis=1) for c in range(3)], axis=1
    )
    return (
        block_out.reshape(block_in.shape),
        input_grad.reshape(block_in.shape),
        qkv_grad,
        out_grad,
        up_grad,
        down_grad,
        gain_grad,
        bias_grad,
    )


def solution(mesh):
    tokens, rows, columns, copied = P("tensor", "dp", None), P("tensor", None), P(None, "tensor"), P()
    heads = P(None, None, "tensor")
    return jax.shard_map(
        body,
        mesh=mesh,
        in_specs=(tokens, P("dp", None), heads, rows, columns, rows, copied, copied, tokens),
        out_specs=(tokens, tokens, heads, rows, columns, rows, copied, copied),
        check_vma=False,
    )
```

```python
import functools

import jax
import jax.numpy as jnp
from jax import lax
from jax.experimental import pallas as pl
from jax.experimental.pallas import tpu as pltpu
from jax.sharding import PartitionSpec as P

HD = 64
PAIR = 128
EPSILON = 1e-05
ROPE_BASE = 10000.0
NEG = -1e30
MESH = pl.DeviceIdType.MESH
BF = jnp.bfloat16
F32 = jnp.float32
NT = (((1,), (1,)), ((), ()))
NN = (((1,), (0,)), ((), ()))
TN = (((0,), (0,)), ((), ()))


def dot(a, b, dims=NN):
    return lax.dot_general(a, b, dims, preferred_element_type=F32)


def layer_norm(values, gain, shift):
    centre = values - jnp.mean(values, axis=-1, keepdims=True)
    spread = jnp.mean(centre * centre, axis=-1, keepdims=True)
    return centre * lax.rsqrt(spread + EPSILON) * gain + shift


def swap(value, axis, offset):
    size = lax.axis_size(axis)
    return lax.ppermute(value, axis, [(i, i ^ offset) for i in range(size)])


def gather_tensor(value):
    parts = [value]
    size = lax.axis_size("tensor")
    step = size // 2
    found = {0: value}
    while step >= 1:
        for place in sorted(found):
            found[place ^ step] = swap(found[place], "tensor", step)
        step //= 2
    parts = [found[d] for d in range(size)]
    return parts


def flip(index, offset):
    bit = 1
    while bit <= offset:
        if offset & bit:
            index = index + bit - 2 * bit * lax.rem(lax.div(index, bit), 2)
        bit *= 2
    return index


def xor(a, b, size):
    total, bit = 0, 1
    while bit < size:
        total = total + bit * lax.rem(lax.div(a, bit) + lax.div(b, bit), 2)
        bit *= 2
    return total


def greet(axes):
    barrier = pltpu.get_barrier_semaphore()
    count = 0
    for axis in axes:
        index = lax.axis_index(axis)
        for d in range(1, lax.axis_size(axis)):
            pl.semaphore_signal(barrier, inc=1, device_id={axis: flip(index, d)}, device_id_type=MESH)
            count += 1
    pl.semaphore_wait(barrier, count)


def tree_sum(parts):
    parts = [part.astype(F32) for part in parts]
    while len(parts) > 1:
        parts = [parts[i] + parts[i + 1] for i in range(0, len(parts), 2)]
    return parts[0]


def push(src, dst, sems, slot, axis, offset):
    return pltpu.make_async_remote_copy(
        src_ref=src,
        dst_ref=dst,
        send_sem=sems.at[0, slot],
        recv_sem=sems.at[1, slot],
        device_id={axis: flip(lax.axis_index(axis), offset)},
        device_id_type=MESH,
    )


def turn(values, cosine, signed_sine):
    lane = lax.broadcasted_iota(jnp.int32, values.shape, 1)
    other = jnp.where(lane % HD < HD // 2, pltpu.roll(values, PAIR - HD // 2, 1), pltpu.roll(values, HD // 2, 1))
    return values * cosine + other * signed_sine


def qkv_kernel(pairs, place_ref, x_ref, w_ref, cos_ref, sin_ref, out_ref):
    x = x_ref[...]
    for part in range(3):
        project = dot(x, w_ref[part])
        for pair in range(pairs):
            piece = project[:, pair * PAIR : (pair + 1) * PAIR]
            if part < 2:
                piece = turn(piece, cos_ref[...], sin_ref[...])
            out_ref[part * pairs + pair] = piece.astype(BF)


def project_qkv(place, tokens, weight, cosine, sine, block):
    length, width = tokens.shape
    columns = weight.shape[2]
    pairs = columns // PAIR
    real = lambda d, place: (d ^ place[0], 0)
    return pl.pallas_call(
        functools.partial(qkv_kernel, pairs),
        out_shape=jax.ShapeDtypeStruct((3 * pairs, length, PAIR), BF),
        grid_spec=pltpu.PrefetchScalarGridSpec(
            num_scalar_prefetch=1,
            grid=(length // block,),
            in_specs=[
                pl.BlockSpec((block, width), lambda d, place: (d, 0)),
                pl.BlockSpec((3, width, columns), lambda d, place: (0, 0, 0)),
                pl.BlockSpec((block, PAIR), real),
                pl.BlockSpec((block, PAIR), real),
            ],
            out_specs=pl.BlockSpec((3 * pairs, block, PAIR), lambda d, place: (0, d, 0)),
        ),
        compiler_params=pltpu.CompilerParams(vmem_limit_bytes=40 << 20),
        cost_estimate=pl.CostEstimate(flops=2 * length * width * 3 * columns, bytes_accessed=2 * length * width, transcendentals=0),
        name="project_qkv",
    )(place, tokens, weight, cosine, sine)


def head_mask(shape, head):
    lane = lax.broadcasted_iota(jnp.int32, shape, 1)
    return lane // HD == head


def forward_kernel(block, place_ref, q_ref, k_ref, v_ref, start_ref, out_ref, log_ref, scores_ref):
    mine = place_ref[0]
    row_block = pl.program_id(0) ^ mine
    queries = q_ref[...] * HD**-0.5
    start = start_ref[...]
    mixed = None
    for head in range(PAIR // HD):
        mask = head_mask(queries.shape, head)
        query = jnp.where(mask, queries, jnp.zeros_like(queries))

        def score(j, top, last):
            keys = k_ref[pl.ds(pl.multiple_of((j ^ mine) * block, block), block), :]
            s = dot(query, keys, NT)
            column = lax.broadcasted_iota(jnp.int32, s.shape, 1)
            visible = column >= start - j * block
            if last:
                visible &= column <= lax.broadcasted_iota(jnp.int32, s.shape, 0)
            s = jnp.where(visible, s, NEG)
            scores_ref[j] = s
            for c in range(0, block, 128):
                top = jnp.maximum(top, s[:, c : c + 128])
            return top

        top = jnp.full((block, 128), NEG, F32)
        top = lax.fori_loop(0, row_block, lambda j, top: score(j, top, False), top)
        top = score(row_block, top, True)
        top = jnp.max(top, axis=1, keepdims=True)

        def mix(j, carry):
            total, acc = carry
            weights = jnp.exp(scores_ref[j] - top)
            for c in range(0, block, 128):
                total = total + weights[:, c : c + 128]
            values = v_ref[pl.ds(pl.multiple_of((j ^ mine) * block, block), block), :]
            return total, acc + dot(weights.astype(BF), values)

        total, acc = lax.fori_loop(
            0, row_block + 1, mix, (jnp.zeros((block, 128), F32), jnp.zeros((block, PAIR), F32))
        )
        total = jnp.sum(total, axis=1, keepdims=True)
        acc = acc / total
        mixed = acc if mixed is None else jnp.where(mask, acc, mixed)
        logs = jnp.broadcast_to(top + jnp.log(total), (block, 128))
        log_ref[head : head + 1, :] = jnp.transpose(logs)[0:1, :]
    out_ref[...] = mixed.astype(BF)


def attend_forward(place, qkv, pair, starts, block):
    pairs3, length, _ = qkv.shape
    pairs = pairs3 // 3
    blocks = length // block
    return pl.pallas_call(
        functools.partial(forward_kernel, block),
        out_shape=(
            jax.ShapeDtypeStruct((length, PAIR), BF),
            jax.ShapeDtypeStruct((8, length), F32),
        ),
        grid_spec=pltpu.PrefetchScalarGridSpec(
            num_scalar_prefetch=1,
            grid=(blocks,),
            in_specs=[
                pl.BlockSpec((None, block, PAIR), lambda d, place: (pair, d, 0)),
                pl.BlockSpec((None, length, PAIR), lambda d, place: (pairs + pair, 0, 0)),
                pl.BlockSpec((None, length, PAIR), lambda d, place: (2 * pairs + pair, 0, 0)),
                pl.BlockSpec((block, 1), lambda d, place: (d ^ place[0], 0)),
            ],
            out_specs=(
                pl.BlockSpec((block, PAIR), lambda d, place: (d, 0)),
                pl.BlockSpec((8, block), lambda d, place: (0, d)),
            ),
            scratch_shapes=[pltpu.VMEM((blocks, block, block), F32)],
        ),
        compiler_params=pltpu.CompilerParams(vmem_limit_bytes=40 << 20),
        cost_estimate=pl.CostEstimate(flops=20 * length * length * PAIR, bytes_accessed=4 * length * PAIR * 2, transcendentals=length * length),
        name="attend_forward",
    )(place, qkv, qkv, qkv, starts)


def backward_kernel(
    block, blocks, pairs, chunks, *refs
):
    (qkv_ref, gh_ref, o_ref, log_ref, start_ref, cos_ref, sin_ref, shared_ref, *refs) = refs
    terms, refs = refs[: chunks - 1], refs[chunks - 1 :]
    (out_ref, *refs) = refs
    pieces, refs = refs[:chunks], refs[chunks:]
    dq_ref, inner_ref, do_ref, *refs = refs
    got_x, refs = refs[:chunks], refs[chunks:]
    half, refs = refs[:chunks], refs[chunks:]
    got_z, refs = refs[:chunks], refs[chunks:]
    got_core, core_sum, got_y, own_ref, head_sems, x_sems, z_sems, core_sems, y_sems = refs
    terms = [*terms, own_ref]

    mine = lax.axis_index("tensor")
    rank = lax.axis_index("dp")
    group = lax.axis_size("dp") // 2
    x_bit, z_place = lax.rem(rank, 2), lax.div(rank, 2)
    heads = PAIR // HD
    greet(("tensor", "dp"))

    head_copies = {}
    for pair in range(pairs):
        for d in range(1, blocks):
            copy = push(
                gh_ref.at[d * pairs + pair], do_ref.at[pair, d], head_sems, pair * (blocks - 1) + d - 1, "tensor", d
            )
            copy.start()
            head_copies[pair, d] = copy
    core_copies = [
        push(shared_ref.at[d + 1], got_core.at[d // 2], core_sems, d // 2, "tensor", 1) for d in range(0, blocks, 2)
    ]
    y_copies = [
        push(core_sum.at[h], got_y.at[h - 1], y_sems, h - 1, "tensor", 2 * h) for h in range(1, blocks // 2)
    ]
    x_copies = [push(terms[c].at[1 - x_bit], got_x[c], x_sems, c, "dp", 1) for c in range(chunks)]
    for copy in [*core_copies, *x_copies[:-1]]:
        copy.start()
    z_copies = {}
    for c in range(chunks):
        for d in range(1, group):
            z_copies[c, d] = push(
                half[c].at[xor(z_place, d, group)], got_z[c].at[d - 1], z_sems, c * (group - 1) + d - 1, "dp", 2 * d
            )

    def halve(c):
        x_copies[c].wait_recv()
        for g in range(group):
            half[c][g] = (terms[c][x_bit, g].astype(F32) + got_x[c][g].astype(F32)).astype(BF)
        for d in range(1, group):
            z_copies[c, d].start()

    def pair_up():
        for h in range(blocks // 2):
            core_copies[h].wait_recv()
            core_sum[h] = (shared_ref[2 * h].astype(F32) + got_core[h].astype(F32)).astype(BF)
        for copy in y_copies:
            copy.start()

    def settle():
        total = core_sum[0].astype(F32)
        for h in range(1, blocks // 2):
            y_copies[h - 1].wait_recv()
            total = total + got_y[h - 1].astype(F32)
        own_ref[...] = total.astype(BF)
        x_copies[-1].start()

    for pair in range(pairs):
        do_ref[pair, 0] = gh_ref[pair]

    def prepare(pair):
        for d in range(1, blocks):
            head_copies[pair, d].wait_recv()
        dq_ref[...] = jnp.zeros_like(dq_ref)
        for b in range(blocks):
            rows = pl.ds(b * block, block)
            product = do_ref[pair, b].astype(F32) * o_ref[pair, rows, :].astype(F32)
            high = product.astype(BF)
            low = (product - high.astype(F32)).astype(BF)
            for head in range(heads):
                ones = head_mask((16, PAIR), head).astype(F32).astype(BF)
                inner = dot(ones, high, NT) + dot(ones, low, NT)
                inner_ref[head : head + 1, rows] = inner[0:1, :]

    def unit(pair, key_block):
        slot = xor(key_block, mine, blocks)
        here = pl.ds(pl.multiple_of(slot * block, block), block)
        keys = qkv_ref[pairs + pair, here, :]
        values = qkv_ref[2 * pairs + pair, here, :]
        dk = jnp.zeros((block, PAIR), F32)
        dv = jnp.zeros((block, PAIR), F32)
        for head in range(heads):
            mask = head_mask(keys.shape, head)
            key = jnp.where(mask, keys * HD**-0.5, jnp.zeros_like(keys))
            value = jnp.where(mask, values, jnp.zeros_like(values))

            def one(i, carry, first):
                dk, dv = carry
                place = xor(i, mine, blocks)
                rows = pl.ds(pl.multiple_of(place * block, block), block)
                real = pl.ds(pl.multiple_of(i * block, block), block)
                query = qkv_ref[pair, rows, :]
                grad = do_ref[pair, place]
                s = dot(key, query, NT)
                row = lax.broadcasted_iota(jnp.int32, s.shape, 0)
                visible = row >= start_ref[0:1, real] - key_block * block
                if first:
                    visible &= row <= lax.broadcasted_iota(jnp.int32, s.shape, 1)
                probs = jnp.where(visible, jnp.exp(s - log_ref[pair, head : head + 1, rows]), 0.0)
                grad_probs = dot(value, grad, NT)
                ds = (probs * (grad_probs - inner_ref[head : head + 1, rows])).astype(BF)
                zero = jnp.zeros_like(query)
                dv = dv + dot(probs.astype(BF), jnp.where(mask, grad, zero))
                dk = dk + dot(ds, jnp.where(mask, query, zero))
                dq_ref[rows, :] += dot(ds, key, TN)
                return dk, dv

            dk, dv = one(key_block, (dk, dv), True)
            dk, dv = lax.fori_loop(key_block + 1, blocks, lambda i, carry: one(i, carry, False), (dk, dv))
        real = pl.ds(pl.multiple_of(key_block * block, block), block)
        out_ref[pairs + pair, here, :] = turn(dk * HD**-0.5, cos_ref[real, :], -sin_ref[real, :]).astype(BF)
        out_ref[2 * pairs + pair, here, :] = dv.astype(BF)

    def finish(pair):
        for b in range(blocks):
            rows = pl.ds(b * block, block)
            real = pl.ds(pl.multiple_of(flip(mine, b) * block, block), block)
            out_ref[pair, rows, :] = turn(dq_ref[rows, :], cos_ref[real, :], -sin_ref[real, :]).astype(BF)

    slots = pairs * blocks

    @pl.loop(0, slots)
    def _(u):
        pair, key_block = lax.div(u, blocks), lax.rem(u, blocks)
        for p in range(pairs):
            pl.when(u == p * blocks)(functools.partial(prepare, p))
        unit(pair, key_block)
        pl.when(key_block == blocks - 1)(functools.partial(finish, pair))
        pl.when(u == 0)(pair_up)
        pl.when(u == slots // 2)(settle)
        for c in range(chunks):
            pl.when(u == min(slots - 1, 2 * c + 1))(functools.partial(halve, c))

    for c in range(chunks):
        for d in range(1, group):
            z_copies[c, d].wait_recv()
        parts = [half[c][z_place]] + [got_z[c][d] for d in range(group - 1)]
        pieces[c][...] = tree_sum(parts).astype(BF)
    for copy in [*head_copies.values(), *core_copies, *y_copies, *x_copies, *z_copies.values()]:
        copy.wait_send()


def attend_backward(qkv, grad_heads, heads_out, logs, start_row, cosine, sine, shared, terms, block):
    pairs3, length, _ = qkv.shape
    pairs = pairs3 // 3
    blocks = length // block
    group = terms[0].shape[1]
    vmem = pl.BlockSpec(memory_space=pltpu.VMEM)
    inner = [term.shape[1:] for term in terms] + [shared.shape[2:]]
    chunks = len(inner)
    copies = pltpu.SemaphoreType.DMA
    return pl.pallas_call(
        functools.partial(backward_kernel, block, blocks, pairs, chunks),
        out_shape=[jax.ShapeDtypeStruct((pairs3, length, PAIR), BF)]
        + [jax.ShapeDtypeStruct(shape[1:], BF) for shape in inner],
        in_specs=[vmem] * (8 + len(terms)),
        out_specs=[vmem] * (1 + chunks),
        scratch_shapes=[
            pltpu.VMEM((length, PAIR), F32),
            pltpu.VMEM((8, length), F32),
            pltpu.VMEM((pairs, blocks, block, PAIR), BF),
            *[pltpu.VMEM(shape, BF) for shape in inner],
            *[pltpu.VMEM(shape, BF) for shape in inner],
            *[pltpu.VMEM((group - 1, *shape[1:]), BF) for shape in inner],
            pltpu.VMEM((blocks // 2, *shared.shape[1:]), BF),
            pltpu.VMEM((blocks // 2, *shared.shape[1:]), BF),
            pltpu.VMEM((blocks // 2 - 1, *shared.shape[1:]), BF),
            pltpu.VMEM(shared.shape[1:], BF),
            copies((2, pairs * (blocks - 1))),
            copies((2, chunks)),
            copies((2, chunks * (group - 1))),
            copies((2, blocks // 2)),
            copies((2, blocks // 2 - 1)),
        ],
        compiler_params=pltpu.CompilerParams(vmem_limit_bytes=56 << 20, collective_id=0, has_side_effects=True),
        cost_estimate=pl.CostEstimate(flops=100 * length * length * PAIR, bytes_accessed=16 * length * PAIR * 2, transcendentals=length * length),
        name="attend_backward",
    )(qkv, grad_heads, heads_out, logs, start_row, cosine, sine, shared, *terms)


def last_kernel(ranks, pieces_count, *refs):
    x_ref, gain_ref, rest_ref, early_ref, tokens_ref, qkv_ref, *refs = refs
    pieces, refs = refs[:pieces_count], refs[pieces_count:]
    input_ref, sums_ref, qkv_out, *refs = refs
    outs, refs = refs[:pieces_count], refs[pieces_count:]
    (got_core, token_sum, got_y, terms, got_t, sum_t, got_d, got_x, half, got_z, own_piece, *refs) = refs
    (core_sems, y_sems, t_sems, d_sems, x_sems, z_sems, zg_sems, xg_sems) = refs
    rank = lax.axis_index("dp")
    group = lax.axis_size("dp") // 2
    x_bit, z_place = lax.rem(rank, 2), lax.div(rank, 2)
    started = []

    def start(copy):
        copy.start()
        started.append(copy)
        return copy

    greet(("tensor", "dp"))
    core = [
        start(push(tokens_ref.at[d + 1], got_core.at[d // 2], core_sems, d // 2, "tensor", 1)) for d in range(0, ranks, 2)
    ]
    x_copy = start(push(qkv_ref.at[1 - x_bit], got_x, x_sems, 0, "dp", 1))
    gathers = {}

    def spread(k, src, out):
        out[x_bit, z_place] = src[...]
        for d in range(1, group):
            gathers[k, d] = start(
                push(src, out.at[x_bit, z_place], zg_sems, k * (group - 1) + d - 1, "dp", 2 * d)
            )

    def share(k, out):
        for d in range(1, group):
            gathers[k, d].wait_recv()
        return start(push(out.at[x_bit], out.at[x_bit], xg_sems, k, "dp", 1))

    for k in range(pieces_count):
        spread(k, pieces[k], outs[k])

    for d in range(0, ranks, 2):
        core[d // 2].wait_recv()
        token_sum[d // 2] = (tokens_ref[d].astype(F32) + got_core[d // 2].astype(F32)).astype(BF)
    ys = [start(push(token_sum.at[h], got_y.at[h - 1], y_sems, h - 1, "tensor", 2 * h)) for h in range(1, ranks // 2)]

    x_copy.wait_recv()
    for g in range(group):
        half[g] = (qkv_ref[x_bit, g].astype(F32) + got_x[g].astype(F32)).astype(BF)
    zs = [
        start(push(half.at[xor(z_place, d, group)], got_z.at[d - 1], z_sems, d - 1, "dp", 2 * d)) for d in range(1, group)
    ]

    for copy in ys:
        copy.wait_recv()
    rows = 64
    count = x_ref.shape[0] // rows
    gain = gain_ref[...]

    def norm(r, carry):
        gain_term, shift_term = carry
        at = pl.ds(pl.multiple_of(r * rows, rows), rows)
        grad = token_sum[0, at, :].astype(F32)
        for h in range(ranks // 2 - 1):
            grad = grad + got_y[h, at, :].astype(F32)
        x = x_ref[at, :].astype(F32)
        centre = x - jnp.mean(x, axis=-1, keepdims=True)
        scale = lax.rsqrt(jnp.mean(centre * centre, axis=-1, keepdims=True) + EPSILON)
        unit = centre * scale
        inside = grad * gain
        first = jnp.mean(inside, axis=-1, keepdims=True)
        second = jnp.mean(inside * unit, axis=-1, keepdims=True)
        input_ref[at, :] = rest_ref[at, :] + scale * (inside - first - unit * second)
        return (
            gain_term + jnp.sum(grad * unit, axis=0, keepdims=True),
            shift_term + jnp.sum(grad, axis=0, keepdims=True),
        )

    zero = jnp.zeros(gain.shape, F32)
    gain_term, shift_term = lax.fori_loop(0, count, norm, (zero, zero))
    terms[...] = early_ref[...]
    terms[0:1, :] = gain_term
    terms[4:5, :] = shift_term
    ts = [start(push(terms, got_t.at[d - 1], t_sems, d - 1, "tensor", d)) for d in range(1, ranks)]
    xs = [share(k, outs[k]) for k in range(pieces_count)]
    for copy in zs:
        copy.wait_recv()
    own_piece[...] = tree_sum([half[z_place]] + [got_z[d] for d in range(group - 1)]).astype(BF)
    spread(pieces_count, own_piece, qkv_out)
    for copy in ts:
        copy.wait_recv()
    sum_t[...] = tree_sum([terms[...]] + [got_t[d] for d in range(ranks - 1)])
    ds = [start(push(sum_t, got_d.at[d - 1], d_sems, d - 1, "dp", d)) for d in range(1, 2 * group)]
    xs.append(share(pieces_count, qkv_out))
    for copy in ds:
        copy.wait_recv()
    sums_ref[...] = tree_sum([sum_t[...]] + [got_d[d] for d in range(2 * group - 1)])
    for copy in xs:
        copy.wait_recv()
    for copy in started:
        copy.wait_send()


def last_stage(block_rows, gain, rest, early, token_terms, qkv_terms, pieces):
    block, width = block_rows.shape
    ranks = token_terms.shape[0]
    group = qkv_terms.shape[1]
    vmem = pl.BlockSpec(memory_space=pltpu.VMEM)
    copies = pltpu.SemaphoreType.DMA
    count = len(pieces)
    return pl.pallas_call(
        functools.partial(last_kernel, ranks, count),
        out_shape=[
            jax.ShapeDtypeStruct((block, width), F32),
            jax.ShapeDtypeStruct((8, width), F32),
            jax.ShapeDtypeStruct(qkv_terms.shape, BF),
        ]
        + [jax.ShapeDtypeStruct((2, group, *piece.shape), BF) for piece in pieces],
        in_specs=[vmem] * (6 + count),
        out_specs=[vmem] * (3 + count),
        scratch_shapes=[
            pltpu.VMEM((ranks // 2, block, width), BF),
            pltpu.VMEM((ranks // 2, block, width), BF),
            pltpu.VMEM((ranks // 2 - 1, block, width), BF),
            pltpu.VMEM((8, width), F32),
            pltpu.VMEM((ranks - 1, 8, width), F32),
            pltpu.VMEM((8, width), F32),
            pltpu.VMEM((2 * group - 1, 8, width), F32),
            pltpu.VMEM(qkv_terms.shape[1:], BF),
            pltpu.VMEM(qkv_terms.shape[1:], BF),
            pltpu.VMEM((group - 1, *qkv_terms.shape[2:]), BF),
            pltpu.VMEM(qkv_terms.shape[2:], BF),
            copies((2, ranks // 2)),
            copies((2, ranks // 2 - 1)),
            copies((2, ranks - 1)),
            copies((2, 2 * group - 1)),
            copies((2, 1)),
            copies((2, group - 1)),
            copies((2, (count + 1) * (group - 1))),
            copies((2, count + 1)),
        ],
        compiler_params=pltpu.CompilerParams(vmem_limit_bytes=56 << 20, collective_id=1, has_side_effects=True),
        name="last_stage",
    )(block_rows, gain, rest, early, token_terms, qkv_terms, *pieces)


def body(block_in, lengths, qkv_weight, out_weight, up_weight, down_weight, norm_gain, norm_bias, cotangent):
    block, row_count, width = block_in.shape
    assert row_count == 1
    ranks = lax.axis_size("tensor")
    length = block * ranks
    local = out_weight.shape[0]
    pairs = local // PAIR
    mine = lax.axis_index("tensor")
    place = mine.astype(jnp.int32).reshape(1)

    residual_in = block_in.reshape(block, width).astype(F32)
    attn_norm, attn_norm_pull = jax.vjp(layer_norm, residual_in, norm_gain[0], norm_bias[0])
    attn_low = attn_norm.astype(BF)
    attn_parts = gather_tensor(attn_low)

    out_late, up_late, down_late, _ = lax.optimization_barrier((out_weight, up_weight, down_weight, attn_parts[ranks // 2]))
    up_parts = gather_tensor(up_late)
    out_parts = gather_tensor(out_late)
    down_parts = gather_tensor(down_late)

    finish = jnp.cumsum(lengths[0])
    begin = finish - lengths[0]
    places = jnp.arange(length, dtype=jnp.int32)
    segment = jnp.sum((places[:, None] >= finish[None, :]).astype(jnp.int32), axis=1)
    picked = segment[:, None] == jnp.arange(lengths.shape[1], dtype=jnp.int32)[None, :]
    starts = jnp.sum(jnp.where(picked, begin[None, :], 0), axis=1)
    position = (places - starts).astype(F32)
    lanes = jnp.arange(PAIR, dtype=jnp.int32)
    inverse = ROPE_BASE ** (-(lanes % (HD // 2)).astype(F32) * 2.0 / HD)
    angles = position[:, None] * inverse
    cosine = jnp.cos(angles)
    sine = jnp.sin(angles) * jnp.where(lanes % HD < HD // 2, -1.0, 1.0).astype(F32)
    start_column = starts.reshape(length, 1)
    start_row = starts.reshape(1, length)

    attn_full = jnp.concatenate(attn_parts, axis=0)
    qkv_swapped = jnp.transpose(qkv_weight, (1, 0, 2))
    qkv = project_qkv(place, attn_full, qkv_swapped, cosine, sine, block)

    heads_parts = [[] for _ in range(ranks)]
    heads_mixed, logs = [], []
    for pair in range(pairs):
        mixed, log_total = attend_forward(place, qkv, pair, start_column, block)
        heads_mixed.append(mixed)
        logs.append(log_total)
        for d in range(ranks):
            piece = mixed[d * block : (d + 1) * block]
            heads_parts[d].append(piece if d == 0 else swap(piece, "tensor", d))
    heads_local = jnp.concatenate([piece for parts in heads_parts for piece in parts], axis=1)

    out_full = jnp.concatenate(out_parts, axis=0)
    attn_proj = dot(heads_local, out_full)
    attn_branch, attn_branch_pull = jax.vjp(layer_norm, attn_proj, norm_gain[1], norm_bias[1])
    middle = residual_in + attn_branch
    mlp_norm, mlp_norm_pull = jax.vjp(layer_norm, middle, norm_gain[2], norm_bias[2])
    mlp_low = mlp_norm.astype(BF)
    mlp_parts = gather_tensor(mlp_low)

    upward = [dot(mlp_low, part) for part in up_parts]
    hidden, gelu_pull = jax.vjp(jax.nn.gelu, upward[0])
    pulls, mlp_proj = [], 0.0
    for d in range(ranks):
        hidden, pull = jax.vjp(jax.nn.gelu, upward[d])
        pulls.append(pull)
        mlp_proj = mlp_proj + dot(hidden.astype(BF), down_parts[d])
    mlp_branch, mlp_branch_pull = jax.vjp(layer_norm, mlp_proj, norm_gain[3], norm_bias[3])
    block_out = (middle + mlp_branch).astype(BF)

    grad_rows = cotangent.reshape(block, width).astype(F32)
    grad_mlp_proj, gain_three, shift_three = mlp_branch_pull(grad_rows)
    grad_mlp_low = grad_mlp_proj.astype(BF)
    grad_mlp_parts = gather_tensor(grad_mlp_low)
    grad_mlp_norm = 0.0
    for d in range(ranks):
        grad_hidden = dot(grad_mlp_low, down_parts[d], NT)
        grad_upward = pulls[d](grad_hidden)[0].astype(BF)
        grad_mlp_norm = grad_mlp_norm + dot(grad_upward, up_parts[d], NT)
    grad_from_norm, gain_two, shift_two = mlp_norm_pull(grad_mlp_norm)
    grad_middle = grad_rows + grad_from_norm
    grad_attn_proj, gain_one, shift_one = attn_branch_pull(grad_middle)
    grad_attn_low = grad_attn_proj.astype(BF)
    grad_heads = dot(grad_attn_low, out_full, NT).astype(BF)

    mlp_full = jnp.concatenate(mlp_parts, axis=0)
    grad_mlp_full = jnp.concatenate(grad_mlp_parts, axis=0)
    upward_own = dot(mlp_full, up_weight)
    hidden_own, gelu_own_pull = jax.vjp(jax.nn.gelu, upward_own)
    grad_hidden_own = dot(grad_mlp_full, down_weight, NT)
    grad_upward_own = gelu_own_pull(grad_hidden_own)[0].astype(BF)
    group = lax.axis_size("dp") // 2
    down_term = dot(hidden_own.astype(BF), grad_mlp_full, TN).astype(BF)
    up_term = dot(mlp_full, grad_upward_own, TN).astype(BF)

    out_partial = dot(heads_local, grad_attn_low, TN).astype(BF)
    shared = out_partial.reshape(ranks, 2, group, local // (2 * group), width)
    terms = []
    half_columns = width // 2
    for term in (down_term, up_term):
        cut = term.reshape(2, group, term.shape[0] // (2 * group), width)
        terms += [cut[..., :half_columns], cut[..., half_columns:]]

    grad_parts = jnp.stack(
        [grad_heads[:, i * PAIR : (i + 1) * PAIR] for i in range(width // PAIR)], axis=0
    )
    grads, *pieces = attend_backward(
        qkv, grad_parts, jnp.stack(heads_mixed), jnp.stack(logs), start_row, cosine, sine, shared, terms, block
    )
    wide = jnp.concatenate([grads[i] for i in range(3 * pairs)], axis=1)
    qkv_flat = qkv_weight.reshape(width, 3 * local)
    token_terms = dot(wide, qkv_flat, NT).astype(BF).reshape(ranks, block, width)
    qkv_term = dot(attn_full, wide, TN).astype(BF).reshape(2, group, width // (2 * group), 3 * local)
    early = jnp.stack([gain_one, gain_one, gain_two, gain_three, shift_one, shift_one, shift_two, shift_three])
    input_grad, sums, qkv_sum, *wholes = last_stage(
        block_in.reshape(block, width), norm_gain[0:1], grad_middle, early, token_terms, qkv_term, pieces
    )
    down_grad, up_grad = [
        jnp.concatenate([left.reshape(-1, half_columns), right.reshape(-1, half_columns)], axis=1).astype(F32)
        for left, right in (wholes[0:2], wholes[2:4])
    ]
    qkv_grad = qkv_sum.reshape(width, 3, local).astype(F32)
    gain_grad, bias_grad = sums[0:4], sums[4:8]
    out_grad = wholes[4].reshape(local, width).astype(F32)
    return (
        block_out.reshape(block_in.shape),
        input_grad.reshape(block_in.shape),
        qkv_grad,
        out_grad,
        up_grad,
        down_grad,
        gain_grad,
        bias_grad,
    )


def solution(mesh):
    tokens, rows, columns, copied = P("tensor", "dp", None), P("tensor", None), P(None, "tensor"), P()
    heads = P(None, None, "tensor")
    return jax.shard_map(
        body,
        mesh=mesh,
        in_specs=(tokens, P("dp", None), heads, rows, columns, rows, copied, copied, tokens),
        out_specs=(tokens, tokens, heads, rows, columns, rows, copied, copied),
        check_vma=False,
    )
```

```python
import functools

import jax
import jax.numpy as jnp
from jax import lax
from jax.experimental import pallas as pl
from jax.experimental.pallas import tpu as pltpu
from jax.sharding import PartitionSpec as P

HD = 64
PAIR = 128
EPSILON = 1e-05
ROPE_BASE = 10000.0
NEG = -1e30
MESH = pl.DeviceIdType.MESH
BF = jnp.bfloat16
F32 = jnp.float32
NT = (((1,), (1,)), ((), ()))
NN = (((1,), (0,)), ((), ()))
TN = (((0,), (0,)), ((), ()))


def dot(a, b, dims=NN):
    return lax.dot_general(a, b, dims, preferred_element_type=F32)


def layer_norm(values, gain, shift):
    centre = values - jnp.mean(values, axis=-1, keepdims=True)
    spread = jnp.mean(centre * centre, axis=-1, keepdims=True)
    return centre * lax.rsqrt(spread + EPSILON) * gain + shift


def swap(value, axis, offset):
    size = lax.axis_size(axis)
    return lax.ppermute(value, axis, [(i, i ^ offset) for i in range(size)])


def gather_tensor(value):
    parts = [value]
    size = lax.axis_size("tensor")
    step = size // 2
    found = {0: value}
    while step >= 1:
        for place in sorted(found):
            found[place ^ step] = swap(found[place], "tensor", step)
        step //= 2
    parts = [found[d] for d in range(size)]
    return parts


def flip(index, offset):
    bit = 1
    while bit <= offset:
        if offset & bit:
            index = index + bit - 2 * bit * lax.rem(lax.div(index, bit), 2)
        bit *= 2
    return index


def xor(a, b, size):
    total, bit = 0, 1
    while bit < size:
        total = total + bit * lax.rem(lax.div(a, bit) + lax.div(b, bit), 2)
        bit *= 2
    return total


def greet(axes):
    barrier = pltpu.get_barrier_semaphore()
    count = 0
    for axis in axes:
        index = lax.axis_index(axis)
        for d in range(1, lax.axis_size(axis)):
            pl.semaphore_signal(barrier, inc=1, device_id={axis: flip(index, d)}, device_id_type=MESH)
            count += 1
    pl.semaphore_wait(barrier, count)


def tree_sum(parts):
    parts = [part.astype(F32) for part in parts]
    while len(parts) > 1:
        parts = [parts[i] + parts[i + 1] for i in range(0, len(parts), 2)]
    return parts[0]


def push(src, dst, sems, slot, axis, offset):
    return pltpu.make_async_remote_copy(
        src_ref=src,
        dst_ref=dst,
        send_sem=sems.at[0, slot],
        recv_sem=sems.at[1, slot],
        device_id={axis: flip(lax.axis_index(axis), offset)},
        device_id_type=MESH,
    )


def turn(values, cosine, signed_sine):
    lane = lax.broadcasted_iota(jnp.int32, values.shape, 1)
    other = jnp.where(lane % HD < HD // 2, pltpu.roll(values, PAIR - HD // 2, 1), pltpu.roll(values, HD // 2, 1))
    return values * cosine + other * signed_sine


def head_mask(shape, head):
    lane = lax.broadcasted_iota(jnp.int32, shape, 1)
    return lane // HD == head


def forward_kernel(block, ranks, pairs, chunks, *refs):
    x_ref, gain_ref, shift_ref, w_ref, cos_ref, sin_ref, start_ref, *refs = refs
    weights, refs = refs[:3], refs[3:]
    qkv_ref, attn_ref, mixed_ref, log_ref, heads_ref, *refs = refs
    rests, refs = refs[:3], refs[3:]
    scores_ref, attn_sems, head_sems, own_sems, y_sems, z_sems, x_sems, core_sems = refs

    mine = lax.axis_index("tensor")
    rank = lax.axis_index("dp")
    group = lax.axis_size("dp") // 2
    x_bit, z_place = lax.rem(rank, 2), lax.div(rank, 2)
    length = block * ranks
    started = []

    def start(copy):
        copy.start()
        started.append(copy)
        return copy

    def cut(array, c, *lead):
        at, (_, low, size) = array.at, chunks[c]
        return at[(*lead, slice(None), pl.ds(low, size))]

    def every(array, c, *lead):
        at, (_, low, size) = array.at, chunks[c]
        return at[(*lead, slice(None), slice(None), pl.ds(low, size))]

    def rest(c):
        return rests[chunks[c][0]]

    y_copies = [
        push(
            cut(weights[chunks[c][0]], c, x_bit, z_place), cut(rest(c), c, 1, x_bit, z_place), y_sems, c, "tensor", 2
        )
        for c in range(len(chunks))
    ]
    z_copies = [
        [
            push(
                cut(rest(c), c, 1, x_bit, z_place),
                cut(rest(c), c, 1, x_bit, z_place),
                z_sems,
                c * (group - 1) + d - 1,
                "dp",
                2 * d,
            )
            for d in range(1, group)
        ]
        for c in range(len(chunks))
    ]
    x_copies = [
        push(every(rest(c), c, 1, x_bit), every(rest(c), c, 1, x_bit), x_sems, c, "dp", 1) for c in range(len(chunks))
    ]
    core_copies = [
        push(
            rest(c).at[1, :, :, :, pl.ds(chunks[c][1], chunks[c][2])],
            rest(c).at[2, :, :, :, pl.ds(chunks[c][1], chunks[c][2])],
            core_sems,
            c,
            "tensor",
            1,
        )
        for c in range(len(chunks))
    ]
    own_copies = [push(weights[a], rests[a].at[0], own_sems, a, "tensor", 1) for a in range(3)]

    def to_z(c):
        y_copies[c].wait_recv()
        for copy in z_copies[c]:
            copy.start()

    def to_x(c):
        for copy in z_copies[c]:
            copy.wait_recv()
        x_copies[c].start()

    def to_core(c):
        x_copies[c].wait_recv()
        core_copies[c].start()

    greet(("tensor", "dp"))
    early = len(chunks) - 2
    for c in range(early):
        y_copies[c].start()

    strips = 4
    strip = block // strips
    gain, shift = gain_ref[...], shift_ref[...]
    across, beside, onward = [], [], []
    for q in range(strips):

        @pl.loop(0, strip // 64)
        def _(r):
            at = pl.ds(pl.multiple_of(q * strip + r * 64, 64), 64)
            attn_ref[0, at, :] = layer_norm(x_ref[at, :].astype(F32), gain, shift).astype(BF)

        at = pl.ds(q * strip, strip)
        across.append(start(push(attn_ref.at[0, at], attn_ref.at[2, at], attn_sems, q, "tensor", 2)))
        beside.append(start(push(attn_ref.at[0, at], attn_ref.at[1, at], attn_sems, strips + q, "tensor", 1)))
        onward.append(push(attn_ref.at[2, at], attn_ref.at[3, at], attn_sems, 2 * strips + q, "tensor", 1))

    def middle():
        for c in range(early):
            to_z(c)
        for q in range(strips):
            across[q].wait_recv()
            onward[q].start()
        for c in range(early, len(chunks)):
            y_copies[c].start()
        for copy in own_copies:
            copy.start()
        for c in range(early - 1):
            to_x(c)

    def beside_here():
        for copy in beside:
            copy.wait_recv()

    def onward_here():
        for copy in onward:
            copy.wait_recv()

    @pl.loop(0, ranks)
    def _(d):
        pl.when(d == 1)(beside_here)
        pl.when(d == 2)(middle)
        pl.when(d == 3)(onward_here)
        x = attn_ref[d]
        rows = pl.ds(pl.multiple_of(d * block, block), block)
        real = pl.ds(pl.multiple_of(xor(d, mine, ranks) * block, block), block)
        for part in range(3):
            project = dot(x, w_ref[part])
            for pair in range(pairs):
                piece = project[:, pair * PAIR : (pair + 1) * PAIR]
                if part < 2:
                    piece = turn(piece, cos_ref[real, :], sin_ref[real, :])
                qkv_ref[part * pairs + pair, rows, :] = piece.astype(BF)

    def unit(pair, d):
        row_block = xor(d, mine, ranks)
        rows = pl.ds(pl.multiple_of(d * block, block), block)
        queries = qkv_ref[pair, rows, :] * HD**-0.5
        begin = start_ref[pl.ds(pl.multiple_of(row_block * block, block), block), :]
        mixed = None
        for head in range(PAIR // HD):
            mask = head_mask(queries.shape, head)
            query = jnp.where(mask, queries, jnp.zeros_like(queries))

            def score(j, top, last):
                at = pl.ds(pl.multiple_of(xor(j, mine, ranks) * block, block), block)
                s = dot(query, qkv_ref[pairs + pair, at, :], NT)
                column = lax.broadcasted_iota(jnp.int32, s.shape, 1)
                visible = column >= begin - j * block
                if last:
                    visible &= column <= lax.broadcasted_iota(jnp.int32, s.shape, 0)
                s = jnp.where(visible, s, NEG)
                scores_ref[j] = s
                for c in range(0, block, 128):
                    top = jnp.maximum(top, s[:, c : c + 128])
                return top

            top = jnp.full((block, 128), NEG, F32)
            top = lax.fori_loop(0, row_block, lambda j, top: score(j, top, False), top)
            top = score(row_block, top, True)
            top = jnp.max(top, axis=1, keepdims=True)

            def mix(j, carry):
                total, acc = carry
                shares = jnp.exp(scores_ref[j] - top)
                for c in range(0, block, 128):
                    total = total + shares[:, c : c + 128]
                at = pl.ds(pl.multiple_of(xor(j, mine, ranks) * block, block), block)
                return total, acc + dot(shares.astype(BF), qkv_ref[2 * pairs + pair, at, :])

            total, acc = lax.fori_loop(
                0, row_block + 1, mix, (jnp.zeros((block, 128), F32), jnp.zeros((block, PAIR), F32))
            )
            total = jnp.sum(total, axis=1, keepdims=True)
            acc = acc / total
            mixed = acc if mixed is None else jnp.where(mask, acc, mixed)
            logs = jnp.broadcast_to(top + jnp.log(total), (block, 128))
            log_ref[pair, head : head + 1, rows] = jnp.transpose(logs)[0:1, :]
        mixed_ref[pair, rows, :] = mixed.astype(BF)

    def head_copy(pair, d):
        slot = d * pairs + pair
        return pltpu.make_async_remote_copy(
            src_ref=mixed_ref.at[pair, pl.ds(pl.multiple_of(d * block, block), block)],
            dst_ref=heads_ref.at[slot],
            send_sem=head_sems.at[0, slot],
            recv_sem=head_sems.at[1, slot],
            device_id={"tensor": xor(mine, d, ranks)},
            device_id_type=MESH,
        )

    last = early - 1
    units = pairs * ranks
    events = {
        0: [lambda: to_x(last), lambda: to_z(early), lambda: to_z(early + 1)],
        2: [lambda c=c: to_core(c) for c in range(last)],
        3: [lambda: to_x(early)],
        4: [lambda: to_core(last)],
        6: [lambda: to_x(early + 1), lambda: to_core(early)],
    }

    @pl.loop(0, units)
    def _(u):
        pair, d = lax.rem(u, pairs), ranks - 1 - lax.div(u, pairs)
        unit(pair, d)
        pl.when(d > 0)(lambda: head_copy(pair, d).start())
        for when, steps in events.items():

            @pl.when(u == min(when, units - 1))
            def _():
                for step in steps:
                    step()

    for pair in range(pairs):
        heads_ref[pair] = mixed_ref[pair, 0:block, :]
    to_core(early + 1)

    @pl.loop(pairs, units)
    def _(slot):
        copy = head_copy(lax.rem(slot, pairs), lax.div(slot, pairs))
        copy.wait_recv()
        copy.wait_send()

    for copy in [*core_copies, *own_copies]:
        copy.wait_recv()
    for copy in [*started, *onward, *own_copies, *y_copies, *x_copies, *core_copies]:
        copy.wait_send()
    for copies in z_copies:
        for copy in copies:
            copy.wait_send()


def attend_forward(tokens, gain, shift, weight, cosine, sine, starts, weights):
    block, width = tokens.shape
    ranks = lax.axis_size("tensor")
    assert ranks == 4
    length = block * ranks
    pairs = weight.shape[2] // PAIR
    group = lax.axis_size("dp") // 2
    views = [w.reshape(2, group, w.shape[0] // (2 * group), w.shape[1]) for w in weights]
    chunks = [(0, 0, width)]
    for a in (1, 2):
        columns = weights[a].shape[1] // 2
        chunks += [(a, 0, columns), (a, columns, columns)]
    vmem = pl.BlockSpec(memory_space=pltpu.VMEM)
    hbm = pl.BlockSpec(memory_space=pl.ANY)
    copies = pltpu.SemaphoreType.DMA
    qkv, attn, mixed, logs, heads, *rests = pl.pallas_call(
        functools.partial(forward_kernel, block, ranks, pairs, chunks),
        out_shape=[
            jax.ShapeDtypeStruct((3 * pairs, length, PAIR), BF),
            jax.ShapeDtypeStruct((ranks, block, width), BF),
            jax.ShapeDtypeStruct((pairs, length, PAIR), BF),
            jax.ShapeDtypeStruct((pairs, 8, length), F32),
            jax.ShapeDtypeStruct((ranks * pairs, block, PAIR), BF),
            *[jax.ShapeDtypeStruct((ranks - 1, *view.shape), BF) for view in views],
        ],
        in_specs=[vmem] * 7 + [hbm] * 3,
        out_specs=[vmem] * 5 + [hbm] * 3,
        scratch_shapes=[
            pltpu.VMEM((ranks, block, block), F32),
            copies((2, 12)),
            copies((2, ranks * pairs)),
            copies((2, 3)),
            copies((2, len(chunks))),
            copies((2, len(chunks) * (group - 1))),
            copies((2, len(chunks))),
            copies((2, len(chunks))),
        ],
        compiler_params=pltpu.CompilerParams(vmem_limit_bytes=56 << 20, collective_id=2, has_side_effects=True),
        name="attend_forward",
    )(tokens, gain, shift, weight, cosine, sine, starts, *views)
    return qkv, attn, mixed, logs, heads, [r.reshape(ranks - 1, *w.shape) for r, w in zip(rests, weights)]


def backward_kernel(
    block, blocks, pairs, chunks, *refs
):
    (qkv_ref, gh_ref, o_ref, log_ref, start_ref, cos_ref, sin_ref, shared_ref, *refs) = refs
    terms, refs = refs[: chunks - 1], refs[chunks - 1 :]
    (out_ref, *refs) = refs
    pieces, refs = refs[:chunks], refs[chunks:]
    dq_ref, inner_ref, do_ref, *refs = refs
    got_x, refs = refs[:chunks], refs[chunks:]
    half, refs = refs[:chunks], refs[chunks:]
    got_z, refs = refs[:chunks], refs[chunks:]
    got_core, core_sum, got_y, own_ref, head_sems, x_sems, z_sems, core_sems, y_sems = refs
    terms = [*terms, own_ref]

    mine = lax.axis_index("tensor")
    rank = lax.axis_index("dp")
    group = lax.axis_size("dp") // 2
    x_bit, z_place = lax.rem(rank, 2), lax.div(rank, 2)
    heads = PAIR // HD
    greet(("tensor", "dp"))

    head_copies = {}
    for pair in range(pairs):
        for d in range(1, blocks):
            copy = push(
                gh_ref.at[d * pairs + pair], do_ref.at[pair, d], head_sems, pair * (blocks - 1) + d - 1, "tensor", d
            )
            copy.start()
            head_copies[pair, d] = copy
    core_copies = [
        push(shared_ref.at[d + 1], got_core.at[d // 2], core_sems, d // 2, "tensor", 1) for d in range(0, blocks, 2)
    ]
    y_copies = [
        push(core_sum.at[h], got_y.at[h - 1], y_sems, h - 1, "tensor", 2 * h) for h in range(1, blocks // 2)
    ]
    x_copies = [push(terms[c].at[1 - x_bit], got_x[c], x_sems, c, "dp", 1) for c in range(chunks)]
    for copy in [*core_copies, *x_copies[:-1]]:
        copy.start()
    z_copies = {}
    for c in range(chunks):
        for d in range(1, group):
            z_copies[c, d] = push(
                half[c].at[xor(z_place, d, group)], got_z[c].at[d - 1], z_sems, c * (group - 1) + d - 1, "dp", 2 * d
            )

    def halve(c):
        x_copies[c].wait_recv()
        for g in range(group):
            half[c][g] = (terms[c][x_bit, g].astype(F32) + got_x[c][g].astype(F32)).astype(BF)
        for d in range(1, group):
            z_copies[c, d].start()

    def pair_up():
        for h in range(blocks // 2):
            core_copies[h].wait_recv()
            core_sum[h] = (shared_ref[2 * h].astype(F32) + got_core[h].astype(F32)).astype(BF)
        for copy in y_copies:
            copy.start()

    def settle():
        total = core_sum[0].astype(F32)
        for h in range(1, blocks // 2):
            y_copies[h - 1].wait_recv()
            total = total + got_y[h - 1].astype(F32)
        own_ref[...] = total.astype(BF)
        x_copies[-1].start()

    for pair in range(pairs):
        do_ref[pair, 0] = gh_ref[pair]

    def prepare(pair):
        for d in range(1, blocks):
            head_copies[pair, d].wait_recv()
        dq_ref[...] = jnp.zeros_like(dq_ref)
        for b in range(blocks):
            rows = pl.ds(b * block, block)
            product = do_ref[pair, b].astype(F32) * o_ref[pair, rows, :].astype(F32)
            high = product.astype(BF)
            low = (product - high.astype(F32)).astype(BF)
            for head in range(heads):
                ones = head_mask((16, PAIR), head).astype(F32).astype(BF)
                inner = dot(ones, high, NT) + dot(ones, low, NT)
                inner_ref[head : head + 1, rows] = inner[0:1, :]

    def unit(pair, key_block):
        slot = xor(key_block, mine, blocks)
        here = pl.ds(pl.multiple_of(slot * block, block), block)
        keys = qkv_ref[pairs + pair, here, :]
        values = qkv_ref[2 * pairs + pair, here, :]
        dk = jnp.zeros((block, PAIR), F32)
        dv = jnp.zeros((block, PAIR), F32)
        for head in range(heads):
            mask = head_mask(keys.shape, head)
            key = jnp.where(mask, keys * HD**-0.5, jnp.zeros_like(keys))
            value = jnp.where(mask, values, jnp.zeros_like(values))

            def one(i, carry, first):
                dk, dv = carry
                place = xor(i, mine, blocks)
                rows = pl.ds(pl.multiple_of(place * block, block), block)
                real = pl.ds(pl.multiple_of(i * block, block), block)
                query = qkv_ref[pair, rows, :]
                grad = do_ref[pair, place]
                s = dot(key, query, NT)
                row = lax.broadcasted_iota(jnp.int32, s.shape, 0)
                visible = row >= start_ref[0:1, real] - key_block * block
                if first:
                    visible &= row <= lax.broadcasted_iota(jnp.int32, s.shape, 1)
                probs = jnp.where(visible, jnp.exp(s - log_ref[pair, head : head + 1, rows]), 0.0)
                grad_probs = dot(value, grad, NT)
                ds = (probs * (grad_probs - inner_ref[head : head + 1, rows])).astype(BF)
                zero = jnp.zeros_like(query)
                dv = dv + dot(probs.astype(BF), jnp.where(mask, grad, zero))
                dk = dk + dot(ds, jnp.where(mask, query, zero))
                dq_ref[rows, :] += dot(ds, key, TN)
                return dk, dv

            dk, dv = one(key_block, (dk, dv), True)
            dk, dv = lax.fori_loop(key_block + 1, blocks, lambda i, carry: one(i, carry, False), (dk, dv))
        real = pl.ds(pl.multiple_of(key_block * block, block), block)
        out_ref[pairs + pair, here, :] = turn(dk * HD**-0.5, cos_ref[real, :], -sin_ref[real, :]).astype(BF)
        out_ref[2 * pairs + pair, here, :] = dv.astype(BF)

    def finish(pair):
        for b in range(blocks):
            rows = pl.ds(b * block, block)
            real = pl.ds(pl.multiple_of(flip(mine, b) * block, block), block)
            out_ref[pair, rows, :] = turn(dq_ref[rows, :], cos_ref[real, :], -sin_ref[real, :]).astype(BF)

    slots = pairs * blocks

    @pl.loop(0, slots)
    def _(u):
        pair, key_block = lax.div(u, blocks), lax.rem(u, blocks)
        for p in range(pairs):
            pl.when(u == p * blocks)(functools.partial(prepare, p))
        unit(pair, key_block)
        pl.when(key_block == blocks - 1)(functools.partial(finish, pair))
        pl.when(u == 0)(pair_up)
        pl.when(u == slots // 2)(settle)
        for c in range(chunks):
            pl.when(u == min(slots - 1, 2 * c + 1))(functools.partial(halve, c))

    for c in range(chunks):
        for d in range(1, group):
            z_copies[c, d].wait_recv()
        parts = [half[c][z_place]] + [got_z[c][d] for d in range(group - 1)]
        pieces[c][...] = tree_sum(parts).astype(BF)
    for copy in [*head_copies.values(), *core_copies, *y_copies, *x_copies, *z_copies.values()]:
        copy.wait_send()


def attend_backward(qkv, grad_heads, heads_out, logs, start_row, cosine, sine, shared, terms, block):
    pairs3, length, _ = qkv.shape
    pairs = pairs3 // 3
    blocks = length // block
    group = terms[0].shape[1]
    vmem = pl.BlockSpec(memory_space=pltpu.VMEM)
    inner = [term.shape[1:] for term in terms] + [shared.shape[2:]]
    chunks = len(inner)
    copies = pltpu.SemaphoreType.DMA
    return pl.pallas_call(
        functools.partial(backward_kernel, block, blocks, pairs, chunks),
        out_shape=[jax.ShapeDtypeStruct((pairs3, length, PAIR), BF)]
        + [jax.ShapeDtypeStruct(shape[1:], BF) for shape in inner],
        in_specs=[vmem] * (8 + len(terms)),
        out_specs=[vmem] * (1 + chunks),
        scratch_shapes=[
            pltpu.VMEM((length, PAIR), F32),
            pltpu.VMEM((8, length), F32),
            pltpu.VMEM((pairs, blocks, block, PAIR), BF),
            *[pltpu.VMEM(shape, BF) for shape in inner],
            *[pltpu.VMEM(shape, BF) for shape in inner],
            *[pltpu.VMEM((group - 1, *shape[1:]), BF) for shape in inner],
            pltpu.VMEM((blocks // 2, *shared.shape[1:]), BF),
            pltpu.VMEM((blocks // 2, *shared.shape[1:]), BF),
            pltpu.VMEM((blocks // 2 - 1, *shared.shape[1:]), BF),
            pltpu.VMEM(shared.shape[1:], BF),
            copies((2, pairs * (blocks - 1))),
            copies((2, chunks)),
            copies((2, chunks * (group - 1))),
            copies((2, blocks // 2)),
            copies((2, blocks // 2 - 1)),
        ],
        compiler_params=pltpu.CompilerParams(vmem_limit_bytes=56 << 20, collective_id=0, has_side_effects=True),
        cost_estimate=pl.CostEstimate(flops=100 * length * length * PAIR, bytes_accessed=16 * length * PAIR * 2, transcendentals=length * length),
        name="attend_backward",
    )(qkv, grad_heads, heads_out, logs, start_row, cosine, sine, shared, *terms)


def last_kernel(ranks, pieces_count, *refs):
    x_ref, gain_ref, rest_ref, early_ref, tokens_ref, qkv_ref, *refs = refs
    pieces, refs = refs[:pieces_count], refs[pieces_count:]
    input_ref, sums_ref, qkv_out, *refs = refs
    outs, refs = refs[:pieces_count], refs[pieces_count:]
    (got_core, token_sum, got_y, terms, got_t, sum_t, got_d, got_x, half, got_z, own_piece, *refs) = refs
    (core_sems, y_sems, t_sems, d_sems, x_sems, z_sems, zg_sems, xg_sems) = refs
    rank = lax.axis_index("dp")
    group = lax.axis_size("dp") // 2
    x_bit, z_place = lax.rem(rank, 2), lax.div(rank, 2)
    started = []

    def start(copy):
        copy.start()
        started.append(copy)
        return copy

    greet(("tensor", "dp"))
    core = [
        start(push(tokens_ref.at[d + 1], got_core.at[d // 2], core_sems, d // 2, "tensor", 1)) for d in range(0, ranks, 2)
    ]
    x_copy = start(push(qkv_ref.at[1 - x_bit], got_x, x_sems, 0, "dp", 1))
    gathers = {}

    def spread(k, src, out):
        out[x_bit, z_place] = src[...]
        for d in range(1, group):
            gathers[k, d] = start(
                push(src, out.at[x_bit, z_place], zg_sems, k * (group - 1) + d - 1, "dp", 2 * d)
            )

    def share(k, out):
        for d in range(1, group):
            gathers[k, d].wait_recv()
        return start(push(out.at[x_bit], out.at[x_bit], xg_sems, k, "dp", 1))

    for k in range(pieces_count):
        spread(k, pieces[k], outs[k])

    for d in range(0, ranks, 2):
        core[d // 2].wait_recv()
        token_sum[d // 2] = (tokens_ref[d].astype(F32) + got_core[d // 2].astype(F32)).astype(BF)
    ys = [start(push(token_sum.at[h], got_y.at[h - 1], y_sems, h - 1, "tensor", 2 * h)) for h in range(1, ranks // 2)]

    x_copy.wait_recv()
    for g in range(group):
        half[g] = (qkv_ref[x_bit, g].astype(F32) + got_x[g].astype(F32)).astype(BF)
    zs = [
        start(push(half.at[xor(z_place, d, group)], got_z.at[d - 1], z_sems, d - 1, "dp", 2 * d)) for d in range(1, group)
    ]

    for copy in ys:
        copy.wait_recv()
    rows = 64
    count = x_ref.shape[0] // rows
    gain = gain_ref[...]

    def norm(r, carry):
        gain_term, shift_term = carry
        at = pl.ds(pl.multiple_of(r * rows, rows), rows)
        grad = token_sum[0, at, :].astype(F32)
        for h in range(ranks // 2 - 1):
            grad = grad + got_y[h, at, :].astype(F32)
        x = x_ref[at, :].astype(F32)
        centre = x - jnp.mean(x, axis=-1, keepdims=True)
        scale = lax.rsqrt(jnp.mean(centre * centre, axis=-1, keepdims=True) + EPSILON)
        unit = centre * scale
        inside = grad * gain
        first = jnp.mean(inside, axis=-1, keepdims=True)
        second = jnp.mean(inside * unit, axis=-1, keepdims=True)
        input_ref[at, :] = rest_ref[at, :] + scale * (inside - first - unit * second)
        return (
            gain_term + jnp.sum(grad * unit, axis=0, keepdims=True),
            shift_term + jnp.sum(grad, axis=0, keepdims=True),
        )

    zero = jnp.zeros(gain.shape, F32)
    gain_term, shift_term = lax.fori_loop(0, count, norm, (zero, zero))
    terms[...] = early_ref[...]
    terms[0:1, :] = gain_term
    terms[4:5, :] = shift_term
    ts = [start(push(terms, got_t.at[d - 1], t_sems, d - 1, "tensor", d)) for d in range(1, ranks)]
    xs = [share(k, outs[k]) for k in range(pieces_count)]
    for copy in zs:
        copy.wait_recv()
    own_piece[...] = tree_sum([half[z_place]] + [got_z[d] for d in range(group - 1)]).astype(BF)
    spread(pieces_count, own_piece, qkv_out)
    for copy in ts:
        copy.wait_recv()
    sum_t[...] = tree_sum([terms[...]] + [got_t[d] for d in range(ranks - 1)])
    ds = [start(push(sum_t, got_d.at[d - 1], d_sems, d - 1, "dp", d)) for d in range(1, 2 * group)]
    xs.append(share(pieces_count, qkv_out))
    for copy in ds:
        copy.wait_recv()
    sums_ref[...] = tree_sum([sum_t[...]] + [got_d[d] for d in range(2 * group - 1)])
    for copy in xs:
        copy.wait_recv()
    for copy in started:
        copy.wait_send()


def last_stage(block_rows, gain, rest, early, token_terms, qkv_terms, pieces):
    block, width = block_rows.shape
    ranks = token_terms.shape[0]
    group = qkv_terms.shape[1]
    vmem = pl.BlockSpec(memory_space=pltpu.VMEM)
    copies = pltpu.SemaphoreType.DMA
    count = len(pieces)
    return pl.pallas_call(
        functools.partial(last_kernel, ranks, count),
        out_shape=[
            jax.ShapeDtypeStruct((block, width), F32),
            jax.ShapeDtypeStruct((8, width), F32),
            jax.ShapeDtypeStruct(qkv_terms.shape, BF),
        ]
        + [jax.ShapeDtypeStruct((2, group, *piece.shape), BF) for piece in pieces],
        in_specs=[vmem] * (6 + count),
        out_specs=[vmem] * (3 + count),
        scratch_shapes=[
            pltpu.VMEM((ranks // 2, block, width), BF),
            pltpu.VMEM((ranks // 2, block, width), BF),
            pltpu.VMEM((ranks // 2 - 1, block, width), BF),
            pltpu.VMEM((8, width), F32),
            pltpu.VMEM((ranks - 1, 8, width), F32),
            pltpu.VMEM((8, width), F32),
            pltpu.VMEM((2 * group - 1, 8, width), F32),
            pltpu.VMEM(qkv_terms.shape[1:], BF),
            pltpu.VMEM(qkv_terms.shape[1:], BF),
            pltpu.VMEM((group - 1, *qkv_terms.shape[2:]), BF),
            pltpu.VMEM(qkv_terms.shape[2:], BF),
            copies((2, ranks // 2)),
            copies((2, ranks // 2 - 1)),
            copies((2, ranks - 1)),
            copies((2, 2 * group - 1)),
            copies((2, 1)),
            copies((2, group - 1)),
            copies((2, (count + 1) * (group - 1))),
            copies((2, count + 1)),
        ],
        compiler_params=pltpu.CompilerParams(vmem_limit_bytes=56 << 20, collective_id=1, has_side_effects=True),
        name="last_stage",
    )(block_rows, gain, rest, early, token_terms, qkv_terms, *pieces)


def body(block_in, lengths, qkv_weight, out_weight, up_weight, down_weight, norm_gain, norm_bias, cotangent):
    block, row_count, width = block_in.shape
    assert row_count == 1
    ranks = lax.axis_size("tensor")
    length = block * ranks
    local = out_weight.shape[0]
    pairs = local // PAIR
    residual_in = block_in.reshape(block, width).astype(F32)
    finish = jnp.cumsum(lengths[0])
    begin = finish - lengths[0]
    places = jnp.arange(length, dtype=jnp.int32)
    segment = jnp.sum((places[:, None] >= finish[None, :]).astype(jnp.int32), axis=1)
    picked = segment[:, None] == jnp.arange(lengths.shape[1], dtype=jnp.int32)[None, :]
    starts = jnp.sum(jnp.where(picked, begin[None, :], 0), axis=1)
    position = (places - starts).astype(F32)
    lanes = jnp.arange(PAIR, dtype=jnp.int32)
    inverse = ROPE_BASE ** (-(lanes % (HD // 2)).astype(F32) * 2.0 / HD)
    angles = position[:, None] * inverse
    cosine = jnp.cos(angles)
    sine = jnp.sin(angles) * jnp.where(lanes % HD < HD // 2, -1.0, 1.0).astype(F32)
    start_column = starts.reshape(length, 1)
    start_row = starts.reshape(1, length)

    qkv, attn_full, heads_mixed, logs, heads_parts, (out_rest, up_rest, down_rest) = attend_forward(
        block_in.reshape(block, width),
        norm_gain[0:1],
        norm_bias[0:1],
        jnp.transpose(qkv_weight, (1, 0, 2)),
        cosine,
        sine,
        start_column,
        (out_weight, up_weight, down_weight),
    )
    attn_full = attn_full.reshape(length, width)
    heads_local = jnp.concatenate([heads_parts[i] for i in range(ranks * pairs)], axis=1)
    up_parts = [up_weight] + [up_rest[d] for d in range(ranks - 1)]
    down_parts = [down_weight] + [down_rest[d] for d in range(ranks - 1)]

    out_full = jnp.concatenate([out_weight, out_rest.reshape(-1, width)], axis=0)
    attn_proj = dot(heads_local, out_full)
    attn_branch, attn_branch_pull = jax.vjp(layer_norm, attn_proj, norm_gain[1], norm_bias[1])
    middle = residual_in + attn_branch
    mlp_norm, mlp_norm_pull = jax.vjp(layer_norm, middle, norm_gain[2], norm_bias[2])
    mlp_low = mlp_norm.astype(BF)
    mlp_parts = gather_tensor(mlp_low)

    upward = [dot(mlp_low, part) for part in up_parts]
    hidden, gelu_pull = jax.vjp(jax.nn.gelu, upward[0])
    pulls, mlp_proj = [], 0.0
    for d in range(ranks):
        hidden, pull = jax.vjp(jax.nn.gelu, upward[d])
        pulls.append(pull)
        mlp_proj = mlp_proj + dot(hidden.astype(BF), down_parts[d])
    mlp_branch, mlp_branch_pull = jax.vjp(layer_norm, mlp_proj, norm_gain[3], norm_bias[3])
    block_out = (middle + mlp_branch).astype(BF)

    grad_rows = cotangent.reshape(block, width).astype(F32)
    grad_mlp_proj, gain_three, shift_three = mlp_branch_pull(grad_rows)
    grad_mlp_low = grad_mlp_proj.astype(BF)
    grad_mlp_parts = gather_tensor(grad_mlp_low)
    grad_mlp_norm = 0.0
    for d in range(ranks):
        grad_hidden = dot(grad_mlp_low, down_parts[d], NT)
        grad_upward = pulls[d](grad_hidden)[0].astype(BF)
        grad_mlp_norm = grad_mlp_norm + dot(grad_upward, up_parts[d], NT)
    grad_from_norm, gain_two, shift_two = mlp_norm_pull(grad_mlp_norm)
    grad_middle = grad_rows + grad_from_norm
    grad_attn_proj, gain_one, shift_one = attn_branch_pull(grad_middle)
    grad_attn_low = grad_attn_proj.astype(BF)
    grad_heads = dot(grad_attn_low, out_full, NT).astype(BF)

    mlp_full = jnp.concatenate(mlp_parts, axis=0)
    grad_mlp_full = jnp.concatenate(grad_mlp_parts, axis=0)
    upward_own = dot(mlp_full, up_weight)
    hidden_own, gelu_own_pull = jax.vjp(jax.nn.gelu, upward_own)
    grad_hidden_own = dot(grad_mlp_full, down_weight, NT)
    grad_upward_own = gelu_own_pull(grad_hidden_own)[0].astype(BF)
    group = lax.axis_size("dp") // 2
    down_term = dot(hidden_own.astype(BF), grad_mlp_full, TN).astype(BF)
    up_term = dot(mlp_full, grad_upward_own, TN).astype(BF)

    out_partial = dot(heads_local, grad_attn_low, TN).astype(BF)
    shared = out_partial.reshape(ranks, 2, group, local // (2 * group), width)
    terms = []
    half_columns = width // 2
    for term in (down_term, up_term):
        cut = term.reshape(2, group, term.shape[0] // (2 * group), width)
        terms += [cut[..., :half_columns], cut[..., half_columns:]]

    grad_parts = jnp.stack(
        [grad_heads[:, i * PAIR : (i + 1) * PAIR] for i in range(width // PAIR)], axis=0
    )
    grads, *pieces = attend_backward(
        qkv, grad_parts, heads_mixed, logs, start_row, cosine, sine, shared, terms, block
    )
    wide = jnp.concatenate([grads[i] for i in range(3 * pairs)], axis=1)
    qkv_flat = qkv_weight.reshape(width, 3 * local)
    token_terms = dot(wide, qkv_flat, NT).astype(BF).reshape(ranks, block, width)
    qkv_term = dot(attn_full, wide, TN).astype(BF).reshape(2, group, width // (2 * group), 3 * local)
    early = jnp.stack([gain_one, gain_one, gain_two, gain_three, shift_one, shift_one, shift_two, shift_three])
    input_grad, sums, qkv_sum, *wholes = last_stage(
        block_in.reshape(block, width), norm_gain[0:1], grad_middle, early, token_terms, qkv_term, pieces
    )
    down_grad, up_grad = [
        jnp.concatenate([left.reshape(-1, half_columns), right.reshape(-1, half_columns)], axis=1).astype(F32)
        for left, right in (wholes[0:2], wholes[2:4])
    ]
    qkv_grad = qkv_sum.reshape(width, 3, local).astype(F32)
    gain_grad, bias_grad = sums[0:4], sums[4:8]
    out_grad = wholes[4].reshape(local, width).astype(F32)
    return (
        block_out.reshape(block_in.shape),
        input_grad.reshape(block_in.shape),
        qkv_grad,
        out_grad,
        up_grad,
        down_grad,
        gain_grad,
        bias_grad,
    )


def solution(mesh):
    tokens, rows, columns, copied = P("tensor", "dp", None), P("tensor", None), P(None, "tensor"), P()
    heads = P(None, None, "tensor")
    return jax.shard_map(
        body,
        mesh=mesh,
        in_specs=(tokens, P("dp", None), heads, rows, columns, rows, copied, copied, tokens),
        out_specs=(tokens, tokens, heads, rows, columns, rows, copied, copied),
        check_vma=False,
    )
```

```python
import functools

import jax
import jax.numpy as jnp
from jax import lax
from jax.experimental import pallas as pl
from jax.experimental.pallas import tpu as pltpu
from jax.sharding import PartitionSpec as P

HD = 64
PAIR = 128
EPSILON = 1e-05
ROPE_BASE = 10000.0
NEG = -1e30
MESH = pl.DeviceIdType.MESH
BF = jnp.bfloat16
F32 = jnp.float32
NT = (((1,), (1,)), ((), ()))
NN = (((1,), (0,)), ((), ()))
TN = (((0,), (0,)), ((), ()))


def dot(a, b, dims=NN):
    return lax.dot_general(a, b, dims, preferred_element_type=F32)


def layer_norm(values, gain, shift):
    centre = values - jnp.mean(values, axis=-1, keepdims=True)
    spread = jnp.mean(centre * centre, axis=-1, keepdims=True)
    return centre * lax.rsqrt(spread + EPSILON) * gain + shift


def flip(index, offset):
    bit = 1
    while bit <= offset:
        if offset & bit:
            index = index + bit - 2 * bit * lax.rem(lax.div(index, bit), 2)
        bit *= 2
    return index


def xor(a, b, size):
    total, bit = 0, 1
    while bit < size:
        total = total + bit * lax.rem(lax.div(a, bit) + lax.div(b, bit), 2)
        bit *= 2
    return total


def greet(axes):
    barrier = pltpu.get_barrier_semaphore()
    count = 0
    for axis in axes:
        index = lax.axis_index(axis)
        for d in range(1, lax.axis_size(axis)):
            pl.semaphore_signal(barrier, inc=1, device_id={axis: flip(index, d)}, device_id_type=MESH)
            count += 1
    pl.semaphore_wait(barrier, count)


def tree_sum(parts):
    parts = [part.astype(F32) for part in parts]
    while len(parts) > 1:
        parts = [parts[i] + parts[i + 1] for i in range(0, len(parts), 2)]
    return parts[0]


def push(src, dst, sems, slot, axis, offset):
    return pltpu.make_async_remote_copy(
        src_ref=src,
        dst_ref=dst,
        send_sem=sems.at[0, slot],
        recv_sem=sems.at[1, slot],
        device_id={axis: flip(lax.axis_index(axis), offset)},
        device_id_type=MESH,
    )


def turn(values, cosine, signed_sine):
    lane = lax.broadcasted_iota(jnp.int32, values.shape, 1)
    other = jnp.where(lane % HD < HD // 2, pltpu.roll(values, PAIR - HD // 2, 1), pltpu.roll(values, HD // 2, 1))
    return values * cosine + other * signed_sine


def head_mask(shape, head):
    lane = lax.broadcasted_iota(jnp.int32, shape, 1)
    return lane // HD == head


def forward_kernel(block, ranks, pairs, chunks, *refs):
    x_ref, gain_ref, shift_ref, w_ref, cos_ref, sin_ref, start_ref, *refs = refs
    weights, refs = refs[:3], refs[3:]
    qkv_ref, attn_ref, mixed_ref, log_ref, heads_ref, *refs = refs
    rests, refs = refs[:3], refs[3:]
    scores_ref, attn_sems, head_sems, own_sems, y_sems, z_sems, x_sems, core_sems = refs

    mine = lax.axis_index("tensor")
    rank = lax.axis_index("dp")
    group = lax.axis_size("dp") // 2
    x_bit, z_place = lax.rem(rank, 2), lax.div(rank, 2)
    length = block * ranks
    started = []

    def start(copy):
        copy.start()
        started.append(copy)
        return copy

    def cut(array, c, *lead):
        at, (_, low, size) = array.at, chunks[c]
        return at[(*lead, slice(None), pl.ds(low, size))]

    def every(array, c, *lead):
        at, (_, low, size) = array.at, chunks[c]
        return at[(*lead, slice(None), slice(None), pl.ds(low, size))]

    def rest(c):
        return rests[chunks[c][0]]

    y_copies = [
        push(
            cut(weights[chunks[c][0]], c, x_bit, z_place), cut(rest(c), c, 1, x_bit, z_place), y_sems, c, "tensor", 2
        )
        for c in range(len(chunks))
    ]
    z_copies = [
        [
            push(
                cut(rest(c), c, 1, x_bit, z_place),
                cut(rest(c), c, 1, x_bit, z_place),
                z_sems,
                c * (group - 1) + d - 1,
                "dp",
                2 * d,
            )
            for d in range(1, group)
        ]
        for c in range(len(chunks))
    ]
    x_copies = [
        push(every(rest(c), c, 1, x_bit), every(rest(c), c, 1, x_bit), x_sems, c, "dp", 1) for c in range(len(chunks))
    ]
    core_copies = [
        push(
            rest(c).at[1, :, :, :, pl.ds(chunks[c][1], chunks[c][2])],
            rest(c).at[2, :, :, :, pl.ds(chunks[c][1], chunks[c][2])],
            core_sems,
            c,
            "tensor",
            1,
        )
        for c in range(len(chunks))
    ]
    own_copies = [push(weights[a], rests[a].at[0], own_sems, a, "tensor", 1) for a in range(3)]

    def to_z(c):
        y_copies[c].wait_recv()
        for copy in z_copies[c]:
            copy.start()

    def to_x(c):
        for copy in z_copies[c]:
            copy.wait_recv()
        x_copies[c].start()

    def to_core(c):
        x_copies[c].wait_recv()
        core_copies[c].start()

    greet(("tensor", "dp"))
    early = len(chunks) - 2
    for c in range(early):
        y_copies[c].start()

    strips = 4
    strip = block // strips
    gain, shift = gain_ref[...], shift_ref[...]
    across, beside, onward = [], [], []
    for q in range(strips):

        @pl.loop(0, strip // 64)
        def _(r):
            at = pl.ds(pl.multiple_of(q * strip + r * 64, 64), 64)
            attn_ref[0, at, :] = layer_norm(x_ref[at, :].astype(F32), gain, shift).astype(BF)

        at = pl.ds(q * strip, strip)
        across.append(start(push(attn_ref.at[0, at], attn_ref.at[2, at], attn_sems, q, "tensor", 2)))
        beside.append(start(push(attn_ref.at[0, at], attn_ref.at[1, at], attn_sems, strips + q, "tensor", 1)))
        onward.append(push(attn_ref.at[2, at], attn_ref.at[3, at], attn_sems, 2 * strips + q, "tensor", 1))

    def middle():
        for c in range(early):
            to_z(c)
        for q in range(strips):
            across[q].wait_recv()
            onward[q].start()
        for c in range(early, len(chunks)):
            y_copies[c].start()
        for copy in own_copies:
            copy.start()
        for c in range(early - 1):
            to_x(c)

    def beside_here():
        for copy in beside:
            copy.wait_recv()

    def onward_here():
        for copy in onward:
            copy.wait_recv()

    @pl.loop(0, ranks)
    def _(d):
        pl.when(d == 1)(beside_here)
        pl.when(d == 2)(middle)
        pl.when(d == 3)(onward_here)
        x = attn_ref[d]
        rows = pl.ds(pl.multiple_of(d * block, block), block)
        real = pl.ds(pl.multiple_of(xor(d, mine, ranks) * block, block), block)
        for part in range(3):
            project = dot(x, w_ref[part])
            for pair in range(pairs):
                piece = project[:, pair * PAIR : (pair + 1) * PAIR]
                if part < 2:
                    piece = turn(piece, cos_ref[real, :], sin_ref[real, :])
                qkv_ref[part * pairs + pair, rows, :] = piece.astype(BF)

    def unit(pair, d):
        row_block = xor(d, mine, ranks)
        rows = pl.ds(pl.multiple_of(d * block, block), block)
        queries = qkv_ref[pair, rows, :] * HD**-0.5
        begin = start_ref[pl.ds(pl.multiple_of(row_block * block, block), block), :]
        mixed = None
        for head in range(PAIR // HD):
            mask = head_mask(queries.shape, head)
            query = jnp.where(mask, queries, jnp.zeros_like(queries))

            def score(j, top, last):
                at = pl.ds(pl.multiple_of(xor(j, mine, ranks) * block, block), block)
                s = dot(query, qkv_ref[pairs + pair, at, :], NT)
                column = lax.broadcasted_iota(jnp.int32, s.shape, 1)
                visible = column >= begin - j * block
                if last:
                    visible &= column <= lax.broadcasted_iota(jnp.int32, s.shape, 0)
                s = jnp.where(visible, s, NEG)
                scores_ref[j] = s
                for c in range(0, block, 128):
                    top = jnp.maximum(top, s[:, c : c + 128])
                return top

            top = jnp.full((block, 128), NEG, F32)
            top = lax.fori_loop(0, row_block, lambda j, top: score(j, top, False), top)
            top = score(row_block, top, True)
            top = jnp.max(top, axis=1, keepdims=True)

            def mix(j, carry):
                total, acc = carry
                shares = jnp.exp(scores_ref[j] - top)
                for c in range(0, block, 128):
                    total = total + shares[:, c : c + 128]
                at = pl.ds(pl.multiple_of(xor(j, mine, ranks) * block, block), block)
                return total, acc + dot(shares.astype(BF), qkv_ref[2 * pairs + pair, at, :])

            total, acc = lax.fori_loop(
                0, row_block + 1, mix, (jnp.zeros((block, 128), F32), jnp.zeros((block, PAIR), F32))
            )
            total = jnp.sum(total, axis=1, keepdims=True)
            acc = acc / total
            mixed = acc if mixed is None else jnp.where(mask, acc, mixed)
            logs = jnp.broadcast_to(top + jnp.log(total), (block, 128))
            log_ref[pair, head : head + 1, rows] = jnp.transpose(logs)[0:1, :]
        mixed_ref[pair, rows, :] = mixed.astype(BF)

    def head_copy(pair, d):
        slot = d * pairs + pair
        return pltpu.make_async_remote_copy(
            src_ref=mixed_ref.at[pair, pl.ds(pl.multiple_of(d * block, block), block)],
            dst_ref=heads_ref.at[slot],
            send_sem=head_sems.at[0, slot],
            recv_sem=head_sems.at[1, slot],
            device_id={"tensor": xor(mine, d, ranks)},
            device_id_type=MESH,
        )

    last = early - 1
    units = pairs * ranks
    events = {
        0: [lambda: to_x(last), lambda: to_z(early), lambda: to_z(early + 1)],
        2: [lambda c=c: to_core(c) for c in range(last)],
        3: [lambda: to_x(early)],
        4: [lambda: to_core(last)],
        6: [lambda: to_x(early + 1), lambda: to_core(early)],
    }

    @pl.loop(0, units)
    def _(u):
        pair, d = lax.rem(u, pairs), ranks - 1 - lax.div(u, pairs)
        unit(pair, d)
        pl.when(d > 0)(lambda: head_copy(pair, d).start())
        for when, steps in events.items():

            @pl.when(u == min(when, units - 1))
            def _():
                for step in steps:
                    step()

    for pair in range(pairs):
        heads_ref[pair] = mixed_ref[pair, 0:block, :]
    to_core(early + 1)

    @pl.loop(pairs, units)
    def _(slot):
        copy = head_copy(lax.rem(slot, pairs), lax.div(slot, pairs))
        copy.wait_recv()
        copy.wait_send()

    for copy in [*core_copies, *own_copies]:
        copy.wait_recv()
    for copy in [*started, *onward, *own_copies, *y_copies, *x_copies, *core_copies]:
        copy.wait_send()
    for copies in z_copies:
        for copy in copies:
            copy.wait_send()


def attend_forward(tokens, gain, shift, weight, cosine, sine, starts, weights):
    block, width = tokens.shape
    ranks = lax.axis_size("tensor")
    assert ranks == 4
    length = block * ranks
    pairs = weight.shape[2] // PAIR
    group = lax.axis_size("dp") // 2
    views = [w.reshape(2, group, w.shape[0] // (2 * group), w.shape[1]) for w in weights]
    chunks = [(0, 0, width)]
    for a in (1, 2):
        columns = weights[a].shape[1] // 2
        chunks += [(a, 0, columns), (a, columns, columns)]
    vmem = pl.BlockSpec(memory_space=pltpu.VMEM)
    hbm = pl.BlockSpec(memory_space=pl.ANY)
    copies = pltpu.SemaphoreType.DMA
    qkv, attn, mixed, logs, heads, *rests = pl.pallas_call(
        functools.partial(forward_kernel, block, ranks, pairs, chunks),
        out_shape=[
            jax.ShapeDtypeStruct((3 * pairs, length, PAIR), BF),
            jax.ShapeDtypeStruct((ranks, block, width), BF),
            jax.ShapeDtypeStruct((pairs, length, PAIR), BF),
            jax.ShapeDtypeStruct((pairs, 8, length), F32),
            jax.ShapeDtypeStruct((ranks * pairs, block, PAIR), BF),
            *[jax.ShapeDtypeStruct((ranks - 1, *view.shape), BF) for view in views],
        ],
        in_specs=[vmem] * 7 + [hbm] * 3,
        out_specs=[vmem] * 5 + [hbm] * 3,
        scratch_shapes=[
            pltpu.VMEM((ranks, block, block), F32),
            copies((2, 12)),
            copies((2, ranks * pairs)),
            copies((2, 3)),
            copies((2, len(chunks))),
            copies((2, len(chunks) * (group - 1))),
            copies((2, len(chunks))),
            copies((2, len(chunks))),
        ],
        compiler_params=pltpu.CompilerParams(vmem_limit_bytes=56 << 20, collective_id=2, has_side_effects=True),
        name="attend_forward",
    )(tokens, gain, shift, weight, cosine, sine, starts, *views)
    return qkv, attn, mixed, logs, heads, [r.reshape(ranks - 1, *w.shape) for r, w in zip(rests, weights)]


def unit_scale(values):
    centre = values - jnp.mean(values, axis=-1, keepdims=True)
    scale = lax.rsqrt(jnp.mean(centre * centre, axis=-1, keepdims=True) + EPSILON)
    return centre * scale, scale


def norm_pull(grad, unit, scale, gain):
    inside = grad * gain
    first = jnp.mean(inside, axis=-1, keepdims=True)
    second = jnp.mean(inside * unit, axis=-1, keepdims=True)
    return scale * (inside - first - unit * second)


def gelu_both(x):
    bend = 0.7978845608028654
    square = x * x
    t = jnp.tanh(bend * (x + 0.044715 * (square * x)))
    side = 0.5 * (1.0 + t)
    return x * side, side + 0.5 * x * (1.0 - t * t) * (bend * (1.0 + 0.134145 * square))


def middle_kernel(block, ranks, pairs, *refs):
    (heads_ref, x_ref, dy_ref, gains_ref, shifts_ref, *refs) = refs
    sources, refs = refs[:6], refs[6:]
    (out_ref, rest_ref, do_ref, shared_ref, down_term, up_term, early_ref, *refs) = refs
    (out_all, up_all, down_all, work_ref, mlp_ref, gmp_ref, middle_ref, proj_ref, acc_ref, gap_ref, gh_ref, *refs) = refs
    (out_sems, up_sems, down_sems, mlp_sems, gmp_sems, head_sems) = refs

    mine = lax.axis_index("tensor")
    width = x_ref.shape[1]
    strips, rows = 4, 64
    strip = block // strips
    columns = width // 2

    def loads(own, rest, array, sems):
        return [
            pltpu.make_async_copy(own if d == 0 else rest.at[d - 1], array.at[d], sems.at[d]) for d in range(ranks)
        ]

    out_loads = loads(sources[0], sources[1], out_all, out_sems)
    up_loads = loads(sources[2], sources[3], up_all, up_sems)
    down_loads = loads(sources[4], sources[5], down_all, down_sems)
    for copy in out_loads:
        copy.start()
    for d in range(ranks):
        up_loads[d].start()
        down_loads[d].start()
    greet(("tensor",))

    def senders(array, sems):
        found = []
        for q in range(strips):
            at = pl.ds(q * strip, strip)
            found.append(
                (
                    push(array.at[0, at], array.at[2, at], sems, q, "tensor", 2),
                    push(array.at[0, at], array.at[1, at], sems, strips + q, "tensor", 1),
                    push(array.at[2, at], array.at[3, at], sems, 2 * strips + q, "tensor", 1),
                )
            )
        return found

    mlp_copies = senders(mlp_ref, mlp_sems)
    gmp_copies = senders(gmp_ref, gmp_sems)

    def send_strip(copies, q):
        copies[q][0].start()
        copies[q][1].start()

    def forward_on(copies):
        for across, _, onward in copies:
            across.wait_recv()
            onward.start()

    for d in range(ranks):
        out_loads[d].wait()
    for c in (0, columns):
        at = pl.ds(c, columns)
        total = None
        for d in range(ranks):
            part = jnp.concatenate([heads_ref[d * pairs + p] for p in range(pairs)], axis=1)
            term = dot(part, out_all[d, :, at])
            total = term if total is None else total + term
        proj_ref[:, at] = total

    gain = [gains_ref[j : j + 1, :] for j in range(4)]
    shift = [shifts_ref[j : j + 1, :] for j in range(4)]

    for q in range(strips):

        @pl.loop(0, strip // rows)
        def _(r):
            at = pl.ds(pl.multiple_of(q * strip + r * rows, rows), rows)
            unit, _ = unit_scale(proj_ref[at, :])
            middle = x_ref[at, :].astype(F32) + (unit * gain[1] + shift[1])
            middle_ref[at, :] = middle
            unit, _ = unit_scale(middle)
            mlp_ref[0, at, :] = (unit * gain[2] + shift[2]).astype(BF)

        send_strip(mlp_copies, q)

    acc_ref[...] = jnp.zeros_like(acc_ref)

    @pl.loop(0, ranks)
    def _(d):
        pltpu.make_async_copy(up_all.at[d], up_all.at[d], up_sems.at[d]).wait()
        pltpu.make_async_copy(down_all.at[d], down_all.at[d], down_sems.at[d]).wait()
        for c in (0, columns):
            at = pl.ds(c, columns)
            hidden, slope = gelu_both(dot(mlp_ref[0], up_all[d, :, at]))
            work_ref[d, :, at] = slope
            acc_ref[...] += dot(hidden.astype(BF), down_all[d, at, :])

    zero = jnp.zeros((1, width), F32)
    gain_three, shift_three = zero, zero
    for q in range(strips):

        def last_norm(r, carry):
            gain_term, shift_term = carry
            at = pl.ds(pl.multiple_of(q * strip + r * rows, rows), rows)
            unit, scale = unit_scale(acc_ref[at, :])
            out_ref[at, :] = (middle_ref[at, :] + (unit * gain[3] + shift[3])).astype(BF)
            dy = dy_ref[at, :].astype(F32)
            gmp_ref[0, at, :] = norm_pull(dy, unit, scale, gain[3]).astype(BF)
            return (
                gain_term + jnp.sum(dy * unit, axis=0, keepdims=True),
                shift_term + jnp.sum(dy, axis=0, keepdims=True),
            )

        gain_three, shift_three = lax.fori_loop(0, strip // rows, last_norm, (gain_three, shift_three))
        send_strip(gmp_copies, q)

    acc_ref[...] = jnp.zeros_like(acc_ref)

    @pl.loop(0, ranks)
    def _(d):
        for c in (0, columns):
            at = pl.ds(c, columns)
            grad = dot(gmp_ref[0], down_all[d, at, :], NT)
            grad = (grad * work_ref[d, :, at]).astype(BF)
            acc_ref[...] += dot(grad, up_all[d, :, at], NT)

    forward_on(mlp_copies)

    def inner_norms(r, carry):
        gain_two, shift_two, gain_one, shift_one = carry
        at = pl.ds(pl.multiple_of(r * rows, rows), rows)
        grad = acc_ref[at, :]
        unit, scale = unit_scale(middle_ref[at, :])
        gain_two = gain_two + jnp.sum(grad * unit, axis=0, keepdims=True)
        shift_two = shift_two + jnp.sum(grad, axis=0, keepdims=True)
        grad = dy_ref[at, :].astype(F32) + norm_pull(grad, unit, scale, gain[2])
        rest_ref[at, :] = grad
        unit, scale = unit_scale(proj_ref[at, :])
        gain_one = gain_one + jnp.sum(grad * unit, axis=0, keepdims=True)
        shift_one = shift_one + jnp.sum(grad, axis=0, keepdims=True)
        gap_ref[at, :] = norm_pull(grad, unit, scale, gain[1]).astype(BF)
        return gain_two, shift_two, gain_one, shift_one

    gain_two, shift_two, gain_one, shift_one = lax.fori_loop(0, block // rows, inner_norms, (zero, zero, zero, zero))
    early_ref[...] = jnp.concatenate(
        [zero, gain_one, gain_two, gain_three, zero, shift_one, shift_two, shift_three], axis=0
    )

    head_copies = []
    for d in [*range(1, ranks), 0]:
        grad = dot(gap_ref[...], out_all[d], NT).astype(BF)
        for pair in range(pairs):
            piece = grad[:, pair * PAIR : (pair + 1) * PAIR]
            if d == 0:
                do_ref[pair, 0] = piece
            else:
                slot = d * pairs + pair
                gh_ref[slot] = piece
                copy = push(gh_ref.at[slot], do_ref.at[pair, d], head_sems, slot, "tensor", d)
                copy.start()
                head_copies.append(copy)
    for d in range(ranks):
        part = jnp.concatenate([heads_ref[d * pairs + p] for p in range(pairs)], axis=1)
        shared_ref[d] = dot(part, gap_ref[...], TN).astype(BF)

    for copies in (mlp_copies, gmp_copies):
        for _, beside, _ in copies:
            beside.wait_recv()
    work_ref[...] = jnp.zeros_like(work_ref)

    def late():
        forward_on(gmp_copies)

    def latest():
        for copies in (mlp_copies, gmp_copies):
            for _, _, onward in copies:
                onward.wait_recv()

    @pl.loop(0, ranks)
    def _(b):
        pl.when(b == 2)(late)
        pl.when(b == 3)(latest)
        tokens, grads = mlp_ref[b], gmp_ref[b]
        for h in range(2):
            at = pl.ds(h * columns, columns)
            hidden, slope = gelu_both(dot(tokens, up_all[0, :, at]))
            grad = (dot(grads, down_all[0, at, :], NT) * slope).astype(BF)
            work_ref[h] += dot(hidden.astype(BF), grads, TN)
            work_ref[2, :, at] += dot(tokens[:, 0:columns], grad, TN)
            work_ref[3, :, at] += dot(tokens[:, columns:], grad, TN)

    for h in range(2):
        at = pl.ds(h * columns, columns)
        down_term[at, :] = work_ref[h].astype(BF)
        up_term[at, :] = work_ref[2 + h].astype(BF)
    for copy in head_copies:
        copy.wait_recv()
        copy.wait_send()
    for copies in (mlp_copies, gmp_copies):
        for group in copies:
            for copy in group:
                copy.wait_send()


def middle_stage(heads, tokens, cotangent, gains, shifts, weights, rests):
    block, width = tokens.shape
    ranks = lax.axis_size("tensor")
    local = weights[0].shape[0]
    pairs = local // PAIR
    hidden = weights[2].shape[0]
    vmem = pl.BlockSpec(memory_space=pltpu.VMEM)
    hbm = pl.BlockSpec(memory_space=pl.ANY)
    copies = pltpu.SemaphoreType.DMA
    assert block * 2 == width and hidden == width
    operands = [array for pair in zip(weights, rests) for array in pair]
    return pl.pallas_call(
        functools.partial(middle_kernel, block, ranks, pairs),
        out_shape=[
            jax.ShapeDtypeStruct((block, width), BF),
            jax.ShapeDtypeStruct((block, width), F32),
            jax.ShapeDtypeStruct((pairs, ranks, block, PAIR), BF),
            jax.ShapeDtypeStruct((ranks, local, width), BF),
            jax.ShapeDtypeStruct((hidden, width), BF),
            jax.ShapeDtypeStruct((width, hidden), BF),
            jax.ShapeDtypeStruct((8, width), F32),
        ],
        in_specs=[vmem] * 5 + [hbm] * 6,
        out_specs=[vmem] * 7,
        scratch_shapes=[
            pltpu.VMEM((ranks, local, width), BF),
            pltpu.VMEM((ranks, width, hidden), BF),
            pltpu.VMEM((ranks, hidden, width), BF),
            pltpu.VMEM((ranks, block, width), F32),
            pltpu.VMEM((ranks, block, width), BF),
            pltpu.VMEM((ranks, block, width), BF),
            pltpu.VMEM((block, width), F32),
            pltpu.VMEM((block, width), F32),
            pltpu.VMEM((block, width), F32),
            pltpu.VMEM((block, width), BF),
            pltpu.VMEM((ranks * pairs, block, PAIR), BF),
            copies((ranks,)),
            copies((ranks,)),
            copies((ranks,)),
            copies((2, 12)),
            copies((2, 12)),
            copies((2, ranks * pairs)),
        ],
        compiler_params=pltpu.CompilerParams(vmem_limit_bytes=62 << 20, collective_id=3, has_side_effects=True),
        name="middle_stage",
    )(heads, tokens, cotangent, gains, shifts, *operands)


def backward_kernel(
    block, blocks, pairs, chunks, *refs
):
    (qkv_ref, do_ref, o_ref, log_ref, start_ref, cos_ref, sin_ref, shared_ref, *refs) = refs
    terms, refs = refs[: chunks - 1], refs[chunks - 1 :]
    (out_ref, *refs) = refs
    pieces, refs = refs[:chunks], refs[chunks:]
    dq_ref, inner_ref, *refs = refs
    got_x, refs = refs[:chunks], refs[chunks:]
    half, refs = refs[:chunks], refs[chunks:]
    got_z, refs = refs[:chunks], refs[chunks:]
    got_core, core_sum, got_y, own_ref, x_sems, z_sems, core_sems, y_sems = refs
    terms = [*terms, own_ref]

    mine = lax.axis_index("tensor")
    rank = lax.axis_index("dp")
    group = lax.axis_size("dp") // 2
    x_bit, z_place = lax.rem(rank, 2), lax.div(rank, 2)
    heads = PAIR // HD
    greet(("tensor", "dp"))

    core_copies = [
        push(shared_ref.at[d + 1], got_core.at[d // 2], core_sems, d // 2, "tensor", 1) for d in range(0, blocks, 2)
    ]
    y_copies = [
        push(core_sum.at[h], got_y.at[h - 1], y_sems, h - 1, "tensor", 2 * h) for h in range(1, blocks // 2)
    ]
    x_copies = [push(terms[c].at[1 - x_bit], got_x[c], x_sems, c, "dp", 1) for c in range(chunks)]
    for copy in [*core_copies, *x_copies[:-1]]:
        copy.start()
    z_copies = {}
    for c in range(chunks):
        for d in range(1, group):
            z_copies[c, d] = push(
                half[c].at[xor(z_place, d, group)], got_z[c].at[d - 1], z_sems, c * (group - 1) + d - 1, "dp", 2 * d
            )

    def halve(c):
        x_copies[c].wait_recv()
        for g in range(group):
            half[c][g] = (terms[c][x_bit, g].astype(F32) + got_x[c][g].astype(F32)).astype(BF)
        for d in range(1, group):
            z_copies[c, d].start()

    def pair_up():
        for h in range(blocks // 2):
            core_copies[h].wait_recv()
            core_sum[h] = (shared_ref[2 * h].astype(F32) + got_core[h].astype(F32)).astype(BF)
        for copy in y_copies:
            copy.start()

    def settle():
        total = core_sum[0].astype(F32)
        for h in range(1, blocks // 2):
            y_copies[h - 1].wait_recv()
            total = total + got_y[h - 1].astype(F32)
        own_ref[...] = total.astype(BF)
        x_copies[-1].start()

    def prepare(pair):
        dq_ref[...] = jnp.zeros_like(dq_ref)
        for b in range(blocks):
            rows = pl.ds(b * block, block)
            product = do_ref[pair, b].astype(F32) * o_ref[pair, rows, :].astype(F32)
            high = product.astype(BF)
            low = (product - high.astype(F32)).astype(BF)
            for head in range(heads):
                ones = head_mask((16, PAIR), head).astype(F32).astype(BF)
                inner = dot(ones, high, NT) + dot(ones, low, NT)
                inner_ref[head : head + 1, rows] = inner[0:1, :]

    def unit(pair, key_block):
        slot = xor(key_block, mine, blocks)
        here = pl.ds(pl.multiple_of(slot * block, block), block)
        keys = qkv_ref[pairs + pair, here, :]
        values = qkv_ref[2 * pairs + pair, here, :]
        dk = jnp.zeros((block, PAIR), F32)
        dv = jnp.zeros((block, PAIR), F32)
        for head in range(heads):
            mask = head_mask(keys.shape, head)
            key = jnp.where(mask, keys * HD**-0.5, jnp.zeros_like(keys))
            value = jnp.where(mask, values, jnp.zeros_like(values))

            def one(i, carry, first):
                dk, dv = carry
                place = xor(i, mine, blocks)
                rows = pl.ds(pl.multiple_of(place * block, block), block)
                real = pl.ds(pl.multiple_of(i * block, block), block)
                query = qkv_ref[pair, rows, :]
                grad = do_ref[pair, place]
                s = dot(key, query, NT)
                row = lax.broadcasted_iota(jnp.int32, s.shape, 0)
                visible = row >= start_ref[0:1, real] - key_block * block
                if first:
                    visible &= row <= lax.broadcasted_iota(jnp.int32, s.shape, 1)
                probs = jnp.where(visible, jnp.exp(s - log_ref[pair, head : head + 1, rows]), 0.0)
                grad_probs = dot(value, grad, NT)
                ds = (probs * (grad_probs - inner_ref[head : head + 1, rows])).astype(BF)
                zero = jnp.zeros_like(query)
                dv = dv + dot(probs.astype(BF), jnp.where(mask, grad, zero))
                dk = dk + dot(ds, jnp.where(mask, query, zero))
                dq_ref[rows, :] += dot(ds, key, TN)
                return dk, dv

            dk, dv = one(key_block, (dk, dv), True)
            dk, dv = lax.fori_loop(key_block + 1, blocks, lambda i, carry: one(i, carry, False), (dk, dv))
        real = pl.ds(pl.multiple_of(key_block * block, block), block)
        out_ref[pairs + pair, here, :] = turn(dk * HD**-0.5, cos_ref[real, :], -sin_ref[real, :]).astype(BF)
        out_ref[2 * pairs + pair, here, :] = dv.astype(BF)

    def finish(pair):
        for b in range(blocks):
            rows = pl.ds(b * block, block)
            real = pl.ds(pl.multiple_of(flip(mine, b) * block, block), block)
            out_ref[pair, rows, :] = turn(dq_ref[rows, :], cos_ref[real, :], -sin_ref[real, :]).astype(BF)

    slots = pairs * blocks

    @pl.loop(0, slots)
    def _(u):
        pair, key_block = lax.div(u, blocks), lax.rem(u, blocks)
        for p in range(pairs):
            pl.when(u == p * blocks)(functools.partial(prepare, p))
        unit(pair, key_block)
        pl.when(key_block == blocks - 1)(functools.partial(finish, pair))
        pl.when(u == 0)(pair_up)
        pl.when(u == slots // 2)(settle)
        for c in range(chunks):
            pl.when(u == min(slots - 1, 2 * c + 1))(functools.partial(halve, c))

    for c in range(chunks):
        for d in range(1, group):
            z_copies[c, d].wait_recv()
        parts = [half[c][z_place]] + [got_z[c][d] for d in range(group - 1)]
        pieces[c][...] = tree_sum(parts).astype(BF)
    for copy in [*core_copies, *y_copies, *x_copies, *z_copies.values()]:
        copy.wait_send()


def attend_backward(qkv, grad_heads, heads_out, logs, start_row, cosine, sine, shared, terms, block):
    pairs3, length, _ = qkv.shape
    pairs = pairs3 // 3
    blocks = length // block
    group = terms[0].shape[1]
    vmem = pl.BlockSpec(memory_space=pltpu.VMEM)
    inner = [term.shape[1:] for term in terms] + [shared.shape[2:]]
    chunks = len(inner)
    copies = pltpu.SemaphoreType.DMA
    return pl.pallas_call(
        functools.partial(backward_kernel, block, blocks, pairs, chunks),
        out_shape=[jax.ShapeDtypeStruct((pairs3, length, PAIR), BF)]
        + [jax.ShapeDtypeStruct(shape[1:], BF) for shape in inner],
        in_specs=[vmem] * (8 + len(terms)),
        out_specs=[vmem] * (1 + chunks),
        scratch_shapes=[
            pltpu.VMEM((length, PAIR), F32),
            pltpu.VMEM((8, length), F32),
            *[pltpu.VMEM(shape, BF) for shape in inner],
            *[pltpu.VMEM(shape, BF) for shape in inner],
            *[pltpu.VMEM((group - 1, *shape[1:]), BF) for shape in inner],
            pltpu.VMEM((blocks // 2, *shared.shape[1:]), BF),
            pltpu.VMEM((blocks // 2, *shared.shape[1:]), BF),
            pltpu.VMEM((blocks // 2 - 1, *shared.shape[1:]), BF),
            pltpu.VMEM(shared.shape[1:], BF),
            copies((2, chunks)),
            copies((2, chunks * (group - 1))),
            copies((2, blocks // 2)),
            copies((2, blocks // 2 - 1)),
        ],
        compiler_params=pltpu.CompilerParams(vmem_limit_bytes=56 << 20, collective_id=0, has_side_effects=True),
        cost_estimate=pl.CostEstimate(flops=100 * length * length * PAIR, bytes_accessed=16 * length * PAIR * 2, transcendentals=length * length),
        name="attend_backward",
    )(qkv, grad_heads, heads_out, logs, start_row, cosine, sine, shared, *terms)


def last_kernel(ranks, pieces_count, *refs):
    x_ref, gain_ref, rest_ref, early_ref, tokens_ref, qkv_ref, *refs = refs
    pieces, refs = refs[:pieces_count], refs[pieces_count:]
    input_ref, sums_ref, qkv_out, *refs = refs
    outs, refs = refs[:pieces_count], refs[pieces_count:]
    (got_core, token_sum, got_y, terms, got_t, sum_t, got_d, got_x, half, got_z, own_piece, *refs) = refs
    (core_sems, y_sems, t_sems, d_sems, x_sems, z_sems, zg_sems, xg_sems) = refs
    rank = lax.axis_index("dp")
    group = lax.axis_size("dp") // 2
    x_bit, z_place = lax.rem(rank, 2), lax.div(rank, 2)
    started = []

    def start(copy):
        copy.start()
        started.append(copy)
        return copy

    greet(("tensor", "dp"))
    core = [
        start(push(tokens_ref.at[d + 1], got_core.at[d // 2], core_sems, d // 2, "tensor", 1)) for d in range(0, ranks, 2)
    ]
    x_copy = start(push(qkv_ref.at[1 - x_bit], got_x, x_sems, 0, "dp", 1))
    gathers = {}

    def spread(k, src, out):
        out[x_bit, z_place] = src[...]
        for d in range(1, group):
            gathers[k, d] = start(
                push(src, out.at[x_bit, z_place], zg_sems, k * (group - 1) + d - 1, "dp", 2 * d)
            )

    def share(k, out):
        for d in range(1, group):
            gathers[k, d].wait_recv()
        return start(push(out.at[x_bit], out.at[x_bit], xg_sems, k, "dp", 1))

    for k in range(pieces_count):
        spread(k, pieces[k], outs[k])

    for d in range(0, ranks, 2):
        core[d // 2].wait_recv()
        token_sum[d // 2] = (tokens_ref[d].astype(F32) + got_core[d // 2].astype(F32)).astype(BF)
    ys = [start(push(token_sum.at[h], got_y.at[h - 1], y_sems, h - 1, "tensor", 2 * h)) for h in range(1, ranks // 2)]

    x_copy.wait_recv()
    for g in range(group):
        half[g] = (qkv_ref[x_bit, g].astype(F32) + got_x[g].astype(F32)).astype(BF)
    zs = [
        start(push(half.at[xor(z_place, d, group)], got_z.at[d - 1], z_sems, d - 1, "dp", 2 * d)) for d in range(1, group)
    ]

    for copy in ys:
        copy.wait_recv()
    rows = 64
    count = x_ref.shape[0] // rows
    gain = gain_ref[...]

    def norm(r, carry):
        gain_term, shift_term = carry
        at = pl.ds(pl.multiple_of(r * rows, rows), rows)
        grad = token_sum[0, at, :].astype(F32)
        for h in range(ranks // 2 - 1):
            grad = grad + got_y[h, at, :].astype(F32)
        x = x_ref[at, :].astype(F32)
        centre = x - jnp.mean(x, axis=-1, keepdims=True)
        scale = lax.rsqrt(jnp.mean(centre * centre, axis=-1, keepdims=True) + EPSILON)
        unit = centre * scale
        inside = grad * gain
        first = jnp.mean(inside, axis=-1, keepdims=True)
        second = jnp.mean(inside * unit, axis=-1, keepdims=True)
        input_ref[at, :] = rest_ref[at, :] + scale * (inside - first - unit * second)
        return (
            gain_term + jnp.sum(grad * unit, axis=0, keepdims=True),
            shift_term + jnp.sum(grad, axis=0, keepdims=True),
        )

    zero = jnp.zeros(gain.shape, F32)
    gain_term, shift_term = lax.fori_loop(0, count, norm, (zero, zero))
    terms[...] = early_ref[...]
    terms[0:1, :] = gain_term
    terms[4:5, :] = shift_term
    ts = [start(push(terms, got_t.at[d - 1], t_sems, d - 1, "tensor", d)) for d in range(1, ranks)]
    xs = [share(k, outs[k]) for k in range(pieces_count)]
    for copy in zs:
        copy.wait_recv()
    own_piece[...] = tree_sum([half[z_place]] + [got_z[d] for d in range(group - 1)]).astype(BF)
    spread(pieces_count, own_piece, qkv_out)
    for copy in ts:
        copy.wait_recv()
    sum_t[...] = tree_sum([terms[...]] + [got_t[d] for d in range(ranks - 1)])
    ds = [start(push(sum_t, got_d.at[d - 1], d_sems, d - 1, "dp", d)) for d in range(1, 2 * group)]
    xs.append(share(pieces_count, qkv_out))
    for copy in ds:
        copy.wait_recv()
    sums_ref[...] = tree_sum([sum_t[...]] + [got_d[d] for d in range(2 * group - 1)])
    for copy in xs:
        copy.wait_recv()
    for copy in started:
        copy.wait_send()


def last_stage(block_rows, gain, rest, early, token_terms, qkv_terms, pieces):
    block, width = block_rows.shape
    ranks = token_terms.shape[0]
    group = qkv_terms.shape[1]
    vmem = pl.BlockSpec(memory_space=pltpu.VMEM)
    copies = pltpu.SemaphoreType.DMA
    count = len(pieces)
    return pl.pallas_call(
        functools.partial(last_kernel, ranks, count),
        out_shape=[
            jax.ShapeDtypeStruct((block, width), F32),
            jax.ShapeDtypeStruct((8, width), F32),
            jax.ShapeDtypeStruct(qkv_terms.shape, BF),
        ]
        + [jax.ShapeDtypeStruct((2, group, *piece.shape), BF) for piece in pieces],
        in_specs=[vmem] * (6 + count),
        out_specs=[vmem] * (3 + count),
        scratch_shapes=[
            pltpu.VMEM((ranks // 2, block, width), BF),
            pltpu.VMEM((ranks // 2, block, width), BF),
            pltpu.VMEM((ranks // 2 - 1, block, width), BF),
            pltpu.VMEM((8, width), F32),
            pltpu.VMEM((ranks - 1, 8, width), F32),
            pltpu.VMEM((8, width), F32),
            pltpu.VMEM((2 * group - 1, 8, width), F32),
            pltpu.VMEM(qkv_terms.shape[1:], BF),
            pltpu.VMEM(qkv_terms.shape[1:], BF),
            pltpu.VMEM((group - 1, *qkv_terms.shape[2:]), BF),
            pltpu.VMEM(qkv_terms.shape[2:], BF),
            copies((2, ranks // 2)),
            copies((2, ranks // 2 - 1)),
            copies((2, ranks - 1)),
            copies((2, 2 * group - 1)),
            copies((2, 1)),
            copies((2, group - 1)),
            copies((2, (count + 1) * (group - 1))),
            copies((2, count + 1)),
        ],
        compiler_params=pltpu.CompilerParams(vmem_limit_bytes=56 << 20, collective_id=1, has_side_effects=True),
        name="last_stage",
    )(block_rows, gain, rest, early, token_terms, qkv_terms, *pieces)


def body(block_in, lengths, qkv_weight, out_weight, up_weight, down_weight, norm_gain, norm_bias, cotangent):
    block, row_count, width = block_in.shape
    assert row_count == 1
    ranks = lax.axis_size("tensor")
    length = block * ranks
    local = out_weight.shape[0]
    pairs = local // PAIR
    finish = jnp.cumsum(lengths[0])
    begin = finish - lengths[0]
    places = jnp.arange(length, dtype=jnp.int32)
    segment = jnp.sum((places[:, None] >= finish[None, :]).astype(jnp.int32), axis=1)
    picked = segment[:, None] == jnp.arange(lengths.shape[1], dtype=jnp.int32)[None, :]
    starts = jnp.sum(jnp.where(picked, begin[None, :], 0), axis=1)
    position = (places - starts).astype(F32)
    lanes = jnp.arange(PAIR, dtype=jnp.int32)
    inverse = ROPE_BASE ** (-(lanes % (HD // 2)).astype(F32) * 2.0 / HD)
    angles = position[:, None] * inverse
    cosine = jnp.cos(angles)
    sine = jnp.sin(angles) * jnp.where(lanes % HD < HD // 2, -1.0, 1.0).astype(F32)
    start_column = starts.reshape(length, 1)
    start_row = starts.reshape(1, length)

    qkv, attn_full, heads_mixed, logs, heads_parts, rests = attend_forward(
        block_in.reshape(block, width),
        norm_gain[0:1],
        norm_bias[0:1],
        jnp.transpose(qkv_weight, (1, 0, 2)),
        cosine,
        sine,
        start_column,
        (out_weight, up_weight, down_weight),
    )
    attn_full = attn_full.reshape(length, width)
    block_out, grad_middle, grad_heads, shared, down_term, up_term, early = middle_stage(
        heads_parts,
        block_in.reshape(block, width),
        cotangent.reshape(block, width),
        norm_gain,
        norm_bias,
        (out_weight, up_weight, down_weight),
        rests,
    )
    group = lax.axis_size("dp") // 2
    shared = shared.reshape(ranks, 2, group, local // (2 * group), width)
    terms = []
    half_columns = width // 2
    for term in (down_term, up_term):
        cut = term.reshape(2, group, term.shape[0] // (2 * group), width)
        terms += [cut[..., :half_columns], cut[..., half_columns:]]

    grads, *pieces = attend_backward(
        qkv, grad_heads, heads_mixed, logs, start_row, cosine, sine, shared, terms, block
    )
    wide = jnp.concatenate([grads[i] for i in range(3 * pairs)], axis=1)
    qkv_flat = qkv_weight.reshape(width, 3 * local)
    token_terms = dot(wide, qkv_flat, NT).astype(BF).reshape(ranks, block, width)
    qkv_term = dot(attn_full, wide, TN).astype(BF).reshape(2, group, width // (2 * group), 3 * local)
    input_grad, sums, qkv_sum, *wholes = last_stage(
        block_in.reshape(block, width), norm_gain[0:1], grad_middle, early, token_terms, qkv_term, pieces
    )
    down_grad, up_grad = [
        jnp.concatenate([left.reshape(-1, half_columns), right.reshape(-1, half_columns)], axis=1).astype(F32)
        for left, right in (wholes[0:2], wholes[2:4])
    ]
    qkv_grad = qkv_sum.reshape(width, 3, local).astype(F32)
    gain_grad, bias_grad = sums[0:4], sums[4:8]
    out_grad = wholes[4].reshape(local, width).astype(F32)
    return (
        block_out.reshape(block_in.shape),
        input_grad.reshape(block_in.shape),
        qkv_grad,
        out_grad,
        up_grad,
        down_grad,
        gain_grad,
        bias_grad,
    )


def solution(mesh):
    tokens, rows, columns, copied = P("tensor", "dp", None), P("tensor", None), P(None, "tensor"), P()
    heads = P(None, None, "tensor")
    return jax.shard_map(
        body,
        mesh=mesh,
        in_specs=(tokens, P("dp", None), heads, rows, columns, rows, copied, copied, tokens),
        out_specs=(tokens, tokens, heads, rows, columns, rows, copied, copied),
        check_vma=False,
    )
```

```python
import functools

import jax
import jax.numpy as jnp
from jax import lax
from jax.experimental import pallas as pl
from jax.experimental.pallas import tpu as pltpu
from jax.sharding import PartitionSpec as P

HD = 64
PAIR = 128
EPSILON = 1e-05
ROPE_BASE = 10000.0
NEG = -1e30
MESH = pl.DeviceIdType.MESH
BF = jnp.bfloat16
F32 = jnp.float32
NT = (((1,), (1,)), ((), ()))
NN = (((1,), (0,)), ((), ()))
TN = (((0,), (0,)), ((), ()))


def dot(a, b, dims=NN):
    return lax.dot_general(a, b, dims, preferred_element_type=F32)


def layer_norm(values, gain, shift):
    centre = values - jnp.mean(values, axis=-1, keepdims=True)
    spread = jnp.mean(centre * centre, axis=-1, keepdims=True)
    return centre * lax.rsqrt(spread + EPSILON) * gain + shift


def flip(index, offset):
    bit = 1
    while bit <= offset:
        if offset & bit:
            index = index + bit - 2 * bit * lax.rem(lax.div(index, bit), 2)
        bit *= 2
    return index


def xor(a, b, size):
    total, bit = 0, 1
    while bit < size:
        total = total + bit * lax.rem(lax.div(a, bit) + lax.div(b, bit), 2)
        bit *= 2
    return total


def greet(axes):
    barrier = pltpu.get_barrier_semaphore()
    count = 0
    for axis in axes:
        index = lax.axis_index(axis)
        for d in range(1, lax.axis_size(axis)):
            pl.semaphore_signal(barrier, inc=1, device_id={axis: flip(index, d)}, device_id_type=MESH)
            count += 1
    pl.semaphore_wait(barrier, count)


def tree_sum(parts):
    parts = [part.astype(F32) for part in parts]
    while len(parts) > 1:
        parts = [parts[i] + parts[i + 1] for i in range(0, len(parts), 2)]
    return parts[0]


def push(src, dst, sems, slot, axis, offset):
    return pltpu.make_async_remote_copy(
        src_ref=src,
        dst_ref=dst,
        send_sem=sems.at[0, slot],
        recv_sem=sems.at[1, slot],
        device_id={axis: flip(lax.axis_index(axis), offset)},
        device_id_type=MESH,
    )


def turn(values, cosine, signed_sine):
    lane = lax.broadcasted_iota(jnp.int32, values.shape, 1)
    other = jnp.where(lane % HD < HD // 2, pltpu.roll(values, PAIR - HD // 2, 1), pltpu.roll(values, HD // 2, 1))
    return values * cosine + other * signed_sine


def head_mask(shape, head):
    lane = lax.broadcasted_iota(jnp.int32, shape, 1)
    return lane // HD == head


def forward_kernel(block, ranks, pairs, chunks, *refs):
    x_ref, gain_ref, shift_ref, w_ref, cos_ref, sin_ref, start_ref, *refs = refs
    weights, refs = refs[:3], refs[3:]
    qkv_ref, attn_ref, mixed_ref, log_ref, heads_ref, *refs = refs
    rests, refs = refs[:3], refs[3:]
    scores_ref, attn_sems, head_sems, own_sems, y_sems, z_sems, x_sems, core_sems = refs

    mine = lax.axis_index("tensor")
    rank = lax.axis_index("dp")
    group = lax.axis_size("dp") // 2
    x_bit, z_place = lax.rem(rank, 2), lax.div(rank, 2)
    length = block * ranks
    started = []

    def start(copy):
        copy.start()
        started.append(copy)
        return copy

    def cut(array, c, *lead):
        at, (_, low, size) = array.at, chunks[c]
        return at[(*lead, slice(None), pl.ds(low, size))]

    def every(array, c, *lead):
        at, (_, low, size) = array.at, chunks[c]
        return at[(*lead, slice(None), slice(None), pl.ds(low, size))]

    def rest(c):
        return rests[chunks[c][0]]

    y_copies = [
        push(
            cut(weights[chunks[c][0]], c, x_bit, z_place), cut(rest(c), c, 1, x_bit, z_place), y_sems, c, "tensor", 2
        )
        for c in range(len(chunks))
    ]
    z_copies = [
        [
            push(
                cut(rest(c), c, 1, x_bit, z_place),
                cut(rest(c), c, 1, x_bit, z_place),
                z_sems,
                c * (group - 1) + d - 1,
                "dp",
                2 * d,
            )
            for d in range(1, group)
        ]
        for c in range(len(chunks))
    ]
    x_copies = [
        push(every(rest(c), c, 1, x_bit), every(rest(c), c, 1, x_bit), x_sems, c, "dp", 1) for c in range(len(chunks))
    ]
    core_copies = [
        push(
            rest(c).at[1, :, :, :, pl.ds(chunks[c][1], chunks[c][2])],
            rest(c).at[2, :, :, :, pl.ds(chunks[c][1], chunks[c][2])],
            core_sems,
            c,
            "tensor",
            1,
        )
        for c in range(len(chunks))
    ]
    own_copies = [push(weights[a], rests[a].at[0], own_sems, a, "tensor", 1) for a in range(3)]

    def to_z(c):
        y_copies[c].wait_recv()
        for copy in z_copies[c]:
            copy.start()

    def to_x(c):
        for copy in z_copies[c]:
            copy.wait_recv()
        x_copies[c].start()

    def to_core(c):
        x_copies[c].wait_recv()
        core_copies[c].start()

    greet(("tensor", "dp"))
    early = len(chunks) - 2
    for c in range(early):
        y_copies[c].start()

    strips = 4
    strip = block // strips
    gain, shift = gain_ref[...], shift_ref[...]
    across, beside, onward = [], [], []
    for q in range(strips):

        @pl.loop(0, strip // 64)
        def _(r):
            at = pl.ds(pl.multiple_of(q * strip + r * 64, 64), 64)
            attn_ref[0, at, :] = layer_norm(x_ref[at, :].astype(F32), gain, shift).astype(BF)

        at = pl.ds(q * strip, strip)
        across.append(start(push(attn_ref.at[0, at], attn_ref.at[2, at], attn_sems, q, "tensor", 2)))
        beside.append(start(push(attn_ref.at[0, at], attn_ref.at[1, at], attn_sems, strips + q, "tensor", 1)))
        onward.append(push(attn_ref.at[2, at], attn_ref.at[3, at], attn_sems, 2 * strips + q, "tensor", 1))

    def middle():
        for c in range(early):
            to_z(c)
        for q in range(strips):
            across[q].wait_recv()
            onward[q].start()
        for c in range(early, len(chunks)):
            y_copies[c].start()
        for copy in own_copies:
            copy.start()
        for c in range(early - 1):
            to_x(c)

    def beside_here():
        for copy in beside:
            copy.wait_recv()

    def onward_here():
        for copy in onward:
            copy.wait_recv()

    @pl.loop(0, ranks)
    def _(d):
        pl.when(d == 1)(beside_here)
        pl.when(d == 2)(middle)
        pl.when(d == 3)(onward_here)
        x = attn_ref[d]
        rows = pl.ds(pl.multiple_of(d * block, block), block)
        real = pl.ds(pl.multiple_of(xor(d, mine, ranks) * block, block), block)
        for part in range(3):
            project = dot(x, w_ref[part])
            for pair in range(pairs):
                piece = project[:, pair * PAIR : (pair + 1) * PAIR]
                if part < 2:
                    piece = turn(piece, cos_ref[real, :], sin_ref[real, :])
                qkv_ref[part * pairs + pair, rows, :] = piece.astype(BF)

    def unit(pair, d):
        row_block = xor(d, mine, ranks)
        rows = pl.ds(pl.multiple_of(d * block, block), block)
        queries = qkv_ref[pair, rows, :] * HD**-0.5
        begin = start_ref[pl.ds(pl.multiple_of(row_block * block, block), block), :]
        mixed = None
        for head in range(PAIR // HD):
            mask = head_mask(queries.shape, head)
            query = jnp.where(mask, queries, jnp.zeros_like(queries))

            def score(j, top, last):
                at = pl.ds(pl.multiple_of(xor(j, mine, ranks) * block, block), block)
                s = dot(query, qkv_ref[pairs + pair, at, :], NT)
                column = lax.broadcasted_iota(jnp.int32, s.shape, 1)
                visible = column >= begin - j * block
                if last:
                    visible &= column <= lax.broadcasted_iota(jnp.int32, s.shape, 0)
                s = jnp.where(visible, s, NEG)
                scores_ref[j] = s
                for c in range(0, block, 128):
                    top = jnp.maximum(top, s[:, c : c + 128])
                return top

            top = jnp.full((block, 128), NEG, F32)
            top = lax.fori_loop(0, row_block, lambda j, top: score(j, top, False), top)
            top = score(row_block, top, True)
            top = jnp.max(top, axis=1, keepdims=True)

            def mix(j, carry):
                total, acc = carry
                shares = jnp.exp(scores_ref[j] - top)
                for c in range(0, block, 128):
                    total = total + shares[:, c : c + 128]
                at = pl.ds(pl.multiple_of(xor(j, mine, ranks) * block, block), block)
                return total, acc + dot(shares.astype(BF), qkv_ref[2 * pairs + pair, at, :])

            total, acc = lax.fori_loop(
                0, row_block + 1, mix, (jnp.zeros((block, 128), F32), jnp.zeros((block, PAIR), F32))
            )
            total = jnp.sum(total, axis=1, keepdims=True)
            acc = acc / total
            mixed = acc if mixed is None else jnp.where(mask, acc, mixed)
            logs = jnp.broadcast_to(top + jnp.log(total), (block, 128))
            log_ref[pair, head : head + 1, rows] = jnp.transpose(logs)[0:1, :]
        mixed_ref[pair, rows, :] = mixed.astype(BF)

    def head_copy(pair, d):
        slot = d * pairs + pair
        return pltpu.make_async_remote_copy(
            src_ref=mixed_ref.at[pair, pl.ds(pl.multiple_of(d * block, block), block)],
            dst_ref=heads_ref.at[slot],
            send_sem=head_sems.at[0, slot],
            recv_sem=head_sems.at[1, slot],
            device_id={"tensor": xor(mine, d, ranks)},
            device_id_type=MESH,
        )

    last = early - 1
    units = pairs * ranks
    events = {
        0: [lambda: to_x(last), lambda: to_z(early), lambda: to_z(early + 1)],
        2: [lambda c=c: to_core(c) for c in range(last)],
        3: [lambda: to_x(early)],
        4: [lambda: to_core(last)],
        6: [lambda: to_x(early + 1), lambda: to_core(early)],
    }

    @pl.loop(0, units)
    def _(u):
        pair, d = lax.rem(u, pairs), ranks - 1 - lax.div(u, pairs)
        unit(pair, d)
        pl.when(d > 0)(lambda: head_copy(pair, d).start())
        for when, steps in events.items():

            @pl.when(u == min(when, units - 1))
            def _():
                for step in steps:
                    step()

    for pair in range(pairs):
        heads_ref[pair] = mixed_ref[pair, 0:block, :]
    to_core(early + 1)

    @pl.loop(pairs, units)
    def _(slot):
        copy = head_copy(lax.rem(slot, pairs), lax.div(slot, pairs))
        copy.wait_recv()
        copy.wait_send()

    for copy in [*core_copies, *own_copies]:
        copy.wait_recv()
    for copy in [*started, *onward, *own_copies, *y_copies, *x_copies, *core_copies]:
        copy.wait_send()
    for copies in z_copies:
        for copy in copies:
            copy.wait_send()


def attend_forward(tokens, gain, shift, weight, cosine, sine, starts, weights):
    block, width = tokens.shape
    ranks = lax.axis_size("tensor")
    assert ranks == 4
    length = block * ranks
    pairs = weight.shape[2] // PAIR
    group = lax.axis_size("dp") // 2
    views = [w.reshape(2, group, w.shape[0] // (2 * group), w.shape[1]) for w in weights]
    chunks = [(0, 0, width)]
    for a in (1, 2):
        columns = weights[a].shape[1] // 2
        chunks += [(a, 0, columns), (a, columns, columns)]
    vmem = pl.BlockSpec(memory_space=pltpu.VMEM)
    hbm = pl.BlockSpec(memory_space=pl.ANY)
    copies = pltpu.SemaphoreType.DMA
    qkv, attn, mixed, logs, heads, *rests = pl.pallas_call(
        functools.partial(forward_kernel, block, ranks, pairs, chunks),
        out_shape=[
            jax.ShapeDtypeStruct((3 * pairs, length, PAIR), BF),
            jax.ShapeDtypeStruct((ranks, block, width), BF),
            jax.ShapeDtypeStruct((pairs, length, PAIR), BF),
            jax.ShapeDtypeStruct((pairs, 8, length), F32),
            jax.ShapeDtypeStruct((ranks * pairs, block, PAIR), BF),
            *[jax.ShapeDtypeStruct((ranks - 1, *view.shape), BF) for view in views],
        ],
        in_specs=[vmem] * 7 + [hbm] * 3,
        out_specs=[vmem] * 5 + [hbm] * 3,
        scratch_shapes=[
            pltpu.VMEM((ranks, block, block), F32),
            copies((2, 12)),
            copies((2, ranks * pairs)),
            copies((2, 3)),
            copies((2, len(chunks))),
            copies((2, len(chunks) * (group - 1))),
            copies((2, len(chunks))),
            copies((2, len(chunks))),
        ],
        compiler_params=pltpu.CompilerParams(vmem_limit_bytes=56 << 20, collective_id=2, has_side_effects=True),
        name="attend_forward",
    )(tokens, gain, shift, weight, cosine, sine, starts, *views)
    return qkv, attn, mixed, logs, heads, [r.reshape(ranks - 1, *w.shape) for r, w in zip(rests, weights)]


def unit_scale(values):
    centre = values - jnp.mean(values, axis=-1, keepdims=True)
    scale = lax.rsqrt(jnp.mean(centre * centre, axis=-1, keepdims=True) + EPSILON)
    return centre * scale, scale


def norm_pull(grad, unit, scale, gain):
    inside = grad * gain
    first = jnp.mean(inside, axis=-1, keepdims=True)
    second = jnp.mean(inside * unit, axis=-1, keepdims=True)
    return scale * (inside - first - unit * second)


def gelu_both(x):
    bend = 0.7978845608028654
    square = x * x
    t = jnp.tanh(bend * (x + 0.044715 * (square * x)))
    side = 0.5 * (1.0 + t)
    return x * side, side + 0.5 * x * (1.0 - t * t) * (bend * (1.0 + 0.134145 * square))


def middle_kernel(block, ranks, pairs, *refs):
    (heads_ref, x_ref, dy_ref, gains_ref, shifts_ref, *refs) = refs
    sources, refs = refs[:6], refs[6:]
    (out_ref, rest_ref, do_ref, shared_ref, terms_ref, early_ref, *refs) = refs
    (out_all, up_all, down_all, work_ref, mlp_ref, gmp_ref, middle_ref, proj_ref, acc_ref, gap_ref, gh_ref, *refs) = refs
    (out_sems, up_sems, down_sems, mlp_sems, gmp_sems, head_sems) = refs

    mine = lax.axis_index("tensor")
    width = x_ref.shape[1]
    strips, rows = 4, 64
    strip = block // strips
    columns = width // 2

    def loads(own, rest, array, sems):
        return [
            pltpu.make_async_copy(own if d == 0 else rest.at[d - 1], array.at[d], sems.at[d]) for d in range(ranks)
        ]

    out_loads = loads(sources[0], sources[1], out_all, out_sems)
    up_loads = loads(sources[2], sources[3], up_all, up_sems)
    down_loads = loads(sources[4], sources[5], down_all, down_sems)
    for copy in out_loads:
        copy.start()
    for d in range(ranks):
        up_loads[d].start()
        down_loads[d].start()
    greet(("tensor",))

    def senders(array, sems):
        found = []
        for q in range(strips):
            at = pl.ds(q * strip, strip)
            found.append(
                (
                    push(array.at[0, at], array.at[2, at], sems, q, "tensor", 2),
                    push(array.at[0, at], array.at[1, at], sems, strips + q, "tensor", 1),
                    push(array.at[2, at], array.at[3, at], sems, 2 * strips + q, "tensor", 1),
                )
            )
        return found

    mlp_copies = senders(mlp_ref, mlp_sems)
    gmp_copies = senders(gmp_ref, gmp_sems)

    def send_strip(copies, q):
        copies[q][0].start()
        copies[q][1].start()

    def forward_on(copies):
        for across, _, onward in copies:
            across.wait_recv()
            onward.start()

    for d in range(ranks):
        out_loads[d].wait()
    for c in (0, columns):
        at = pl.ds(c, columns)
        total = None
        for d in range(ranks):
            part = jnp.concatenate([heads_ref[d * pairs + p] for p in range(pairs)], axis=1)
            term = dot(part, out_all[d, :, at])
            total = term if total is None else total + term
        proj_ref[:, at] = total

    gain = [gains_ref[j : j + 1, :] for j in range(4)]
    shift = [shifts_ref[j : j + 1, :] for j in range(4)]

    for q in range(strips):

        @pl.loop(0, strip // rows)
        def _(r):
            at = pl.ds(pl.multiple_of(q * strip + r * rows, rows), rows)
            unit, _ = unit_scale(proj_ref[at, :])
            middle = x_ref[at, :].astype(F32) + (unit * gain[1] + shift[1])
            middle_ref[at, :] = middle
            unit, _ = unit_scale(middle)
            mlp_ref[0, at, :] = (unit * gain[2] + shift[2]).astype(BF)

        send_strip(mlp_copies, q)

    acc_ref[...] = jnp.zeros_like(acc_ref)

    @pl.loop(0, ranks)
    def _(d):
        pltpu.make_async_copy(up_all.at[d], up_all.at[d], up_sems.at[d]).wait()
        pltpu.make_async_copy(down_all.at[d], down_all.at[d], down_sems.at[d]).wait()
        for c in (0, columns):
            at = pl.ds(c, columns)
            hidden, slope = gelu_both(dot(mlp_ref[0], up_all[d, :, at]))
            work_ref[d, :, at] = slope
            acc_ref[...] += dot(hidden.astype(BF), down_all[d, at, :])

    zero = jnp.zeros((1, width), F32)
    gain_three, shift_three = zero, zero
    for q in range(strips):

        def last_norm(r, carry):
            gain_term, shift_term = carry
            at = pl.ds(pl.multiple_of(q * strip + r * rows, rows), rows)
            unit, scale = unit_scale(acc_ref[at, :])
            out_ref[at, :] = (middle_ref[at, :] + (unit * gain[3] + shift[3])).astype(BF)
            dy = dy_ref[at, :].astype(F32)
            gmp_ref[0, at, :] = norm_pull(dy, unit, scale, gain[3]).astype(BF)
            return (
                gain_term + jnp.sum(dy * unit, axis=0, keepdims=True),
                shift_term + jnp.sum(dy, axis=0, keepdims=True),
            )

        gain_three, shift_three = lax.fori_loop(0, strip // rows, last_norm, (gain_three, shift_three))
        send_strip(gmp_copies, q)

    acc_ref[...] = jnp.zeros_like(acc_ref)

    @pl.loop(0, ranks)
    def _(d):
        for c in (0, columns):
            at = pl.ds(c, columns)
            grad = dot(gmp_ref[0], down_all[d, at, :], NT)
            grad = (grad * work_ref[d, :, at]).astype(BF)
            acc_ref[...] += dot(grad, up_all[d, :, at], NT)

    forward_on(mlp_copies)

    def inner_norms(r, carry):
        gain_two, shift_two, gain_one, shift_one = carry
        at = pl.ds(pl.multiple_of(r * rows, rows), rows)
        grad = acc_ref[at, :]
        unit, scale = unit_scale(middle_ref[at, :])
        gain_two = gain_two + jnp.sum(grad * unit, axis=0, keepdims=True)
        shift_two = shift_two + jnp.sum(grad, axis=0, keepdims=True)
        grad = dy_ref[at, :].astype(F32) + norm_pull(grad, unit, scale, gain[2])
        rest_ref[at, :] = grad
        unit, scale = unit_scale(proj_ref[at, :])
        gain_one = gain_one + jnp.sum(grad * unit, axis=0, keepdims=True)
        shift_one = shift_one + jnp.sum(grad, axis=0, keepdims=True)
        gap_ref[at, :] = norm_pull(grad, unit, scale, gain[1]).astype(BF)
        return gain_two, shift_two, gain_one, shift_one

    gain_two, shift_two, gain_one, shift_one = lax.fori_loop(0, block // rows, inner_norms, (zero, zero, zero, zero))
    early_ref[...] = jnp.concatenate(
        [zero, gain_one, gain_two, gain_three, zero, shift_one, shift_two, shift_three], axis=0
    )

    head_copies = []
    for d in [*range(1, ranks), 0]:
        grad = dot(gap_ref[...], out_all[d], NT).astype(BF)
        for pair in range(pairs):
            piece = grad[:, pair * PAIR : (pair + 1) * PAIR]
            if d == 0:
                do_ref[pair, 0] = piece
            else:
                slot = d * pairs + pair
                gh_ref[slot] = piece
                copy = push(gh_ref.at[slot], do_ref.at[pair, d], head_sems, slot, "tensor", d)
                copy.start()
                head_copies.append(copy)
    for d in range(ranks):
        part = jnp.concatenate([heads_ref[d * pairs + p] for p in range(pairs)], axis=1)
        shared_ref[d] = dot(part, gap_ref[...], TN).astype(BF)

    for copies in (mlp_copies, gmp_copies):
        for _, beside, _ in copies:
            beside.wait_recv()
    work_ref[...] = jnp.zeros_like(work_ref)

    def late():
        forward_on(gmp_copies)

    def latest():
        for copies in (mlp_copies, gmp_copies):
            for _, _, onward in copies:
                onward.wait_recv()

    @pl.loop(0, ranks)
    def _(b):
        pl.when(b == 2)(late)
        pl.when(b == 3)(latest)
        tokens, grads = mlp_ref[b], gmp_ref[b]
        for h in range(2):
            at = pl.ds(h * columns, columns)
            hidden, slope = gelu_both(dot(tokens, up_all[0, :, at]))
            grad = (dot(grads, down_all[0, at, :], NT) * slope).astype(BF)
            work_ref[h] += dot(hidden.astype(BF), grads, TN)
            work_ref[2, :, at] += dot(tokens[:, 0:columns], grad, TN)
            work_ref[3, :, at] += dot(tokens[:, columns:], grad, TN)

    for h in range(2):
        at = pl.ds(h * columns, columns)
        for side in range(2):
            there = pl.ds(side * columns, columns)
            terms_ref[side, at, :] = work_ref[h, :, there].astype(BF)
            terms_ref[2 + side, at, :] = work_ref[2 + h, :, there].astype(BF)
    for copy in head_copies:
        copy.wait_recv()
        copy.wait_send()
    for copies in (mlp_copies, gmp_copies):
        for group in copies:
            for copy in group:
                copy.wait_send()


def middle_stage(heads, tokens, cotangent, gains, shifts, weights, rests):
    block, width = tokens.shape
    ranks = lax.axis_size("tensor")
    local = weights[0].shape[0]
    pairs = local // PAIR
    hidden = weights[2].shape[0]
    vmem = pl.BlockSpec(memory_space=pltpu.VMEM)
    hbm = pl.BlockSpec(memory_space=pl.ANY)
    copies = pltpu.SemaphoreType.DMA
    assert block * 2 == width and hidden == width
    operands = [array for pair in zip(weights, rests) for array in pair]
    return pl.pallas_call(
        functools.partial(middle_kernel, block, ranks, pairs),
        out_shape=[
            jax.ShapeDtypeStruct((block, width), BF),
            jax.ShapeDtypeStruct((block, width), F32),
            jax.ShapeDtypeStruct((pairs, ranks, block, PAIR), BF),
            jax.ShapeDtypeStruct((ranks, local, width), BF),
            jax.ShapeDtypeStruct((4, width, width // 2), BF),
            jax.ShapeDtypeStruct((8, width), F32),
        ],
        in_specs=[vmem] * 5 + [hbm] * 6,
        out_specs=[vmem] * 6,
        scratch_shapes=[
            pltpu.VMEM((ranks, local, width), BF),
            pltpu.VMEM((ranks, width, hidden), BF),
            pltpu.VMEM((ranks, hidden, width), BF),
            pltpu.VMEM((ranks, block, width), F32),
            pltpu.VMEM((ranks, block, width), BF),
            pltpu.VMEM((ranks, block, width), BF),
            pltpu.VMEM((block, width), F32),
            pltpu.VMEM((block, width), F32),
            pltpu.VMEM((block, width), F32),
            pltpu.VMEM((block, width), BF),
            pltpu.VMEM((ranks * pairs, block, PAIR), BF),
            copies((ranks,)),
            copies((ranks,)),
            copies((ranks,)),
            copies((2, 12)),
            copies((2, 12)),
            copies((2, ranks * pairs)),
        ],
        compiler_params=pltpu.CompilerParams(vmem_limit_bytes=62 << 20, collective_id=3, has_side_effects=True),
        name="middle_stage",
    )(heads, tokens, cotangent, gains, shifts, *operands)


def finish_kernel(block, blocks, pairs, orders, *refs):
    (qkv_ref, do_ref, o_ref, log_ref, start_ref, cos_ref, sin_ref, *refs) = refs
    (shared_ref, terms_ref, attn_ref, w_ref, x_ref, gain_ref, rest_ref, early_ref, *refs) = refs
    (input_ref, sums_ref, mlp_out, own_out, qkv_out, *refs) = refs
    (dq_ref, inner_ref, grads_ref, own_ref, wide_ref, token_ref, core_sum, got_y, *refs) = refs
    (token_sum, token_y, norm_ref, got_t, sum_t, got_d, *refs) = refs
    chunks, steps = len(orders), len(orders[0])
    count = chunks * steps
    got, refs = refs[:count], refs[count:]
    (rs_sems, ag_sems, core_sems, y_sems, token_core_sems, token_y_sems, t_sems, d_sems) = refs

    mine = lax.axis_index("tensor")
    rank = lax.axis_index("dp")
    ranks_dp = lax.axis_size("dp")
    heads = PAIR // HD
    mlp_chunks = terms_ref.shape[0]
    started = []

    def start(copy):
        copy.start()
        started.append(copy)
        return copy

    sources = [terms_ref.at[c] for c in range(mlp_chunks)] + [own_ref] + [wide_ref.at[p] for p in range(pairs)]
    results = [mlp_out.at[c] for c in range(mlp_chunks)] + [own_out] + [qkv_out.at[p] for p in range(pairs)]
    bits = [[lax.rem(lax.div(rank, 1 << o), 2) for o in order] for order in orders]
    rs_copies, ag_copies = {}, {}

    def held(c, k):
        return sources[c] if k == 0 else got[c * steps + k - 1]

    for c in range(chunks):
        for k in range(steps):
            far = 1 << orders[c][k]
            rs_copies[c, k] = push(held(c, k).at[1 - bits[c][k]], got[c * steps + k], rs_sems, c * steps + k, "dp", far)
            region = results[c].at[tuple(bits[c][: k + 1])]
            ag_copies[c, k] = push(region, region, ag_sems, c * steps + k, "dp", far)

    def begin(c):
        rs_copies[c, 0].start()

    def halve(c, k):
        at = c * steps + k
        rs_copies[c, k].wait_recv()
        total = held(c, k)[bits[c][k]].astype(F32) + got[at][...].astype(F32)
        got[at][...] = total.astype(BF)
        if k + 1 < steps:
            rs_copies[c, k + 1].start()
        else:
            results[c][tuple(bits[c])] = total.astype(BF)
            ag_copies[c, k].start()

    def double(c, k):
        ag_copies[c, k].wait_recv()
        if k > 0:
            ag_copies[c, k - 1].start()

    core_copies = [
        push(shared_ref.at[d + 1], core_sum.at[d // 2], core_sems, d // 2, "tensor", 1) for d in range(0, blocks, 2)
    ]
    y_copies = [
        push(core_sum.at[h], got_y.at[h - 1], y_sems, h - 1, "tensor", 2 * h) for h in range(1, blocks // 2)
    ]

    def pair_up():
        for h in range(blocks // 2):
            core_copies[h].wait_recv()
            core_sum[h] = (shared_ref[2 * h].astype(F32) + core_sum[h].astype(F32)).astype(BF)
        for copy in y_copies:
            copy.start()

    def settle():
        total = core_sum[0].astype(F32)
        for h in range(1, blocks // 2):
            y_copies[h - 1].wait_recv()
            total = total + got_y[h - 1].astype(F32)
        own_ref[...] = total.astype(BF)

    def prepare(pair):
        dq_ref[...] = jnp.zeros_like(dq_ref)
        for b in range(blocks):
            rows = pl.ds(b * block, block)
            product = do_ref[pair, b].astype(F32) * o_ref[pair, rows, :].astype(F32)
            high = product.astype(BF)
            low = (product - high.astype(F32)).astype(BF)
            for head in range(heads):
                ones = head_mask((16, PAIR), head).astype(F32).astype(BF)
                inner = dot(ones, high, NT) + dot(ones, low, NT)
                inner_ref[head : head + 1, rows] = inner[0:1, :]

    def unit(pair, key_block):
        slot = xor(key_block, mine, blocks)
        here = pl.ds(pl.multiple_of(slot * block, block), block)
        keys = qkv_ref[pairs + pair, here, :]
        values = qkv_ref[2 * pairs + pair, here, :]
        dk = jnp.zeros((block, PAIR), F32)
        dv = jnp.zeros((block, PAIR), F32)
        for head in range(heads):
            mask = head_mask(keys.shape, head)
            key = jnp.where(mask, keys * HD**-0.5, jnp.zeros_like(keys))
            value = jnp.where(mask, values, jnp.zeros_like(values))

            def one(i, carry, first):
                dk, dv = carry
                place = xor(i, mine, blocks)
                rows = pl.ds(pl.multiple_of(place * block, block), block)
                real = pl.ds(pl.multiple_of(i * block, block), block)
                query = qkv_ref[pair, rows, :]
                grad = do_ref[pair, place]
                s = dot(key, query, NT)
                row = lax.broadcasted_iota(jnp.int32, s.shape, 0)
                visible = row >= start_ref[0:1, real] - key_block * block
                if first:
                    visible &= row <= lax.broadcasted_iota(jnp.int32, s.shape, 1)
                probs = jnp.where(visible, jnp.exp(s - log_ref[pair, head : head + 1, rows]), 0.0)
                grad_probs = dot(value, grad, NT)
                ds = (probs * (grad_probs - inner_ref[head : head + 1, rows])).astype(BF)
                zero = jnp.zeros_like(query)
                dv = dv + dot(probs.astype(BF), jnp.where(mask, grad, zero))
                dk = dk + dot(ds, jnp.where(mask, query, zero))
                dq_ref[rows, :] += dot(ds, key, TN)
                return dk, dv

            dk, dv = one(key_block, (dk, dv), True)
            dk, dv = lax.fori_loop(key_block + 1, blocks, lambda i, carry: one(i, carry, False), (dk, dv))
        real = pl.ds(pl.multiple_of(key_block * block, block), block)
        grads_ref[pairs + pair, here, :] = turn(dk * HD**-0.5, cos_ref[real, :], -sin_ref[real, :]).astype(BF)
        grads_ref[2 * pairs + pair, here, :] = dv.astype(BF)

    def close(pair):
        for b in range(blocks):
            rows = pl.ds(b * block, block)
            real = pl.ds(pl.multiple_of(flip(mine, b) * block, block), block)
            grads_ref[pair, rows, :] = turn(dq_ref[rows, :], cos_ref[real, :], -sin_ref[real, :]).astype(BF)
        total = None
        for b in range(blocks):
            rows = pl.ds(b * block, block)
            wide = jnp.concatenate([grads_ref[c * pairs + pair, rows, :] for c in range(3)], axis=1)
            term = dot(attn_ref[b], wide, TN)
            total = term if total is None else total + term
        wide_ref[pair] = total.astype(BF).reshape(wide_ref.shape[1:])

    greet(("tensor", "dp"))
    for copy in core_copies:
        copy.start()
    first_q = mlp_chunks + 1
    begin(0)
    begin(3)
    begin(1)
    slots = pairs * blocks
    events = {
        0: [pair_up],
        2: [lambda: halve(0, 0), lambda: halve(3, 0), lambda: begin(2)],
        3: [settle, lambda: begin(mlp_chunks)],
        4: [lambda: halve(1, 0), lambda: halve(0, 1)],
        5: [lambda: begin(first_q), lambda: halve(3, 1), lambda: halve(1, 1), lambda: halve(0, 2)],
        6: [lambda: halve(2, 0), lambda: halve(3, 2), lambda: halve(1, 2), lambda: double(0, 2)],
        7: [lambda: halve(4, 0), lambda: halve(2, 1), lambda: double(0, 1), lambda: double(3, 2), lambda: double(1, 2)],
    }

    @pl.loop(0, slots)
    def _(u):
        pair, key_block = lax.div(u, blocks), lax.rem(u, blocks)
        for when, todo in events.items():

            @pl.when(u == when)
            def _():
                for step in todo:
                    step()

        for p in range(pairs):
            pl.when(u == p * blocks)(functools.partial(prepare, p))
        unit(pair, key_block)
        for p in range(pairs):
            pl.when(u == p * blocks + blocks - 1)(functools.partial(close, p))

    begin(first_q + 1)

    def token_term(d):
        rows = pl.ds(d * block, block)
        total = None
        for c in range(3):
            wide = jnp.concatenate([grads_ref[c * pairs + p, rows, :] for p in range(pairs)], axis=1)
            term = dot(wide, w_ref[c], NT)
            total = term if total is None else total + term
        token_ref[d] = total.astype(BF)

    token_copies = []
    for d in range(0, blocks, 2):
        token_term(d + 1)
        token_copies.append(start(push(token_ref.at[d + 1], token_sum.at[d // 2], token_core_sems, d // 2, "tensor", 1)))
    halve(2, 2)
    double(1, 1)
    for d in range(blocks - 2, -1, -2):
        token_term(d)
        token_copies[d // 2].wait_recv()
        token_sum[d // 2] = (token_ref[d].astype(F32) + token_sum[d // 2].astype(F32)).astype(BF)
        if d > 0:
            across = start(push(token_sum.at[d // 2], token_y.at[d // 2 - 1], token_y_sems, d // 2 - 1, "tensor", d))
    halve(4, 1)
    halve(5, 0)
    double(3, 1)
    double(2, 2)
    halve(4, 2)
    halve(5, 1)
    halve(6, 0)
    double(2, 1)
    double(4, 2)
    halve(5, 2)
    halve(6, 1)

    across.wait_recv()
    rows = 64
    gain = gain_ref[...]

    def norm(r, carry):
        gain_term, shift_term = carry
        at = pl.ds(pl.multiple_of(r * rows, rows), rows)
        grad = token_sum[0, at, :].astype(F32)
        for h in range(blocks // 2 - 1):
            grad = grad + token_y[h, at, :].astype(F32)
        unit, scale = unit_scale(x_ref[at, :].astype(F32))
        input_ref[at, :] = rest_ref[at, :] + norm_pull(grad, unit, scale, gain)
        return (
            gain_term + jnp.sum(grad * unit, axis=0, keepdims=True),
            shift_term + jnp.sum(grad, axis=0, keepdims=True),
        )

    zero = jnp.zeros(gain.shape, F32)
    gain_term, shift_term = lax.fori_loop(0, block // rows, norm, (zero, zero))
    norm_ref[...] = early_ref[...]
    norm_ref[0:1, :] = gain_term
    norm_ref[4:5, :] = shift_term
    ts = [start(push(norm_ref, got_t.at[d - 1], t_sems, d - 1, "tensor", d)) for d in range(1, blocks)]
    double(4, 1)
    halve(6, 2)
    double(5, 2)
    double(5, 1)
    for copy in ts:
        copy.wait_recv()
    sum_t[...] = tree_sum([norm_ref[...]] + [got_t[d] for d in range(blocks - 1)])
    ds = [start(push(sum_t, got_d.at[d - 1], d_sems, d - 1, "dp", d)) for d in range(1, ranks_dp)]
    for k in range(steps - 1, 0, -1):
        double(6, k)
    for copy in ds:
        copy.wait_recv()
    sums_ref[...] = tree_sum([sum_t[...]] + [got_d[d] for d in range(ranks_dp - 1)])
    for c in range(chunks):
        double(c, 0)
    for copy in [*started, *core_copies, *y_copies, *rs_copies.values(), *ag_copies.values()]:
        copy.wait_send()


def finish_stage(qkv, grad_heads, heads_out, logs, start_row, cosine, sine, shared, terms, attn, weight, tokens, gain, rest, early):
    pairs3, length, _ = qkv.shape
    pairs = pairs3 // 3
    block, width = tokens.shape
    blocks = length // block
    ranks_dp = lax.axis_size("dp")
    steps = ranks_dp.bit_length() - 1
    straight = list(range(steps))
    orders = [straight] * 3 + [[1, 0, *straight[2:]]] + [straight] * 3
    cut = (2,) * steps
    local = shared.shape[1]
    shared = shared.reshape(blocks, *cut, local // ranks_dp, width)
    terms = terms.reshape(terms.shape[0], *cut, terms.shape[1] // ranks_dp, terms.shape[2])
    wide = (*cut, width // ranks_dp, 3 * PAIR)
    shapes = [terms.shape[1:]] * terms.shape[0] + [shared.shape[1:]] + [wide] * pairs
    parts = [shape[k + 1 :] for shape in shapes for k in range(steps)]
    vmem = pl.BlockSpec(memory_space=pltpu.VMEM)
    copies = pltpu.SemaphoreType.DMA
    outs = pl.pallas_call(
        functools.partial(finish_kernel, block, blocks, pairs, orders),
        out_shape=[
            jax.ShapeDtypeStruct((block, width), F32),
            jax.ShapeDtypeStruct((8, width), F32),
            jax.ShapeDtypeStruct(terms.shape, BF),
            jax.ShapeDtypeStruct(shared.shape[1:], BF),
            jax.ShapeDtypeStruct((pairs, *wide), BF),
        ],
        in_specs=[vmem] * 15,
        out_specs=[vmem] * 5,
        scratch_shapes=[
            pltpu.VMEM((length, PAIR), F32),
            pltpu.VMEM((8, length), F32),
            pltpu.VMEM((pairs3, length, PAIR), BF),
            pltpu.VMEM(shared.shape[1:], BF),
            pltpu.VMEM((pairs, *wide), BF),
            pltpu.VMEM((blocks, block, width), BF),
            pltpu.VMEM((blocks // 2, *shared.shape[1:]), BF),
            pltpu.VMEM((blocks // 2 - 1, *shared.shape[1:]), BF),
            pltpu.VMEM((blocks // 2, block, width), BF),
            pltpu.VMEM((blocks // 2 - 1, block, width), BF),
            pltpu.VMEM((8, width), F32),
            pltpu.VMEM((blocks - 1, 8, width), F32),
            pltpu.VMEM((8, width), F32),
            pltpu.VMEM((ranks_dp - 1, 8, width), F32),
            *[pltpu.VMEM(shape, BF) for shape in parts],
            copies((2, len(parts))),
            copies((2, len(parts))),
            copies((2, blocks // 2)),
            copies((2, blocks // 2 - 1)),
            copies((2, blocks // 2)),
            copies((2, blocks // 2 - 1)),
            copies((2, blocks - 1)),
            copies((2, ranks_dp - 1)),
        ],
        compiler_params=pltpu.CompilerParams(vmem_limit_bytes=62 << 20, collective_id=0, has_side_effects=True),
        name="finish_stage",
    )(qkv, grad_heads, heads_out, logs, start_row, cosine, sine, shared, terms, attn, weight, tokens, gain, rest, early)
    input_grad, sums, mlp, own, wides = outs
    return input_grad, sums, mlp.reshape(4, width, -1), own.reshape(local, width), wides.reshape(pairs, width, 3 * PAIR)


def body(block_in, lengths, qkv_weight, out_weight, up_weight, down_weight, norm_gain, norm_bias, cotangent):
    block, row_count, width = block_in.shape
    assert row_count == 1
    ranks = lax.axis_size("tensor")
    length = block * ranks
    local = out_weight.shape[0]
    pairs = local // PAIR
    qkv_swapped = jnp.transpose(qkv_weight, (1, 0, 2))

    finish = jnp.cumsum(lengths[0])
    begin = finish - lengths[0]
    places = jnp.arange(length, dtype=jnp.int32)
    segment = jnp.sum((places[:, None] >= finish[None, :]).astype(jnp.int32), axis=1)
    picked = segment[:, None] == jnp.arange(lengths.shape[1], dtype=jnp.int32)[None, :]
    starts = jnp.sum(jnp.where(picked, begin[None, :], 0), axis=1)
    position = (places - starts).astype(F32)
    lanes = jnp.arange(PAIR, dtype=jnp.int32)
    inverse = ROPE_BASE ** (-(lanes % (HD // 2)).astype(F32) * 2.0 / HD)
    angles = position[:, None] * inverse
    cosine = jnp.cos(angles)
    sine = jnp.sin(angles) * jnp.where(lanes % HD < HD // 2, -1.0, 1.0).astype(F32)
    start_column = starts.reshape(length, 1)
    start_row = starts.reshape(1, length)

    qkv, attn_full, heads_mixed, logs, heads_parts, rests = attend_forward(
        block_in.reshape(block, width),
        norm_gain[0:1],
        norm_bias[0:1],
        qkv_swapped,
        cosine,
        sine,
        start_column,
        (out_weight, up_weight, down_weight),
    )
    block_out, grad_middle, grad_heads, shared, terms, early = middle_stage(
        heads_parts,
        block_in.reshape(block, width),
        cotangent.reshape(block, width),
        norm_gain,
        norm_bias,
        (out_weight, up_weight, down_weight),
        rests,
    )
    input_grad, sums, mlp_sums, out_sum, qkv_sums = finish_stage(
        qkv,
        grad_heads,
        heads_mixed,
        logs,
        start_row,
        cosine,
        sine,
        shared,
        terms,
        attn_full,
        qkv_swapped,
        block_in.reshape(block, width),
        norm_gain[0:1],
        grad_middle,
        early,
    )
    down_grad, up_grad = [jnp.concatenate([mlp_sums[i], mlp_sums[i + 1]], axis=1).astype(F32) for i in (0, 2)]
    qkv_grad = jnp.stack(
        [jnp.concatenate([qkv_sums[p, :, c * PAIR : (c + 1) * PAIR] for p in range(pairs)], axis=1) for c in range(3)]
    ).astype(F32)
    qkv_grad = jnp.transpose(qkv_grad, (1, 0, 2))
    out_grad = out_sum.astype(F32)
    gain_grad, bias_grad = sums[0:4], sums[4:8]
    return (
        block_out.reshape(block_in.shape),
        input_grad.reshape(block_in.shape),
        qkv_grad,
        out_grad,
        up_grad,
        down_grad,
        gain_grad,
        bias_grad,
    )


def solution(mesh):
    tokens, rows, columns, copied = P("tensor", "dp", None), P("tensor", None), P(None, "tensor"), P()
    heads = P(None, None, "tensor")
    return jax.shard_map(
        body,
        mesh=mesh,
        in_specs=(tokens, P("dp", None), heads, rows, columns, rows, copied, copied, tokens),
        out_specs=(tokens, tokens, heads, rows, columns, rows, copied, copied),
        check_vma=False,
    )
```

```python
import functools

import jax
import jax.numpy as jnp
import numpy as np
from jax import lax
from jax.experimental import pallas as pl
from jax.experimental.pallas import tpu as pltpu
from jax.sharding import PartitionSpec as P

HD = 64
PAIR = 128
EPSILON = 1e-05
ROPE_BASE = 10000.0
NEG = -1e30
MESH = pl.DeviceIdType.MESH
BF = jnp.bfloat16
F32 = jnp.float32
NT = (((1,), (1,)), ((), ()))
NN = (((1,), (0,)), ((), ()))
TN = (((0,), (0,)), ((), ()))


def dot(a, b, dims=NN):
    return lax.dot_general(a, b, dims, preferred_element_type=F32)


def layer_norm(values, gain, shift):
    centre = values - jnp.mean(values, axis=-1, keepdims=True)
    spread = jnp.mean(centre * centre, axis=-1, keepdims=True)
    return centre * lax.rsqrt(spread + EPSILON) * gain + shift


def flip(index, offset):
    bit = 1
    while bit <= offset:
        if offset & bit:
            index = index + bit - 2 * bit * lax.rem(lax.div(index, bit), 2)
        bit *= 2
    return index


def xor(a, b, size):
    total, bit = 0, 1
    while bit < size:
        total = total + bit * lax.rem(lax.div(a, bit) + lax.div(b, bit), 2)
        bit *= 2
    return total


def greet(axes):
    barrier = pltpu.get_barrier_semaphore()
    count = 0
    for axis in axes:
        index = lax.axis_index(axis)
        for d in range(1, lax.axis_size(axis)):
            pl.semaphore_signal(barrier, inc=1, device_id={axis: flip(index, d)}, device_id_type=MESH)
            count += 1
    pl.semaphore_wait(barrier, count)


def tree_sum(parts):
    parts = [part.astype(F32) for part in parts]
    while len(parts) > 1:
        parts = [parts[i] + parts[i + 1] for i in range(0, len(parts), 2)]
    return parts[0]


def push(src, dst, sems, slot, axis, offset):
    return pltpu.make_async_remote_copy(
        src_ref=src,
        dst_ref=dst,
        send_sem=sems.at[0, slot],
        recv_sem=sems.at[1, slot],
        device_id={axis: flip(lax.axis_index(axis), offset)},
        device_id_type=MESH,
    )


def turn(values, cosine, signed_sine):
    lane = lax.broadcasted_iota(jnp.int32, values.shape, 1)
    other = jnp.where(lane % HD < HD // 2, pltpu.roll(values, PAIR - HD // 2, 1), pltpu.roll(values, HD // 2, 1))
    return values * cosine + other * signed_sine


def head_mask(shape, head):
    lane = lax.broadcasted_iota(jnp.int32, shape, 1)
    return lane // HD == head


def document_start(lengths_ref, spot):
    begin = jnp.zeros_like(spot)
    total = jnp.int32(0)
    for j in range(lengths_ref.shape[1] - 1):
        total = total + lengths_ref[0, j]
        begin = jnp.where(spot >= total, total, begin)
    return begin


def forward_kernel(block, ranks, pairs, chunks, *refs):
    lengths_ref, x_ref, gain_ref, shift_ref, w_ref, freq_ref, *refs = refs
    weights, refs = refs[:3], refs[3:]
    mixed_ref, log_ref, heads_ref, qkv_out, attn_out, cos_out, sin_out, *refs = refs
    rests, refs = refs[:3], refs[3:]
    scores_ref, qkv_ref, attn_ref, cos_ref, sin_ref, start_ref, out_sems, attn_sems, head_sems, own_sems, y_sems, z_sems, x_sems, core_sems = refs

    mine = lax.axis_index("tensor")
    rank = lax.axis_index("dp")
    group = lax.axis_size("dp") // 2
    x_bit, z_place = lax.rem(rank, 2), lax.div(rank, 2)
    direct = len(chunks) - 1
    started = []

    def start(copy):
        copy.start()
        started.append(copy)
        return copy

    outward = [
        pltpu.make_async_copy(src, dst, out_sems.at[i])
        for i, (src, dst) in enumerate(
            [(attn_ref, attn_out), (qkv_ref, qkv_out), (cos_ref, cos_out), (sin_ref, sin_out)]
        )
    ]

    def cut(array, c, *lead):
        at, (_, low, size) = array.at, chunks[c]
        return at[(*lead, slice(None), pl.ds(low, size))]

    def every(array, c, *lead):
        at, (_, low, size) = array.at, chunks[c]
        return at[(*lead, slice(None), slice(None), pl.ds(low, size))]

    def rest(c):
        return rests[chunks[c][0]]

    y_copies = [
        push(
            cut(weights[chunks[c][0]], c, x_bit, z_place), cut(rest(c), c, 1, x_bit, z_place), y_sems, c, "tensor", 2
        )
        for c in range(direct)
    ]
    whole = lambda array, c, *lead: array.at[(*lead, slice(None), slice(None), slice(None), pl.ds(*chunks[c][1:]))]
    y_copies.append(
        push(whole(weights[chunks[direct][0]], direct), whole(rest(direct), direct, 1), y_sems, direct, "tensor", 2)
    )
    z_copies = [
        [
            push(
                cut(rest(c), c, 1, x_bit, z_place),
                cut(rest(c), c, 1, x_bit, z_place),
                z_sems,
                c * (group - 1) + d - 1,
                "dp",
                2 * d,
            )
            for d in range(1, group)
        ]
        for c in range(direct)
    ]
    x_copies = [
        push(every(rest(c), c, 1, x_bit), every(rest(c), c, 1, x_bit), x_sems, c, "dp", 1) for c in range(direct)
    ]
    core_copies = [
        push(whole(rest(c), c, 1), whole(rest(c), c, 2), core_sems, c, "tensor", 1) for c in range(len(chunks))
    ]
    own_copies = [push(weights[a], rests[a].at[0], own_sems, a, "tensor", 1) for a in range(3)]

    def to_z(c):
        y_copies[c].wait_recv()
        for copy in z_copies[c]:
            copy.start()

    def to_x(c):
        for copy in z_copies[c]:
            copy.wait_recv()
        x_copies[c].start()

    def to_core(c):
        (y_copies if c == direct else x_copies)[c].wait_recv()
        core_copies[c].start()

    greet(("tensor", "dp"))
    for c in range(direct - 1):
        y_copies[c].start()

    strips = 4
    strip = block // strips
    gain, shift = gain_ref[0:1, :], shift_ref[0:1, :]
    across, beside, onward = [], [], []
    for q in range(strips):

        @pl.loop(0, strip // 64)
        def _(r):
            at = pl.ds(pl.multiple_of(q * strip + r * 64, 64), 64)
            attn_ref[0, at, :] = layer_norm(x_ref[at, :].astype(F32), gain, shift).astype(BF)

        at = pl.ds(q * strip, strip)
        across.append(start(push(attn_ref.at[0, at], attn_ref.at[2, at], attn_sems, q, "tensor", 2)))
        beside.append(start(push(attn_ref.at[0, at], attn_ref.at[1, at], attn_sems, strips + q, "tensor", 1)))
        onward.append(push(attn_ref.at[2, at], attn_ref.at[3, at], attn_sems, 2 * strips + q, "tensor", 1))

    y_copies[direct - 1].start()
    to_z(0)

    lane = lax.broadcasted_iota(jnp.int32, (64, PAIR), 1)
    sign = jnp.where(lane % HD < HD // 2, -1.0, 1.0)

    @pl.loop(0, ranks * block // 64)
    def _(r):
        at = pl.ds(pl.multiple_of(r * 64, 64), 64)
        spot = r * 64 + lax.broadcasted_iota(jnp.int32, (64, PAIR), 0)
        begin = document_start(lengths_ref, spot)
        start_ref[at, :] = begin
        angle = (spot - begin).astype(F32) * freq_ref[...]
        cos_ref[at, :] = jnp.cos(angle)
        sin_ref[at, :] = jnp.sin(angle) * sign

    def middle():
        to_x(0)
        to_z(1)
        for q in range(strips - 1):
            across[q].wait_recv()
            onward[q].start()
        to_x(1)
        to_z(2)
        across[strips - 1].wait_recv()
        onward[strips - 1].start()
        y_copies[direct].start()
        for copy in own_copies:
            copy.start()

    def beside_here():
        for copy in beside:
            copy.wait_recv()

    def onward_here():
        for copy in onward:
            copy.wait_recv()

    @pl.loop(0, ranks)
    def _(d):
        pl.when(d == 1)(beside_here)
        pl.when(d == 2)(middle)
        pl.when(d == 3)(onward_here)
        x = attn_ref[d]
        rows = pl.ds(pl.multiple_of(d * block, block), block)
        real = pl.ds(pl.multiple_of(xor(d, mine, ranks) * block, block), block)
        for part in range(3):
            project = dot(x, w_ref[part])
            for pair in range(pairs):
                piece = project[:, pair * PAIR : (pair + 1) * PAIR]
                if part < 2:
                    piece = turn(piece, cos_ref[real, :], sin_ref[real, :])
                qkv_ref[part * pairs + pair, rows, :] = piece.astype(BF)

    def unit(pair, d):
        row_block = xor(d, mine, ranks)
        rows = pl.ds(pl.multiple_of(d * block, block), block)
        queries = qkv_ref[pair, rows, :] * HD**-0.5
        begin = start_ref[pl.ds(pl.multiple_of(row_block * block, block), block), :]
        begin = jnp.concatenate([begin] * (block // PAIR), axis=1)
        mixed = None
        for head in range(PAIR // HD):
            mask = head_mask(queries.shape, head)
            query = jnp.where(mask, queries, jnp.zeros_like(queries))

            def score(j, top, last):
                at = pl.ds(pl.multiple_of(xor(j, mine, ranks) * block, block), block)
                s = dot(query, qkv_ref[pairs + pair, at, :], NT)
                column = lax.broadcasted_iota(jnp.int32, s.shape, 1)
                visible = column >= begin - j * block
                if last:
                    visible &= column <= lax.broadcasted_iota(jnp.int32, s.shape, 0)
                s = jnp.where(visible, s, NEG)
                scores_ref[j] = s
                for c in range(0, block, 128):
                    top = jnp.maximum(top, s[:, c : c + 128])
                return top

            top = jnp.full((block, 128), NEG, F32)
            top = lax.fori_loop(0, row_block, lambda j, top: score(j, top, False), top)
            top = score(row_block, top, True)
            top = jnp.max(top, axis=1, keepdims=True)

            def mix(j, carry):
                total, acc = carry
                shares = jnp.exp(scores_ref[j] - top)
                for c in range(0, block, 128):
                    total = total + shares[:, c : c + 128]
                at = pl.ds(pl.multiple_of(xor(j, mine, ranks) * block, block), block)
                return total, acc + dot(shares.astype(BF), qkv_ref[2 * pairs + pair, at, :])

            total, acc = lax.fori_loop(
                0, row_block + 1, mix, (jnp.zeros((block, 128), F32), jnp.zeros((block, PAIR), F32))
            )
            total = jnp.sum(total, axis=1, keepdims=True)
            acc = acc / total
            mixed = acc if mixed is None else jnp.where(mask, acc, mixed)
            logs = jnp.broadcast_to(top + jnp.log(total), (block, 128))
            log_ref[pair, head : head + 1, rows] = jnp.transpose(logs)[0:1, :]
        mixed_ref[pair, rows, :] = mixed.astype(BF)

    def head_copy(pair, d):
        slot = d * pairs + pair
        return pltpu.make_async_remote_copy(
            src_ref=mixed_ref.at[pair, pl.ds(pl.multiple_of(d * block, block), block)],
            dst_ref=heads_ref.at[slot],
            send_sem=head_sems.at[0, slot],
            recv_sem=head_sems.at[1, slot],
            device_id={"tensor": xor(mine, d, ranks)},
            device_id_type=MESH,
        )

    for copy in outward:
        copy.start()
    units = pairs * ranks
    events = {
        0: [lambda: to_x(2), lambda: to_z(3), lambda: to_core(0), lambda: to_core(1)],
        3: [lambda: to_x(3), lambda: to_core(2)],
        6: [lambda: to_core(3), lambda: to_core(direct)],
    }

    @pl.loop(0, units)
    def _(u):
        pair, d = lax.rem(u, pairs), ranks - 1 - lax.div(u, pairs)
        unit(pair, d)
        pl.when(d > 0)(lambda: head_copy(pair, d).start())
        for when, steps in events.items():

            @pl.when(u == min(when, units - 1))
            def _():
                for step in steps:
                    step()

    for pair in range(pairs):
        heads_ref[pair] = mixed_ref[pair, 0:block, :]

    @pl.loop(pairs, units)
    def _(slot):
        copy = head_copy(lax.rem(slot, pairs), lax.div(slot, pairs))
        copy.wait_recv()
        copy.wait_send()

    for copy in [*core_copies, *own_copies]:
        copy.wait_recv()
    for copy in [*started, *onward, *own_copies, *y_copies, *x_copies, *core_copies]:
        copy.wait_send()
    for copies in z_copies:
        for copy in copies:
            copy.wait_send()
    for copy in outward:
        copy.wait()


def attend_forward(lengths, tokens, gains, shifts, weight, weights):
    block, width = tokens.shape
    ranks = lax.axis_size("tensor")
    assert ranks == 4
    length = block * ranks
    pairs = weight.shape[2] // PAIR
    group = lax.axis_size("dp") // 2
    views = [w.reshape(2, group, w.shape[0] // (2 * group), w.shape[1]) for w in weights]
    chunks = [(0, 0, width)]
    for a in (1, 2):
        columns = weights[a].shape[1] // 2
        chunks += [(a, 0, columns), (a, columns, columns)]
    vmem = pl.BlockSpec(memory_space=pltpu.VMEM)
    hbm = pl.BlockSpec(memory_space=pl.ANY)
    copies = pltpu.SemaphoreType.DMA
    lane = np.arange(PAIR) % (HD // 2)
    frequencies = jnp.asarray((ROPE_BASE ** (-lane * 2.0 / HD))[None, :], F32)
    smem = pl.BlockSpec(memory_space=pltpu.SMEM)
    mixed, logs, heads, qkv, attn, cosine, sine, *rests = pl.pallas_call(
        functools.partial(forward_kernel, block, ranks, pairs, chunks),
        out_shape=[
            jax.ShapeDtypeStruct((pairs, length, PAIR), BF),
            jax.ShapeDtypeStruct((pairs, 8, length), F32),
            jax.ShapeDtypeStruct((ranks * pairs, block, PAIR), BF),
            jax.ShapeDtypeStruct((3 * pairs, length, PAIR), BF),
            jax.ShapeDtypeStruct((ranks, block, width), BF),
            jax.ShapeDtypeStruct((length, PAIR), F32),
            jax.ShapeDtypeStruct((length, PAIR), F32),
            *[jax.ShapeDtypeStruct((ranks - 1, *view.shape), BF) for view in views],
        ],
        in_specs=[smem] + [vmem] * 5 + [hbm] * 3,
        out_specs=[vmem] * 3 + [hbm] * 7,
        scratch_shapes=[
            pltpu.VMEM((ranks, block, block), F32),
            pltpu.VMEM((3 * pairs, length, PAIR), BF),
            pltpu.VMEM((ranks, block, width), BF),
            pltpu.VMEM((length, PAIR), F32),
            pltpu.VMEM((length, PAIR), F32),
            pltpu.VMEM((length, PAIR), jnp.int32),
            copies((4,)),
            copies((2, 12)),
            copies((2, ranks * pairs)),
            copies((2, 3)),
            copies((2, len(chunks))),
            copies((2, len(chunks) * (group - 1))),
            copies((2, len(chunks))),
            copies((2, len(chunks))),
        ],
        compiler_params=pltpu.CompilerParams(vmem_limit_bytes=56 << 20, collective_id=2, has_side_effects=True),
        name="attend_forward",
    )(lengths, tokens, gains, shifts, weight, frequencies, *views)
    rests = [r.reshape(ranks - 1, *w.shape) for r, w in zip(rests, weights)]
    return qkv, attn, mixed, logs, heads, cosine, sine, rests


def unit_scale(values):
    centre = values - jnp.mean(values, axis=-1, keepdims=True)
    scale = lax.rsqrt(jnp.mean(centre * centre, axis=-1, keepdims=True) + EPSILON)
    return centre * scale, scale


def norm_pull(grad, unit, scale, gain):
    inside = grad * gain
    first = jnp.mean(inside, axis=-1, keepdims=True)
    second = jnp.mean(inside * unit, axis=-1, keepdims=True)
    return scale * (inside - first - unit * second)


def gelu_both(x):
    bend = 0.7978845608028654
    square = x * x
    t = jnp.tanh(bend * (x + 0.044715 * (square * x)))
    side = 0.5 * (1.0 + t)
    return x * side, side + 0.5 * x * (1.0 - t * t) * (bend * (1.0 + 0.134145 * square))


def middle_kernel(block, ranks, pairs, *refs):
    (heads_ref, x_ref, dy_ref, gains_ref, shifts_ref, *refs) = refs
    sources, refs = refs[:6], refs[6:]
    (out_ref, rest_ref, do_ref, shared_ref, terms_ref, early_ref, *refs) = refs
    (out_all, up_all, down_all, work_ref, mlp_ref, gmp_ref, middle_ref, proj_ref, acc_ref, gap_ref, gh_ref, *refs) = refs
    (out_sems, up_sems, down_sems, mlp_sems, gmp_sems, head_sems) = refs

    mine = lax.axis_index("tensor")
    width = x_ref.shape[1]
    strips, rows = 4, 64
    strip = block // strips
    columns = width // 2

    def loads(own, rest, array, sems):
        return [
            pltpu.make_async_copy(own if d == 0 else rest.at[d - 1], array.at[d], sems.at[d]) for d in range(ranks)
        ]

    out_loads = loads(sources[0], sources[1], out_all, out_sems)
    up_loads = loads(sources[2], sources[3], up_all, up_sems)
    down_loads = loads(sources[4], sources[5], down_all, down_sems)
    for copy in out_loads:
        copy.start()
    for d in range(ranks):
        up_loads[d].start()
        down_loads[d].start()
    greet(("tensor",))

    def senders(array, sems):
        found = []
        for q in range(strips):
            at = pl.ds(q * strip, strip)
            found.append(
                (
                    push(array.at[0, at], array.at[2, at], sems, q, "tensor", 2),
                    push(array.at[0, at], array.at[1, at], sems, strips + q, "tensor", 1),
                    push(array.at[2, at], array.at[3, at], sems, 2 * strips + q, "tensor", 1),
                )
            )
        return found

    mlp_copies = senders(mlp_ref, mlp_sems)
    gmp_copies = senders(gmp_ref, gmp_sems)

    def send_strip(copies, q):
        copies[q][0].start()
        copies[q][1].start()

    def forward_on(copies):
        for across, _, onward in copies:
            across.wait_recv()
            onward.start()

    for d in range(ranks):
        out_loads[d].wait()
    for c in (0, columns):
        at = pl.ds(c, columns)
        total = None
        for d in range(ranks):
            part = jnp.concatenate([heads_ref[d * pairs + p] for p in range(pairs)], axis=1)
            term = dot(part, out_all[d, :, at])
            total = term if total is None else total + term
        proj_ref[:, at] = total

    gain = [gains_ref[j : j + 1, :] for j in range(4)]
    shift = [shifts_ref[j : j + 1, :] for j in range(4)]

    for q in range(strips):

        @pl.loop(0, strip // rows)
        def _(r):
            at = pl.ds(pl.multiple_of(q * strip + r * rows, rows), rows)
            unit, _ = unit_scale(proj_ref[at, :])
            middle = x_ref[at, :].astype(F32) + (unit * gain[1] + shift[1])
            middle_ref[at, :] = middle
            unit, _ = unit_scale(middle)
            mlp_ref[0, at, :] = (unit * gain[2] + shift[2]).astype(BF)

        send_strip(mlp_copies, q)

    acc_ref[...] = jnp.zeros_like(acc_ref)

    @pl.loop(0, ranks)
    def _(d):
        pltpu.make_async_copy(up_all.at[d], up_all.at[d], up_sems.at[d]).wait()
        pltpu.make_async_copy(down_all.at[d], down_all.at[d], down_sems.at[d]).wait()
        for c in (0, columns):
            at = pl.ds(c, columns)
            hidden, slope = gelu_both(dot(mlp_ref[0], up_all[d, :, at]))
            work_ref[d, :, at] = slope
            acc_ref[...] += dot(hidden.astype(BF), down_all[d, at, :])

    zero = jnp.zeros((1, width), F32)
    gain_three, shift_three = zero, zero
    for q in range(strips):

        def last_norm(r, carry):
            gain_term, shift_term = carry
            at = pl.ds(pl.multiple_of(q * strip + r * rows, rows), rows)
            unit, scale = unit_scale(acc_ref[at, :])
            out_ref[at, :] = (middle_ref[at, :] + (unit * gain[3] + shift[3])).astype(BF)
            dy = dy_ref[at, :].astype(F32)
            gmp_ref[0, at, :] = norm_pull(dy, unit, scale, gain[3]).astype(BF)
            return (
                gain_term + jnp.sum(dy * unit, axis=0, keepdims=True),
                shift_term + jnp.sum(dy, axis=0, keepdims=True),
            )

        gain_three, shift_three = lax.fori_loop(0, strip // rows, last_norm, (gain_three, shift_three))
        send_strip(gmp_copies, q)

    acc_ref[...] = jnp.zeros_like(acc_ref)

    @pl.loop(0, ranks)
    def _(d):
        for c in (0, columns):
            at = pl.ds(c, columns)
            grad = dot(gmp_ref[0], down_all[d, at, :], NT)
            grad = (grad * work_ref[d, :, at]).astype(BF)
            acc_ref[...] += dot(grad, up_all[d, :, at], NT)

    forward_on(mlp_copies)

    def inner_norms(r, carry):
        gain_two, shift_two, gain_one, shift_one = carry
        at = pl.ds(pl.multiple_of(r * rows, rows), rows)
        grad = acc_ref[at, :]
        unit, scale = unit_scale(middle_ref[at, :])
        gain_two = gain_two + jnp.sum(grad * unit, axis=0, keepdims=True)
        shift_two = shift_two + jnp.sum(grad, axis=0, keepdims=True)
        grad = dy_ref[at, :].astype(F32) + norm_pull(grad, unit, scale, gain[2])
        rest_ref[at, :] = grad
        unit, scale = unit_scale(proj_ref[at, :])
        gain_one = gain_one + jnp.sum(grad * unit, axis=0, keepdims=True)
        shift_one = shift_one + jnp.sum(grad, axis=0, keepdims=True)
        gap_ref[at, :] = norm_pull(grad, unit, scale, gain[1]).astype(BF)
        return gain_two, shift_two, gain_one, shift_one

    gain_two, shift_two, gain_one, shift_one = lax.fori_loop(0, block // rows, inner_norms, (zero, zero, zero, zero))
    early_ref[...] = jnp.concatenate(
        [zero, gain_one, gain_two, gain_three, zero, shift_one, shift_two, shift_three], axis=0
    )

    head_copies = []
    for d in [*range(1, ranks), 0]:
        grad = dot(gap_ref[...], out_all[d], NT).astype(BF)
        for pair in range(pairs):
            piece = grad[:, pair * PAIR : (pair + 1) * PAIR]
            if d == 0:
                do_ref[pair, 0] = piece
            else:
                slot = d * pairs + pair
                gh_ref[slot] = piece
                copy = push(gh_ref.at[slot], do_ref.at[pair, d], head_sems, slot, "tensor", d)
                copy.start()
                head_copies.append(copy)
    for d in range(ranks):
        part = jnp.concatenate([heads_ref[d * pairs + p] for p in range(pairs)], axis=1)
        shared_ref[d] = dot(part, gap_ref[...], TN).astype(BF)

    for copies in (mlp_copies, gmp_copies):
        for _, beside, _ in copies:
            beside.wait_recv()
    work_ref[...] = jnp.zeros_like(work_ref)

    def late():
        forward_on(gmp_copies)

    def latest():
        for copies in (mlp_copies, gmp_copies):
            for _, _, onward in copies:
                onward.wait_recv()

    @pl.loop(0, ranks)
    def _(b):
        pl.when(b == 2)(late)
        pl.when(b == 3)(latest)
        tokens, grads = mlp_ref[b], gmp_ref[b]
        for h in range(2):
            at = pl.ds(h * columns, columns)
            hidden, slope = gelu_both(dot(tokens, up_all[0, :, at]))
            grad = (dot(grads, down_all[0, at, :], NT) * slope).astype(BF)
            work_ref[h] += dot(hidden.astype(BF), grads, TN)
            work_ref[2, :, at] += dot(tokens[:, 0:columns], grad, TN)
            work_ref[3, :, at] += dot(tokens[:, columns:], grad, TN)

    for h in range(2):
        at = pl.ds(h * columns, columns)
        for side in range(2):
            there = pl.ds(side * columns, columns)
            terms_ref[side, at, :] = work_ref[h, :, there].astype(BF)
            terms_ref[2 + side, at, :] = work_ref[2 + h, :, there].astype(BF)
    for copy in head_copies:
        copy.wait_recv()
        copy.wait_send()
    for copies in (mlp_copies, gmp_copies):
        for group in copies:
            for copy in group:
                copy.wait_send()


def middle_stage(heads, tokens, cotangent, gains, shifts, weights, rests):
    block, width = tokens.shape
    ranks = lax.axis_size("tensor")
    local = weights[0].shape[0]
    pairs = local // PAIR
    hidden = weights[2].shape[0]
    vmem = pl.BlockSpec(memory_space=pltpu.VMEM)
    hbm = pl.BlockSpec(memory_space=pl.ANY)
    copies = pltpu.SemaphoreType.DMA
    assert block * 2 == width and hidden == width
    operands = [array for pair in zip(weights, rests) for array in pair]
    return pl.pallas_call(
        functools.partial(middle_kernel, block, ranks, pairs),
        out_shape=[
            jax.ShapeDtypeStruct((block, width), BF),
            jax.ShapeDtypeStruct((block, width), F32),
            jax.ShapeDtypeStruct((pairs, ranks, block, PAIR), BF),
            jax.ShapeDtypeStruct((ranks, local, width), BF),
            jax.ShapeDtypeStruct((4, width, width // 2), BF),
            jax.ShapeDtypeStruct((8, width), F32),
        ],
        in_specs=[vmem] * 5 + [hbm] * 6,
        out_specs=[vmem] * 6,
        scratch_shapes=[
            pltpu.VMEM((ranks, local, width), BF),
            pltpu.VMEM((ranks, width, hidden), BF),
            pltpu.VMEM((ranks, hidden, width), BF),
            pltpu.VMEM((ranks, block, width), F32),
            pltpu.VMEM((ranks, block, width), BF),
            pltpu.VMEM((ranks, block, width), BF),
            pltpu.VMEM((block, width), F32),
            pltpu.VMEM((block, width), F32),
            pltpu.VMEM((block, width), F32),
            pltpu.VMEM((block, width), BF),
            pltpu.VMEM((ranks * pairs, block, PAIR), BF),
            copies((ranks,)),
            copies((ranks,)),
            copies((ranks,)),
            copies((2, 12)),
            copies((2, 12)),
            copies((2, ranks * pairs)),
        ],
        compiler_params=pltpu.CompilerParams(vmem_limit_bytes=62 << 20, collective_id=3, has_side_effects=True),
        name="middle_stage",
    )(heads, tokens, cotangent, gains, shifts, *operands)


def finish_kernel(block, blocks, pairs, orders, *refs):
    (lengths_ref, qkv_ref, do_ref, o_ref, log_ref, cos_ref, sin_ref, *refs) = refs
    (shared_ref, terms_ref, attn_ref, w_ref, x_ref, gain_ref, rest_ref, early_ref, *refs) = refs
    (input_ref, sums_ref, mlp_out, own_out, qkv_out, *refs) = refs
    (start_ref, dq_ref, inner_ref, grads_ref, own_ref, wide_ref, token_ref, core_sum, got_y, *refs) = refs
    (token_sum, token_y, norm_ref, got_t, sum_t, got_d, *refs) = refs
    chunks, steps = len(orders), len(orders[0])
    count = chunks * steps
    got, refs = refs[:count], refs[count:]
    (rs_sems, ag_sems, core_sems, y_sems, token_core_sems, token_y_sems, t_sems, d_sems) = refs

    mine = lax.axis_index("tensor")
    rank = lax.axis_index("dp")
    ranks_dp = lax.axis_size("dp")
    heads = PAIR // HD
    mlp_chunks = terms_ref.shape[0]
    started = []

    def start(copy):
        copy.start()
        started.append(copy)
        return copy

    sources = [terms_ref.at[c] for c in range(mlp_chunks)] + [own_ref] + [wide_ref.at[p] for p in range(pairs)]
    results = [mlp_out.at[c] for c in range(mlp_chunks)] + [own_out] + [qkv_out.at[p] for p in range(pairs)]
    bits = [[lax.rem(lax.div(rank, 1 << o), 2) for o in order] for order in orders]
    rs_copies, ag_copies = {}, {}

    def held(c, k):
        return sources[c] if k == 0 else got[c * steps + k - 1]

    for c in range(chunks):
        for k in range(steps):
            far = 1 << orders[c][k]
            rs_copies[c, k] = push(held(c, k).at[1 - bits[c][k]], got[c * steps + k], rs_sems, c * steps + k, "dp", far)
            region = results[c].at[tuple(bits[c][: k + 1])]
            ag_copies[c, k] = push(region, region, ag_sems, c * steps + k, "dp", far)

    def begin(c):
        rs_copies[c, 0].start()

    def halve(c, k):
        at = c * steps + k
        rs_copies[c, k].wait_recv()
        total = held(c, k)[bits[c][k]].astype(F32) + got[at][...].astype(F32)
        got[at][...] = total.astype(BF)
        if k + 1 < steps:
            rs_copies[c, k + 1].start()
        else:
            results[c][tuple(bits[c])] = total.astype(BF)
            ag_copies[c, k].start()

    def double(c, k):
        ag_copies[c, k].wait_recv()
        if k > 0:
            ag_copies[c, k - 1].start()

    core_copies = [
        push(shared_ref.at[d + 1], core_sum.at[d // 2], core_sems, d // 2, "tensor", 1) for d in range(0, blocks, 2)
    ]
    y_copies = [
        push(core_sum.at[h], got_y.at[h - 1], y_sems, h - 1, "tensor", 2 * h) for h in range(1, blocks // 2)
    ]

    def pair_up():
        for h in range(blocks // 2):
            core_copies[h].wait_recv()
            core_sum[h] = (shared_ref[2 * h].astype(F32) + core_sum[h].astype(F32)).astype(BF)
        for copy in y_copies:
            copy.start()

    def settle():
        total = core_sum[0].astype(F32)
        for h in range(1, blocks // 2):
            y_copies[h - 1].wait_recv()
            total = total + got_y[h - 1].astype(F32)
        own_ref[...] = total.astype(BF)

    def prepare(pair):
        dq_ref[...] = jnp.zeros_like(dq_ref)
        for b in range(blocks):
            rows = pl.ds(b * block, block)
            product = do_ref[pair, b].astype(F32) * o_ref[pair, rows, :].astype(F32)
            high = product.astype(BF)
            low = (product - high.astype(F32)).astype(BF)
            for head in range(heads):
                ones = head_mask((16, PAIR), head).astype(F32).astype(BF)
                inner = dot(ones, high, NT) + dot(ones, low, NT)
                inner_ref[head : head + 1, rows] = inner[0:1, :]

    def unit(pair, key_block):
        slot = xor(key_block, mine, blocks)
        here = pl.ds(pl.multiple_of(slot * block, block), block)
        keys = qkv_ref[pairs + pair, here, :]
        values = qkv_ref[2 * pairs + pair, here, :]
        dk = jnp.zeros((block, PAIR), F32)
        dv = jnp.zeros((block, PAIR), F32)
        for head in range(heads):
            mask = head_mask(keys.shape, head)
            key = jnp.where(mask, keys * HD**-0.5, jnp.zeros_like(keys))
            value = jnp.where(mask, values, jnp.zeros_like(values))

            def one(i, carry, first):
                dk, dv = carry
                place = xor(i, mine, blocks)
                rows = pl.ds(pl.multiple_of(place * block, block), block)
                real = pl.ds(pl.multiple_of(i * block, block), block)
                query = qkv_ref[pair, rows, :]
                grad = do_ref[pair, place]
                s = dot(key, query, NT)
                row = lax.broadcasted_iota(jnp.int32, s.shape, 0)
                visible = row >= start_ref[0:1, real] - key_block * block
                if first:
                    visible &= row <= lax.broadcasted_iota(jnp.int32, s.shape, 1)
                probs = jnp.where(visible, jnp.exp(s - log_ref[pair, head : head + 1, rows]), 0.0)
                grad_probs = dot(value, grad, NT)
                ds = (probs * (grad_probs - inner_ref[head : head + 1, rows])).astype(BF)
                zero = jnp.zeros_like(query)
                dv = dv + dot(probs.astype(BF), jnp.where(mask, grad, zero))
                dk = dk + dot(ds, jnp.where(mask, query, zero))
                dq_ref[rows, :] += dot(ds, key, TN)
                return dk, dv

            dk, dv = one(key_block, (dk, dv), True)
            dk, dv = lax.fori_loop(key_block + 1, blocks, lambda i, carry: one(i, carry, False), (dk, dv))
        real = pl.ds(pl.multiple_of(key_block * block, block), block)
        grads_ref[pairs + pair, here, :] = turn(dk * HD**-0.5, cos_ref[real, :], -sin_ref[real, :]).astype(BF)
        grads_ref[2 * pairs + pair, here, :] = dv.astype(BF)

    def close(pair):
        for b in range(blocks):
            rows = pl.ds(b * block, block)
            real = pl.ds(pl.multiple_of(flip(mine, b) * block, block), block)
            grads_ref[pair, rows, :] = turn(dq_ref[rows, :], cos_ref[real, :], -sin_ref[real, :]).astype(BF)
        total = None
        for b in range(blocks):
            rows = pl.ds(b * block, block)
            wide = jnp.concatenate([grads_ref[c * pairs + pair, rows, :] for c in range(3)], axis=1)
            term = dot(attn_ref[b], wide, TN)
            total = term if total is None else total + term
        wide_ref[pair] = total.astype(BF).reshape(wide_ref.shape[1:])

    greet(("tensor", "dp"))
    for copy in core_copies:
        copy.start()
    first_q = mlp_chunks + 1
    begin(0)
    begin(3)
    begin(1)
    start_ref[...] = document_start(lengths_ref, lax.broadcasted_iota(jnp.int32, start_ref.shape, 1))
    slots = pairs * blocks
    events = {
        0: [pair_up],
        2: [lambda: halve(0, 0), lambda: halve(3, 0), lambda: begin(2)],
        3: [settle, lambda: begin(mlp_chunks)],
        4: [lambda: halve(1, 0), lambda: halve(0, 1)],
        5: [lambda: begin(first_q), lambda: halve(3, 1), lambda: halve(1, 1), lambda: halve(0, 2)],
        6: [lambda: halve(2, 0), lambda: halve(3, 2), lambda: halve(1, 2), lambda: double(0, 2)],
        7: [lambda: halve(4, 0), lambda: halve(2, 1), lambda: double(0, 1), lambda: double(3, 2), lambda: double(1, 2)],
    }

    @pl.loop(0, slots)
    def _(u):
        pair, key_block = lax.div(u, blocks), lax.rem(u, blocks)
        for when, todo in events.items():

            @pl.when(u == when)
            def _():
                for step in todo:
                    step()

        for p in range(pairs):
            pl.when(u == p * blocks)(functools.partial(prepare, p))
        unit(pair, key_block)
        for p in range(pairs):
            pl.when(u == p * blocks + blocks - 1)(functools.partial(close, p))

    begin(first_q + 1)

    def token_term(d):
        rows = pl.ds(d * block, block)
        total = None
        for c in range(3):
            wide = jnp.concatenate([grads_ref[c * pairs + p, rows, :] for p in range(pairs)], axis=1)
            term = dot(wide, w_ref[c], NT)
            total = term if total is None else total + term
        token_ref[d] = total.astype(BF)

    token_copies = []
    for d in range(0, blocks, 2):
        token_term(d + 1)
        token_copies.append(start(push(token_ref.at[d + 1], token_sum.at[d // 2], token_core_sems, d // 2, "tensor", 1)))
    halve(2, 2)
    double(1, 1)
    for d in range(blocks - 2, -1, -2):
        token_term(d)
        token_copies[d // 2].wait_recv()
        token_sum[d // 2] = (token_ref[d].astype(F32) + token_sum[d // 2].astype(F32)).astype(BF)
        if d > 0:
            across = start(push(token_sum.at[d // 2], token_y.at[d // 2 - 1], token_y_sems, d // 2 - 1, "tensor", d))
    halve(4, 1)
    halve(5, 0)
    double(3, 1)
    double(2, 2)
    halve(4, 2)
    halve(5, 1)
    halve(6, 0)
    double(2, 1)
    double(4, 2)
    halve(5, 2)
    halve(6, 1)

    across.wait_recv()
    rows = 64
    lanes = x_ref.shape[1] // 128
    gain = gain_ref[0:1, :]

    def norm(r, carry):
        gain_term, shift_term = carry
        at = pl.ds(pl.multiple_of(r * rows, rows), rows)
        grad = token_sum[0, at, :].astype(F32)
        for h in range(blocks // 2 - 1):
            grad = grad + token_y[h, at, :].astype(F32)
        unit, scale = unit_scale(x_ref[at, :].astype(F32))
        total = rest_ref[at, :] + norm_pull(grad, unit, scale, gain)
        for c in range(lanes):
            there = pl.ds(pl.multiple_of(r * (rows * lanes), rows * lanes) + c, rows, stride=lanes)
            input_ref[there, :] = total[:, c * 128 : (c + 1) * 128]
        return (
            gain_term + jnp.sum(grad * unit, axis=0, keepdims=True),
            shift_term + jnp.sum(grad, axis=0, keepdims=True),
        )

    zero = jnp.zeros(gain.shape, F32)
    gain_term, shift_term = lax.fori_loop(0, block // rows, norm, (zero, zero))
    norm_ref[...] = early_ref[...]
    norm_ref[0:1, :] = gain_term
    norm_ref[4:5, :] = shift_term
    ts = [start(push(norm_ref, got_t.at[d - 1], t_sems, d - 1, "tensor", d)) for d in range(1, blocks)]
    double(4, 1)
    halve(6, 2)
    double(5, 2)
    double(5, 1)
    for copy in ts:
        copy.wait_recv()
    sum_t[...] = tree_sum([norm_ref[...]] + [got_t[d] for d in range(blocks - 1)])
    ds = [start(push(sum_t, got_d.at[d - 1], d_sems, d - 1, "dp", d)) for d in range(1, ranks_dp)]
    for k in range(steps - 1, 0, -1):
        double(6, k)
    for copy in ds:
        copy.wait_recv()
    sums_ref[...] = tree_sum([sum_t[...]] + [got_d[d] for d in range(ranks_dp - 1)])
    for c in range(chunks):
        double(c, 0)
    for copy in [*started, *core_copies, *y_copies, *rs_copies.values(), *ag_copies.values()]:
        copy.wait_send()


def finish_stage(lengths, qkv, grad_heads, heads_out, logs, cosine, sine, shared, terms, attn, weight, tokens, gain, rest, early):
    pairs3, length, _ = qkv.shape
    pairs = pairs3 // 3
    block, width = tokens.shape
    blocks = length // block
    ranks_dp = lax.axis_size("dp")
    steps = ranks_dp.bit_length() - 1
    straight = list(range(steps))
    orders = [straight] * 3 + [[1, 0, *straight[2:]]] + [straight] * 3
    cut = (2,) * steps
    local = shared.shape[1]
    shared = shared.reshape(blocks, *cut, local // ranks_dp, width)
    terms = terms.reshape(terms.shape[0], *cut, terms.shape[1] // ranks_dp, terms.shape[2])
    wide = (*cut, width // ranks_dp, 3 * PAIR)
    shapes = [terms.shape[1:]] * terms.shape[0] + [shared.shape[1:]] + [wide] * pairs
    parts = [shape[k + 1 :] for shape in shapes for k in range(steps)]
    vmem = pl.BlockSpec(memory_space=pltpu.VMEM)
    copies = pltpu.SemaphoreType.DMA
    outs = pl.pallas_call(
        functools.partial(finish_kernel, block, blocks, pairs, orders),
        out_shape=[
            jax.ShapeDtypeStruct((block * width // 128, 128), F32),
            jax.ShapeDtypeStruct((8, width), F32),
            jax.ShapeDtypeStruct(terms.shape, BF),
            jax.ShapeDtypeStruct(shared.shape[1:], BF),
            jax.ShapeDtypeStruct((pairs, *wide), BF),
        ],
        in_specs=[pl.BlockSpec(memory_space=pltpu.SMEM)] + [vmem] * 14,
        out_specs=[vmem] * 5,
        scratch_shapes=[
            pltpu.VMEM((8, length), jnp.int32),
            pltpu.VMEM((length, PAIR), F32),
            pltpu.VMEM((8, length), F32),
            pltpu.VMEM((pairs3, length, PAIR), BF),
            pltpu.VMEM(shared.shape[1:], BF),
            pltpu.VMEM((pairs, *wide), BF),
            pltpu.VMEM((blocks, block, width), BF),
            pltpu.VMEM((blocks // 2, *shared.shape[1:]), BF),
            pltpu.VMEM((blocks // 2 - 1, *shared.shape[1:]), BF),
            pltpu.VMEM((blocks // 2, block, width), BF),
            pltpu.VMEM((blocks // 2 - 1, block, width), BF),
            pltpu.VMEM((8, width), F32),
            pltpu.VMEM((blocks - 1, 8, width), F32),
            pltpu.VMEM((8, width), F32),
            pltpu.VMEM((ranks_dp - 1, 8, width), F32),
            *[pltpu.VMEM(shape, BF) for shape in parts],
            copies((2, len(parts))),
            copies((2, len(parts))),
            copies((2, blocks // 2)),
            copies((2, blocks // 2 - 1)),
            copies((2, blocks // 2)),
            copies((2, blocks // 2 - 1)),
            copies((2, blocks - 1)),
            copies((2, ranks_dp - 1)),
        ],
        compiler_params=pltpu.CompilerParams(vmem_limit_bytes=62 << 20, collective_id=0, has_side_effects=True),
        name="finish_stage",
    )(lengths, qkv, grad_heads, heads_out, logs, cosine, sine, shared, terms, attn, weight, tokens, gain, rest, early)
    input_grad, sums, mlp, own, wides = outs
    return input_grad, sums, mlp.reshape(4, width, -1), own.reshape(local, width), wides.reshape(pairs, width, 3 * PAIR)


def body(block_in, lengths, qkv_weight, out_weight, up_weight, down_weight, norm_gain, norm_bias, cotangent):
    block, row_count, width = block_in.shape
    assert row_count == 1
    pairs = out_weight.shape[0] // PAIR
    qkv_swapped = jnp.transpose(qkv_weight, (1, 0, 2))

    qkv, attn_full, heads_mixed, logs, heads_parts, cosine, sine, rests = attend_forward(
        lengths,
        block_in.reshape(block, width),
        norm_gain,
        norm_bias,
        qkv_swapped,
        (out_weight, up_weight, down_weight),
    )
    block_out, grad_middle, grad_heads, shared, terms, early = middle_stage(
        heads_parts,
        block_in.reshape(block, width),
        cotangent.reshape(block, width),
        norm_gain,
        norm_bias,
        (out_weight, up_weight, down_weight),
        rests,
    )
    input_grad, sums, mlp_sums, out_sum, qkv_sums = finish_stage(
        lengths,
        qkv,
        grad_heads,
        heads_mixed,
        logs,
        cosine,
        sine,
        shared,
        terms,
        attn_full,
        qkv_swapped,
        block_in.reshape(block, width),
        norm_gain,
        grad_middle,
        early,
    )
    down_grad, up_grad = [jnp.concatenate([mlp_sums[i], mlp_sums[i + 1]], axis=1).astype(F32) for i in (0, 2)]
    qkv_grad = jnp.stack(
        [jnp.concatenate([qkv_sums[p, :, c * PAIR : (c + 1) * PAIR] for p in range(pairs)], axis=1) for c in range(3)]
    ).astype(F32)
    qkv_grad = jnp.transpose(qkv_grad, (1, 0, 2))
    out_grad = out_sum.astype(F32)
    gain_grad, bias_grad = sums[0:4], sums[4:8]
    return (
        block_out.reshape(block_in.shape),
        input_grad.reshape(block_in.shape),
        qkv_grad,
        out_grad,
        up_grad,
        down_grad,
        gain_grad,
        bias_grad,
    )


def solution(mesh):
    tokens, rows, columns, copied = P("tensor", "dp", None), P("tensor", None), P(None, "tensor"), P()
    heads = P(None, None, "tensor")
    return jax.shard_map(
        body,
        mesh=mesh,
        in_specs=(tokens, P("dp", None), heads, rows, columns, rows, copied, copied, tokens),
        out_specs=(tokens, tokens, heads, rows, columns, rows, copied, copied),
        check_vma=False,
    )
```

```python
import functools

import jax
import jax.numpy as jnp
import numpy as np
from jax import lax
from jax.experimental import pallas as pl
from jax.experimental.pallas import tpu as pltpu
from jax.sharding import PartitionSpec as P

HD = 64
PAIR = 128
EPSILON = 1e-05
ROPE_BASE = 10000.0
NEG = -1e30
MESH = pl.DeviceIdType.MESH
BF = jnp.bfloat16
F32 = jnp.float32
NT = (((1,), (1,)), ((), ()))
NN = (((1,), (0,)), ((), ()))
TN = (((0,), (0,)), ((), ()))


def dot(a, b, dims=NN):
    return lax.dot_general(a, b, dims, preferred_element_type=F32)


def layer_norm(values, gain, shift):
    centre = values - jnp.mean(values, axis=-1, keepdims=True)
    spread = jnp.mean(centre * centre, axis=-1, keepdims=True)
    return centre * lax.rsqrt(spread + EPSILON) * gain + shift


def flip(index, offset):
    bit = 1
    while bit <= offset:
        if offset & bit:
            index = index + bit - 2 * bit * lax.rem(lax.div(index, bit), 2)
        bit *= 2
    return index


def xor(a, b, size):
    total, bit = 0, 1
    while bit < size:
        total = total + bit * lax.rem(lax.div(a, bit) + lax.div(b, bit), 2)
        bit *= 2
    return total


def greet(axes):
    barrier = pltpu.get_barrier_semaphore()
    count = 0
    for axis in axes:
        index = lax.axis_index(axis)
        for d in range(1, lax.axis_size(axis)):
            pl.semaphore_signal(barrier, inc=1, device_id={axis: flip(index, d)}, device_id_type=MESH)
            count += 1
    pl.semaphore_wait(barrier, count)


def tree_sum(parts):
    parts = [part.astype(F32) for part in parts]
    while len(parts) > 1:
        parts = [parts[i] + parts[i + 1] for i in range(0, len(parts), 2)]
    return parts[0]


def push(src, dst, sems, slot, axis, offset):
    return pltpu.make_async_remote_copy(
        src_ref=src,
        dst_ref=dst,
        send_sem=sems.at[0, slot],
        recv_sem=sems.at[1, slot],
        device_id={axis: flip(lax.axis_index(axis), offset)},
        device_id_type=MESH,
    )


def turn(values, cosine, signed_sine):
    lane = lax.broadcasted_iota(jnp.int32, values.shape, 1)
    other = jnp.where(lane % HD < HD // 2, pltpu.roll(values, PAIR - HD // 2, 1), pltpu.roll(values, HD // 2, 1))
    return values * cosine + other * signed_sine


def head_mask(shape, head):
    lane = lax.broadcasted_iota(jnp.int32, shape, 1)
    return lane // HD == head


def document_start(lengths_ref, spot):
    begin = jnp.zeros_like(spot)
    total = jnp.int32(0)
    for j in range(lengths_ref.shape[1] - 1):
        total = total + lengths_ref[0, j]
        begin = jnp.where(spot >= total, total, begin)
    return begin


def forward_kernel(block, ranks, pairs, chunks, *refs):
    lengths_ref, x_ref, gain_ref, shift_ref, w_ref, freq_ref, *refs = refs
    weights, refs = refs[:3], refs[3:]
    mixed_ref, log_ref, heads_ref, qkv_out, attn_out, cos_out, sin_out, *refs = refs
    rests, refs = refs[:3], refs[3:]
    scores_ref, qkv_ref, attn_ref, cos_ref, sin_ref, start_ref, out_sems, attn_sems, head_sems, own_sems, y_sems, z_sems, x_sems, core_sems = refs

    mine = lax.axis_index("tensor")
    rank = lax.axis_index("dp")
    group = lax.axis_size("dp") // 2
    x_bit, z_place = lax.rem(rank, 2), lax.div(rank, 2)
    direct = len(chunks) - 1
    started = []

    def start(copy):
        copy.start()
        started.append(copy)
        return copy

    outward = [
        pltpu.make_async_copy(src, dst, out_sems.at[i])
        for i, (src, dst) in enumerate(
            [(attn_ref, attn_out), (qkv_ref, qkv_out), (cos_ref, cos_out), (sin_ref, sin_out)]
        )
    ]

    def cut(array, c, *lead):
        at, (_, low, size) = array.at, chunks[c]
        return at[(*lead, slice(None), pl.ds(low, size))]

    def every(array, c, *lead):
        at, (_, low, size) = array.at, chunks[c]
        return at[(*lead, slice(None), slice(None), pl.ds(low, size))]

    def rest(c):
        return rests[chunks[c][0]]

    y_copies = [
        push(
            cut(weights[chunks[c][0]], c, x_bit, z_place), cut(rest(c), c, 1, x_bit, z_place), y_sems, c, "tensor", 2
        )
        for c in range(direct)
    ]
    whole = lambda array, c, *lead: array.at[(*lead, slice(None), slice(None), slice(None), pl.ds(*chunks[c][1:]))]
    y_copies.append(
        push(whole(weights[chunks[direct][0]], direct), whole(rest(direct), direct, 1), y_sems, direct, "tensor", 2)
    )
    z_copies = [
        [
            push(
                cut(rest(c), c, 1, x_bit, z_place),
                cut(rest(c), c, 1, x_bit, z_place),
                z_sems,
                c * (group - 1) + d - 1,
                "dp",
                2 * d,
            )
            for d in range(1, group)
        ]
        for c in range(direct)
    ]
    x_copies = [
        push(every(rest(c), c, 1, x_bit), every(rest(c), c, 1, x_bit), x_sems, c, "dp", 1) for c in range(direct - 1)
    ]
    core_copies = {
        c: push(whole(rest(c), c, 1), whole(rest(c), c, 2), core_sems, c, "tensor", 1)
        for c in [*range(direct - 1), direct]
    }
    own_copies = [push(weights[a], rests[a].at[0], own_sems, a, "tensor", 1) for a in range(3)]

    def to_z(c):
        y_copies[c].wait_recv()
        for copy in z_copies[c]:
            copy.start()

    def to_x(c):
        for copy in z_copies[c]:
            copy.wait_recv()
        x_copies[c].start()

    def to_core(c):
        (y_copies if c == direct else x_copies)[c].wait_recv()
        core_copies[c].start()

    greet(("tensor", "dp"))
    for c in range(direct - 1):
        y_copies[c].start()

    strips = 4
    strip = block // strips
    gain, shift = gain_ref[0:1, :], shift_ref[0:1, :]
    across, beside, onward = [], [], []
    for q in range(strips):

        @pl.loop(0, strip // 64)
        def _(r):
            at = pl.ds(pl.multiple_of(q * strip + r * 64, 64), 64)
            attn_ref[0, at, :] = layer_norm(x_ref[at, :].astype(F32), gain, shift).astype(BF)

        at = pl.ds(q * strip, strip)
        across.append(start(push(attn_ref.at[0, at], attn_ref.at[2, at], attn_sems, q, "tensor", 2)))
        beside.append(start(push(attn_ref.at[0, at], attn_ref.at[1, at], attn_sems, strips + q, "tensor", 1)))
        onward.append(push(attn_ref.at[2, at], attn_ref.at[3, at], attn_sems, 2 * strips + q, "tensor", 1))

    y_copies[direct - 1].start()
    to_z(0)

    lane = lax.broadcasted_iota(jnp.int32, (64, PAIR), 1)
    sign = jnp.where(lane % HD < HD // 2, -1.0, 1.0)

    @pl.loop(0, ranks * block // 64)
    def _(r):
        at = pl.ds(pl.multiple_of(r * 64, 64), 64)
        spot = r * 64 + lax.broadcasted_iota(jnp.int32, (64, PAIR), 0)
        begin = document_start(lengths_ref, spot)
        start_ref[at, :] = begin
        angle = (spot - begin).astype(F32) * freq_ref[...]
        cos_ref[at, :] = jnp.cos(angle)
        sin_ref[at, :] = jnp.sin(angle) * sign

    def middle():
        to_x(0)
        to_z(1)
        for q in range(strips - 1):
            across[q].wait_recv()
            onward[q].start()
        to_x(1)
        to_z(2)
        across[strips - 1].wait_recv()
        onward[strips - 1].start()
        y_copies[direct].start()
        for copy in own_copies:
            copy.start()

    def beside_here():
        for copy in beside:
            copy.wait_recv()

    def onward_here():
        for copy in onward:
            copy.wait_recv()

    @pl.loop(0, ranks)
    def _(d):
        pl.when(d == 1)(beside_here)
        pl.when(d == 2)(middle)
        pl.when(d == 3)(onward_here)
        x = attn_ref[d]
        rows = pl.ds(pl.multiple_of(d * block, block), block)
        real = pl.ds(pl.multiple_of(xor(d, mine, ranks) * block, block), block)
        for part in range(3):
            project = dot(x, w_ref[part])
            for pair in range(pairs):
                piece = project[:, pair * PAIR : (pair + 1) * PAIR]
                if part < 2:
                    piece = turn(piece, cos_ref[real, :], sin_ref[real, :])
                qkv_ref[part * pairs + pair, rows, :] = piece.astype(BF)

    sub = block // 2

    def unit(pair, d):
        row_block = xor(d, mine, ranks)
        rows = pl.ds(pl.multiple_of(d * block, block), block)
        begin = start_ref[pl.ds(pl.multiple_of(row_block * block, block), block), :]
        queries = qkv_ref[pair, rows, :] * HD**-0.5
        heads = range(PAIR // HD)
        masks = [head_mask(queries.shape, head) for head in heads]
        parts = [jnp.where(mask, queries, jnp.zeros_like(queries)) for mask in masks]
        column = lax.broadcasted_iota(jnp.int32, (block, 128), 1)

        def score(j, tops, last):
            at = pl.ds(pl.multiple_of(xor(j, mine, ranks) * block, block), block)
            keys = qkv_ref[pairs + pair, at, :]
            tops = list(tops)
            for low in range(0, block, sub):
                for head in heads:
                    s = dot(parts[head], keys[low : low + sub], NT)
                    for c in range(0, sub, 128):
                        visible = column + (low + c) >= begin - j * block
                        if last:
                            visible &= column + (low + c) <= lax.broadcasted_iota(jnp.int32, (block, 128), 0)
                        piece = jnp.where(visible, s[:, c : c + 128], NEG)
                        scores_ref[head, j, :, low + c : low + c + 128] = piece
                        tops[head] = jnp.maximum(tops[head], piece)
            return tuple(tops)

        tops = tuple(jnp.full((block, 128), NEG, F32) for _ in heads)
        tops = lax.fori_loop(0, row_block, lambda j, tops: score(j, tops, False), tops)
        tops = score(row_block, tops, True)
        tops = [jnp.broadcast_to(jnp.max(top, axis=1, keepdims=True), (block, 128)) for top in tops]

        def mix(j, accs):
            at = pl.ds(pl.multiple_of(xor(j, mine, ranks) * block, block), block)
            values = qkv_ref[2 * pairs + pair, at, :]
            accs = list(accs)
            for low in range(0, block, sub):
                for head in heads:
                    filled = jnp.where(masks[head], values, jnp.ones_like(values))[low : low + sub]
                    shares = [
                        jnp.exp(scores_ref[head, j, :, low + c : low + c + 128] - tops[head]).astype(BF)
                        for c in range(0, sub, 128)
                    ]
                    accs[head] = accs[head] + dot(jnp.concatenate(shares, axis=1), filled)
            return tuple(accs)

        accs = lax.fori_loop(0, row_block + 1, mix, tuple(jnp.zeros((block, PAIR), F32) for _ in heads))
        totals = [pltpu.roll(acc, HD, 1) for acc in accs]
        mixed_ref[pair, rows, :] = jnp.where(masks[0], accs[0] / totals[0], accs[1] / totals[1]).astype(BF)
        for head in heads:
            logs = tops[head] + jnp.log(jnp.where(masks[head], totals[head], accs[head]))
            log_ref[pair, head : head + 1, rows] = jnp.transpose(logs)[0:1, :]

    def head_copy(pair, d):
        slot = d * pairs + pair
        return pltpu.make_async_remote_copy(
            src_ref=mixed_ref.at[pair, pl.ds(pl.multiple_of(d * block, block), block)],
            dst_ref=heads_ref.at[slot],
            send_sem=head_sems.at[0, slot],
            recv_sem=head_sems.at[1, slot],
            device_id={"tensor": xor(mine, d, ranks)},
            device_id_type=MESH,
        )

    for copy in outward:
        copy.start()
    units = pairs * ranks
    events = {
        0: [lambda: to_x(2), lambda: to_z(3), lambda: to_z(4), lambda: to_core(0), lambda: to_core(1)],
        3: [lambda: to_x(3)],
        5: [lambda: to_core(2)],
    }

    @pl.loop(0, units)
    def _(u):
        pair, d = lax.rem(u, pairs), ranks - 1 - lax.div(u, pairs)
        unit(pair, d)
        pl.when(d > 0)(lambda: head_copy(pair, d).start())
        for when, steps in events.items():

            @pl.when(u == min(when, units - 1))
            def _():
                for step in steps:
                    step()

    for pair in range(pairs):
        heads_ref[pair] = mixed_ref[pair, 0:block, :]
    to_core(3)
    to_core(direct)

    @pl.loop(pairs, units)
    def _(slot):
        copy = head_copy(lax.rem(slot, pairs), lax.div(slot, pairs))
        copy.wait_recv()
        copy.wait_send()

    for copy in [*core_copies.values(), *own_copies, *z_copies[direct - 1]]:
        copy.wait_recv()
    for copy in [*started, *onward, *own_copies, *y_copies, *x_copies, *core_copies.values()]:
        copy.wait_send()
    for copies in z_copies:
        for copy in copies:
            copy.wait_send()
    for copy in outward:
        copy.wait()


def attend_forward(lengths, tokens, gains, shifts, weight, weights):
    block, width = tokens.shape
    ranks = lax.axis_size("tensor")
    assert ranks == 4
    length = block * ranks
    pairs = weight.shape[2] // PAIR
    group = lax.axis_size("dp") // 2
    views = [w.reshape(2, group, w.shape[0] // (2 * group), w.shape[1]) for w in weights]
    chunks = [(0, 0, width)]
    for a in (1, 2):
        columns = weights[a].shape[1] // 2
        chunks += [(a, 0, columns), (a, columns, columns)]
    chunks[3:] = [(2, columns, columns // 2), (2, 0, columns), (2, columns + columns // 2, columns // 2)]
    vmem = pl.BlockSpec(memory_space=pltpu.VMEM)
    hbm = pl.BlockSpec(memory_space=pl.ANY)
    copies = pltpu.SemaphoreType.DMA
    lane = np.arange(PAIR) % (HD // 2)
    frequencies = jnp.asarray((ROPE_BASE ** (-lane * 2.0 / HD))[None, :], F32)
    smem = pl.BlockSpec(memory_space=pltpu.SMEM)
    mixed, logs, heads, qkv, attn, cosine, sine, *rests = pl.pallas_call(
        functools.partial(forward_kernel, block, ranks, pairs, chunks),
        out_shape=[
            jax.ShapeDtypeStruct((pairs, length, PAIR), BF),
            jax.ShapeDtypeStruct((pairs, 8, length), F32),
            jax.ShapeDtypeStruct((ranks * pairs, block, PAIR), BF),
            jax.ShapeDtypeStruct((3 * pairs, length, PAIR), BF),
            jax.ShapeDtypeStruct((ranks, block, width), BF),
            jax.ShapeDtypeStruct((length, PAIR), F32),
            jax.ShapeDtypeStruct((length, PAIR), F32),
            *[jax.ShapeDtypeStruct((ranks - 1, *view.shape), BF) for view in views],
        ],
        in_specs=[smem] + [vmem] * 5 + [hbm] * 3,
        out_specs=[vmem] * 3 + [hbm] * 7,
        scratch_shapes=[
            pltpu.VMEM((PAIR // HD, ranks, block, block), F32),
            pltpu.VMEM((3 * pairs, length, PAIR), BF),
            pltpu.VMEM((ranks, block, width), BF),
            pltpu.VMEM((length, PAIR), F32),
            pltpu.VMEM((length, PAIR), F32),
            pltpu.VMEM((length, PAIR), jnp.int32),
            copies((4,)),
            copies((2, 12)),
            copies((2, ranks * pairs)),
            copies((2, 3)),
            copies((2, len(chunks))),
            copies((2, len(chunks) * (group - 1))),
            copies((2, len(chunks))),
            copies((2, len(chunks))),
        ],
        compiler_params=pltpu.CompilerParams(vmem_limit_bytes=56 << 20, collective_id=2, has_side_effects=True),
        name="attend_forward",
    )(lengths, tokens, gains, shifts, weight, frequencies, *views)
    rests = [r.reshape(ranks - 1, *w.shape) for r, w in zip(rests, weights)]
    return qkv, attn, mixed, logs, heads, cosine, sine, rests


def unit_scale(values):
    centre = values - jnp.mean(values, axis=-1, keepdims=True)
    scale = lax.rsqrt(jnp.mean(centre * centre, axis=-1, keepdims=True) + EPSILON)
    return centre * scale, scale


def norm_pull(grad, unit, scale, gain):
    inside = grad * gain
    first = jnp.mean(inside, axis=-1, keepdims=True)
    second = jnp.mean(inside * unit, axis=-1, keepdims=True)
    return scale * (inside - first - unit * second)


def gelu_both(x):
    bend = 0.7978845608028654
    square = x * x
    t = jnp.tanh(bend * (x + 0.044715 * (square * x)))
    side = 0.5 * (1.0 + t)
    return x * side, side + 0.5 * x * (1.0 - t * t) * (bend * (1.0 + 0.134145 * square))


def middle_kernel(block, ranks, pairs, *refs):
    (heads_ref, x_ref, dy_ref, gains_ref, shifts_ref, *refs) = refs
    sources, refs = refs[:6], refs[6:]
    (out_ref, rest_ref, do_ref, shared_ref, down_ref, up_ref, got_down, got_up, early_ref, *refs) = refs
    (out_all, up_all, down_all, work_ref, mlp_ref, gmp_ref, middle_ref, proj_ref, acc_ref, gap_ref, gh_ref, *refs) = refs
    (out_sems, up_sems, down_sems, part_sems, cross_sems, mlp_sems, gmp_sems, head_sems, sum_sems) = refs

    mine = lax.axis_index("tensor")
    width = x_ref.shape[1]
    strips, rows = 4, 64
    strip = block // strips
    columns = width // 2

    def loads(own, rest, array, sems):
        return [
            pltpu.make_async_copy(own if d == 0 else rest.at[d - 1], array.at[d], sems.at[d]) for d in range(ranks)
        ]

    out_loads = loads(sources[0], sources[1], out_all, out_sems)
    up_loads = loads(sources[2], sources[3], up_all, up_sems)
    down_loads = loads(sources[4], sources[5], down_all, down_sems)[:2]
    rank = lax.axis_index("dp")
    near = pl.ds(pl.multiple_of(lax.rem(rank, 2) * columns, columns), columns)
    left, inner = pl.ds(0, columns), pl.ds(columns, columns)
    far_down = sources[5]
    part_loads = [
        pltpu.make_async_copy(far_down.at[1, near, left], down_all.at[2, near, left], part_sems.at[0]),
        pltpu.make_async_copy(far_down.at[1, :, inner], down_all.at[2, :, inner], part_sems.at[1]),
        pltpu.make_async_copy(far_down.at[2, :, inner], down_all.at[3, :, inner], part_sems.at[2]),
    ]
    part_copies = [
        push(far_down.at[1, near, left], down_all.at[2, near, left], cross_sems, 0, "dp", 1),
        push(down_all.at[2, :, left], down_all.at[3, :, left], cross_sems, 1, "tensor", 1),
    ]
    for copy in out_loads:
        copy.start()
    for d in range(ranks):
        up_loads[d].start()
        if d < 2:
            down_loads[d].start()
    for load in part_loads:
        load.start()
    greet(("tensor", "dp"))
    part_copies[0].start()

    def senders(array, sems):
        found = []
        for q in range(strips):
            at = pl.ds(q * strip, strip)
            found.append(
                (
                    push(array.at[0, at], array.at[2, at], sems, q, "tensor", 2),
                    push(array.at[0, at], array.at[1, at], sems, strips + q, "tensor", 1),
                    push(array.at[2, at], array.at[3, at], sems, 2 * strips + q, "tensor", 1),
                )
            )
        return found

    mlp_copies = senders(mlp_ref, mlp_sems)
    gmp_copies = senders(gmp_ref, gmp_sems)

    def send_strip(copies, q):
        copies[q][0].start()
        copies[q][1].start()

    def forward_on(copies):
        for across, _, onward in copies:
            across.wait_recv()
            onward.start()

    for d in range(ranks):
        out_loads[d].wait()
    for c in (0, columns):
        at = pl.ds(c, columns)
        total = None
        for d in range(ranks):
            part = jnp.concatenate([heads_ref[d * pairs + p] for p in range(pairs)], axis=1)
            term = dot(part, out_all[d, :, at])
            total = term if total is None else total + term
        proj_ref[:, at] = total

    gain = [gains_ref[j : j + 1, :] for j in range(4)]
    shift = [shifts_ref[j : j + 1, :] for j in range(4)]

    for q in range(strips):

        @pl.loop(0, strip // rows)
        def _(r):
            at = pl.ds(pl.multiple_of(q * strip + r * rows, rows), rows)
            unit, _ = unit_scale(proj_ref[at, :])
            middle = x_ref[at, :].astype(F32) + (unit * gain[1] + shift[1])
            middle_ref[at, :] = middle
            unit, _ = unit_scale(middle)
            mlp_ref[0, at, :] = (unit * gain[2] + shift[2]).astype(BF)

        send_strip(mlp_copies, q)

    acc_ref[...] = jnp.zeros_like(acc_ref)

    @pl.loop(0, ranks)
    def _(d):
        pltpu.make_async_copy(up_all.at[d], up_all.at[d], up_sems.at[d]).wait()

        @pl.when(d < 2)
        def _():
            pltpu.make_async_copy(down_all.at[d], down_all.at[d], down_sems.at[d]).wait()

        @pl.when(d == 2)
        def _():
            for load in part_loads[:2]:
                load.wait()
            part_copies[0].wait_recv()
            part_copies[1].start()

        @pl.when(d == 3)
        def _():
            part_loads[2].wait()
            part_copies[1].wait_recv()

        for c in (0, columns):
            at = pl.ds(c, columns)
            hidden, slope = gelu_both(dot(mlp_ref[0], up_all[d, :, at]))
            work_ref[d, :, at] = slope
            acc_ref[...] += dot(hidden.astype(BF), down_all[d, at, :])

    zero = jnp.zeros((1, width), F32)
    gain_three, shift_three = zero, zero
    for q in range(strips):

        def last_norm(r, carry):
            gain_term, shift_term = carry
            at = pl.ds(pl.multiple_of(q * strip + r * rows, rows), rows)
            unit, scale = unit_scale(acc_ref[at, :])
            out_ref[at, :] = (middle_ref[at, :] + (unit * gain[3] + shift[3])).astype(BF)
            dy = dy_ref[at, :].astype(F32)
            gmp_ref[0, at, :] = norm_pull(dy, unit, scale, gain[3]).astype(BF)
            return (
                gain_term + jnp.sum(dy * unit, axis=0, keepdims=True),
                shift_term + jnp.sum(dy, axis=0, keepdims=True),
            )

        gain_three, shift_three = lax.fori_loop(0, strip // rows, last_norm, (gain_three, shift_three))
        send_strip(gmp_copies, q)

    acc_ref[...] = jnp.zeros_like(acc_ref)

    @pl.loop(0, ranks)
    def _(d):
        for c in (0, columns):
            at = pl.ds(c, columns)
            grad = dot(gmp_ref[0], down_all[d, at, :], NT)
            grad = (grad * work_ref[d, :, at]).astype(BF)
            acc_ref[...] += dot(grad, up_all[d, :, at], NT)

    forward_on(mlp_copies)

    def inner_norms(r, carry):
        gain_two, shift_two, gain_one, shift_one = carry
        at = pl.ds(pl.multiple_of(r * rows, rows), rows)
        grad = acc_ref[at, :]
        unit, scale = unit_scale(middle_ref[at, :])
        gain_two = gain_two + jnp.sum(grad * unit, axis=0, keepdims=True)
        shift_two = shift_two + jnp.sum(grad, axis=0, keepdims=True)
        grad = dy_ref[at, :].astype(F32) + norm_pull(grad, unit, scale, gain[2])
        rest_ref[at, :] = grad
        unit, scale = unit_scale(proj_ref[at, :])
        gain_one = gain_one + jnp.sum(grad * unit, axis=0, keepdims=True)
        shift_one = shift_one + jnp.sum(grad, axis=0, keepdims=True)
        gap_ref[at, :] = norm_pull(grad, unit, scale, gain[1]).astype(BF)
        return gain_two, shift_two, gain_one, shift_one

    gain_two, shift_two, gain_one, shift_one = lax.fori_loop(0, block // rows, inner_norms, (zero, zero, zero, zero))
    early_ref[...] = jnp.concatenate(
        [zero, gain_one, gain_two, gain_three, zero, shift_one, shift_two, shift_three], axis=0
    )

    head_copies = []
    for d in [*range(1, ranks), 0]:
        grad = dot(gap_ref[...], out_all[d], NT).astype(BF)
        for pair in range(pairs):
            piece = grad[:, pair * PAIR : (pair + 1) * PAIR]
            if d == 0:
                do_ref[pair, 0] = piece
            else:
                slot = d * pairs + pair
                gh_ref[slot] = piece
                head_copies.append(push(gh_ref.at[slot], do_ref.at[pair, d], head_sems, slot, "tensor", d))
    for d in range(ranks):
        part = jnp.concatenate([heads_ref[d * pairs + p] for p in range(pairs)], axis=1)
        shared_ref[d] = dot(part, gap_ref[...], TN).astype(BF)

    for copies in (mlp_copies, gmp_copies):
        for _, beside, _ in copies:
            beside.wait_recv()
    work_ref[...] = jnp.zeros_like(work_ref)

    def late():
        forward_on(gmp_copies)
        for copy in head_copies:
            copy.start()

    def latest():
        for copies in (mlp_copies, gmp_copies):
            for _, _, onward in copies:
                onward.wait_recv()

    sums = [
        push(ref.at[0, 1 - lax.rem(lax.div(rank, 1 << o), 2)], got, sum_sems, o, "dp", 1 << o)
        for o, (ref, got) in enumerate([(down_ref, got_down), (up_ref, got_up)])
    ]
    half = columns // 2

    @pl.loop(0, 2 * ranks)
    def _(step):
        part = lax.div(step + 1, 3)
        i = step + 1 - 3 * part
        first, last, up = lax.div(2 - part, 2), lax.div(part, 2), lax.div(i + 1, 2)
        centre = 1 - first - last
        h = centre * (1 - up) + last
        b = first * (i - 1) + centre * (i + up) + last * (i + 1)
        pl.when(step == 3)(late)
        pl.when(step == 4)(latest)
        at = pl.ds(pl.multiple_of(h * columns, columns), columns)
        tokens, grads = mlp_ref[b], gmp_ref[b]
        hidden, slope = gelu_both(dot(tokens, up_all[0, :, at]))
        grad = (dot(grads, down_all[0, at, :], NT) * slope).astype(BF)
        work_ref[2 * h] += dot(hidden.astype(BF), grads, TN)
        work_ref[2 * h + 1, :, 0:columns] += dot(tokens[:, 0:columns], grad, TN)
        work_ref[2 * h + 1, :, columns:] += dot(tokens[:, columns:], grad, TN)

        @pl.when(b == ranks - 1)
        def _():
            for side in range(2):
                down_ref[h, side] = work_ref[2 * h, side * half : (side + 1) * half, :].astype(BF)
                up_ref[h, side] = work_ref[2 * h + 1, :, side * columns : (side + 1) * columns].astype(BF)

        @pl.when(step == 4)
        def _():
            for copy in sums:
                copy.start()

    for copy in sums:
        copy.wait()
    for copy in head_copies:
        copy.wait_recv()
        copy.wait_send()
    for copy in part_copies:
        copy.wait_send()
    for copies in (mlp_copies, gmp_copies):
        for group in copies:
            for copy in group:
                copy.wait_send()


def middle_stage(heads, tokens, cotangent, gains, shifts, weights, rests):
    block, width = tokens.shape
    ranks = lax.axis_size("tensor")
    local = weights[0].shape[0]
    pairs = local // PAIR
    hidden = weights[2].shape[0]
    vmem = pl.BlockSpec(memory_space=pltpu.VMEM)
    hbm = pl.BlockSpec(memory_space=pl.ANY)
    copies = pltpu.SemaphoreType.DMA
    assert block * 2 == width and hidden == width
    operands = [array for pair in zip(weights, rests) for array in pair]
    return pl.pallas_call(
        functools.partial(middle_kernel, block, ranks, pairs),
        out_shape=[
            jax.ShapeDtypeStruct((block, width), BF),
            jax.ShapeDtypeStruct((block, width), F32),
            jax.ShapeDtypeStruct((pairs, ranks, block, PAIR), BF),
            jax.ShapeDtypeStruct((ranks, local, width), BF),
            jax.ShapeDtypeStruct((2, 2, block // 2, width), BF),
            jax.ShapeDtypeStruct((2, 2, block, width // 2), BF),
            jax.ShapeDtypeStruct((block // 2, width), BF),
            jax.ShapeDtypeStruct((block, width // 2), BF),
            jax.ShapeDtypeStruct((8, width), F32),
        ],
        in_specs=[vmem] * 5 + [hbm] * 6,
        out_specs=[vmem] * 9,
        scratch_shapes=[
            pltpu.VMEM((ranks, local, width), BF),
            pltpu.VMEM((ranks, width, hidden), BF),
            pltpu.VMEM((ranks, hidden, width), BF),
            pltpu.VMEM((ranks, block, width), F32),
            pltpu.VMEM((ranks, block, width), BF),
            pltpu.VMEM((ranks, block, width), BF),
            pltpu.VMEM((block, width), F32),
            pltpu.VMEM((block, width), F32),
            pltpu.VMEM((block, width), F32),
            pltpu.VMEM((block, width), BF),
            pltpu.VMEM((ranks * pairs, block, PAIR), BF),
            copies((ranks,)),
            copies((ranks,)),
            copies((2,)),
            copies((3,)),
            copies((2, 2)),
            copies((2, 12)),
            copies((2, 12)),
            copies((2, ranks * pairs)),
            copies((2, 2)),
        ],
        compiler_params=pltpu.CompilerParams(vmem_limit_bytes=62 << 20, collective_id=3, has_side_effects=True),
        name="middle_stage",
    )(heads, tokens, cotangent, gains, shifts, *operands)


def finish_kernel(block, blocks, pairs, orders, *refs):
    (lengths_ref, down_ref, up_ref, first_down, first_up, shared_ref, log_ref, gain_ref, early_ref, *refs) = refs
    far_refs, refs = refs[:9], refs[9:]
    (input_ref, sums_ref, down_out, up_out, own_out, qkv_out, *refs) = refs
    near_refs, refs = refs[:9], refs[9:]
    (qkv_ref, do_ref, o_ref, cos_ref, sin_ref, attn_ref, w_ref, x_ref, rest_ref) = near_refs
    (start_ref, dq_ref, inner_ref, grads_ref, own_ref, wide_ref, token_ref, core_sum, got_y, *refs) = refs
    (token_sum, token_y, norm_ref, got_t, sum_t, got_d, *refs) = refs
    chunks, steps = len(orders), len(orders[0])
    count = chunks * steps
    got, refs = refs[:count], refs[count:]
    (load_sems, rs_sems, ag_sems, core_sems, y_sems, token_core_sems, token_y_sems, t_sems, d_sems) = refs

    mine = lax.axis_index("tensor")
    rank = lax.axis_index("dp")
    ranks_dp = lax.axis_size("dp")
    heads = PAIR // HD
    started = []
    loads = [
        pltpu.make_async_copy(far, near, load_sems.at[i]) for i, (far, near) in enumerate(zip(far_refs, near_refs))
    ]
    for load in loads:
        load.start()

    def start(copy):
        copy.start()
        started.append(copy)
        return copy

    sources = [down_ref.at[0], up_ref.at[0], down_ref.at[1], up_ref.at[1], own_ref] + [wide_ref.at[p] for p in range(pairs)]
    results = [down_out.at[0], up_out.at[0], down_out.at[1], up_out.at[1], own_out] + [qkv_out.at[p] for p in range(pairs)]
    firsts = {0: first_down, 1: first_up}
    bits = [[lax.rem(lax.div(rank, 1 << o), 2) for o in order] for order in orders]
    rs_copies, ag_copies = {}, {}

    def held(c, k):
        return sources[c] if k == 0 else got[c * steps + k - 1]

    for c in range(chunks):
        for k in range(steps):
            far = 1 << orders[c][k]
            if k > 0 or c not in firsts:
                source = held(c, k).at[1 - bits[c][k]]
                rs_copies[c, k] = push(source, got[c * steps + k], rs_sems, c * steps + k, "dp", far)
            region = results[c].at[tuple(bits[c][: k + 1])]
            ag_copies[c, k] = push(region, region, ag_sems, c * steps + k, "dp", far)

    def begin(c):
        rs_copies[c, 0].start()

    def halve(c, k):
        at = c * steps + k
        if (c, k) in rs_copies:
            rs_copies[c, k].wait_recv()
            term = got[at][...]
        else:
            term = firsts[c][...]
        total = held(c, k)[bits[c][k]].astype(F32) + term.astype(F32)
        got[at][...] = total.astype(BF)
        if k + 1 < steps:
            rs_copies[c, k + 1].start()
        else:
            results[c][tuple(bits[c])] = total.astype(BF)
            ag_copies[c, k].start()

    def double(c, k):
        ag_copies[c, k].wait_recv()
        if k > 0:
            ag_copies[c, k - 1].start()

    core_copies = [
        push(shared_ref.at[d + 1], core_sum.at[d // 2], core_sems, d // 2, "tensor", 1) for d in range(0, blocks, 2)
    ]
    y_copies = [
        push(core_sum.at[h], got_y.at[h - 1], y_sems, h - 1, "tensor", 2 * h) for h in range(1, blocks // 2)
    ]

    def pair_up():
        for h in range(blocks // 2):
            core_copies[h].wait_recv()
            core_sum[h] = (shared_ref[2 * h].astype(F32) + core_sum[h].astype(F32)).astype(BF)
        for copy in y_copies:
            copy.start()

    def settle():
        total = core_sum[0].astype(F32)
        for h in range(1, blocks // 2):
            y_copies[h - 1].wait_recv()
            total = total + got_y[h - 1].astype(F32)
        own_ref[...] = total.astype(BF)

    def prepare(pair):
        dq_ref[...] = jnp.zeros_like(dq_ref)
        for b in range(blocks):
            rows = pl.ds(b * block, block)
            product = do_ref[pair, b].astype(F32) * o_ref[pair, rows, :].astype(F32)
            high = product.astype(BF)
            low = (product - high.astype(F32)).astype(BF)
            for head in range(heads):
                ones = head_mask((16, PAIR), head).astype(F32).astype(BF)
                inner = dot(ones, high, NT) + dot(ones, low, NT)
                inner_ref[head : head + 1, rows] = inner[0:1, :]

    def unit(pair, key_block):
        slot = xor(key_block, mine, blocks)
        here = pl.ds(pl.multiple_of(slot * block, block), block)
        keys = qkv_ref[pairs + pair, here, :]
        values = qkv_ref[2 * pairs + pair, here, :]
        dk = jnp.zeros((block, PAIR), F32)
        dv = jnp.zeros((block, PAIR), F32)
        for head in range(heads):
            mask = head_mask(keys.shape, head)
            key = jnp.where(mask, keys * HD**-0.5, jnp.zeros_like(keys))
            value = jnp.where(mask, values, jnp.zeros_like(values))

            def one(i, carry, first):
                dk, dv = carry
                place = xor(i, mine, blocks)
                rows = pl.ds(pl.multiple_of(place * block, block), block)
                real = pl.ds(pl.multiple_of(i * block, block), block)
                query = qkv_ref[pair, rows, :]
                grad = do_ref[pair, place]
                s = dot(key, query, NT)
                row = lax.broadcasted_iota(jnp.int32, s.shape, 0)
                visible = row >= start_ref[0:1, real] - key_block * block
                if first:
                    visible &= row <= lax.broadcasted_iota(jnp.int32, s.shape, 1)
                probs = jnp.where(visible, jnp.exp(s - log_ref[pair, head : head + 1, rows]), 0.0)
                grad_probs = dot(value, grad, NT)
                ds = (probs * (grad_probs - inner_ref[head : head + 1, rows])).astype(BF)
                zero = jnp.zeros_like(query)
                dv = dv + dot(probs.astype(BF), jnp.where(mask, grad, zero))
                dk = dk + dot(ds, jnp.where(mask, query, zero))
                dq_ref[rows, :] += dot(ds, key, TN)
                return dk, dv

            dk, dv = one(key_block, (dk, dv), True)
            dk, dv = lax.fori_loop(key_block + 1, blocks, lambda i, carry: one(i, carry, False), (dk, dv))
        real = pl.ds(pl.multiple_of(key_block * block, block), block)
        grads_ref[pairs + pair, here, :] = turn(dk * HD**-0.5, cos_ref[real, :], -sin_ref[real, :]).astype(BF)
        grads_ref[2 * pairs + pair, here, :] = dv.astype(BF)

    def close(pair):
        for b in range(blocks):
            rows = pl.ds(b * block, block)
            real = pl.ds(pl.multiple_of(flip(mine, b) * block, block), block)
            grads_ref[pair, rows, :] = turn(dq_ref[rows, :], cos_ref[real, :], -sin_ref[real, :]).astype(BF)
        total = None
        for b in range(blocks):
            rows = pl.ds(b * block, block)
            wide = jnp.concatenate([grads_ref[c * pairs + pair, rows, :] for c in range(3)], axis=1)
            term = dot(attn_ref[b], wide, TN)
            total = term if total is None else total + term
        wide_ref[pair] = total.astype(BF).reshape(wide_ref.shape[1:])

    greet(("tensor", "dp"))
    for copy in core_copies:
        copy.start()
    begin(3)
    begin(2)
    halve(0, 0)
    halve(1, 0)
    start_ref[...] = document_start(lengths_ref, lax.broadcasted_iota(jnp.int32, start_ref.shape, 1))
    for load in loads[:5]:
        load.wait()
    slots = pairs * blocks
    halving = lambda *steps: [functools.partial(halve, c, k) for c, k in steps]
    doubling = lambda *steps: [functools.partial(double, c, k) for c, k in steps]
    beginning = lambda c: [functools.partial(begin, c)]
    events = {
        0: [pair_up],
        2: [settle] + beginning(4) + halving((0, 1), (3, 0), (1, 1), (2, 0)),
        3: [lambda: [load.wait() for load in loads[5:]]],
        4: beginning(5) + halving((0, 2), (4, 0), (3, 1), (1, 2)),
        5: halving((2, 1)),
        6: halving((4, 1)) + doubling((0, 2)),
        7: halving((3, 2)) + doubling((1, 2)),
    }

    @pl.loop(0, slots)
    def _(u):
        pair, key_block = lax.div(u, blocks), lax.rem(u, blocks)
        for when, todo in events.items():

            @pl.when(u == when)
            def _():
                for step in todo:
                    step()

        for p in range(pairs):
            pl.when(u == p * blocks)(functools.partial(prepare, p))
        unit(pair, key_block)
        for p in range(pairs):
            pl.when(u == p * blocks + blocks - 1)(functools.partial(close, p))

    begin(6)
    halve(4, 2)
    halve(2, 2)

    def token_term(d):
        rows = pl.ds(d * block, block)
        total = None
        for c in range(3):
            wide = jnp.concatenate([grads_ref[c * pairs + p, rows, :] for p in range(pairs)], axis=1)
            term = dot(wide, w_ref[c], NT)
            total = term if total is None else total + term
        token_ref[d] = total.astype(BF)

    token_copies = []
    for d in range(0, blocks, 2):
        token_term(d + 1)
        token_copies.append(start(push(token_ref.at[d + 1], token_sum.at[d // 2], token_core_sems, d // 2, "tensor", 1)))
    double(1, 1)
    for d in range(blocks - 2, -1, -2):
        token_term(d)
        token_copies[d // 2].wait_recv()
        token_sum[d // 2] = (token_ref[d].astype(F32) + token_sum[d // 2].astype(F32)).astype(BF)
        if d > 0:
            across = start(push(token_sum.at[d // 2], token_y.at[d // 2 - 1], token_y_sems, d // 2 - 1, "tensor", d))
    double(3, 2)
    halve(5, 0)
    double(4, 2)
    halve(6, 0)
    double(0, 1)
    double(2, 2)
    double(3, 1)
    halve(5, 1)
    double(4, 1)

    across.wait_recv()
    rows = 64
    lanes = x_ref.shape[1] // 128
    gain = gain_ref[0:1, :]

    def norm(r, carry):
        gain_term, shift_term = carry
        at = pl.ds(pl.multiple_of(r * rows, rows), rows)
        grad = token_sum[0, at, :].astype(F32)
        for h in range(blocks // 2 - 1):
            grad = grad + token_y[h, at, :].astype(F32)
        unit, scale = unit_scale(x_ref[at, :].astype(F32))
        total = rest_ref[at, :] + norm_pull(grad, unit, scale, gain)
        for c in range(lanes):
            there = pl.ds(pl.multiple_of(r * (rows * lanes), rows * lanes) + c, rows, stride=lanes)
            input_ref[there, :] = total[:, c * 128 : (c + 1) * 128]
        return (
            gain_term + jnp.sum(grad * unit, axis=0, keepdims=True),
            shift_term + jnp.sum(grad, axis=0, keepdims=True),
        )

    zero = jnp.zeros(gain.shape, F32)
    gain_term, shift_term = lax.fori_loop(0, block // rows, norm, (zero, zero))
    norm_ref[...] = early_ref[...]
    norm_ref[0:1, :] = gain_term
    norm_ref[4:5, :] = shift_term
    ts = [start(push(norm_ref, got_t.at[d - 1], t_sems, d - 1, "tensor", d)) for d in range(1, blocks)]
    halve(6, 1)
    halve(5, 2)
    for copy in ts:
        copy.wait_recv()
    sum_t[...] = tree_sum([norm_ref[...]] + [got_t[d] for d in range(blocks - 1)])
    ds = [start(push(sum_t, got_d.at[d - 1], d_sems, d - 1, "dp", d)) for d in range(1, ranks_dp)]
    double(2, 1)
    halve(6, 2)
    double(5, 2)
    double(6, 2)
    double(5, 1)
    double(6, 1)
    for copy in ds:
        copy.wait_recv()
    sums_ref[...] = tree_sum([sum_t[...]] + [got_d[d] for d in range(ranks_dp - 1)])
    for c in range(chunks):
        double(c, 0)
    for copy in [*started, *core_copies, *y_copies, *rs_copies.values(), *ag_copies.values()]:
        copy.wait_send()


def finish_stage(
    lengths, qkv, grad_heads, heads_out, logs, cosine, sine, attn, weight, tokens, rest, shared, terms, firsts, gains, early
):
    pairs3, length, _ = qkv.shape
    pairs = pairs3 // 3
    block, width = tokens.shape
    blocks = length // block
    ranks_dp = lax.axis_size("dp")
    steps = ranks_dp.bit_length() - 1
    straight = list(range(steps))
    crossed = [1, 0, *straight[2:]]
    orders = [straight, crossed, straight, crossed, straight, crossed, straight]
    assert pairs == 2 and steps >= 3
    cut = (2,) * steps
    local = shared.shape[1]
    shared = shared.reshape(blocks, *cut, local // ranks_dp, width)
    terms = [term.reshape(2, *cut, -1, term.shape[-1]) for term in terms]
    firsts = [first.reshape(*cut[1:], -1, first.shape[-1]) for first in firsts]
    wide = (*cut, width // ranks_dp, 3 * PAIR)
    shapes = [term.shape[1:] for term in terms] * 2 + [shared.shape[1:]] + [wide] * pairs
    far = (qkv, grad_heads, heads_out, cosine, sine, attn, weight, tokens, rest)
    parts = [shape[k + 1 :] for shape in shapes for k in range(steps)]
    vmem = pl.BlockSpec(memory_space=pltpu.VMEM)
    copies = pltpu.SemaphoreType.DMA
    outs = pl.pallas_call(
        functools.partial(finish_kernel, block, blocks, pairs, orders),
        out_shape=[
            jax.ShapeDtypeStruct((block * width // 128, 128), F32),
            jax.ShapeDtypeStruct((8, width), F32),
            *[jax.ShapeDtypeStruct(term.shape, BF) for term in terms],
            jax.ShapeDtypeStruct(shared.shape[1:], BF),
            jax.ShapeDtypeStruct((pairs, *wide), BF),
        ],
        in_specs=[pl.BlockSpec(memory_space=pltpu.SMEM)] + [vmem] * 8 + [pl.BlockSpec(memory_space=pl.ANY)] * 9,
        out_specs=[vmem] * 6,
        scratch_shapes=[
            *[pltpu.VMEM(array.shape, array.dtype) for array in far],
            pltpu.VMEM((8, length), jnp.int32),
            pltpu.VMEM((length, PAIR), F32),
            pltpu.VMEM((8, length), F32),
            pltpu.VMEM((pairs3, length, PAIR), BF),
            pltpu.VMEM(shared.shape[1:], BF),
            pltpu.VMEM((pairs, *wide), BF),
            pltpu.VMEM((blocks, block, width), BF),
            pltpu.VMEM((blocks // 2, *shared.shape[1:]), BF),
            pltpu.VMEM((blocks // 2 - 1, *shared.shape[1:]), BF),
            pltpu.VMEM((blocks // 2, block, width), BF),
            pltpu.VMEM((blocks // 2 - 1, block, width), BF),
            pltpu.VMEM((8, width), F32),
            pltpu.VMEM((blocks - 1, 8, width), F32),
            pltpu.VMEM((8, width), F32),
            pltpu.VMEM((ranks_dp - 1, 8, width), F32),
            *[pltpu.VMEM(shape, BF) for shape in parts],
            copies((9,)),
            copies((2, len(parts))),
            copies((2, len(parts))),
            copies((2, blocks // 2)),
            copies((2, blocks // 2 - 1)),
            copies((2, blocks // 2)),
            copies((2, blocks // 2 - 1)),
            copies((2, blocks - 1)),
            copies((2, ranks_dp - 1)),
        ],
        compiler_params=pltpu.CompilerParams(vmem_limit_bytes=62 << 20, collective_id=0, has_side_effects=True),
        name="finish_stage",
    )(lengths, *terms, *firsts, shared, logs, gains, early, *far)
    input_grad, sums, down, up, own, wides = outs
    return (
        input_grad,
        sums,
        down.reshape(width, width),
        up.reshape(2, width, -1),
        own.reshape(local, width),
        wides.reshape(pairs, width, 3 * PAIR),
    )


def body(block_in, lengths, qkv_weight, out_weight, up_weight, down_weight, norm_gain, norm_bias, cotangent):
    block, row_count, width = block_in.shape
    assert row_count == 1
    pairs = out_weight.shape[0] // PAIR
    qkv_swapped = jnp.transpose(qkv_weight, (1, 0, 2))

    qkv, attn_full, heads_mixed, logs, heads_parts, cosine, sine, rests = attend_forward(
        lengths,
        block_in.reshape(block, width),
        norm_gain,
        norm_bias,
        qkv_swapped,
        (out_weight, up_weight, down_weight),
    )
    block_out, grad_middle, grad_heads, shared, down_terms, up_terms, down_first, up_first, early = middle_stage(
        heads_parts,
        block_in.reshape(block, width),
        cotangent.reshape(block, width),
        norm_gain,
        norm_bias,
        (out_weight, up_weight, down_weight),
        rests,
    )
    input_grad, sums, down_sum, up_sums, out_sum, qkv_sums = finish_stage(
        lengths,
        qkv,
        grad_heads,
        heads_mixed,
        logs,
        cosine,
        sine,
        attn_full,
        qkv_swapped,
        block_in.reshape(block, width),
        grad_middle,
        shared,
        (down_terms, up_terms),
        (down_first, up_first),
        norm_gain,
        early,
    )
    down_grad = down_sum.astype(F32)
    up_grad = jnp.concatenate([up_sums[0], up_sums[1]], axis=1).astype(F32)
    qkv_grad = jnp.stack(
        [jnp.concatenate([qkv_sums[p, :, c * PAIR : (c + 1) * PAIR] for p in range(pairs)], axis=1) for c in range(3)]
    ).astype(F32)
    qkv_grad = jnp.transpose(qkv_grad, (1, 0, 2))
    out_grad = out_sum.astype(F32)
    gain_grad, bias_grad = sums[0:4], sums[4:8]
    return (
        block_out.reshape(block_in.shape),
        input_grad.reshape(block_in.shape),
        qkv_grad,
        out_grad,
        up_grad,
        down_grad,
        gain_grad,
        bias_grad,
    )


def solution(mesh):
    tokens, rows, columns, copied = P("tensor", "dp", None), P("tensor", None), P(None, "tensor"), P()
    heads = P(None, None, "tensor")
    return jax.shard_map(
        body,
        mesh=mesh,
        in_specs=(tokens, P("dp", None), heads, rows, columns, rows, copied, copied, tokens),
        out_specs=(tokens, tokens, heads, rows, columns, rows, copied, copied),
        check_vma=False,
    )
```

```python
import functools

import jax
import jax.numpy as jnp
import numpy as np
from jax import lax
from jax.experimental import pallas as pl
from jax.experimental.pallas import tpu as pltpu
from jax.sharding import PartitionSpec as P

HD = 64
PAIR = 128
EPSILON = 1e-05
ROPE_BASE = 10000.0
NEG = -1e30
MESH = pl.DeviceIdType.MESH
BF = jnp.bfloat16
F32 = jnp.float32
NT = (((1,), (1,)), ((), ()))
NN = (((1,), (0,)), ((), ()))
TN = (((0,), (0,)), ((), ()))


def dot(a, b, dims=NN):
    return lax.dot_general(a, b, dims, preferred_element_type=F32)


def layer_norm(values, gain, shift):
    centre = values - jnp.mean(values, axis=-1, keepdims=True)
    spread = jnp.mean(centre * centre, axis=-1, keepdims=True)
    return centre * lax.rsqrt(spread + EPSILON) * gain + shift


def flip(index, offset):
    bit = 1
    while bit <= offset:
        if offset & bit:
            index = index + bit - 2 * bit * lax.rem(lax.div(index, bit), 2)
        bit *= 2
    return index


def xor(a, b, size):
    total, bit = 0, 1
    while bit < size:
        total = total + bit * lax.rem(lax.div(a, bit) + lax.div(b, bit), 2)
        bit *= 2
    return total


def greet(axes):
    barrier = pltpu.get_barrier_semaphore()
    count = 0
    for axis in axes:
        index = lax.axis_index(axis)
        for d in range(1, lax.axis_size(axis)):
            pl.semaphore_signal(barrier, inc=1, device_id={axis: flip(index, d)}, device_id_type=MESH)
            count += 1
    pl.semaphore_wait(barrier, count)


def tree_sum(parts):
    parts = [part.astype(F32) for part in parts]
    while len(parts) > 1:
        parts = [parts[i] + parts[i + 1] for i in range(0, len(parts), 2)]
    return parts[0]


def push(src, dst, sems, slot, axis, offset):
    return pltpu.make_async_remote_copy(
        src_ref=src,
        dst_ref=dst,
        send_sem=sems.at[0, slot],
        recv_sem=sems.at[1, slot],
        device_id={axis: flip(lax.axis_index(axis), offset)},
        device_id_type=MESH,
    )


def turn(values, cosine, signed_sine):
    lane = lax.broadcasted_iota(jnp.int32, values.shape, 1)
    other = jnp.where(lane % HD < HD // 2, pltpu.roll(values, PAIR - HD // 2, 1), pltpu.roll(values, HD // 2, 1))
    return values * cosine + other * signed_sine


def head_mask(shape, head):
    lane = lax.broadcasted_iota(jnp.int32, shape, 1)
    return lane // HD == head


def document_start(lengths_ref, spot):
    begin = jnp.zeros_like(spot)
    total = jnp.int32(0)
    for j in range(lengths_ref.shape[1] - 1):
        total = total + lengths_ref[0, j]
        begin = jnp.where(spot >= total, total, begin)
    return begin


def forward_kernel(block, ranks, pairs, chunks, *refs):
    lengths_ref, x_ref, gain_ref, shift_ref, w_ref, freq_ref, *refs = refs
    weights, refs = refs[:3], refs[3:]
    mixed_ref, log_ref, heads_ref, qkv_out, attn_out, cos_out, sin_out, *refs = refs
    rests, refs = refs[:3], refs[3:]
    scores_ref, qkv_ref, attn_ref, cos_ref, sin_ref, start_ref, out_sems, attn_sems, head_sems, own_sems, y_sems, z_sems, x_sems, core_sems = refs

    mine = lax.axis_index("tensor")
    rank = lax.axis_index("dp")
    group = lax.axis_size("dp") // 2
    x_bit, z_place = lax.rem(rank, 2), lax.div(rank, 2)
    direct = len(chunks) - 1
    started = []

    def start(copy):
        copy.start()
        started.append(copy)
        return copy

    outward = [
        pltpu.make_async_copy(src, dst, out_sems.at[i])
        for i, (src, dst) in enumerate(
            [(attn_ref, attn_out), (qkv_ref, qkv_out), (cos_ref, cos_out), (sin_ref, sin_out)]
        )
    ]

    def cut(array, c, *lead):
        at, (_, low, size) = array.at, chunks[c]
        return at[(*lead, slice(None), pl.ds(low, size))]

    def every(array, c, *lead):
        at, (_, low, size) = array.at, chunks[c]
        return at[(*lead, slice(None), slice(None), pl.ds(low, size))]

    def rest(c):
        return rests[chunks[c][0]]

    y_copies = [
        push(
            cut(weights[chunks[c][0]], c, x_bit, z_place), cut(rest(c), c, 1, x_bit, z_place), y_sems, c, "tensor", 2
        )
        for c in range(direct)
    ]
    whole = lambda array, c, *lead: array.at[(*lead, slice(None), slice(None), slice(None), pl.ds(*chunks[c][1:]))]
    y_copies.append(
        push(whole(weights[chunks[direct][0]], direct), whole(rest(direct), direct, 1), y_sems, direct, "tensor", 2)
    )
    z_copies = [
        [
            push(
                cut(rest(c), c, 1, x_bit, z_place),
                cut(rest(c), c, 1, x_bit, z_place),
                z_sems,
                c * (group - 1) + d - 1,
                "dp",
                2 * d,
            )
            for d in range(1, group)
        ]
        for c in range(direct)
    ]
    x_copies = [
        push(every(rest(c), c, 1, x_bit), every(rest(c), c, 1, x_bit), x_sems, c, "dp", 1) for c in range(direct - 1)
    ]
    core_copies = {
        c: push(whole(rest(c), c, 1), whole(rest(c), c, 2), core_sems, c, "tensor", 1)
        for c in [*range(direct - 1), direct]
    }
    own_copies = [push(weights[a], rests[a].at[0], own_sems, a, "tensor", 1) for a in range(3)]

    def to_z(c):
        y_copies[c].wait_recv()
        for copy in z_copies[c]:
            copy.start()

    def to_x(c):
        for copy in z_copies[c]:
            copy.wait_recv()
        x_copies[c].start()

    def to_core(c):
        (y_copies if c == direct else x_copies)[c].wait_recv()
        core_copies[c].start()

    greet(("tensor", "dp"))
    for c in range(direct - 1):
        y_copies[c].start()

    strips = 4
    strip = block // strips
    gain, shift = gain_ref[0:1, :], shift_ref[0:1, :]
    across, beside, onward = [], [], []
    for q in range(strips):

        @pl.loop(0, strip // 64)
        def _(r):
            at = pl.ds(pl.multiple_of(q * strip + r * 64, 64), 64)
            attn_ref[0, at, :] = layer_norm(x_ref[at, :].astype(F32), gain, shift).astype(BF)

        at = pl.ds(q * strip, strip)
        across.append(start(push(attn_ref.at[0, at], attn_ref.at[2, at], attn_sems, q, "tensor", 2)))
        beside.append(start(push(attn_ref.at[0, at], attn_ref.at[1, at], attn_sems, strips + q, "tensor", 1)))
        onward.append(push(attn_ref.at[2, at], attn_ref.at[3, at], attn_sems, 2 * strips + q, "tensor", 1))

    y_copies[direct - 1].start()
    to_z(0)

    lane = lax.broadcasted_iota(jnp.int32, (64, PAIR), 1)
    sign = jnp.where(lane % HD < HD // 2, -1.0, 1.0)

    @pl.loop(0, ranks * block // 64)
    def _(r):
        at = pl.ds(pl.multiple_of(r * 64, 64), 64)
        spot = r * 64 + lax.broadcasted_iota(jnp.int32, (64, PAIR), 0)
        begin = document_start(lengths_ref, spot)
        start_ref[at, :] = begin
        angle = (spot - begin).astype(F32) * freq_ref[...]
        cos_ref[at, :] = jnp.cos(angle)
        sin_ref[at, :] = jnp.sin(angle) * sign

    def middle():
        to_x(0)
        to_z(1)
        for q in range(strips - 1):
            across[q].wait_recv()
            onward[q].start()
        to_x(1)
        to_z(2)
        across[strips - 1].wait_recv()
        onward[strips - 1].start()
        y_copies[direct].start()
        for copy in own_copies:
            copy.start()

    def beside_here():
        for copy in beside:
            copy.wait_recv()

    def onward_here():
        for copy in onward:
            copy.wait_recv()

    @pl.loop(0, ranks)
    def _(d):
        pl.when(d == 1)(beside_here)
        pl.when(d == 2)(middle)
        pl.when(d == 3)(onward_here)
        x = attn_ref[d]
        rows = pl.ds(pl.multiple_of(d * block, block), block)
        real = pl.ds(pl.multiple_of(xor(d, mine, ranks) * block, block), block)
        for part in range(3):
            project = dot(x, w_ref[part])
            for pair in range(pairs):
                piece = project[:, pair * PAIR : (pair + 1) * PAIR]
                if part < 2:
                    piece = turn(piece, cos_ref[real, :], sin_ref[real, :])
                qkv_ref[part * pairs + pair, rows, :] = piece.astype(BF)

    sub = block // 2

    def unit(pair, d):
        row_block = xor(d, mine, ranks)
        rows = pl.ds(pl.multiple_of(d * block, block), block)
        begin = start_ref[pl.ds(pl.multiple_of(row_block * block, block), block), :]
        queries = qkv_ref[pair, rows, :] * HD**-0.5
        heads = range(PAIR // HD)
        masks = [head_mask(queries.shape, head) for head in heads]
        parts = [jnp.where(mask, queries, jnp.zeros_like(queries)) for mask in masks]
        column = lax.broadcasted_iota(jnp.int32, (block, 128), 1)

        def score(j, tops, last):
            at = pl.ds(pl.multiple_of(xor(j, mine, ranks) * block, block), block)
            keys = qkv_ref[pairs + pair, at, :]
            tops = list(tops)
            for low in range(0, block, sub):
                for head in heads:
                    s = dot(parts[head], keys[low : low + sub], NT)
                    for c in range(0, sub, 128):
                        visible = column + (low + c) >= begin - j * block
                        if last:
                            visible &= column + (low + c) <= lax.broadcasted_iota(jnp.int32, (block, 128), 0)
                        piece = jnp.where(visible, s[:, c : c + 128], NEG)
                        scores_ref[head, j, :, low + c : low + c + 128] = piece
                        tops[head] = jnp.maximum(tops[head], piece)
            return tuple(tops)

        tops = tuple(jnp.full((block, 128), NEG, F32) for _ in heads)
        tops = lax.fori_loop(0, row_block, lambda j, tops: score(j, tops, False), tops)
        tops = score(row_block, tops, True)
        tops = [jnp.broadcast_to(jnp.max(top, axis=1, keepdims=True), (block, 128)) for top in tops]

        def mix(j, accs):
            at = pl.ds(pl.multiple_of(xor(j, mine, ranks) * block, block), block)
            values = qkv_ref[2 * pairs + pair, at, :]
            accs = list(accs)
            for low in range(0, block, sub):
                for head in heads:
                    filled = jnp.where(masks[head], values, jnp.ones_like(values))[low : low + sub]
                    shares = [
                        jnp.exp(scores_ref[head, j, :, low + c : low + c + 128] - tops[head]).astype(BF)
                        for c in range(0, sub, 128)
                    ]
                    accs[head] = accs[head] + dot(jnp.concatenate(shares, axis=1), filled)
            return tuple(accs)

        accs = lax.fori_loop(0, row_block + 1, mix, tuple(jnp.zeros((block, PAIR), F32) for _ in heads))
        totals = [pltpu.roll(acc, HD, 1) for acc in accs]
        mixed_ref[pair, rows, :] = jnp.where(masks[0], accs[0] / totals[0], accs[1] / totals[1]).astype(BF)
        for head in heads:
            logs = tops[head] + jnp.log(jnp.where(masks[head], totals[head], accs[head]))
            log_ref[pair, head : head + 1, rows] = jnp.transpose(logs)[0:1, :]

    def head_copy(pair, d):
        slot = d * pairs + pair
        return pltpu.make_async_remote_copy(
            src_ref=mixed_ref.at[pair, pl.ds(pl.multiple_of(d * block, block), block)],
            dst_ref=heads_ref.at[slot],
            send_sem=head_sems.at[0, slot],
            recv_sem=head_sems.at[1, slot],
            device_id={"tensor": xor(mine, d, ranks)},
            device_id_type=MESH,
        )

    for copy in outward:
        copy.start()
    units = pairs * ranks
    events = {
        0: [lambda: to_x(2), lambda: to_z(3), lambda: to_z(4), lambda: to_core(0), lambda: to_core(1)],
        3: [lambda: to_x(3)],
        5: [lambda: to_core(2)],
    }

    @pl.loop(0, units)
    def _(u):
        pair, d = lax.rem(u, pairs), ranks - 1 - lax.div(u, pairs)
        unit(pair, d)
        pl.when(d > 0)(lambda: head_copy(pair, d).start())
        for when, steps in events.items():

            @pl.when(u == min(when, units - 1))
            def _():
                for step in steps:
                    step()

    for pair in range(pairs):
        heads_ref[pair] = mixed_ref[pair, 0:block, :]
    to_core(3)
    to_core(direct)

    @pl.loop(pairs, units)
    def _(slot):
        copy = head_copy(lax.rem(slot, pairs), lax.div(slot, pairs))
        copy.wait_recv()
        copy.wait_send()

    for copy in [*core_copies.values(), *own_copies, *z_copies[direct - 1]]:
        copy.wait_recv()
    for copy in [*started, *onward, *own_copies, *y_copies, *x_copies, *core_copies.values()]:
        copy.wait_send()
    for copies in z_copies:
        for copy in copies:
            copy.wait_send()
    for copy in outward:
        copy.wait()


def attend_forward(lengths, tokens, gains, shifts, weight, weights):
    block, width = tokens.shape
    ranks = lax.axis_size("tensor")
    assert ranks == 4
    length = block * ranks
    pairs = weight.shape[2] // PAIR
    group = lax.axis_size("dp") // 2
    views = [w.reshape(2, group, w.shape[0] // (2 * group), w.shape[1]) for w in weights]
    chunks = [(0, 0, width)]
    for a in (1, 2):
        columns = weights[a].shape[1] // 2
        chunks += [(a, 0, columns), (a, columns, columns)]
    chunks[3:] = [(2, columns, columns // 2), (2, 0, columns), (2, columns + columns // 2, columns // 2)]
    vmem = pl.BlockSpec(memory_space=pltpu.VMEM)
    hbm = pl.BlockSpec(memory_space=pl.ANY)
    copies = pltpu.SemaphoreType.DMA
    lane = np.arange(PAIR) % (HD // 2)
    frequencies = jnp.asarray((ROPE_BASE ** (-lane * 2.0 / HD))[None, :], F32)
    smem = pl.BlockSpec(memory_space=pltpu.SMEM)
    mixed, logs, heads, qkv, attn, cosine, sine, *rests = pl.pallas_call(
        functools.partial(forward_kernel, block, ranks, pairs, chunks),
        out_shape=[
            jax.ShapeDtypeStruct((pairs, length, PAIR), BF),
            jax.ShapeDtypeStruct((pairs, 8, length), F32),
            jax.ShapeDtypeStruct((ranks * pairs, block, PAIR), BF),
            jax.ShapeDtypeStruct((3 * pairs, length, PAIR), BF),
            jax.ShapeDtypeStruct((ranks, block, width), BF),
            jax.ShapeDtypeStruct((length, PAIR), F32),
            jax.ShapeDtypeStruct((length, PAIR), F32),
            *[jax.ShapeDtypeStruct((ranks - 1, *view.shape), BF) for view in views],
        ],
        in_specs=[smem] + [vmem] * 5 + [hbm] * 3,
        out_specs=[vmem] * 3 + [hbm] * 7,
        scratch_shapes=[
            pltpu.VMEM((PAIR // HD, ranks, block, block), F32),
            pltpu.VMEM((3 * pairs, length, PAIR), BF),
            pltpu.VMEM((ranks, block, width), BF),
            pltpu.VMEM((length, PAIR), F32),
            pltpu.VMEM((length, PAIR), F32),
            pltpu.VMEM((length, PAIR), jnp.int32),
            copies((4,)),
            copies((2, 12)),
            copies((2, ranks * pairs)),
            copies((2, 3)),
            copies((2, len(chunks))),
            copies((2, len(chunks) * (group - 1))),
            copies((2, len(chunks))),
            copies((2, len(chunks))),
        ],
        compiler_params=pltpu.CompilerParams(vmem_limit_bytes=56 << 20, collective_id=2, has_side_effects=True),
        name="attend_forward",
    )(lengths, tokens, gains, shifts, weight, frequencies, *views)
    rests = [r.reshape(ranks - 1, *w.shape) for r, w in zip(rests, weights)]
    return qkv, attn, mixed, logs, heads, cosine, sine, rests


def unit_scale(values):
    centre = values - jnp.mean(values, axis=-1, keepdims=True)
    scale = lax.rsqrt(jnp.mean(centre * centre, axis=-1, keepdims=True) + EPSILON)
    return centre * scale, scale


def norm_pull(grad, unit, scale, gain):
    inside = grad * gain
    first = jnp.mean(inside, axis=-1, keepdims=True)
    second = jnp.mean(inside * unit, axis=-1, keepdims=True)
    return scale * (inside - first - unit * second)


def gelu_both(x):
    bend = 0.7978845608028654
    square = x * x
    t = jnp.tanh(bend * (x + 0.044715 * (square * x)))
    side = 0.5 * (1.0 + t)
    return x * side, side + 0.5 * x * (1.0 - t * t) * (bend * (1.0 + 0.134145 * square))


def middle_kernel(block, ranks, pairs, *refs):
    (heads_ref, x_ref, dy_ref, gains_ref, shifts_ref, *refs) = refs
    sources, refs = refs[:6], refs[6:]
    (do_ref, down_ref, up_ref, got_down, got_up, early_ref, out_far, rest_far, shared_far, *refs) = refs
    (out_ref, rest_ref, shared_ref, leave_sems, out_all, up_all, down_all, work_ref, mlp_ref, gmp_ref, middle_ref, proj_ref, acc_ref, gap_ref, gh_ref, *refs) = refs
    (out_sems, up_sems, down_sems, part_sems, cross_sems, mlp_sems, gmp_sems, head_sems, sum_sems) = refs

    mine = lax.axis_index("tensor")
    width = x_ref.shape[1]
    strips, rows = 4, 64
    strip = block // strips
    columns = width // 2

    def loads(own, rest, array, sems):
        return [
            pltpu.make_async_copy(own if d == 0 else rest.at[d - 1], array.at[d], sems.at[d]) for d in range(ranks)
        ]

    out_loads = loads(sources[0], sources[1], out_all, out_sems)
    up_loads = loads(sources[2], sources[3], up_all, up_sems)
    down_loads = loads(sources[4], sources[5], down_all, down_sems)[:2]
    rank = lax.axis_index("dp")
    near = pl.ds(pl.multiple_of(lax.rem(rank, 2) * columns, columns), columns)
    left, inner = pl.ds(0, columns), pl.ds(columns, columns)
    far_down = sources[5]
    part_loads = [
        pltpu.make_async_copy(far_down.at[1, near, left], down_all.at[2, near, left], part_sems.at[0]),
        pltpu.make_async_copy(far_down.at[1, :, inner], down_all.at[2, :, inner], part_sems.at[1]),
        pltpu.make_async_copy(far_down.at[2, :, inner], down_all.at[3, :, inner], part_sems.at[2]),
    ]
    part_copies = [
        push(far_down.at[1, near, left], down_all.at[2, near, left], cross_sems, 0, "dp", 1),
        push(down_all.at[2, :, left], down_all.at[3, :, left], cross_sems, 1, "tensor", 1),
    ]
    for copy in out_loads:
        copy.start()
    for d in range(ranks):
        up_loads[d].start()
        if d < 2:
            down_loads[d].start()
    for load in part_loads:
        load.start()
    greet(("tensor", "dp"))
    part_copies[0].start()

    def senders(array, sems):
        found = []
        for q in range(strips):
            at = pl.ds(q * strip, strip)
            found.append(
                (
                    push(array.at[0, at], array.at[2, at], sems, q, "tensor", 2),
                    push(array.at[0, at], array.at[1, at], sems, strips + q, "tensor", 1),
                    push(array.at[2, at], array.at[3, at], sems, 2 * strips + q, "tensor", 1),
                )
            )
        return found

    mlp_copies = senders(mlp_ref, mlp_sems)
    gmp_copies = senders(gmp_ref, gmp_sems)

    def send_strip(copies, q):
        copies[q][0].start()
        copies[q][1].start()

    def forward_on(copies):
        for across, _, onward in copies:
            across.wait_recv()
            onward.start()

    for d in range(ranks):
        out_loads[d].wait()
    for c in (0, columns):
        at = pl.ds(c, columns)
        total = None
        for d in range(ranks):
            part = jnp.concatenate([heads_ref[d * pairs + p] for p in range(pairs)], axis=1)
            term = dot(part, out_all[d, :, at])
            total = term if total is None else total + term
        proj_ref[:, at] = total

    gain = [gains_ref[j : j + 1, :] for j in range(4)]
    shift = [shifts_ref[j : j + 1, :] for j in range(4)]

    for q in range(strips):

        @pl.loop(0, strip // rows)
        def _(r):
            at = pl.ds(pl.multiple_of(q * strip + r * rows, rows), rows)
            unit, _ = unit_scale(proj_ref[at, :])
            middle = x_ref[at, :].astype(F32) + (unit * gain[1] + shift[1])
            middle_ref[at, :] = middle
            unit, _ = unit_scale(middle)
            mlp_ref[0, at, :] = (unit * gain[2] + shift[2]).astype(BF)

        send_strip(mlp_copies, q)

    acc_ref[...] = jnp.zeros_like(acc_ref)

    @pl.loop(0, ranks)
    def _(d):
        pltpu.make_async_copy(up_all.at[d], up_all.at[d], up_sems.at[d]).wait()

        @pl.when(d < 2)
        def _():
            pltpu.make_async_copy(down_all.at[d], down_all.at[d], down_sems.at[d]).wait()

        @pl.when(d == 2)
        def _():
            for load in part_loads[:2]:
                load.wait()
            part_copies[0].wait_recv()
            part_copies[1].start()

        @pl.when(d == 3)
        def _():
            part_loads[2].wait()
            part_copies[1].wait_recv()

        for c in (0, columns):
            at = pl.ds(c, columns)
            hidden, slope = gelu_both(dot(mlp_ref[0], up_all[d, :, at]))
            work_ref[d, :, at] = slope
            acc_ref[...] += dot(hidden.astype(BF), down_all[d, at, :])

    zero = jnp.zeros((1, width), F32)
    gain_three, shift_three = zero, zero
    for q in range(strips):

        def last_norm(r, carry):
            gain_term, shift_term = carry
            at = pl.ds(pl.multiple_of(q * strip + r * rows, rows), rows)
            unit, scale = unit_scale(acc_ref[at, :])
            out_ref[at, :] = (middle_ref[at, :] + (unit * gain[3] + shift[3])).astype(BF)
            dy = dy_ref[at, :].astype(F32)
            gmp_ref[0, at, :] = norm_pull(dy, unit, scale, gain[3]).astype(BF)
            return (
                gain_term + jnp.sum(dy * unit, axis=0, keepdims=True),
                shift_term + jnp.sum(dy, axis=0, keepdims=True),
            )

        gain_three, shift_three = lax.fori_loop(0, strip // rows, last_norm, (gain_three, shift_three))
        send_strip(gmp_copies, q)

    acc_ref[...] = jnp.zeros_like(acc_ref)

    @pl.loop(0, ranks)
    def _(d):
        for c in (0, columns):
            at = pl.ds(c, columns)
            grad = dot(gmp_ref[0], down_all[d, at, :], NT)
            grad = (grad * work_ref[d, :, at]).astype(BF)
            acc_ref[...] += dot(grad, up_all[d, :, at], NT)

    forward_on(mlp_copies)

    def inner_norms(r, carry):
        gain_two, shift_two, gain_one, shift_one = carry
        at = pl.ds(pl.multiple_of(r * rows, rows), rows)
        grad = acc_ref[at, :]
        unit, scale = unit_scale(middle_ref[at, :])
        gain_two = gain_two + jnp.sum(grad * unit, axis=0, keepdims=True)
        shift_two = shift_two + jnp.sum(grad, axis=0, keepdims=True)
        grad = dy_ref[at, :].astype(F32) + norm_pull(grad, unit, scale, gain[2])
        rest_ref[at, :] = grad
        unit, scale = unit_scale(proj_ref[at, :])
        gain_one = gain_one + jnp.sum(grad * unit, axis=0, keepdims=True)
        shift_one = shift_one + jnp.sum(grad, axis=0, keepdims=True)
        gap_ref[at, :] = norm_pull(grad, unit, scale, gain[1]).astype(BF)
        return gain_two, shift_two, gain_one, shift_one

    gain_two, shift_two, gain_one, shift_one = lax.fori_loop(0, block // rows, inner_norms, (zero, zero, zero, zero))
    early_ref[...] = jnp.concatenate(
        [zero, gain_one, gain_two, gain_three, zero, shift_one, shift_two, shift_three], axis=0
    )

    head_copies = []
    for d in [*range(1, ranks), 0]:
        grad = dot(gap_ref[...], out_all[d], NT).astype(BF)
        for pair in range(pairs):
            piece = grad[:, pair * PAIR : (pair + 1) * PAIR]
            if d == 0:
                do_ref[pair, 0] = piece
            else:
                slot = d * pairs + pair
                gh_ref[slot] = piece
                head_copies.append(push(gh_ref.at[slot], do_ref.at[pair, d], head_sems, slot, "tensor", d))
    for d in range(ranks):
        part = jnp.concatenate([heads_ref[d * pairs + p] for p in range(pairs)], axis=1)
        shared_ref[d] = dot(part, gap_ref[...], TN).astype(BF)

    leaving = [
        pltpu.make_async_copy(near_ref, far_ref, leave_sems.at[i])
        for i, (near_ref, far_ref) in enumerate([(out_ref, out_far), (rest_ref, rest_far), (shared_ref, shared_far)])
    ]
    for copy in leaving:
        copy.start()

    for copies in (mlp_copies, gmp_copies):
        for _, beside, _ in copies:
            beside.wait_recv()
    work_ref[...] = jnp.zeros_like(work_ref)

    def late():
        forward_on(gmp_copies)
        for copy in head_copies:
            copy.start()

    def latest():
        for copies in (mlp_copies, gmp_copies):
            for _, _, onward in copies:
                onward.wait_recv()

    sums = [
        push(ref.at[0, 1 - lax.rem(lax.div(rank, 1 << o), 2)], got, sum_sems, o, "dp", 1 << o)
        for o, (ref, got) in enumerate([(down_ref, got_down), (up_ref, got_up)])
    ]
    half = columns // 2

    @pl.loop(0, 2 * ranks)
    def _(step):
        part = lax.div(step + 1, 3)
        i = step + 1 - 3 * part
        first, last, up = lax.div(2 - part, 2), lax.div(part, 2), lax.div(i + 1, 2)
        centre = 1 - first - last
        h = centre * (1 - up) + last
        b = first * (i - 1) + centre * (i + up) + last * (i + 1)
        pl.when(step == 3)(late)
        pl.when(step == 4)(latest)
        at = pl.ds(pl.multiple_of(h * columns, columns), columns)
        tokens, grads = mlp_ref[b], gmp_ref[b]
        hidden, slope = gelu_both(dot(tokens, up_all[0, :, at]))
        grad = (dot(grads, down_all[0, at, :], NT) * slope).astype(BF)
        work_ref[2 * h] += dot(hidden.astype(BF), grads, TN)
        work_ref[2 * h + 1, :, 0:columns] += dot(tokens[:, 0:columns], grad, TN)
        work_ref[2 * h + 1, :, columns:] += dot(tokens[:, columns:], grad, TN)

        @pl.when(b == ranks - 1)
        def _():
            for side in range(2):
                down_ref[h, side] = work_ref[2 * h, side * half : (side + 1) * half, :].astype(BF)
                up_ref[h, side] = work_ref[2 * h + 1, :, side * columns : (side + 1) * columns].astype(BF)

        @pl.when(step == 4)
        def _():
            for copy in sums:
                copy.start()

    for copy in sums:
        copy.wait()
    for copy in head_copies:
        copy.wait_recv()
        copy.wait_send()
    for copy in part_copies:
        copy.wait_send()
    for copy in leaving:
        copy.wait()
    for copies in (mlp_copies, gmp_copies):
        for group in copies:
            for copy in group:
                copy.wait_send()


def middle_stage(heads, tokens, cotangent, gains, shifts, weights, rests):
    block, width = tokens.shape
    ranks = lax.axis_size("tensor")
    local = weights[0].shape[0]
    pairs = local // PAIR
    hidden = weights[2].shape[0]
    vmem = pl.BlockSpec(memory_space=pltpu.VMEM)
    hbm = pl.BlockSpec(memory_space=pl.ANY)
    copies = pltpu.SemaphoreType.DMA
    assert block * 2 == width and hidden == width
    early = [
        jax.ShapeDtypeStruct((block, width), BF),
        jax.ShapeDtypeStruct((block, width), F32),
        jax.ShapeDtypeStruct((ranks, local, width), BF),
    ]
    operands = [array for pair in zip(weights, rests) for array in pair]
    done = pl.pallas_call(
        functools.partial(middle_kernel, block, ranks, pairs),
        out_shape=[
            jax.ShapeDtypeStruct((pairs, ranks, block, PAIR), BF),
            jax.ShapeDtypeStruct((2, 2, block // 2, width), BF),
            jax.ShapeDtypeStruct((2, 2, block, width // 2), BF),
            jax.ShapeDtypeStruct((block // 2, width), BF),
            jax.ShapeDtypeStruct((block, width // 2), BF),
            jax.ShapeDtypeStruct((8, width), F32),
            *early,
        ],
        in_specs=[vmem] * 5 + [hbm] * 6,
        out_specs=[vmem] * 6 + [hbm] * 3,
        scratch_shapes=[
            *[pltpu.VMEM(array.shape, array.dtype) for array in early],
            copies((3,)),
            pltpu.VMEM((ranks, local, width), BF),
            pltpu.VMEM((ranks, width, hidden), BF),
            pltpu.VMEM((ranks, hidden, width), BF),
            pltpu.VMEM((ranks, block, width), F32),
            pltpu.VMEM((ranks, block, width), BF),
            pltpu.VMEM((ranks, block, width), BF),
            pltpu.VMEM((block, width), F32),
            pltpu.VMEM((block, width), F32),
            pltpu.VMEM((block, width), F32),
            pltpu.VMEM((block, width), BF),
            pltpu.VMEM((ranks * pairs, block, PAIR), BF),
            copies((ranks,)),
            copies((ranks,)),
            copies((2,)),
            copies((3,)),
            copies((2, 2)),
            copies((2, 12)),
            copies((2, 12)),
            copies((2, ranks * pairs)),
            copies((2, 2)),
        ],
        compiler_params=pltpu.CompilerParams(vmem_limit_bytes=62 << 20, collective_id=3, has_side_effects=True),
        name="middle_stage",
    )(heads, tokens, cotangent, gains, shifts, *operands)
    grad_heads, down, up, first_down, first_up, sums, block_out, rest, shared = done
    return block_out, rest, grad_heads, shared, down, up, first_down, first_up, sums


def finish_kernel(block, blocks, pairs, orders, *refs):
    (lengths_ref, down_ref, up_ref, first_down, first_up, shared_ref, log_ref, gain_ref, early_ref, *refs) = refs
    far_refs, refs = refs[:9], refs[9:]
    (input_ref, sums_ref, down_out, up_out, own_out, qkv_out, *refs) = refs
    near_refs, refs = refs[:9], refs[9:]
    (qkv_ref, do_ref, o_ref, cos_ref, sin_ref, attn_ref, w_ref, x_ref, rest_ref) = near_refs
    (start_ref, dq_ref, inner_ref, grads_ref, own_ref, wide_ref, token_ref, core_sum, got_y, *refs) = refs
    (token_sum, token_y, norm_ref, got_t, sum_t, got_d, *refs) = refs
    chunks, steps = len(orders), len(orders[0])
    count = chunks * steps
    got, refs = refs[:count], refs[count:]
    (load_sems, rs_sems, ag_sems, core_sems, y_sems, token_core_sems, token_y_sems, t_sems, d_sems) = refs

    mine = lax.axis_index("tensor")
    rank = lax.axis_index("dp")
    ranks_dp = lax.axis_size("dp")
    heads = PAIR // HD
    started = []
    loads = [
        pltpu.make_async_copy(far, near, load_sems.at[i]) for i, (far, near) in enumerate(zip(far_refs, near_refs))
    ]
    for load in loads:
        load.start()

    def start(copy):
        copy.start()
        started.append(copy)
        return copy

    sources = [down_ref.at[0], up_ref.at[0], down_ref.at[1], up_ref.at[1], own_ref] + [wide_ref.at[p] for p in range(pairs)]
    results = [down_out.at[0], up_out.at[0], down_out.at[1], up_out.at[1], own_out] + [qkv_out.at[p] for p in range(pairs)]
    firsts = {0: first_down, 1: first_up}
    bits = [[lax.rem(lax.div(rank, 1 << o), 2) for o in order] for order in orders]
    rs_copies, ag_copies = {}, {}

    def held(c, k):
        return sources[c] if k == 0 else got[c * steps + k - 1]

    for c in range(chunks):
        for k in range(steps):
            far = 1 << orders[c][k]
            if k > 0 or c not in firsts:
                source = held(c, k).at[1 - bits[c][k]]
                rs_copies[c, k] = push(source, got[c * steps + k], rs_sems, c * steps + k, "dp", far)
            region = results[c].at[tuple(bits[c][: k + 1])]
            ag_copies[c, k] = push(region, region, ag_sems, c * steps + k, "dp", far)

    def begin(c):
        rs_copies[c, 0].start()

    def halve(c, k):
        at = c * steps + k
        if (c, k) in rs_copies:
            rs_copies[c, k].wait_recv()
            term = got[at]
        else:
            term = firsts[c]
        mine_half = held(c, k).at[bits[c][k]]
        strip = min(16, got[at].shape[-2])
        lead = (slice(None),) * (len(got[at].shape) - 2)

        @pl.loop(0, got[at].shape[-2] // strip)
        def _(r):
            where = (*lead, pl.ds(pl.multiple_of(r * strip, strip), strip), slice(None))
            total = (mine_half[where].astype(F32) + term[where].astype(F32)).astype(BF)
            got[at][where] = total
            if k + 1 == steps:
                results[c].at[tuple(bits[c])][where] = total

        (rs_copies[c, k + 1] if k + 1 < steps else ag_copies[c, k]).start()

    def double(c, k):
        ag_copies[c, k].wait_recv()
        if k > 0:
            ag_copies[c, k - 1].start()

    core_copies = [
        push(shared_ref.at[d + 1], core_sum.at[d // 2], core_sems, d // 2, "tensor", 1) for d in range(0, blocks, 2)
    ]
    y_copies = [
        push(core_sum.at[h], got_y.at[h - 1], y_sems, h - 1, "tensor", 2 * h) for h in range(1, blocks // 2)
    ]

    def pair_up():
        for h in range(blocks // 2):
            core_copies[h].wait_recv()
            core_sum[h] = (shared_ref[2 * h].astype(F32) + core_sum[h].astype(F32)).astype(BF)
        for copy in y_copies:
            copy.start()

    def settle():
        total = core_sum[0].astype(F32)
        for h in range(1, blocks // 2):
            y_copies[h - 1].wait_recv()
            total = total + got_y[h - 1].astype(F32)
        own_ref[...] = total.astype(BF)

    def prepare(pair):
        dq_ref[...] = jnp.zeros_like(dq_ref)
        for b in range(blocks):
            rows = pl.ds(b * block, block)
            product = do_ref[pair, b].astype(F32) * o_ref[pair, rows, :].astype(F32)
            high = product.astype(BF)
            low = (product - high.astype(F32)).astype(BF)
            for head in range(heads):
                ones = head_mask((16, PAIR), head).astype(F32).astype(BF)
                inner = dot(ones, high, NT) + dot(ones, low, NT)
                inner_ref[head : head + 1, rows] = inner[0:1, :]

    def unit(pair, key_block):
        slot = xor(key_block, mine, blocks)
        here = pl.ds(pl.multiple_of(slot * block, block), block)
        keys = qkv_ref[pairs + pair, here, :]
        values = qkv_ref[2 * pairs + pair, here, :]
        dk = jnp.zeros((block, PAIR), F32)
        dv = jnp.zeros((block, PAIR), F32)
        for head in range(heads):
            mask = head_mask(keys.shape, head)
            key = jnp.where(mask, keys * HD**-0.5, jnp.zeros_like(keys))
            value = jnp.where(mask, values, jnp.zeros_like(values))

            def one(i, carry, first):
                dk, dv = carry
                place = xor(i, mine, blocks)
                rows = pl.ds(pl.multiple_of(place * block, block), block)
                real = pl.ds(pl.multiple_of(i * block, block), block)
                query = qkv_ref[pair, rows, :]
                grad = do_ref[pair, place]
                s = dot(key, query, NT)
                row = lax.broadcasted_iota(jnp.int32, s.shape, 0)
                visible = row >= start_ref[0:1, real] - key_block * block
                if first:
                    visible &= row <= lax.broadcasted_iota(jnp.int32, s.shape, 1)
                probs = jnp.where(visible, jnp.exp(s - log_ref[pair, head : head + 1, rows]), 0.0)
                grad_probs = dot(value, grad, NT)
                ds = (probs * (grad_probs - inner_ref[head : head + 1, rows])).astype(BF)
                zero = jnp.zeros_like(query)
                dv = dv + dot(probs.astype(BF), jnp.where(mask, grad, zero))
                dk = dk + dot(ds, jnp.where(mask, query, zero))
                dq_ref[rows, :] += dot(ds, key, TN)
                return dk, dv

            dk, dv = one(key_block, (dk, dv), True)
            dk, dv = lax.fori_loop(key_block + 1, blocks, lambda i, carry: one(i, carry, False), (dk, dv))
        real = pl.ds(pl.multiple_of(key_block * block, block), block)
        grads_ref[pairs + pair, here, :] = turn(dk * HD**-0.5, cos_ref[real, :], -sin_ref[real, :]).astype(BF)
        grads_ref[2 * pairs + pair, here, :] = dv.astype(BF)

    def close(pair):
        for b in range(blocks):
            rows = pl.ds(b * block, block)
            real = pl.ds(pl.multiple_of(flip(mine, b) * block, block), block)
            grads_ref[pair, rows, :] = turn(dq_ref[rows, :], cos_ref[real, :], -sin_ref[real, :]).astype(BF)
        total = None
        for b in range(blocks):
            rows = pl.ds(b * block, block)
            wide = jnp.concatenate([grads_ref[c * pairs + pair, rows, :] for c in range(3)], axis=1)
            term = dot(attn_ref[b], wide, TN)
            total = term if total is None else total + term
        wide_ref[pair] = total.astype(BF).reshape(wide_ref.shape[1:])

    greet(("tensor", "dp"))
    for copy in core_copies:
        copy.start()
    begin(3)
    begin(2)
    halve(0, 0)
    halve(1, 0)
    start_ref[...] = document_start(lengths_ref, lax.broadcasted_iota(jnp.int32, start_ref.shape, 1))
    for load in loads[:5]:
        load.wait()
    slots = pairs * blocks
    halving = lambda *steps: [functools.partial(halve, c, k) for c, k in steps]
    doubling = lambda *steps: [functools.partial(double, c, k) for c, k in steps]
    beginning = lambda c: [functools.partial(begin, c)]
    events = {
        0: [pair_up],
        2: [settle] + beginning(4) + halving((0, 1), (3, 0), (1, 1), (2, 0)),
        3: [lambda: [load.wait() for load in loads[5:]]],
        4: beginning(5) + halving((0, 2), (4, 0), (3, 1), (1, 2)),
        5: halving((2, 1)),
        6: halving((4, 1)) + doubling((0, 2)),
        7: halving((3, 2)) + doubling((1, 2)),
    }

    @pl.loop(0, slots)
    def _(u):
        pair, key_block = lax.div(u, blocks), lax.rem(u, blocks)
        for when, todo in events.items():

            @pl.when(u == when)
            def _():
                for step in todo:
                    step()

        for p in range(pairs):
            pl.when(u == p * blocks)(functools.partial(prepare, p))
        unit(pair, key_block)
        for p in range(pairs):
            pl.when(u == p * blocks + blocks - 1)(functools.partial(close, p))

    begin(6)
    halve(4, 2)
    halve(2, 2)

    def token_term(d):
        rows = pl.ds(d * block, block)
        total = None
        for c in range(3):
            wide = jnp.concatenate([grads_ref[c * pairs + p, rows, :] for p in range(pairs)], axis=1)
            term = dot(wide, w_ref[c], NT)
            total = term if total is None else total + term
        token_ref[d] = total.astype(BF)

    token_copies = []
    for d in range(0, blocks, 2):
        token_term(d + 1)
        token_copies.append(start(push(token_ref.at[d + 1], token_sum.at[d // 2], token_core_sems, d // 2, "tensor", 1)))
    double(1, 1)
    for d in range(blocks - 2, -1, -2):
        token_term(d)
        token_copies[d // 2].wait_recv()
        token_sum[d // 2] = (token_ref[d].astype(F32) + token_sum[d // 2].astype(F32)).astype(BF)
        if d > 0:
            across = start(push(token_sum.at[d // 2], token_y.at[d // 2 - 1], token_y_sems, d // 2 - 1, "tensor", d))
    double(3, 2)
    halve(5, 0)
    double(4, 2)
    halve(6, 0)
    double(0, 1)
    double(2, 2)
    double(3, 1)
    halve(5, 1)
    double(4, 1)

    across.wait_recv()
    rows = 64
    lanes = x_ref.shape[1] // 128
    gain = gain_ref[0:1, :]

    def norm(r, carry):
        gain_term, shift_term = carry
        at = pl.ds(pl.multiple_of(r * rows, rows), rows)
        grad = token_sum[0, at, :].astype(F32)
        for h in range(blocks // 2 - 1):
            grad = grad + token_y[h, at, :].astype(F32)
        unit, scale = unit_scale(x_ref[at, :].astype(F32))
        total = rest_ref[at, :] + norm_pull(grad, unit, scale, gain)
        for c in range(lanes):
            there = pl.ds(pl.multiple_of(r * (rows * lanes), rows * lanes) + c, rows, stride=lanes)
            input_ref[there, :] = total[:, c * 128 : (c + 1) * 128]
        return (
            gain_term + jnp.sum(grad * unit, axis=0, keepdims=True),
            shift_term + jnp.sum(grad, axis=0, keepdims=True),
        )

    zero = jnp.zeros(gain.shape, F32)
    gain_term, shift_term = lax.fori_loop(0, block // rows, norm, (zero, zero))
    norm_ref[...] = early_ref[...]
    norm_ref[0:1, :] = gain_term
    norm_ref[4:5, :] = shift_term
    ts = [start(push(norm_ref, got_t.at[d - 1], t_sems, d - 1, "tensor", d)) for d in range(1, blocks)]
    halve(6, 1)
    halve(5, 2)
    for copy in ts:
        copy.wait_recv()
    sum_t[...] = tree_sum([norm_ref[...]] + [got_t[d] for d in range(blocks - 1)])
    ds = [start(push(sum_t, got_d.at[d - 1], d_sems, d - 1, "dp", d)) for d in range(1, ranks_dp)]
    double(2, 1)
    halve(6, 2)
    double(5, 2)
    double(6, 2)
    double(5, 1)
    double(6, 1)
    for copy in ds:
        copy.wait_recv()
    sums_ref[...] = tree_sum([sum_t[...]] + [got_d[d] for d in range(ranks_dp - 1)])
    for c in range(chunks):
        double(c, 0)
    for copy in [*started, *core_copies, *y_copies, *rs_copies.values(), *ag_copies.values()]:
        copy.wait_send()


def finish_stage(
    lengths, qkv, grad_heads, heads_out, logs, cosine, sine, attn, weight, tokens, rest, shared, terms, firsts, gains, early
):
    pairs3, length, _ = qkv.shape
    pairs = pairs3 // 3
    block, width = tokens.shape
    blocks = length // block
    ranks_dp = lax.axis_size("dp")
    steps = ranks_dp.bit_length() - 1
    straight = list(range(steps))
    crossed = [1, 0, *straight[2:]]
    orders = [straight, crossed, straight, crossed, straight, crossed, straight]
    assert pairs == 2 and steps >= 3
    cut = (2,) * steps
    local = shared.shape[1]
    shared = shared.reshape(blocks, *cut, local // ranks_dp, width)
    terms = [term.reshape(2, *cut, -1, term.shape[-1]) for term in terms]
    firsts = [first.reshape(*cut[1:], -1, first.shape[-1]) for first in firsts]
    wide = (*cut, width // ranks_dp, 3 * PAIR)
    shapes = [term.shape[1:] for term in terms] * 2 + [shared.shape[1:]] + [wide] * pairs
    far = (qkv, grad_heads, heads_out, cosine, sine, attn, weight, tokens, rest)
    parts = [shape[k + 1 :] for shape in shapes for k in range(steps)]
    vmem = pl.BlockSpec(memory_space=pltpu.VMEM)
    copies = pltpu.SemaphoreType.DMA
    outs = pl.pallas_call(
        functools.partial(finish_kernel, block, blocks, pairs, orders),
        out_shape=[
            jax.ShapeDtypeStruct((block * width // 128, 128), F32),
            jax.ShapeDtypeStruct((8, width), F32),
            *[jax.ShapeDtypeStruct(term.shape, BF) for term in terms],
            jax.ShapeDtypeStruct(shared.shape[1:], BF),
            jax.ShapeDtypeStruct((pairs, *wide), BF),
        ],
        in_specs=[pl.BlockSpec(memory_space=pltpu.SMEM)] + [vmem] * 8 + [pl.BlockSpec(memory_space=pl.ANY)] * 9,
        out_specs=[vmem] * 6,
        scratch_shapes=[
            *[pltpu.VMEM(array.shape, array.dtype) for array in far],
            pltpu.VMEM((8, length), jnp.int32),
            pltpu.VMEM((length, PAIR), F32),
            pltpu.VMEM((8, length), F32),
            pltpu.VMEM((pairs3, length, PAIR), BF),
            pltpu.VMEM(shared.shape[1:], BF),
            pltpu.VMEM((pairs, *wide), BF),
            pltpu.VMEM((blocks, block, width), BF),
            pltpu.VMEM((blocks // 2, *shared.shape[1:]), BF),
            pltpu.VMEM((blocks // 2 - 1, *shared.shape[1:]), BF),
            pltpu.VMEM((blocks // 2, block, width), BF),
            pltpu.VMEM((blocks // 2 - 1, block, width), BF),
            pltpu.VMEM((8, width), F32),
            pltpu.VMEM((blocks - 1, 8, width), F32),
            pltpu.VMEM((8, width), F32),
            pltpu.VMEM((ranks_dp - 1, 8, width), F32),
            *[pltpu.VMEM(shape, BF) for shape in parts],
            copies((9,)),
            copies((2, len(parts))),
            copies((2, len(parts))),
            copies((2, blocks // 2)),
            copies((2, blocks // 2 - 1)),
            copies((2, blocks // 2)),
            copies((2, blocks // 2 - 1)),
            copies((2, blocks - 1)),
            copies((2, ranks_dp - 1)),
        ],
        compiler_params=pltpu.CompilerParams(vmem_limit_bytes=62 << 20, collective_id=0, has_side_effects=True),
        name="finish_stage",
    )(lengths, *terms, *firsts, shared, logs, gains, early, *far)
    input_grad, sums, down, up, own, wides = outs
    return (
        input_grad,
        sums,
        down.reshape(width, width),
        up.reshape(2, width, -1),
        own.reshape(local, width),
        wides.reshape(pairs, width, 3 * PAIR),
    )


def widen_kernel(pairs, down_ref, up_ref, own_ref, wide_ref, out_ref, input_ref, sums_ref, *refs):
    down_out, up_out, own_out, qkv_out, out_out, input_out, gain_out, bias_out = refs
    gain_out[...] = sums_ref[0:4, :]
    bias_out[...] = sums_ref[4:8, :]
    down_out[...] = down_ref[...].astype(F32)
    half = up_ref.shape[2]
    for side in range(2):
        up_out[:, side * half : (side + 1) * half] = up_ref[side].astype(F32)
    own_out[...] = own_ref[...].astype(F32)
    for c in range(3):
        for pair in range(pairs):
            piece = wide_ref[pair, :, c * PAIR : (c + 1) * PAIR]
            qkv_out[c, :, pair * PAIR : (pair + 1) * PAIR] = piece.astype(F32)
    out_out[...] = out_ref[...]
    input_out[...] = input_ref[...]


def widen(down, up, own, wides, block_out, input_grad, sums):
    pairs, width, _ = wides.shape
    steps = 8
    rows = lambda array: pl.BlockSpec((array.shape[0] // steps, *array.shape[1:]), lambda i: (i, 0))
    deep = lambda array: pl.BlockSpec(
        (array.shape[0], array.shape[1] // steps, array.shape[2]), lambda i: (0, i, 0)
    )
    still = lambda array: pl.BlockSpec(array.shape, lambda i: (0, 0))
    norm = jax.ShapeDtypeStruct((sums.shape[0] // 2, width), F32)
    qkv = jax.ShapeDtypeStruct((3, width, pairs * PAIR), F32)
    ups = jax.ShapeDtypeStruct((up.shape[1], 2 * up.shape[2]), F32)
    return pl.pallas_call(
        functools.partial(widen_kernel, pairs),
        grid=(steps,),
        out_shape=[
            jax.ShapeDtypeStruct(down.shape, F32),
            ups,
            jax.ShapeDtypeStruct(own.shape, F32),
            qkv,
            jax.ShapeDtypeStruct(block_out.shape, block_out.dtype),
            jax.ShapeDtypeStruct(input_grad.shape, F32),
            norm,
            norm,
        ],
        in_specs=[rows(down), deep(up), rows(own), deep(wides), rows(block_out), rows(input_grad), still(sums)],
        out_specs=[rows(down), rows(ups), rows(own), deep(qkv), rows(block_out), rows(input_grad), still(norm), still(norm)],
        compiler_params=pltpu.CompilerParams(vmem_limit_bytes=62 << 20),
        name="widen",
    )(down, up, own, wides, block_out, input_grad, sums)


def body(block_in, lengths, qkv_weight, out_weight, up_weight, down_weight, norm_gain, norm_bias, cotangent):
    block, row_count, width = block_in.shape
    assert row_count == 1
    pairs = out_weight.shape[0] // PAIR
    qkv_swapped = jnp.transpose(qkv_weight, (1, 0, 2))

    qkv, attn_full, heads_mixed, logs, heads_parts, cosine, sine, rests = attend_forward(
        lengths,
        block_in.reshape(block, width),
        norm_gain,
        norm_bias,
        qkv_swapped,
        (out_weight, up_weight, down_weight),
    )
    block_out, grad_middle, grad_heads, shared, down_terms, up_terms, down_first, up_first, early = middle_stage(
        heads_parts,
        block_in.reshape(block, width),
        cotangent.reshape(block, width),
        norm_gain,
        norm_bias,
        (out_weight, up_weight, down_weight),
        rests,
    )
    input_grad, sums, down_sum, up_sums, out_sum, qkv_sums = finish_stage(
        lengths,
        qkv,
        grad_heads,
        heads_mixed,
        logs,
        cosine,
        sine,
        attn_full,
        qkv_swapped,
        block_in.reshape(block, width),
        grad_middle,
        shared,
        (down_terms, up_terms),
        (down_first, up_first),
        norm_gain,
        early,
    )
    down_grad, up_grad, out_grad, qkv_grad, block_out, input_grad, gain_grad, bias_grad = widen(
        down_sum, up_sums, out_sum, qkv_sums, block_out, input_grad, sums
    )
    qkv_grad = jnp.transpose(qkv_grad, (1, 0, 2))
    return (
        block_out.reshape(block_in.shape),
        input_grad.reshape(block_in.shape),
        qkv_grad,
        out_grad,
        up_grad,
        down_grad,
        gain_grad,
        bias_grad,
    )


def solution(mesh):
    tokens, rows, columns, copied = P("tensor", "dp", None), P("tensor", None), P(None, "tensor"), P()
    heads = P(None, None, "tensor")
    return jax.shard_map(
        body,
        mesh=mesh,
        in_specs=(tokens, P("dp", None), heads, rows, columns, rows, copied, copied, tokens),
        out_specs=(tokens, tokens, heads, rows, columns, rows, copied, copied),
        check_vma=False,
    )
```

```python
import functools

import jax
import jax.numpy as jnp
import numpy as np
from jax import lax
from jax.experimental import pallas as pl
from jax.experimental.pallas import tpu as pltpu
from jax.sharding import PartitionSpec as P

HD = 64
PAIR = 128
EPSILON = 1e-05
ROPE_BASE = 10000.0
NEG = -1e30
MESH = pl.DeviceIdType.MESH
BF = jnp.bfloat16
F32 = jnp.float32
NT = (((1,), (1,)), ((), ()))
NN = (((1,), (0,)), ((), ()))
TN = (((0,), (0,)), ((), ()))


def dot(a, b, dims=NN):
    return lax.dot_general(a, b, dims, preferred_element_type=F32)


def layer_norm(values, gain, shift):
    centre = values - jnp.mean(values, axis=-1, keepdims=True)
    spread = jnp.mean(centre * centre, axis=-1, keepdims=True)
    return centre * lax.rsqrt(spread + EPSILON) * gain + shift


def flip(index, offset):
    bit = 1
    while bit <= offset:
        if offset & bit:
            index = index + bit - 2 * bit * lax.rem(lax.div(index, bit), 2)
        bit *= 2
    return index


def xor(a, b, size):
    total, bit = 0, 1
    while bit < size:
        total = total + bit * lax.rem(lax.div(a, bit) + lax.div(b, bit), 2)
        bit *= 2
    return total


def greet(axes):
    barrier = pltpu.get_barrier_semaphore()
    count = 0
    for axis in axes:
        index = lax.axis_index(axis)
        for d in range(1, lax.axis_size(axis)):
            pl.semaphore_signal(barrier, inc=1, device_id={axis: flip(index, d)}, device_id_type=MESH)
            count += 1
    pl.semaphore_wait(barrier, count)


def tree_sum(parts):
    parts = [part.astype(F32) for part in parts]
    while len(parts) > 1:
        parts = [parts[i] + parts[i + 1] for i in range(0, len(parts), 2)]
    return parts[0]


def push(src, dst, sems, slot, axis, offset):
    return pltpu.make_async_remote_copy(
        src_ref=src,
        dst_ref=dst,
        send_sem=sems.at[0, slot],
        recv_sem=sems.at[1, slot],
        device_id={axis: flip(lax.axis_index(axis), offset)},
        device_id_type=MESH,
    )


def turn(values, cosine, signed_sine):
    lane = lax.broadcasted_iota(jnp.int32, values.shape, 1)
    other = jnp.where(lane % HD < HD // 2, pltpu.roll(values, PAIR - HD // 2, 1), pltpu.roll(values, HD // 2, 1))
    return values * cosine + other * signed_sine


def head_mask(shape, head):
    lane = lax.broadcasted_iota(jnp.int32, shape, 1)
    return lane // HD == head


def document_start(lengths_ref, spot):
    begin = jnp.zeros_like(spot)
    total = jnp.int32(0)
    for j in range(lengths_ref.shape[1] - 1):
        total = total + lengths_ref[0, j]
        begin = jnp.where(spot >= total, total, begin)
    return begin


def forward_kernel(block, ranks, pairs, chunks, *refs):
    lengths_ref, x_ref, gain_ref, shift_ref, w_ref, freq_ref, *refs = refs
    weights, refs = refs[:3], refs[3:]
    mixed_ref, log_ref, heads_ref, qkv_out, attn_out, cos_out, sin_out, *refs = refs
    rests, refs = refs[:3], refs[3:]
    scores_ref, qkv_ref, attn_ref, cos_ref, sin_ref, query_marks, key_marks, out_sems, attn_sems, head_sems, own_sems, y_sems, z_sems, x_sems, core_sems = refs

    mine = lax.axis_index("tensor")
    rank = lax.axis_index("dp")
    group = lax.axis_size("dp") // 2
    x_bit, z_place = lax.rem(rank, 2), lax.div(rank, 2)
    direct = len(chunks) - 1
    started = []

    def start(copy):
        copy.start()
        started.append(copy)
        return copy

    outward = [
        pltpu.make_async_copy(src, dst, out_sems.at[i])
        for i, (src, dst) in enumerate(
            [(attn_ref, attn_out), (qkv_ref, qkv_out), (cos_ref, cos_out), (sin_ref, sin_out)]
        )
    ]

    def cut(array, c, *lead):
        at, (_, low, size) = array.at, chunks[c]
        return at[(*lead, slice(None), pl.ds(low, size))]

    def every(array, c, *lead):
        at, (_, low, size) = array.at, chunks[c]
        return at[(*lead, slice(None), slice(None), pl.ds(low, size))]

    def rest(c):
        return rests[chunks[c][0]]

    y_copies = [
        push(
            cut(weights[chunks[c][0]], c, x_bit, z_place), cut(rest(c), c, 1, x_bit, z_place), y_sems, c, "tensor", 2
        )
        for c in range(direct)
    ]
    whole = lambda array, c, *lead: array.at[(*lead, slice(None), slice(None), slice(None), pl.ds(*chunks[c][1:]))]
    y_copies.append(
        push(whole(weights[chunks[direct][0]], direct), whole(rest(direct), direct, 1), y_sems, direct, "tensor", 2)
    )
    z_copies = [
        [
            push(
                cut(rest(c), c, 1, x_bit, z_place),
                cut(rest(c), c, 1, x_bit, z_place),
                z_sems,
                c * (group - 1) + d - 1,
                "dp",
                2 * d,
            )
            for d in range(1, group)
        ]
        for c in range(direct)
    ]
    x_copies = [
        push(every(rest(c), c, 1, x_bit), every(rest(c), c, 1, x_bit), x_sems, c, "dp", 1) for c in range(direct - 1)
    ]
    core_copies = {
        c: push(whole(rest(c), c, 1), whole(rest(c), c, 2), core_sems, c, "tensor", 1)
        for c in [*range(direct - 1), direct]
    }
    own_copies = [push(weights[a], rests[a].at[0], own_sems, a, "tensor", 1) for a in range(3)]

    def to_z(c):
        y_copies[c].wait_recv()
        for copy in z_copies[c]:
            copy.start()

    def to_x(c):
        for copy in z_copies[c]:
            copy.wait_recv()
        x_copies[c].start()

    def to_core(c):
        (y_copies if c == direct else x_copies)[c].wait_recv()
        core_copies[c].start()

    greet(("tensor", "dp"))
    for c in range(direct - 1):
        y_copies[c].start()

    strips = 4
    strip = block // strips
    gain, shift = gain_ref[0:1, :], shift_ref[0:1, :]
    across, beside, onward = [], [], []
    for q in range(strips):

        @pl.loop(0, strip // 64)
        def _(r):
            at = pl.ds(pl.multiple_of(q * strip + r * 64, 64), 64)
            attn_ref[0, at, :] = layer_norm(x_ref[at, :].astype(F32), gain, shift).astype(BF)

        at = pl.ds(q * strip, strip)
        across.append(start(push(attn_ref.at[0, at], attn_ref.at[2, at], attn_sems, q, "tensor", 2)))
        beside.append(start(push(attn_ref.at[0, at], attn_ref.at[1, at], attn_sems, strips + q, "tensor", 1)))
        onward.append(push(attn_ref.at[2, at], attn_ref.at[3, at], attn_sems, 2 * strips + q, "tensor", 1))

    y_copies[direct - 1].start()
    to_z(0)

    lane = lax.broadcasted_iota(jnp.int32, (64, PAIR), 1)
    sign = jnp.where(lane % HD < HD // 2, -1.0, 1.0)
    first, past = jnp.zeros_like(lane), jnp.zeros_like(lane)
    total = jnp.int32(0)
    for j in range(lengths_ref.shape[1]):
        first = jnp.where(lane % HD == j, total, first)
        total = total + lengths_ref[0, j]
        past = jnp.where(lane % HD == j, total, past)

    @pl.loop(0, ranks * block // 64)
    def _(r):
        at = pl.ds(pl.multiple_of(r * 64, 64), 64)
        spot = r * 64 + lax.broadcasted_iota(jnp.int32, (64, PAIR), 0)
        begin = document_start(lengths_ref, spot)
        inside = (spot >= first) & (spot < past)
        query_marks[at, :] = jnp.where(inside, 1.0, 0.0).astype(BF)
        key_marks[at, :] = jnp.where(inside, 0.0, NEG).astype(BF)
        angle = (spot - begin).astype(F32) * freq_ref[...]
        cos_ref[at, :] = jnp.cos(angle)
        sin_ref[at, :] = jnp.sin(angle) * sign

    def middle():
        to_x(0)
        to_z(1)
        for q in range(strips - 1):
            across[q].wait_recv()
            onward[q].start()
        to_x(1)
        to_z(2)
        across[strips - 1].wait_recv()
        onward[strips - 1].start()
        y_copies[direct].start()
        for copy in own_copies:
            copy.start()

    def beside_here():
        for copy in beside:
            copy.wait_recv()

    def onward_here():
        for copy in onward:
            copy.wait_recv()

    @pl.loop(0, ranks)
    def _(d):
        pl.when(d == 1)(beside_here)
        pl.when(d == 2)(middle)
        pl.when(d == 3)(onward_here)
        x = attn_ref[d]
        rows = pl.ds(pl.multiple_of(d * block, block), block)
        real = pl.ds(pl.multiple_of(xor(d, mine, ranks) * block, block), block)
        for part in range(3):
            project = dot(x, w_ref[part])
            for pair in range(pairs):
                piece = project[:, pair * PAIR : (pair + 1) * PAIR]
                if part < 2:
                    piece = turn(piece, cos_ref[real, :], sin_ref[real, :])
                qkv_ref[part * pairs + pair, rows, :] = piece.astype(BF)

    sub = block // 2

    def unit(pair, d):
        row_block = xor(d, mine, ranks)
        rows = pl.ds(pl.multiple_of(d * block, block), block)
        queries = qkv_ref[pair, rows, :] * HD**-0.5
        marks = query_marks[pl.ds(pl.multiple_of(row_block * block, block), block), :]
        heads = range(PAIR // HD)
        masks = [head_mask(queries.shape, head) for head in heads]
        parts = [jnp.where(mask, queries, marks) for mask in masks]
        column = lax.broadcasted_iota(jnp.int32, (block, 128), 1)

        def score(j, tops, last):
            at = pl.ds(pl.multiple_of(xor(j, mine, ranks) * block, block), block)
            keys = qkv_ref[pairs + pair, at, :]
            marks = key_marks[pl.ds(pl.multiple_of(j * block, block), block), :]
            keys = [jnp.where(mask, keys, marks) for mask in masks]
            tops = list(tops)
            for low in range(0, block, sub):
                for head in heads:
                    s = dot(parts[head], keys[head][low : low + sub], NT)
                    for c in range(0, sub, 128):
                        piece = s[:, c : c + 128]
                        if last:
                            visible = column + (low + c) <= lax.broadcasted_iota(jnp.int32, (block, 128), 0)
                            piece = jnp.where(visible, piece, NEG)
                        scores_ref[head, j, :, low + c : low + c + 128] = piece
                        tops[head] = jnp.maximum(tops[head], piece)
            return tuple(tops)

        tops = tuple(jnp.full((block, 128), NEG, F32) for _ in heads)
        tops = lax.fori_loop(0, row_block, lambda j, tops: score(j, tops, False), tops)
        tops = score(row_block, tops, True)
        tops = [jnp.broadcast_to(jnp.max(top, axis=1, keepdims=True), (block, 128)) for top in tops]

        def mix(j, accs):
            at = pl.ds(pl.multiple_of(xor(j, mine, ranks) * block, block), block)
            values = qkv_ref[2 * pairs + pair, at, :]
            accs = list(accs)
            for low in range(0, block, sub):
                for head in heads:
                    filled = jnp.where(masks[head], values, jnp.ones_like(values))[low : low + sub]
                    shares = [
                        jnp.exp(scores_ref[head, j, :, low + c : low + c + 128] - tops[head]).astype(BF)
                        for c in range(0, sub, 128)
                    ]
                    accs[head] = accs[head] + dot(jnp.concatenate(shares, axis=1), filled)
            return tuple(accs)

        accs = lax.fori_loop(0, row_block + 1, mix, tuple(jnp.zeros((block, PAIR), F32) for _ in heads))
        totals = [pltpu.roll(acc, HD, 1) for acc in accs]
        mixed_ref[pair, rows, :] = jnp.where(masks[0], accs[0] / totals[0], accs[1] / totals[1]).astype(BF)
        for head in heads:
            logs = tops[head] + jnp.log(jnp.where(masks[head], totals[head], accs[head]))
            log_ref[pair, head : head + 1, rows] = jnp.transpose(logs)[0:1, :]

    def head_copy(pair, d):
        slot = d * pairs + pair
        return pltpu.make_async_remote_copy(
            src_ref=mixed_ref.at[pair, pl.ds(pl.multiple_of(d * block, block), block)],
            dst_ref=heads_ref.at[slot],
            send_sem=head_sems.at[0, slot],
            recv_sem=head_sems.at[1, slot],
            device_id={"tensor": xor(mine, d, ranks)},
            device_id_type=MESH,
        )

    for copy in outward:
        copy.start()
    units = pairs * ranks
    events = {
        0: [lambda: to_x(2), lambda: to_z(3), lambda: to_z(4), lambda: to_core(0), lambda: to_core(1)],
        3: [lambda: to_x(3)],
        5: [lambda: to_core(2)],
    }

    @pl.loop(0, units)
    def _(u):
        pair, d = lax.rem(u, pairs), ranks - 1 - lax.div(u, pairs)
        unit(pair, d)
        pl.when(d > 0)(lambda: head_copy(pair, d).start())
        for when, steps in events.items():

            @pl.when(u == min(when, units - 1))
            def _():
                for step in steps:
                    step()

    for pair in range(pairs):
        heads_ref[pair] = mixed_ref[pair, 0:block, :]
    to_core(3)
    to_core(direct)

    @pl.loop(pairs, units)
    def _(slot):
        copy = head_copy(lax.rem(slot, pairs), lax.div(slot, pairs))
        copy.wait_recv()
        copy.wait_send()

    for copy in [*core_copies.values(), *own_copies, *z_copies[direct - 1]]:
        copy.wait_recv()
    for copy in [*started, *onward, *own_copies, *y_copies, *x_copies, *core_copies.values()]:
        copy.wait_send()
    for copies in z_copies:
        for copy in copies:
            copy.wait_send()
    for copy in outward:
        copy.wait()


def attend_forward(lengths, tokens, gains, shifts, weight, weights):
    block, width = tokens.shape
    ranks = lax.axis_size("tensor")
    assert ranks == 4
    length = block * ranks
    pairs = weight.shape[2] // PAIR
    group = lax.axis_size("dp") // 2
    views = [w.reshape(2, group, w.shape[0] // (2 * group), w.shape[1]) for w in weights]
    chunks = [(0, 0, width)]
    for a in (1, 2):
        columns = weights[a].shape[1] // 2
        chunks += [(a, 0, columns), (a, columns, columns)]
    chunks[3:] = [(2, columns, columns // 2), (2, 0, columns), (2, columns + columns // 2, columns // 2)]
    vmem = pl.BlockSpec(memory_space=pltpu.VMEM)
    hbm = pl.BlockSpec(memory_space=pl.ANY)
    copies = pltpu.SemaphoreType.DMA
    lane = np.arange(PAIR) % (HD // 2)
    frequencies = jnp.asarray((ROPE_BASE ** (-lane * 2.0 / HD))[None, :], F32)
    smem = pl.BlockSpec(memory_space=pltpu.SMEM)
    mixed, logs, heads, qkv, attn, cosine, sine, *rests = pl.pallas_call(
        functools.partial(forward_kernel, block, ranks, pairs, chunks),
        out_shape=[
            jax.ShapeDtypeStruct((pairs, length, PAIR), BF),
            jax.ShapeDtypeStruct((pairs, 8, length), F32),
            jax.ShapeDtypeStruct((ranks * pairs, block, PAIR), BF),
            jax.ShapeDtypeStruct((3 * pairs, length, PAIR), BF),
            jax.ShapeDtypeStruct((ranks, block, width), BF),
            jax.ShapeDtypeStruct((length, PAIR), F32),
            jax.ShapeDtypeStruct((length, PAIR), F32),
            *[jax.ShapeDtypeStruct((ranks - 1, *view.shape), BF) for view in views],
        ],
        in_specs=[smem] + [vmem] * 5 + [hbm] * 3,
        out_specs=[vmem] * 3 + [hbm] * 7,
        scratch_shapes=[
            pltpu.VMEM((PAIR // HD, ranks, block, block), F32),
            pltpu.VMEM((3 * pairs, length, PAIR), BF),
            pltpu.VMEM((ranks, block, width), BF),
            pltpu.VMEM((length, PAIR), F32),
            pltpu.VMEM((length, PAIR), F32),
            pltpu.VMEM((length, PAIR), BF),
            pltpu.VMEM((length, PAIR), BF),
            copies((4,)),
            copies((2, 12)),
            copies((2, ranks * pairs)),
            copies((2, 3)),
            copies((2, len(chunks))),
            copies((2, len(chunks) * (group - 1))),
            copies((2, len(chunks))),
            copies((2, len(chunks))),
        ],
        compiler_params=pltpu.CompilerParams(vmem_limit_bytes=56 << 20, collective_id=2, has_side_effects=True),
        name="attend_forward",
    )(lengths, tokens, gains, shifts, weight, frequencies, *views)
    rests = [r.reshape(ranks - 1, *w.shape) for r, w in zip(rests, weights)]
    return qkv, attn, mixed, logs, heads, cosine, sine, rests


def unit_scale(values):
    centre = values - jnp.mean(values, axis=-1, keepdims=True)
    scale = lax.rsqrt(jnp.mean(centre * centre, axis=-1, keepdims=True) + EPSILON)
    return centre * scale, scale


def norm_pull(grad, unit, scale, gain):
    inside = grad * gain
    first = jnp.mean(inside, axis=-1, keepdims=True)
    second = jnp.mean(inside * unit, axis=-1, keepdims=True)
    return scale * (inside - first - unit * second)


def gelu_both(x):
    bend = 0.7978845608028654
    square = x * x
    t = jnp.tanh(bend * (x + 0.044715 * (square * x)))
    side = 0.5 * (1.0 + t)
    return x * side, side + 0.5 * x * (1.0 - t * t) * (bend * (1.0 + 0.134145 * square))


def middle_kernel(block, ranks, pairs, *refs):
    (heads_ref, x_ref, dy_ref, gains_ref, shifts_ref, *refs) = refs
    sources, refs = refs[:6], refs[6:]
    (down_ref, up_ref, early_ref, do_ref, got_down, got_up, out_far, rest_far, shared_far, *refs) = refs
    (out_ref, rest_ref, shared_ref, leave_sems, out_all, up_all, down_all, work_ref, mlp_ref, gmp_ref, middle_ref, proj_ref, acc_ref, gap_ref, gh_ref, *refs) = refs
    (out_sems, up_sems, down_sems, part_sems, cross_sems, mlp_sems, gmp_sems, head_sems, sum_sems) = refs

    mine = lax.axis_index("tensor")
    width = x_ref.shape[1]
    strips, rows = 4, 64
    strip = block // strips
    columns = width // 2

    def loads(own, rest, array, sems):
        return [
            pltpu.make_async_copy(own if d == 0 else rest.at[d - 1], array.at[d], sems.at[d]) for d in range(ranks)
        ]

    out_loads = loads(sources[0], sources[1], out_all, out_sems)
    up_loads = loads(sources[2], sources[3], up_all, up_sems)
    down_loads = loads(sources[4], sources[5], down_all, down_sems)[:2]
    rank = lax.axis_index("dp")
    near = pl.ds(pl.multiple_of(lax.rem(rank, 2) * columns, columns), columns)
    left, inner = pl.ds(0, columns), pl.ds(columns, columns)
    far_down = sources[5]
    part_loads = [
        pltpu.make_async_copy(far_down.at[1, near, left], down_all.at[2, near, left], part_sems.at[0]),
        pltpu.make_async_copy(far_down.at[1, :, inner], down_all.at[2, :, inner], part_sems.at[1]),
        pltpu.make_async_copy(far_down.at[2, :, inner], down_all.at[3, :, inner], part_sems.at[2]),
    ]
    part_copies = [
        push(far_down.at[1, near, left], down_all.at[2, near, left], cross_sems, 0, "dp", 1),
        push(down_all.at[2, :, left], down_all.at[3, :, left], cross_sems, 1, "tensor", 1),
    ]
    for copy in out_loads:
        copy.start()
    for d in range(ranks):
        up_loads[d].start()
        if d < 2:
            down_loads[d].start()
    for load in part_loads:
        load.start()
    greet(("tensor", "dp"))
    part_copies[0].start()

    def senders(array, sems):
        found = []
        for q in range(strips):
            at = pl.ds(q * strip, strip)
            found.append(
                (
                    push(array.at[0, at], array.at[2, at], sems, q, "tensor", 2),
                    push(array.at[0, at], array.at[1, at], sems, strips + q, "tensor", 1),
                    push(array.at[2, at], array.at[3, at], sems, 2 * strips + q, "tensor", 1),
                )
            )
        return found

    mlp_copies = senders(mlp_ref, mlp_sems)
    gmp_copies = senders(gmp_ref, gmp_sems)

    def send_strip(copies, q):
        copies[q][0].start()
        copies[q][1].start()

    def forward_on(copies):
        for across, _, onward in copies:
            across.wait_recv()
            onward.start()

    for d in range(ranks):
        out_loads[d].wait()
    for c in (0, columns):
        at = pl.ds(c, columns)
        total = None
        for d in range(ranks):
            part = jnp.concatenate([heads_ref[d * pairs + p] for p in range(pairs)], axis=1)
            term = dot(part, out_all[d, :, at])
            total = term if total is None else total + term
        proj_ref[:, at] = total

    gain = [gains_ref[j : j + 1, :] for j in range(4)]
    shift = [shifts_ref[j : j + 1, :] for j in range(4)]

    for q in range(strips):

        @pl.loop(0, strip // rows)
        def _(r):
            at = pl.ds(pl.multiple_of(q * strip + r * rows, rows), rows)
            unit, _ = unit_scale(proj_ref[at, :])
            middle = x_ref[at, :].astype(F32) + (unit * gain[1] + shift[1])
            middle_ref[at, :] = middle
            unit, _ = unit_scale(middle)
            mlp_ref[0, at, :] = (unit * gain[2] + shift[2]).astype(BF)

        send_strip(mlp_copies, q)

    acc_ref[...] = jnp.zeros_like(acc_ref)

    @pl.loop(0, ranks)
    def _(d):
        pltpu.make_async_copy(up_all.at[d], up_all.at[d], up_sems.at[d]).wait()

        @pl.when(d < 2)
        def _():
            pltpu.make_async_copy(down_all.at[d], down_all.at[d], down_sems.at[d]).wait()

        @pl.when(d == 2)
        def _():
            for load in part_loads[:2]:
                load.wait()
            part_copies[0].wait_recv()
            part_copies[1].start()

        @pl.when(d == 3)
        def _():
            part_loads[2].wait()
            part_copies[1].wait_recv()

        for c in (0, columns):
            at = pl.ds(c, columns)
            hidden, slope = gelu_both(dot(mlp_ref[0], up_all[d, :, at]))
            work_ref[d, :, at] = slope
            acc_ref[...] += dot(hidden.astype(BF), down_all[d, at, :])

    zero = jnp.zeros((1, width), F32)
    gain_three, shift_three = zero, zero
    for q in range(strips):

        def last_norm(r, carry):
            gain_term, shift_term = carry
            at = pl.ds(pl.multiple_of(q * strip + r * rows, rows), rows)
            unit, scale = unit_scale(acc_ref[at, :])
            out_ref[at, :] = (middle_ref[at, :] + (unit * gain[3] + shift[3])).astype(BF)
            dy = dy_ref[at, :].astype(F32)
            gmp_ref[0, at, :] = norm_pull(dy, unit, scale, gain[3]).astype(BF)
            return (
                gain_term + jnp.sum(dy * unit, axis=0, keepdims=True),
                shift_term + jnp.sum(dy, axis=0, keepdims=True),
            )

        gain_three, shift_three = lax.fori_loop(0, strip // rows, last_norm, (gain_three, shift_three))
        send_strip(gmp_copies, q)

    acc_ref[...] = jnp.zeros_like(acc_ref)

    @pl.loop(0, ranks)
    def _(d):
        for c in (0, columns):
            at = pl.ds(c, columns)
            grad = dot(gmp_ref[0], down_all[d, at, :], NT)
            grad = (grad * work_ref[d, :, at]).astype(BF)
            acc_ref[...] += dot(grad, up_all[d, :, at], NT)

    forward_on(mlp_copies)

    def inner_norms(r, carry):
        gain_two, shift_two, gain_one, shift_one = carry
        at = pl.ds(pl.multiple_of(r * rows, rows), rows)
        grad = acc_ref[at, :]
        unit, scale = unit_scale(middle_ref[at, :])
        gain_two = gain_two + jnp.sum(grad * unit, axis=0, keepdims=True)
        shift_two = shift_two + jnp.sum(grad, axis=0, keepdims=True)
        grad = dy_ref[at, :].astype(F32) + norm_pull(grad, unit, scale, gain[2])
        rest_ref[at, :] = grad
        unit, scale = unit_scale(proj_ref[at, :])
        gain_one = gain_one + jnp.sum(grad * unit, axis=0, keepdims=True)
        shift_one = shift_one + jnp.sum(grad, axis=0, keepdims=True)
        gap_ref[at, :] = norm_pull(grad, unit, scale, gain[1]).astype(BF)
        return gain_two, shift_two, gain_one, shift_one

    gain_two, shift_two, gain_one, shift_one = lax.fori_loop(0, block // rows, inner_norms, (zero, zero, zero, zero))
    early_ref[...] = jnp.concatenate(
        [zero, gain_one, gain_two, gain_three, zero, shift_one, shift_two, shift_three], axis=0
    )

    head_copies = []
    for d in [*range(1, ranks), 0]:
        grad = dot(gap_ref[...], out_all[d], NT).astype(BF)
        for pair in range(pairs):
            piece = grad[:, pair * PAIR : (pair + 1) * PAIR]
            slot = d * pairs + pair
            gh_ref[slot] = piece
            if d > 0:
                head_copies.append(push(gh_ref.at[slot], do_ref.at[pair, d], head_sems, slot, "tensor", d))
    for d in range(ranks):
        part = jnp.concatenate([heads_ref[d * pairs + p] for p in range(pairs)], axis=1)
        shared_ref[d] = dot(part, gap_ref[...], TN).astype(BF)

    leaving = [
        pltpu.make_async_copy(near_ref, far_ref, leave_sems.at[i])
        for i, (near_ref, far_ref) in enumerate([(out_ref, out_far), (rest_ref, rest_far), (shared_ref, shared_far)])
    ]
    leaving += [
        pltpu.make_async_copy(gh_ref.at[pair], do_ref.at[pair, 0], leave_sems.at[3 + pair]) for pair in range(pairs)
    ]
    for copy in leaving:
        copy.start()

    for copies in (mlp_copies, gmp_copies):
        for _, beside, _ in copies:
            beside.wait_recv()
    work_ref[...] = jnp.zeros_like(work_ref)

    def late():
        forward_on(gmp_copies)
        for copy in head_copies:
            copy.start()

    def latest():
        for copies in (mlp_copies, gmp_copies):
            for _, _, onward in copies:
                onward.wait_recv()

    sums = [
        push(ref.at[0, 1 - lax.rem(lax.div(rank, 1 << o), 2)], got, sum_sems, o, "dp", 1 << o)
        for o, (ref, got) in enumerate([(down_ref, got_down), (up_ref, got_up)])
    ]
    half = columns // 2

    @pl.loop(0, 2 * ranks)
    def _(step):
        part = lax.div(step + 1, 3)
        i = step + 1 - 3 * part
        first, last, up = lax.div(2 - part, 2), lax.div(part, 2), lax.div(i + 1, 2)
        centre = 1 - first - last
        h = centre * (1 - up) + last
        b = first * (i - 1) + centre * (i + up) + last * (i + 1)
        pl.when(step == 3)(late)
        pl.when(step == 4)(latest)
        at = pl.ds(pl.multiple_of(h * columns, columns), columns)
        tokens, grads = mlp_ref[b], gmp_ref[b]
        hidden, slope = gelu_both(dot(tokens, up_all[0, :, at]))
        grad = (dot(grads, down_all[0, at, :], NT) * slope).astype(BF)
        work_ref[2 * h] += dot(hidden.astype(BF), grads, TN)
        work_ref[2 * h + 1, :, 0:columns] += dot(tokens[:, 0:columns], grad, TN)
        work_ref[2 * h + 1, :, columns:] += dot(tokens[:, columns:], grad, TN)

        @pl.when(b == ranks - 1)
        def _():
            for side in range(2):
                down_ref[h, side] = work_ref[2 * h, side * half : (side + 1) * half, :].astype(BF)
                up_ref[h, side] = work_ref[2 * h + 1, :, side * columns : (side + 1) * columns].astype(BF)

        @pl.when(step == 4)
        def _():
            for copy in sums:
                copy.start()

    for copy in sums:
        copy.wait()
    for copy in head_copies:
        copy.wait_recv()
        copy.wait_send()
    for copy in part_copies:
        copy.wait_send()
    for copy in leaving:
        copy.wait()
    for copies in (mlp_copies, gmp_copies):
        for group in copies:
            for copy in group:
                copy.wait_send()


def middle_stage(heads, tokens, cotangent, gains, shifts, weights, rests):
    block, width = tokens.shape
    ranks = lax.axis_size("tensor")
    local = weights[0].shape[0]
    pairs = local // PAIR
    hidden = weights[2].shape[0]
    vmem = pl.BlockSpec(memory_space=pltpu.VMEM)
    hbm = pl.BlockSpec(memory_space=pl.ANY)
    copies = pltpu.SemaphoreType.DMA
    assert block * 2 == width and hidden == width
    early = [
        jax.ShapeDtypeStruct((block, width), BF),
        jax.ShapeDtypeStruct((block, width), F32),
        jax.ShapeDtypeStruct((ranks, local, width), BF),
    ]
    operands = [array for pair in zip(weights, rests) for array in pair]
    done = pl.pallas_call(
        functools.partial(middle_kernel, block, ranks, pairs),
        out_shape=[
            jax.ShapeDtypeStruct((2, 2, block // 2, width), BF),
            jax.ShapeDtypeStruct((2, 2, block, width // 2), BF),
            jax.ShapeDtypeStruct((8, width), F32),
            jax.ShapeDtypeStruct((pairs, ranks, block, PAIR), BF),
            jax.ShapeDtypeStruct((block // 2, width), BF),
            jax.ShapeDtypeStruct((block, width // 2), BF),
            *early,
        ],
        in_specs=[vmem] * 5 + [hbm] * 6,
        out_specs=[vmem] * 3 + [hbm] * 6,
        scratch_shapes=[
            *[pltpu.VMEM(array.shape, array.dtype) for array in early],
            copies((3 + pairs,)),
            pltpu.VMEM((ranks, local, width), BF),
            pltpu.VMEM((ranks, width, hidden), BF),
            pltpu.VMEM((ranks, hidden, width), BF),
            pltpu.VMEM((ranks, block, width), F32),
            pltpu.VMEM((ranks, block, width), BF),
            pltpu.VMEM((ranks, block, width), BF),
            pltpu.VMEM((block, width), F32),
            pltpu.VMEM((block, width), F32),
            pltpu.VMEM((block, width), F32),
            pltpu.VMEM((block, width), BF),
            pltpu.VMEM((ranks * pairs, block, PAIR), BF),
            copies((ranks,)),
            copies((ranks,)),
            copies((2,)),
            copies((3,)),
            copies((2, 2)),
            copies((2, 12)),
            copies((2, 12)),
            copies((2, ranks * pairs)),
            copies((2, 2)),
        ],
        compiler_params=pltpu.CompilerParams(vmem_limit_bytes=62 << 20, collective_id=3, has_side_effects=True),
        name="middle_stage",
    )(heads, tokens, cotangent, gains, shifts, *operands)
    down, up, sums, grad_heads, first_down, first_up, block_out, rest, shared = done
    return block_out, rest, grad_heads, shared, down, up, first_down, first_up, sums


def finish_kernel(block, blocks, pairs, orders, *refs):
    (lengths_ref, first_down, first_up, log_ref, gain_ref, early_ref, *refs) = refs
    far_refs, refs = refs[:12], refs[12:]
    (input_ref, sums_ref, down_out, up_out, own_out, qkv_out, *refs) = refs
    near_refs, refs = refs[:12], refs[12:]
    (down_ref, up_ref, shared_ref, qkv_ref, do_ref, o_ref, cos_ref, sin_ref, attn_ref, w_ref, x_ref, rest_ref) = near_refs
    down_far, up_far, shared_far = far_refs[:3]
    (start_ref, dq_ref, inner_ref, grads_ref, own_ref, wide_ref, token_ref, core_sum, got_y, *refs) = refs
    (token_sum, token_y, norm_ref, got_t, sum_t, got_d, *refs) = refs
    chunks, steps = len(orders), len(orders[0])
    count = chunks * steps
    got, refs = refs[:count], refs[count:]
    (load_sems, rs_sems, ag_sems, core_sems, y_sems, token_core_sems, token_y_sems, t_sems, d_sems) = refs

    mine = lax.axis_index("tensor")
    rank = lax.axis_index("dp")
    ranks_dp = lax.axis_size("dp")
    heads = PAIR // HD
    started = []
    loads = [
        pltpu.make_async_copy(far, near, load_sems.at[i]) for i, (far, near) in enumerate(zip(far_refs, near_refs))
    ]
    for load in loads:
        load.start()

    def start(copy):
        copy.start()
        started.append(copy)
        return copy

    sources = [down_ref.at[0], up_ref.at[0], down_ref.at[1], up_ref.at[1], own_ref] + [wide_ref.at[p] for p in range(pairs)]
    results = [down_out.at[0], up_out.at[0], down_out.at[1], up_out.at[1], own_out] + [qkv_out.at[p] for p in range(pairs)]
    firsts = {0: first_down, 1: first_up}
    bits = [[lax.rem(lax.div(rank, 1 << o), 2) for o in order] for order in orders]
    rs_copies, ag_copies = {}, {}

    def held(c, k):
        return sources[c] if k == 0 else got[c * steps + k - 1]

    for c in range(chunks):
        for k in range(steps):
            far = 1 << orders[c][k]
            if k > 0 or c not in firsts:
                source = {2: down_far.at[1], 3: up_far.at[1]}.get(c, held(c, k)) if k == 0 else held(c, k)
                source = source.at[1 - bits[c][k]]
                rs_copies[c, k] = push(source, got[c * steps + k], rs_sems, c * steps + k, "dp", far)
            region = results[c].at[tuple(bits[c][: k + 1])]
            ag_copies[c, k] = push(region, region, ag_sems, c * steps + k, "dp", far)

    def begin(c):
        rs_copies[c, 0].start()

    def halve(c, k):
        at = c * steps + k
        if (c, k) in rs_copies:
            rs_copies[c, k].wait_recv()
            term = got[at]
        else:
            term = firsts[c]
        mine_half = held(c, k).at[bits[c][k]]
        strip = min(16, got[at].shape[-2])
        lead = (slice(None),) * (len(got[at].shape) - 2)

        @pl.loop(0, got[at].shape[-2] // strip)
        def _(r):
            where = (*lead, pl.ds(pl.multiple_of(r * strip, strip), strip), slice(None))
            total = (mine_half[where].astype(F32) + term[where].astype(F32)).astype(BF)
            got[at][where] = total
            if k + 1 == steps:
                results[c].at[tuple(bits[c])][where] = total

        (rs_copies[c, k + 1] if k + 1 < steps else ag_copies[c, k]).start()

    def double(c, k):
        ag_copies[c, k].wait_recv()
        if k > 0:
            ag_copies[c, k - 1].start()

    core_copies = [
        push(shared_far.at[d + 1], core_sum.at[d // 2], core_sems, d // 2, "tensor", 1) for d in range(0, blocks, 2)
    ]
    y_copies = [
        push(core_sum.at[h], got_y.at[h - 1], y_sems, h - 1, "tensor", 2 * h) for h in range(1, blocks // 2)
    ]

    def pair_up():
        for h in range(blocks // 2):
            core_copies[h].wait_recv()
            core_sum[h] = (shared_ref[2 * h].astype(F32) + core_sum[h].astype(F32)).astype(BF)
        for copy in y_copies:
            copy.start()

    def settle():
        total = core_sum[0].astype(F32)
        for h in range(1, blocks // 2):
            y_copies[h - 1].wait_recv()
            total = total + got_y[h - 1].astype(F32)
        own_ref[...] = total.astype(BF)

    def prepare(pair):
        dq_ref[...] = jnp.zeros_like(dq_ref)
        for b in range(blocks):
            rows = pl.ds(b * block, block)
            product = do_ref[pair, b].astype(F32) * o_ref[pair, rows, :].astype(F32)
            high = product.astype(BF)
            low = (product - high.astype(F32)).astype(BF)
            for head in range(heads):
                ones = head_mask((16, PAIR), head).astype(F32).astype(BF)
                inner = dot(ones, high, NT) + dot(ones, low, NT)
                inner_ref[head : head + 1, rows] = inner[0:1, :]

    def unit(pair, key_block):
        slot = xor(key_block, mine, blocks)
        here = pl.ds(pl.multiple_of(slot * block, block), block)
        keys = qkv_ref[pairs + pair, here, :]
        values = qkv_ref[2 * pairs + pair, here, :]
        dk = jnp.zeros((block, PAIR), F32)
        dv = jnp.zeros((block, PAIR), F32)
        for head in range(heads):
            mask = head_mask(keys.shape, head)
            key = jnp.where(mask, keys * HD**-0.5, jnp.zeros_like(keys))
            value = jnp.where(mask, values, jnp.zeros_like(values))

            def one(i, carry, first):
                dk, dv = carry
                place = xor(i, mine, blocks)
                rows = pl.ds(pl.multiple_of(place * block, block), block)
                real = pl.ds(pl.multiple_of(i * block, block), block)
                query = qkv_ref[pair, rows, :]
                grad = do_ref[pair, place]
                s = dot(key, query, NT)
                row = lax.broadcasted_iota(jnp.int32, s.shape, 0)
                visible = row >= start_ref[0:1, real] - key_block * block
                if first:
                    visible &= row <= lax.broadcasted_iota(jnp.int32, s.shape, 1)
                probs = jnp.where(visible, jnp.exp(s - log_ref[pair, head : head + 1, rows]), 0.0)
                grad_probs = dot(value, grad, NT)
                ds = (probs * (grad_probs - inner_ref[head : head + 1, rows])).astype(BF)
                zero = jnp.zeros_like(query)
                dv = dv + dot(probs.astype(BF), jnp.where(mask, grad, zero))
                dk = dk + dot(ds, jnp.where(mask, query, zero))
                dq_ref[rows, :] += dot(ds, key, TN)
                return dk, dv

            dk, dv = one(key_block, (dk, dv), True)
            dk, dv = lax.fori_loop(key_block + 1, blocks, lambda i, carry: one(i, carry, False), (dk, dv))
        real = pl.ds(pl.multiple_of(key_block * block, block), block)
        grads_ref[pairs + pair, here, :] = turn(dk * HD**-0.5, cos_ref[real, :], -sin_ref[real, :]).astype(BF)
        grads_ref[2 * pairs + pair, here, :] = dv.astype(BF)

    def close(pair):
        for b in range(blocks):
            rows = pl.ds(b * block, block)
            real = pl.ds(pl.multiple_of(flip(mine, b) * block, block), block)
            grads_ref[pair, rows, :] = turn(dq_ref[rows, :], cos_ref[real, :], -sin_ref[real, :]).astype(BF)
        total = None
        for b in range(blocks):
            rows = pl.ds(b * block, block)
            wide = jnp.concatenate([grads_ref[c * pairs + pair, rows, :] for c in range(3)], axis=1)
            term = dot(attn_ref[b], wide, TN)
            total = term if total is None else total + term
        wide_ref[pair] = total.astype(BF).reshape(wide_ref.shape[1:])

    greet(("tensor", "dp"))
    for copy in core_copies:
        copy.start()
    begin(3)
    begin(2)
    for load in loads[:3]:
        load.wait()
    halve(0, 0)
    halve(1, 0)
    start_ref[...] = document_start(lengths_ref, lax.broadcasted_iota(jnp.int32, start_ref.shape, 1))
    for load in loads[3:8]:
        load.wait()
    slots = pairs * blocks
    halving = lambda *steps: [functools.partial(halve, c, k) for c, k in steps]
    doubling = lambda *steps: [functools.partial(double, c, k) for c, k in steps]
    beginning = lambda c: [functools.partial(begin, c)]
    events = {
        0: [pair_up],
        2: [settle] + beginning(4) + halving((0, 1), (3, 0), (1, 1), (2, 0)),
        3: [lambda: [load.wait() for load in loads[8:]]],
        4: beginning(5) + halving((0, 2), (4, 0), (3, 1), (1, 2)),
        5: halving((2, 1)),
        6: halving((4, 1)) + doubling((0, 2)),
        7: halving((3, 2)) + doubling((1, 2)),
    }

    @pl.loop(0, slots)
    def _(u):
        pair, key_block = lax.div(u, blocks), lax.rem(u, blocks)
        for when, todo in events.items():

            @pl.when(u == when)
            def _():
                for step in todo:
                    step()

        for p in range(pairs):
            pl.when(u == p * blocks)(functools.partial(prepare, p))
        unit(pair, key_block)
        for p in range(pairs):
            pl.when(u == p * blocks + blocks - 1)(functools.partial(close, p))

    begin(6)
    halve(4, 2)
    halve(2, 2)

    def token_term(d):
        rows = pl.ds(d * block, block)
        total = None
        for c in range(3):
            wide = jnp.concatenate([grads_ref[c * pairs + p, rows, :] for p in range(pairs)], axis=1)
            term = dot(wide, w_ref[c], NT)
            total = term if total is None else total + term
        token_ref[d] = total.astype(BF)

    token_copies = []
    for d in range(0, blocks, 2):
        token_term(d + 1)
        token_copies.append(start(push(token_ref.at[d + 1], token_sum.at[d // 2], token_core_sems, d // 2, "tensor", 1)))
    double(1, 1)
    for d in range(blocks - 2, -1, -2):
        token_term(d)
        token_copies[d // 2].wait_recv()
        token_sum[d // 2] = (token_ref[d].astype(F32) + token_sum[d // 2].astype(F32)).astype(BF)
        if d > 0:
            across = start(push(token_sum.at[d // 2], token_y.at[d // 2 - 1], token_y_sems, d // 2 - 1, "tensor", d))
    double(3, 2)
    halve(5, 0)
    double(4, 2)
    halve(6, 0)
    double(0, 1)
    double(2, 2)
    double(3, 1)
    halve(5, 1)
    double(4, 1)

    across.wait_recv()
    rows = 64
    lanes = x_ref.shape[1] // 128
    gain = gain_ref[0:1, :]

    def norm(r, carry):
        gain_term, shift_term = carry
        at = pl.ds(pl.multiple_of(r * rows, rows), rows)
        grad = token_sum[0, at, :].astype(F32)
        for h in range(blocks // 2 - 1):
            grad = grad + token_y[h, at, :].astype(F32)
        unit, scale = unit_scale(x_ref[at, :].astype(F32))
        total = rest_ref[at, :] + norm_pull(grad, unit, scale, gain)
        for c in range(lanes):
            there = pl.ds(pl.multiple_of(r * (rows * lanes), rows * lanes) + c, rows, stride=lanes)
            input_ref[there, :] = total[:, c * 128 : (c + 1) * 128]
        return (
            gain_term + jnp.sum(grad * unit, axis=0, keepdims=True),
            shift_term + jnp.sum(grad, axis=0, keepdims=True),
        )

    zero = jnp.zeros(gain.shape, F32)
    gain_term, shift_term = lax.fori_loop(0, block // rows, norm, (zero, zero))
    norm_ref[...] = early_ref[...]
    norm_ref[0:1, :] = gain_term
    norm_ref[4:5, :] = shift_term
    ts = [start(push(norm_ref, got_t.at[d - 1], t_sems, d - 1, "tensor", d)) for d in range(1, blocks)]
    halve(6, 1)
    halve(5, 2)
    for copy in ts:
        copy.wait_recv()
    sum_t[...] = tree_sum([norm_ref[...]] + [got_t[d] for d in range(blocks - 1)])
    ds = [start(push(sum_t, got_d.at[d - 1], d_sems, d - 1, "dp", d)) for d in range(1, ranks_dp)]
    double(2, 1)
    halve(6, 2)
    double(5, 2)
    double(6, 2)
    double(5, 1)
    double(6, 1)
    for copy in ds:
        copy.wait_recv()
    sums_ref[...] = tree_sum([sum_t[...]] + [got_d[d] for d in range(ranks_dp - 1)])
    for c in range(chunks):
        double(c, 0)
    for copy in [*started, *core_copies, *y_copies, *rs_copies.values(), *ag_copies.values()]:
        copy.wait_send()


def finish_stage(
    lengths, qkv, grad_heads, heads_out, logs, cosine, sine, attn, weight, tokens, rest, shared, terms, firsts, gains, early
):
    pairs3, length, _ = qkv.shape
    pairs = pairs3 // 3
    block, width = tokens.shape
    blocks = length // block
    ranks_dp = lax.axis_size("dp")
    steps = ranks_dp.bit_length() - 1
    straight = list(range(steps))
    crossed = [1, 0, *straight[2:]]
    orders = [straight, crossed, straight, crossed, straight, crossed, straight]
    assert pairs == 2 and steps >= 3
    cut = (2,) * steps
    local = shared.shape[1]
    shared = shared.reshape(blocks, *cut, local // ranks_dp, width)
    terms = [term.reshape(2, *cut, -1, term.shape[-1]) for term in terms]
    firsts = [first.reshape(*cut[1:], -1, first.shape[-1]) for first in firsts]
    wide = (*cut, width // ranks_dp, 3 * PAIR)
    shapes = [term.shape[1:] for term in terms] * 2 + [shared.shape[1:]] + [wide] * pairs
    far = (*terms, shared, qkv, grad_heads, heads_out, cosine, sine, attn, weight, tokens, rest)
    parts = [shape[k + 1 :] for shape in shapes for k in range(steps)]
    vmem = pl.BlockSpec(memory_space=pltpu.VMEM)
    copies = pltpu.SemaphoreType.DMA
    outs = pl.pallas_call(
        functools.partial(finish_kernel, block, blocks, pairs, orders),
        out_shape=[
            jax.ShapeDtypeStruct((block * width // 128, 128), F32),
            jax.ShapeDtypeStruct((8, width), F32),
            *[jax.ShapeDtypeStruct(term.shape, BF) for term in terms],
            jax.ShapeDtypeStruct(shared.shape[1:], BF),
            jax.ShapeDtypeStruct((pairs, *wide), BF),
        ],
        in_specs=[pl.BlockSpec(memory_space=pltpu.SMEM)] + [vmem] * 5 + [pl.BlockSpec(memory_space=pl.ANY)] * 12,
        out_specs=[vmem] * 6,
        scratch_shapes=[
            *[pltpu.VMEM(array.shape, array.dtype) for array in far],
            pltpu.VMEM((8, length), jnp.int32),
            pltpu.VMEM((length, PAIR), F32),
            pltpu.VMEM((8, length), F32),
            pltpu.VMEM((pairs3, length, PAIR), BF),
            pltpu.VMEM(shared.shape[1:], BF),
            pltpu.VMEM((pairs, *wide), BF),
            pltpu.VMEM((blocks, block, width), BF),
            pltpu.VMEM((blocks // 2, *shared.shape[1:]), BF),
            pltpu.VMEM((blocks // 2 - 1, *shared.shape[1:]), BF),
            pltpu.VMEM((blocks // 2, block, width), BF),
            pltpu.VMEM((blocks // 2 - 1, block, width), BF),
            pltpu.VMEM((8, width), F32),
            pltpu.VMEM((blocks - 1, 8, width), F32),
            pltpu.VMEM((8, width), F32),
            pltpu.VMEM((ranks_dp - 1, 8, width), F32),
            *[pltpu.VMEM(shape, BF) for shape in parts],
            copies((12,)),
            copies((2, len(parts))),
            copies((2, len(parts))),
            copies((2, blocks // 2)),
            copies((2, blocks // 2 - 1)),
            copies((2, blocks // 2)),
            copies((2, blocks // 2 - 1)),
            copies((2, blocks - 1)),
            copies((2, ranks_dp - 1)),
        ],
        compiler_params=pltpu.CompilerParams(vmem_limit_bytes=62 << 20, collective_id=0, has_side_effects=True),
        name="finish_stage",
    )(lengths, *firsts, logs, gains, early, *far)
    input_grad, sums, down, up, own, wides = outs
    return (
        input_grad,
        sums,
        down.reshape(width, width),
        up.reshape(2, width, -1),
        own.reshape(local, width),
        wides.reshape(pairs, width, 3 * PAIR),
    )


def widen_kernel(pairs, down_ref, up_ref, own_ref, wide_ref, out_ref, input_ref, sums_ref, *refs):
    down_out, up_out, own_out, qkv_out, out_out, input_out, gain_out, bias_out = refs
    gain_out[...] = sums_ref[0:4, :]
    bias_out[...] = sums_ref[4:8, :]
    down_out[...] = down_ref[...].astype(F32)
    half = up_ref.shape[2]
    for side in range(2):
        up_out[:, side * half : (side + 1) * half] = up_ref[side].astype(F32)
    own_out[...] = own_ref[...].astype(F32)
    for c in range(3):
        for pair in range(pairs):
            piece = wide_ref[pair, :, c * PAIR : (c + 1) * PAIR]
            qkv_out[c, :, pair * PAIR : (pair + 1) * PAIR] = piece.astype(F32)
    out_out[...] = out_ref[...]
    input_out[...] = input_ref[...]


def widen(down, up, own, wides, block_out, input_grad, sums):
    pairs, width, _ = wides.shape
    steps = 8
    rows = lambda array: pl.BlockSpec((array.shape[0] // steps, *array.shape[1:]), lambda i: (i, 0))
    deep = lambda array: pl.BlockSpec(
        (array.shape[0], array.shape[1] // steps, array.shape[2]), lambda i: (0, i, 0)
    )
    still = lambda array: pl.BlockSpec(array.shape, lambda i: (0, 0))
    norm = jax.ShapeDtypeStruct((sums.shape[0] // 2, width), F32)
    qkv = jax.ShapeDtypeStruct((3, width, pairs * PAIR), F32)
    ups = jax.ShapeDtypeStruct((up.shape[1], 2 * up.shape[2]), F32)
    return pl.pallas_call(
        functools.partial(widen_kernel, pairs),
        grid=(steps,),
        out_shape=[
            jax.ShapeDtypeStruct(down.shape, F32),
            ups,
            jax.ShapeDtypeStruct(own.shape, F32),
            qkv,
            jax.ShapeDtypeStruct(block_out.shape, block_out.dtype),
            jax.ShapeDtypeStruct(input_grad.shape, F32),
            norm,
            norm,
        ],
        in_specs=[rows(down), deep(up), rows(own), deep(wides), rows(block_out), rows(input_grad), still(sums)],
        out_specs=[rows(down), rows(ups), rows(own), deep(qkv), rows(block_out), rows(input_grad), still(norm), still(norm)],
        compiler_params=pltpu.CompilerParams(vmem_limit_bytes=62 << 20),
        name="widen",
    )(down, up, own, wides, block_out, input_grad, sums)


def body(block_in, lengths, qkv_weight, out_weight, up_weight, down_weight, norm_gain, norm_bias, cotangent):
    block, row_count, width = block_in.shape
    assert row_count == 1
    pairs = out_weight.shape[0] // PAIR
    qkv_swapped = jnp.transpose(qkv_weight, (1, 0, 2))

    qkv, attn_full, heads_mixed, logs, heads_parts, cosine, sine, rests = attend_forward(
        lengths,
        block_in.reshape(block, width),
        norm_gain,
        norm_bias,
        qkv_swapped,
        (out_weight, up_weight, down_weight),
    )
    block_out, grad_middle, grad_heads, shared, down_terms, up_terms, down_first, up_first, early = middle_stage(
        heads_parts,
        block_in.reshape(block, width),
        cotangent.reshape(block, width),
        norm_gain,
        norm_bias,
        (out_weight, up_weight, down_weight),
        rests,
    )
    input_grad, sums, down_sum, up_sums, out_sum, qkv_sums = finish_stage(
        lengths,
        qkv,
        grad_heads,
        heads_mixed,
        logs,
        cosine,
        sine,
        attn_full,
        qkv_swapped,
        block_in.reshape(block, width),
        grad_middle,
        shared,
        (down_terms, up_terms),
        (down_first, up_first),
        norm_gain,
        early,
    )
    down_grad, up_grad, out_grad, qkv_grad, block_out, input_grad, gain_grad, bias_grad = widen(
        down_sum, up_sums, out_sum, qkv_sums, block_out, input_grad, sums
    )
    qkv_grad = jnp.transpose(qkv_grad, (1, 0, 2))
    return (
        block_out.reshape(block_in.shape),
        input_grad.reshape(block_in.shape),
        qkv_grad,
        out_grad,
        up_grad,
        down_grad,
        gain_grad,
        bias_grad,
    )


def solution(mesh):
    tokens, rows, columns, copied = P("tensor", "dp", None), P("tensor", None), P(None, "tensor"), P()
    heads = P(None, None, "tensor")
    return jax.shard_map(
        body,
        mesh=mesh,
        in_specs=(tokens, P("dp", None), heads, rows, columns, rows, copied, copied, tokens),
        out_specs=(tokens, tokens, heads, rows, columns, rows, copied, copied),
        check_vma=False,
    )
```

```python
import functools

import jax
import jax.numpy as jnp
import numpy as np
from jax import lax
from jax.experimental import pallas as pl
from jax.experimental.pallas import tpu as pltpu
from jax.sharding import PartitionSpec as P

HD = 64
PAIR = 128
EPSILON = 1e-05
ROPE_BASE = 10000.0
NEG = -1e30
MESH = pl.DeviceIdType.MESH
BF = jnp.bfloat16
F32 = jnp.float32
NT = (((1,), (1,)), ((), ()))
NN = (((1,), (0,)), ((), ()))
TN = (((0,), (0,)), ((), ()))


def dot(a, b, dims=NN):
    return lax.dot_general(a, b, dims, preferred_element_type=F32)


def layer_norm(values, gain, shift):
    centre = values - jnp.mean(values, axis=-1, keepdims=True)
    spread = jnp.mean(centre * centre, axis=-1, keepdims=True)
    return centre * lax.rsqrt(spread + EPSILON) * gain + shift


def flip(index, offset):
    bit = 1
    while bit <= offset:
        if offset & bit:
            index = index + bit - 2 * bit * lax.rem(lax.div(index, bit), 2)
        bit *= 2
    return index


def xor(a, b, size):
    total, bit = 0, 1
    while bit < size:
        total = total + bit * lax.rem(lax.div(a, bit) + lax.div(b, bit), 2)
        bit *= 2
    return total


def greet(axes):
    barrier = pltpu.get_barrier_semaphore()
    count = 0
    for axis in axes:
        index = lax.axis_index(axis)
        for d in range(1, lax.axis_size(axis)):
            pl.semaphore_signal(barrier, inc=1, device_id={axis: flip(index, d)}, device_id_type=MESH)
            count += 1
    pl.semaphore_wait(barrier, count)


def tree_sum(parts):
    parts = [part.astype(F32) for part in parts]
    while len(parts) > 1:
        parts = [parts[i] + parts[i + 1] for i in range(0, len(parts), 2)]
    return parts[0]


def push(src, dst, sems, slot, axis, offset):
    return pltpu.make_async_remote_copy(
        src_ref=src,
        dst_ref=dst,
        send_sem=sems.at[0, slot],
        recv_sem=sems.at[1, slot],
        device_id={axis: flip(lax.axis_index(axis), offset)},
        device_id_type=MESH,
    )


def turn(values, cosine, signed_sine):
    lane = lax.broadcasted_iota(jnp.int32, values.shape, 1)
    other = jnp.where(lane % HD < HD // 2, pltpu.roll(values, PAIR - HD // 2, 1), pltpu.roll(values, HD // 2, 1))
    return values * cosine + other * signed_sine


def head_mask(shape, head):
    lane = lax.broadcasted_iota(jnp.int32, shape, 1)
    return lane // HD == head


def document_start(lengths_ref, spot):
    begin = jnp.zeros_like(spot)
    total = jnp.int32(0)
    for j in range(lengths_ref.shape[1] - 1):
        total = total + lengths_ref[0, j]
        begin = jnp.where(spot >= total, total, begin)
    return begin


def forward_kernel(block, ranks, pairs, chunks, *refs):
    lengths_ref, x_ref, gain_ref, shift_ref, w_ref, freq_ref, *refs = refs
    weights, refs = refs[:3], refs[3:]
    mixed_ref, log_ref, heads_ref, qkv_out, attn_out, cos_out, sin_out, *refs = refs
    rests, refs = refs[:3], refs[3:]
    scores_ref, qkv_ref, attn_ref, cos_ref, sin_ref, query_marks, key_marks, out_sems, attn_sems, head_sems, own_sems, y_sems, z_sems, x_sems, core_sems = refs

    mine = lax.axis_index("tensor")
    rank = lax.axis_index("dp")
    group = lax.axis_size("dp") // 2
    x_bit, z_place = lax.rem(rank, 2), lax.div(rank, 2)
    direct = len(chunks) - 1
    started = []

    def start(copy):
        copy.start()
        started.append(copy)
        return copy

    outward = [
        pltpu.make_async_copy(src, dst, out_sems.at[i])
        for i, (src, dst) in enumerate(
            [(attn_ref, attn_out), (qkv_ref, qkv_out), (cos_ref, cos_out), (sin_ref, sin_out)]
        )
    ]

    def cut(array, c, *lead):
        at, (_, low, size) = array.at, chunks[c]
        return at[(*lead, slice(None), pl.ds(low, size))]

    def every(array, c, *lead):
        at, (_, low, size) = array.at, chunks[c]
        return at[(*lead, slice(None), slice(None), pl.ds(low, size))]

    def rest(c):
        return rests[chunks[c][0]]

    y_copies = [
        push(
            cut(weights[chunks[c][0]], c, x_bit, z_place), cut(rest(c), c, 1, x_bit, z_place), y_sems, c, "tensor", 2
        )
        for c in range(direct)
    ]
    whole = lambda array, c, *lead: array.at[(*lead, slice(None), slice(None), slice(None), pl.ds(*chunks[c][1:]))]
    y_copies.append(
        push(whole(weights[chunks[direct][0]], direct), whole(rest(direct), direct, 1), y_sems, direct, "tensor", 2)
    )
    z_copies = [
        [
            push(
                cut(rest(c), c, 1, x_bit, z_place),
                cut(rest(c), c, 1, x_bit, z_place),
                z_sems,
                c * (group - 1) + d - 1,
                "dp",
                2 * d,
            )
            for d in range(1, group)
        ]
        for c in range(direct)
    ]
    x_copies = [
        push(every(rest(c), c, 1, x_bit), every(rest(c), c, 1, x_bit), x_sems, c, "dp", 1) for c in range(direct - 1)
    ]
    core_copies = {
        c: push(whole(rest(c), c, 1), whole(rest(c), c, 2), core_sems, c, "tensor", 1)
        for c in [*range(direct - 1), direct]
    }
    own_copies = [push(weights[a], rests[a].at[0], own_sems, a, "tensor", 1) for a in range(3)]

    def to_z(c):
        y_copies[c].wait_recv()
        for copy in z_copies[c]:
            copy.start()

    def to_x(c):
        for copy in z_copies[c]:
            copy.wait_recv()
        x_copies[c].start()

    def to_core(c):
        (y_copies if c == direct else x_copies)[c].wait_recv()
        core_copies[c].start()

    greet(("tensor", "dp"))
    for c in range(direct - 1):
        y_copies[c].start()

    strips = 4
    strip = block // strips
    gain, shift = gain_ref[0:1, :], shift_ref[0:1, :]
    across, beside, onward = [], [], []
    for q in range(strips):

        @pl.loop(0, strip // 64)
        def _(r):
            at = pl.ds(pl.multiple_of(q * strip + r * 64, 64), 64)
            attn_ref[0, at, :] = layer_norm(x_ref[at, :].astype(F32), gain, shift).astype(BF)

        at = pl.ds(q * strip, strip)
        across.append(start(push(attn_ref.at[0, at], attn_ref.at[2, at], attn_sems, q, "tensor", 2)))
        beside.append(start(push(attn_ref.at[0, at], attn_ref.at[1, at], attn_sems, strips + q, "tensor", 1)))
        onward.append(push(attn_ref.at[2, at], attn_ref.at[3, at], attn_sems, 2 * strips + q, "tensor", 1))

    y_copies[direct - 1].start()
    to_z(0)

    lane = lax.broadcasted_iota(jnp.int32, (64, PAIR), 1)
    sign = jnp.where(lane % HD < HD // 2, -1.0, 1.0)
    first, past = jnp.zeros_like(lane), jnp.zeros_like(lane)
    total = jnp.int32(0)
    for j in range(lengths_ref.shape[1]):
        first = jnp.where(lane % HD == j, total, first)
        total = total + lengths_ref[0, j]
        past = jnp.where(lane % HD == j, total, past)

    @pl.loop(0, ranks * block // 64)
    def _(r):
        at = pl.ds(pl.multiple_of(r * 64, 64), 64)
        spot = r * 64 + lax.broadcasted_iota(jnp.int32, (64, PAIR), 0)
        begin = document_start(lengths_ref, spot)
        inside = (spot >= first) & (spot < past)
        query_marks[at, :] = jnp.where(inside, 1.0, 0.0).astype(BF)
        key_marks[at, :] = jnp.where(inside, 0.0, NEG).astype(BF)
        angle = (spot - begin).astype(F32) * freq_ref[...]
        cos_ref[at, :] = jnp.cos(angle)
        sin_ref[at, :] = jnp.sin(angle) * sign

    def middle():
        to_x(0)
        to_z(1)
        for q in range(strips - 1):
            across[q].wait_recv()
            onward[q].start()
        to_x(1)
        to_z(2)
        across[strips - 1].wait_recv()
        onward[strips - 1].start()
        y_copies[direct].start()
        for copy in own_copies:
            copy.start()

    def beside_here():
        for copy in beside:
            copy.wait_recv()

    def onward_here():
        for copy in onward:
            copy.wait_recv()

    @pl.loop(0, ranks)
    def _(d):
        pl.when(d == 1)(beside_here)
        pl.when(d == 2)(middle)
        pl.when(d == 3)(onward_here)
        x = attn_ref[d]
        rows = pl.ds(pl.multiple_of(d * block, block), block)
        real = pl.ds(pl.multiple_of(xor(d, mine, ranks) * block, block), block)
        for part in range(3):
            project = dot(x, w_ref[part])
            for pair in range(pairs):
                piece = project[:, pair * PAIR : (pair + 1) * PAIR]
                if part < 2:
                    piece = turn(piece, cos_ref[real, :], sin_ref[real, :])
                qkv_ref[part * pairs + pair, rows, :] = piece.astype(BF)

    sub = block // 2

    def unit(pair, d):
        row_block = xor(d, mine, ranks)
        rows = pl.ds(pl.multiple_of(d * block, block), block)
        queries = qkv_ref[pair, rows, :] * HD**-0.5
        marks = query_marks[pl.ds(pl.multiple_of(row_block * block, block), block), :]
        heads = range(PAIR // HD)
        masks = [head_mask(queries.shape, head) for head in heads]
        parts = [jnp.where(mask, queries, marks) for mask in masks]
        column = lax.broadcasted_iota(jnp.int32, (block, 128), 1)

        def score(j, tops, last):
            at = pl.ds(pl.multiple_of(xor(j, mine, ranks) * block, block), block)
            keys = qkv_ref[pairs + pair, at, :]
            marks = key_marks[pl.ds(pl.multiple_of(j * block, block), block), :]
            keys = [jnp.where(mask, keys, marks) for mask in masks]
            tops = list(tops)
            for low in range(0, block, sub):
                for head in heads:
                    s = dot(parts[head], keys[head][low : low + sub], NT)
                    for c in range(0, sub, 128):
                        piece = s[:, c : c + 128]
                        if last:
                            visible = column + (low + c) <= lax.broadcasted_iota(jnp.int32, (block, 128), 0)
                            piece = jnp.where(visible, piece, NEG)
                        scores_ref[head, j, :, low + c : low + c + 128] = piece
                        tops[head] = jnp.maximum(tops[head], piece)
            return tuple(tops)

        tops = tuple(jnp.full((block, 128), NEG, F32) for _ in heads)
        tops = lax.fori_loop(0, row_block, lambda j, tops: score(j, tops, False), tops)
        tops = score(row_block, tops, True)
        tops = [jnp.broadcast_to(jnp.max(top, axis=1, keepdims=True), (block, 128)) for top in tops]

        def mix(j, accs):
            at = pl.ds(pl.multiple_of(xor(j, mine, ranks) * block, block), block)
            values = qkv_ref[2 * pairs + pair, at, :]
            accs = list(accs)
            for low in range(0, block, sub):
                for head in heads:
                    filled = jnp.where(masks[head], values, jnp.ones_like(values))[low : low + sub]
                    shares = [
                        jnp.exp(scores_ref[head, j, :, low + c : low + c + 128] - tops[head]).astype(BF)
                        for c in range(0, sub, 128)
                    ]
                    accs[head] = accs[head] + dot(jnp.concatenate(shares, axis=1), filled)
            return tuple(accs)

        accs = lax.fori_loop(0, row_block + 1, mix, tuple(jnp.zeros((block, PAIR), F32) for _ in heads))
        totals = [pltpu.roll(acc, HD, 1) for acc in accs]
        mixed_ref[pair, rows, :] = jnp.where(masks[0], accs[0] / totals[0], accs[1] / totals[1]).astype(BF)
        for head in heads:
            logs = tops[head] + jnp.log(jnp.where(masks[head], totals[head], accs[head]))
            log_ref[pair, head : head + 1, rows] = jnp.transpose(logs)[0:1, :]

    def head_copy(pair, d):
        slot = d * pairs + pair
        return pltpu.make_async_remote_copy(
            src_ref=mixed_ref.at[pair, pl.ds(pl.multiple_of(d * block, block), block)],
            dst_ref=heads_ref.at[slot],
            send_sem=head_sems.at[0, slot],
            recv_sem=head_sems.at[1, slot],
            device_id={"tensor": xor(mine, d, ranks)},
            device_id_type=MESH,
        )

    for copy in outward:
        copy.start()
    units = pairs * ranks
    events = {
        0: [lambda: to_x(2), lambda: to_z(3), lambda: to_z(4), lambda: to_core(0), lambda: to_core(1)],
    }
    far = lax.div(mine, 2)

    @pl.loop(0, units)
    def _(u):
        pair, d = lax.rem(u, pairs), ranks - 1 - lax.div(u, pairs)
        unit(pair, d)
        pl.when(d > 0)(lambda: head_copy(pair, d).start())
        pl.when(u == 2 + 3 * far)(lambda: to_x(3))
        pl.when(u == 5 + far)(lambda: to_core(2))
        for when, steps in events.items():

            @pl.when(u == min(when, units - 1))
            def _():
                for step in steps:
                    step()

    for pair in range(pairs):
        heads_ref[pair] = mixed_ref[pair, 0:block, :]
    to_core(3)
    to_core(direct)

    @pl.loop(pairs, units)
    def _(slot):
        copy = head_copy(lax.rem(slot, pairs), lax.div(slot, pairs))
        copy.wait_recv()
        copy.wait_send()

    for copy in [*core_copies.values(), *own_copies, *z_copies[direct - 1]]:
        copy.wait_recv()
    for copy in [*started, *onward, *own_copies, *y_copies, *x_copies, *core_copies.values()]:
        copy.wait_send()
    for copies in z_copies:
        for copy in copies:
            copy.wait_send()
    for copy in outward:
        copy.wait()


def attend_forward(lengths, tokens, gains, shifts, weight, weights):
    block, width = tokens.shape
    ranks = lax.axis_size("tensor")
    assert ranks == 4
    length = block * ranks
    pairs = weight.shape[2] // PAIR
    group = lax.axis_size("dp") // 2
    views = [w.reshape(2, group, w.shape[0] // (2 * group), w.shape[1]) for w in weights]
    chunks = [(0, 0, width)]
    for a in (1, 2):
        columns = weights[a].shape[1] // 2
        chunks += [(a, 0, columns), (a, columns, columns)]
    chunks[3:] = [(2, columns, columns // 2), (2, 0, columns), (2, columns + columns // 2, columns // 2)]
    vmem = pl.BlockSpec(memory_space=pltpu.VMEM)
    hbm = pl.BlockSpec(memory_space=pl.ANY)
    copies = pltpu.SemaphoreType.DMA
    lane = np.arange(PAIR) % (HD // 2)
    frequencies = jnp.asarray((ROPE_BASE ** (-lane * 2.0 / HD))[None, :], F32)
    smem = pl.BlockSpec(memory_space=pltpu.SMEM)
    mixed, logs, heads, qkv, attn, cosine, sine, *rests = pl.pallas_call(
        functools.partial(forward_kernel, block, ranks, pairs, chunks),
        out_shape=[
            jax.ShapeDtypeStruct((pairs, length, PAIR), BF),
            jax.ShapeDtypeStruct((pairs, 8, length), F32),
            jax.ShapeDtypeStruct((ranks * pairs, block, PAIR), BF),
            jax.ShapeDtypeStruct((3 * pairs, length, PAIR), BF),
            jax.ShapeDtypeStruct((ranks, block, width), BF),
            jax.ShapeDtypeStruct((length, PAIR), F32),
            jax.ShapeDtypeStruct((length, PAIR), F32),
            *[jax.ShapeDtypeStruct((ranks - 1, *view.shape), BF) for view in views],
        ],
        in_specs=[smem] + [vmem] * 5 + [hbm] * 3,
        out_specs=[vmem] * 3 + [hbm] * 7,
        scratch_shapes=[
            pltpu.VMEM((PAIR // HD, ranks, block, block), F32),
            pltpu.VMEM((3 * pairs, length, PAIR), BF),
            pltpu.VMEM((ranks, block, width), BF),
            pltpu.VMEM((length, PAIR), F32),
            pltpu.VMEM((length, PAIR), F32),
            pltpu.VMEM((length, PAIR), BF),
            pltpu.VMEM((length, PAIR), BF),
            copies((4,)),
            copies((2, 12)),
            copies((2, ranks * pairs)),
            copies((2, 3)),
            copies((2, len(chunks))),
            copies((2, len(chunks) * (group - 1))),
            copies((2, len(chunks))),
            copies((2, len(chunks))),
        ],
        compiler_params=pltpu.CompilerParams(vmem_limit_bytes=56 << 20, collective_id=2, has_side_effects=True),
        name="attend_forward",
    )(lengths, tokens, gains, shifts, weight, frequencies, *views)
    rests = [r.reshape(ranks - 1, *w.shape) for r, w in zip(rests, weights)]
    return qkv, attn, mixed, logs, heads, cosine, sine, rests


def unit_scale(values):
    centre = values - jnp.mean(values, axis=-1, keepdims=True)
    scale = lax.rsqrt(jnp.mean(centre * centre, axis=-1, keepdims=True) + EPSILON)
    return centre * scale, scale


def norm_pull(grad, unit, scale, gain):
    inside = grad * gain
    first = jnp.mean(inside, axis=-1, keepdims=True)
    second = jnp.mean(inside * unit, axis=-1, keepdims=True)
    return scale * (inside - first - unit * second)


def gelu_both(x):
    bend = 0.7978845608028654
    square = x * x
    t = jnp.tanh(bend * (x + 0.044715 * (square * x)))
    side = 0.5 * (1.0 + t)
    return x * side, side + 0.5 * x * (1.0 - t * t) * (bend * (1.0 + 0.134145 * square))


def middle_kernel(block, ranks, pairs, *refs):
    (heads_ref, x_ref, dy_ref, gains_ref, shifts_ref, *refs) = refs
    sources, refs = refs[:6], refs[6:]
    (down_ref, up_ref, early_ref, do_ref, got_down, got_up, out_far, rest_far, shared_far, *refs) = refs
    (out_ref, rest_ref, shared_ref, leave_sems, out_all, up_all, down_all, work_ref, mlp_ref, gmp_ref, middle_ref, proj_ref, acc_ref, gap_ref, gh_ref, *refs) = refs
    (out_sems, up_sems, down_sems, part_sems, cross_sems, mlp_sems, gmp_sems, head_sems, sum_sems) = refs

    mine = lax.axis_index("tensor")
    width = x_ref.shape[1]
    strips, rows = 4, 64
    strip = block // strips
    columns = width // 2

    def loads(own, rest, array, sems):
        return [
            pltpu.make_async_copy(own if d == 0 else rest.at[d - 1], array.at[d], sems.at[d]) for d in range(ranks)
        ]

    out_loads = loads(sources[0], sources[1], out_all, out_sems)
    up_loads = loads(sources[2], sources[3], up_all, up_sems)
    down_loads = loads(sources[4], sources[5], down_all, down_sems)[:2]
    rank = lax.axis_index("dp")
    near = pl.ds(pl.multiple_of(lax.rem(rank, 2) * columns, columns), columns)
    left, inner = pl.ds(0, columns), pl.ds(columns, columns)
    far_down = sources[5]
    part_loads = [
        pltpu.make_async_copy(far_down.at[1, near, left], down_all.at[2, near, left], part_sems.at[0]),
        pltpu.make_async_copy(far_down.at[1, :, inner], down_all.at[2, :, inner], part_sems.at[1]),
        pltpu.make_async_copy(far_down.at[2, :, inner], down_all.at[3, :, inner], part_sems.at[2]),
    ]
    part_copies = [
        push(far_down.at[1, near, left], down_all.at[2, near, left], cross_sems, 0, "dp", 1),
        push(down_all.at[2, :, left], down_all.at[3, :, left], cross_sems, 1, "tensor", 1),
    ]
    for copy in out_loads:
        copy.start()
    for d in range(ranks):
        up_loads[d].start()
        if d < 2:
            down_loads[d].start()
    for load in part_loads:
        load.start()
    greet(("tensor", "dp"))
    part_copies[0].start()

    def senders(array, sems):
        found = []
        for q in range(strips):
            at = pl.ds(q * strip, strip)
            found.append(
                (
                    push(array.at[0, at], array.at[2, at], sems, q, "tensor", 2),
                    push(array.at[0, at], array.at[1, at], sems, strips + q, "tensor", 1),
                    push(array.at[2, at], array.at[3, at], sems, 2 * strips + q, "tensor", 1),
                )
            )
        return found

    mlp_copies = senders(mlp_ref, mlp_sems)
    gmp_copies = senders(gmp_ref, gmp_sems)

    def send_strip(copies, q):
        copies[q][0].start()
        copies[q][1].start()

    def forward_on(copies):
        for across, _, onward in copies:
            across.wait_recv()
            onward.start()

    for d in range(ranks):
        out_loads[d].wait()
    for c in (0, columns):
        at = pl.ds(c, columns)
        total = None
        for d in range(ranks):
            part = jnp.concatenate([heads_ref[d * pairs + p] for p in range(pairs)], axis=1)
            term = dot(part, out_all[d, :, at])
            total = term if total is None else total + term
        proj_ref[:, at] = total

    gain = [gains_ref[j : j + 1, :] for j in range(4)]
    shift = [shifts_ref[j : j + 1, :] for j in range(4)]

    for q in range(strips):

        @pl.loop(0, strip // rows)
        def _(r):
            at = pl.ds(pl.multiple_of(q * strip + r * rows, rows), rows)
            unit, _ = unit_scale(proj_ref[at, :])
            middle = x_ref[at, :].astype(F32) + (unit * gain[1] + shift[1])
            middle_ref[at, :] = middle
            unit, _ = unit_scale(middle)
            mlp_ref[0, at, :] = (unit * gain[2] + shift[2]).astype(BF)

        send_strip(mlp_copies, q)

    acc_ref[...] = jnp.zeros_like(acc_ref)

    @pl.loop(0, ranks)
    def _(d):
        pltpu.make_async_copy(up_all.at[d], up_all.at[d], up_sems.at[d]).wait()

        @pl.when(d < 2)
        def _():
            pltpu.make_async_copy(down_all.at[d], down_all.at[d], down_sems.at[d]).wait()

        @pl.when(d == 2)
        def _():
            for load in part_loads[:2]:
                load.wait()
            part_copies[0].wait_recv()
            part_copies[1].start()

        @pl.when(d == 3)
        def _():
            part_loads[2].wait()
            part_copies[1].wait_recv()

        for c in (0, columns):
            at = pl.ds(c, columns)
            hidden, slope = gelu_both(dot(mlp_ref[0], up_all[d, :, at]))
            work_ref[d, :, at] = slope
            acc_ref[...] += dot(hidden.astype(BF), down_all[d, at, :])

    zero = jnp.zeros((1, width), F32)
    gain_three, shift_three = zero, zero
    for q in range(strips):

        def last_norm(r, carry):
            gain_term, shift_term = carry
            at = pl.ds(pl.multiple_of(q * strip + r * rows, rows), rows)
            unit, scale = unit_scale(acc_ref[at, :])
            out_ref[at, :] = (middle_ref[at, :] + (unit * gain[3] + shift[3])).astype(BF)
            dy = dy_ref[at, :].astype(F32)
            gmp_ref[0, at, :] = norm_pull(dy, unit, scale, gain[3]).astype(BF)
            return (
                gain_term + jnp.sum(dy * unit, axis=0, keepdims=True),
                shift_term + jnp.sum(dy, axis=0, keepdims=True),
            )

        gain_three, shift_three = lax.fori_loop(0, strip // rows, last_norm, (gain_three, shift_three))
        send_strip(gmp_copies, q)

    acc_ref[...] = jnp.zeros_like(acc_ref)

    @pl.loop(0, ranks)
    def _(d):
        for c in (0, columns):
            at = pl.ds(c, columns)
            grad = dot(gmp_ref[0], down_all[d, at, :], NT)
            grad = (grad * work_ref[d, :, at]).astype(BF)
            acc_ref[...] += dot(grad, up_all[d, :, at], NT)

    forward_on(mlp_copies)

    def inner_norms(r, carry):
        gain_two, shift_two, gain_one, shift_one = carry
        at = pl.ds(pl.multiple_of(r * rows, rows), rows)
        grad = acc_ref[at, :]
        unit, scale = unit_scale(middle_ref[at, :])
        gain_two = gain_two + jnp.sum(grad * unit, axis=0, keepdims=True)
        shift_two = shift_two + jnp.sum(grad, axis=0, keepdims=True)
        grad = dy_ref[at, :].astype(F32) + norm_pull(grad, unit, scale, gain[2])
        rest_ref[at, :] = grad
        unit, scale = unit_scale(proj_ref[at, :])
        gain_one = gain_one + jnp.sum(grad * unit, axis=0, keepdims=True)
        shift_one = shift_one + jnp.sum(grad, axis=0, keepdims=True)
        gap_ref[at, :] = norm_pull(grad, unit, scale, gain[1]).astype(BF)
        return gain_two, shift_two, gain_one, shift_one

    gain_two, shift_two, gain_one, shift_one = lax.fori_loop(0, block // rows, inner_norms, (zero, zero, zero, zero))
    early_ref[...] = jnp.concatenate(
        [zero, gain_one, gain_two, gain_three, zero, shift_one, shift_two, shift_three], axis=0
    )

    head_copies = []
    for d in [*range(1, ranks), 0]:
        grad = dot(gap_ref[...], out_all[d], NT).astype(BF)
        for pair in range(pairs):
            piece = grad[:, pair * PAIR : (pair + 1) * PAIR]
            slot = d * pairs + pair
            gh_ref[slot] = piece
            if d > 0:
                head_copies.append(push(gh_ref.at[slot], do_ref.at[pair, d], head_sems, slot, "tensor", d))
    for d in range(ranks):
        part = jnp.concatenate([heads_ref[d * pairs + p] for p in range(pairs)], axis=1)
        shared_ref[d] = dot(part, gap_ref[...], TN).astype(BF)

    leaving = [
        pltpu.make_async_copy(near_ref, far_ref, leave_sems.at[i])
        for i, (near_ref, far_ref) in enumerate([(out_ref, out_far), (rest_ref, rest_far), (shared_ref, shared_far)])
    ]
    leaving += [
        pltpu.make_async_copy(gh_ref.at[pair], do_ref.at[pair, 0], leave_sems.at[3 + pair]) for pair in range(pairs)
    ]
    for copy in leaving:
        copy.start()

    for copies in (mlp_copies, gmp_copies):
        for _, beside, _ in copies:
            beside.wait_recv()
    work_ref[...] = jnp.zeros_like(work_ref)

    def late():
        forward_on(gmp_copies)
        for copy in head_copies:
            copy.start()

    def latest():
        for copies in (mlp_copies, gmp_copies):
            for _, _, onward in copies:
                onward.wait_recv()

    sums = [
        push(ref.at[0, 1 - lax.rem(lax.div(rank, 1 << o), 2)], got, sum_sems, o, "dp", 1 << o)
        for o, (ref, got) in enumerate([(down_ref, got_down), (up_ref, got_up)])
    ]
    half = columns // 2

    @pl.loop(0, 2 * ranks)
    def _(step):
        part = lax.div(step + 1, 3)
        i = step + 1 - 3 * part
        first, last, up = lax.div(2 - part, 2), lax.div(part, 2), lax.div(i + 1, 2)
        centre = 1 - first - last
        h = centre * (1 - up) + last
        b = first * (i - 1) + centre * (i + up) + last * (i + 1)
        pl.when(step == 3)(late)
        pl.when(step == 4)(latest)
        at = pl.ds(pl.multiple_of(h * columns, columns), columns)
        tokens, grads = mlp_ref[b], gmp_ref[b]
        hidden, slope = gelu_both(dot(tokens, up_all[0, :, at]))
        grad = (dot(grads, down_all[0, at, :], NT) * slope).astype(BF)
        work_ref[2 * h] += dot(hidden.astype(BF), grads, TN)
        work_ref[2 * h + 1, :, 0:columns] += dot(tokens[:, 0:columns], grad, TN)
        work_ref[2 * h + 1, :, columns:] += dot(tokens[:, columns:], grad, TN)

        @pl.when(b == ranks - 1)
        def _():
            for side in range(2):
                down_ref[h, side] = work_ref[2 * h, side * half : (side + 1) * half, :].astype(BF)
                up_ref[h, side] = work_ref[2 * h + 1, :, side * columns : (side + 1) * columns].astype(BF)

        @pl.when(step == 4)
        def _():
            for copy in sums:
                copy.start()

    for copy in sums:
        copy.wait()
    for copy in head_copies:
        copy.wait_recv()
        copy.wait_send()
    for copy in part_copies:
        copy.wait_send()
    for copy in leaving:
        copy.wait()
    for copies in (mlp_copies, gmp_copies):
        for group in copies:
            for copy in group:
                copy.wait_send()


def middle_stage(heads, tokens, cotangent, gains, shifts, weights, rests):
    block, width = tokens.shape
    ranks = lax.axis_size("tensor")
    local = weights[0].shape[0]
    pairs = local // PAIR
    hidden = weights[2].shape[0]
    vmem = pl.BlockSpec(memory_space=pltpu.VMEM)
    hbm = pl.BlockSpec(memory_space=pl.ANY)
    copies = pltpu.SemaphoreType.DMA
    assert block * 2 == width and hidden == width
    early = [
        jax.ShapeDtypeStruct((block, width), BF),
        jax.ShapeDtypeStruct((block, width), F32),
        jax.ShapeDtypeStruct((ranks, local, width), BF),
    ]
    operands = [array for pair in zip(weights, rests) for array in pair]
    done = pl.pallas_call(
        functools.partial(middle_kernel, block, ranks, pairs),
        out_shape=[
            jax.ShapeDtypeStruct((2, 2, block // 2, width), BF),
            jax.ShapeDtypeStruct((2, 2, block, width // 2), BF),
            jax.ShapeDtypeStruct((8, width), F32),
            jax.ShapeDtypeStruct((pairs, ranks, block, PAIR), BF),
            jax.ShapeDtypeStruct((block // 2, width), BF),
            jax.ShapeDtypeStruct((block, width // 2), BF),
            *early,
        ],
        in_specs=[vmem] * 5 + [hbm] * 6,
        out_specs=[vmem] * 3 + [hbm] * 6,
        scratch_shapes=[
            *[pltpu.VMEM(array.shape, array.dtype) for array in early],
            copies((3 + pairs,)),
            pltpu.VMEM((ranks, local, width), BF),
            pltpu.VMEM((ranks, width, hidden), BF),
            pltpu.VMEM((ranks, hidden, width), BF),
            pltpu.VMEM((ranks, block, width), F32),
            pltpu.VMEM((ranks, block, width), BF),
            pltpu.VMEM((ranks, block, width), BF),
            pltpu.VMEM((block, width), F32),
            pltpu.VMEM((block, width), F32),
            pltpu.VMEM((block, width), F32),
            pltpu.VMEM((block, width), BF),
            pltpu.VMEM((ranks * pairs, block, PAIR), BF),
            copies((ranks,)),
            copies((ranks,)),
            copies((2,)),
            copies((3,)),
            copies((2, 2)),
            copies((2, 12)),
            copies((2, 12)),
            copies((2, ranks * pairs)),
            copies((2, 2)),
        ],
        compiler_params=pltpu.CompilerParams(vmem_limit_bytes=62 << 20, collective_id=3, has_side_effects=True),
        name="middle_stage",
    )(heads, tokens, cotangent, gains, shifts, *operands)
    down, up, sums, grad_heads, first_down, first_up, block_out, rest, shared = done
    return block_out, rest, grad_heads, shared, down, up, first_down, first_up, sums


def finish_kernel(block, blocks, pairs, orders, *refs):
    (lengths_ref, first_down, first_up, log_ref, gain_ref, early_ref, *refs) = refs
    far_refs, refs = refs[:12], refs[12:]
    (input_ref, sums_ref, down_out, up_out, own_out, qkv_out, *refs) = refs
    near_refs, refs = refs[:12], refs[12:]
    (down_ref, up_ref, shared_ref, qkv_ref, do_ref, o_ref, cos_ref, sin_ref, attn_ref, w_ref, x_ref, rest_ref) = near_refs
    down_far, up_far, shared_far = far_refs[:3]
    (start_ref, dq_ref, inner_ref, grads_ref, own_ref, wide_ref, token_ref, core_sum, got_y, *refs) = refs
    (token_sum, token_y, norm_ref, got_t, sum_t, got_d, *refs) = refs
    chunks, steps = len(orders), len(orders[0])
    count = chunks * steps
    got, refs = refs[:count], refs[count:]
    (load_sems, rs_sems, ag_sems, core_sems, y_sems, token_core_sems, token_y_sems, t_sems, d_sems) = refs

    mine = lax.axis_index("tensor")
    rank = lax.axis_index("dp")
    ranks_dp = lax.axis_size("dp")
    heads = PAIR // HD
    started = []
    loads = [
        pltpu.make_async_copy(far, near, load_sems.at[i]) for i, (far, near) in enumerate(zip(far_refs, near_refs))
    ]
    for load in loads:
        load.start()

    def start(copy):
        copy.start()
        started.append(copy)
        return copy

    sources = [down_ref.at[0], up_ref.at[0], down_ref.at[1], up_ref.at[1], own_ref] + [wide_ref.at[p] for p in range(pairs)]
    results = [down_out.at[0], up_out.at[0], down_out.at[1], up_out.at[1], own_out] + [qkv_out.at[p] for p in range(pairs)]
    firsts = {0: first_down, 1: first_up}
    bits = [[lax.rem(lax.div(rank, 1 << o), 2) for o in order] for order in orders]
    rs_copies, ag_copies = {}, {}

    def held(c, k):
        return sources[c] if k == 0 else got[c * steps + k - 1]

    for c in range(chunks):
        for k in range(steps):
            far = 1 << orders[c][k]
            if k > 0 or c not in firsts:
                source = {2: down_far.at[1], 3: up_far.at[1]}.get(c, held(c, k)) if k == 0 else held(c, k)
                source = source.at[1 - bits[c][k]]
                rs_copies[c, k] = push(source, got[c * steps + k], rs_sems, c * steps + k, "dp", far)
            region = results[c].at[tuple(bits[c][: k + 1])]
            ag_copies[c, k] = push(region, region, ag_sems, c * steps + k, "dp", far)

    def begin(c):
        rs_copies[c, 0].start()

    def halve(c, k):
        at = c * steps + k
        if (c, k) in rs_copies:
            rs_copies[c, k].wait_recv()
            term = got[at]
        else:
            term = firsts[c]
        mine_half = held(c, k).at[bits[c][k]]
        strip = min(16, got[at].shape[-2])
        lead = (slice(None),) * (len(got[at].shape) - 2)

        @pl.loop(0, got[at].shape[-2] // strip)
        def _(r):
            where = (*lead, pl.ds(pl.multiple_of(r * strip, strip), strip), slice(None))
            total = (mine_half[where].astype(F32) + term[where].astype(F32)).astype(BF)
            got[at][where] = total
            if k + 1 == steps:
                results[c].at[tuple(bits[c])][where] = total

        (rs_copies[c, k + 1] if k + 1 < steps else ag_copies[c, k]).start()

    def double(c, k):
        ag_copies[c, k].wait_recv()
        if k > 0:
            ag_copies[c, k - 1].start()

    core_copies = [
        push(shared_far.at[d + 1], core_sum.at[d // 2], core_sems, d // 2, "tensor", 1) for d in range(0, blocks, 2)
    ]
    y_copies = [
        push(core_sum.at[h], got_y.at[h - 1], y_sems, h - 1, "tensor", 2 * h) for h in range(1, blocks // 2)
    ]

    def pair_up():
        for h in range(blocks // 2):
            core_copies[h].wait_recv()
            core_sum[h] = (shared_ref[2 * h].astype(F32) + core_sum[h].astype(F32)).astype(BF)
        for copy in y_copies:
            copy.start()

    def settle():
        total = core_sum[0].astype(F32)
        for h in range(1, blocks // 2):
            y_copies[h - 1].wait_recv()
            total = total + got_y[h - 1].astype(F32)
        own_ref[...] = total.astype(BF)

    def prepare(pair):
        dq_ref[...] = jnp.zeros_like(dq_ref)
        for b in range(blocks):
            rows = pl.ds(b * block, block)
            product = do_ref[pair, b].astype(F32) * o_ref[pair, rows, :].astype(F32)
            high = product.astype(BF)
            low = (product - high.astype(F32)).astype(BF)
            for head in range(heads):
                ones = head_mask((16, PAIR), head).astype(F32).astype(BF)
                inner = dot(ones, high, NT) + dot(ones, low, NT)
                inner_ref[head : head + 1, rows] = inner[0:1, :]

    def unit(pair, key_block):
        slot = xor(key_block, mine, blocks)
        here = pl.ds(pl.multiple_of(slot * block, block), block)
        keys = qkv_ref[pairs + pair, here, :]
        values = qkv_ref[2 * pairs + pair, here, :]
        dk = jnp.zeros((block, PAIR), F32)
        dv = jnp.zeros((block, PAIR), F32)
        for head in range(heads):
            mask = head_mask(keys.shape, head)
            key = jnp.where(mask, keys * HD**-0.5, jnp.zeros_like(keys))
            value = jnp.where(mask, values, jnp.zeros_like(values))

            def one(i, carry, first):
                dk, dv = carry
                place = xor(i, mine, blocks)
                rows = pl.ds(pl.multiple_of(place * block, block), block)
                real = pl.ds(pl.multiple_of(i * block, block), block)
                query = qkv_ref[pair, rows, :]
                grad = do_ref[pair, place]
                s = dot(key, query, NT)
                row = lax.broadcasted_iota(jnp.int32, s.shape, 0)
                visible = row >= start_ref[0:1, real] - key_block * block
                if first:
                    visible &= row <= lax.broadcasted_iota(jnp.int32, s.shape, 1)
                probs = jnp.where(visible, jnp.exp(s - log_ref[pair, head : head + 1, rows]), 0.0)
                grad_probs = dot(value, grad, NT)
                ds = (probs * (grad_probs - inner_ref[head : head + 1, rows])).astype(BF)
                zero = jnp.zeros_like(query)
                dv = dv + dot(probs.astype(BF), jnp.where(mask, grad, zero))
                dk = dk + dot(ds, jnp.where(mask, query, zero))
                dq_ref[rows, :] += dot(ds, key, TN)
                return dk, dv

            dk, dv = one(key_block, (dk, dv), True)
            dk, dv = lax.fori_loop(key_block + 1, blocks, lambda i, carry: one(i, carry, False), (dk, dv))
        real = pl.ds(pl.multiple_of(key_block * block, block), block)
        grads_ref[pairs + pair, here, :] = turn(dk * HD**-0.5, cos_ref[real, :], -sin_ref[real, :]).astype(BF)
        grads_ref[2 * pairs + pair, here, :] = dv.astype(BF)

    def close(pair):
        for b in range(blocks):
            rows = pl.ds(b * block, block)
            real = pl.ds(pl.multiple_of(flip(mine, b) * block, block), block)
            grads_ref[pair, rows, :] = turn(dq_ref[rows, :], cos_ref[real, :], -sin_ref[real, :]).astype(BF)
        total = None
        for b in range(blocks):
            rows = pl.ds(b * block, block)
            wide = jnp.concatenate([grads_ref[c * pairs + pair, rows, :] for c in range(3)], axis=1)
            term = dot(attn_ref[b], wide, TN)
            total = term if total is None else total + term
        wide_ref[pair] = total.astype(BF).reshape(wide_ref.shape[1:])

    greet(("tensor", "dp"))
    for copy in core_copies:
        copy.start()
    begin(3)
    begin(2)
    for load in loads[:3]:
        load.wait()
    halve(0, 0)
    halve(1, 0)
    start_ref[...] = document_start(lengths_ref, lax.broadcasted_iota(jnp.int32, start_ref.shape, 1))
    for load in loads[3:8]:
        load.wait()
    slots = pairs * blocks
    halving = lambda *steps: [functools.partial(halve, c, k) for c, k in steps]
    doubling = lambda *steps: [functools.partial(double, c, k) for c, k in steps]
    beginning = lambda c: [functools.partial(begin, c)]
    events = {
        0: [pair_up],
        2: [settle] + beginning(4) + halving((0, 1), (3, 0), (1, 1), (2, 0)),
        3: [lambda: [load.wait() for load in loads[8:]]],
        4: beginning(5) + halving((0, 2), (4, 0), (3, 1), (1, 2)),
        5: halving((2, 1)),
        6: halving((4, 1)) + doubling((0, 2)),
        7: halving((3, 2)) + doubling((1, 2)),
    }

    @pl.loop(0, slots)
    def _(u):
        pair, key_block = lax.div(u, blocks), lax.rem(u, blocks)
        for when, todo in events.items():

            @pl.when(u == when)
            def _():
                for step in todo:
                    step()

        for p in range(pairs):
            pl.when(u == p * blocks)(functools.partial(prepare, p))
        unit(pair, key_block)
        for p in range(pairs):
            pl.when(u == p * blocks + blocks - 1)(functools.partial(close, p))

    begin(6)
    halve(4, 2)
    halve(2, 2)

    def token_term(d):
        rows = pl.ds(d * block, block)
        total = None
        for c in range(3):
            wide = jnp.concatenate([grads_ref[c * pairs + p, rows, :] for p in range(pairs)], axis=1)
            term = dot(wide, w_ref[c], NT)
            total = term if total is None else total + term
        token_ref[d] = total.astype(BF)

    token_copies = []
    for d in range(0, blocks, 2):
        token_term(d + 1)
        token_copies.append(start(push(token_ref.at[d + 1], token_sum.at[d // 2], token_core_sems, d // 2, "tensor", 1)))
    double(1, 1)
    for d in range(blocks - 2, -1, -2):
        token_term(d)
        token_copies[d // 2].wait_recv()
        token_sum[d // 2] = (token_ref[d].astype(F32) + token_sum[d // 2].astype(F32)).astype(BF)
        if d > 0:
            across = start(push(token_sum.at[d // 2], token_y.at[d // 2 - 1], token_y_sems, d // 2 - 1, "tensor", d))
    double(3, 2)
    halve(5, 0)
    double(4, 2)
    halve(6, 0)
    double(0, 1)
    double(2, 2)
    double(3, 1)
    halve(5, 1)
    double(4, 1)

    across.wait_recv()
    rows = 64
    lanes = x_ref.shape[1] // 128
    gain = gain_ref[0:1, :]

    def norm(r, carry):
        gain_term, shift_term = carry
        at = pl.ds(pl.multiple_of(r * rows, rows), rows)
        grad = token_sum[0, at, :].astype(F32)
        for h in range(blocks // 2 - 1):
            grad = grad + token_y[h, at, :].astype(F32)
        unit, scale = unit_scale(x_ref[at, :].astype(F32))
        total = rest_ref[at, :] + norm_pull(grad, unit, scale, gain)
        for c in range(lanes):
            there = pl.ds(pl.multiple_of(r * (rows * lanes), rows * lanes) + c, rows, stride=lanes)
            input_ref[there, :] = total[:, c * 128 : (c + 1) * 128]
        return (
            gain_term + jnp.sum(grad * unit, axis=0, keepdims=True),
            shift_term + jnp.sum(grad, axis=0, keepdims=True),
        )

    zero = jnp.zeros(gain.shape, F32)
    gain_term, shift_term = lax.fori_loop(0, block // rows, norm, (zero, zero))
    norm_ref[...] = early_ref[...]
    norm_ref[0:1, :] = gain_term
    norm_ref[4:5, :] = shift_term
    ts = [start(push(norm_ref, got_t.at[d - 1], t_sems, d - 1, "tensor", d)) for d in range(1, blocks)]
    halve(6, 1)
    halve(5, 2)
    for copy in ts:
        copy.wait_recv()
    sum_t[...] = tree_sum([norm_ref[...]] + [got_t[d] for d in range(blocks - 1)])
    ds = [start(push(sum_t, got_d.at[d - 1], d_sems, d - 1, "dp", d)) for d in range(1, ranks_dp)]
    double(2, 1)
    halve(6, 2)
    double(5, 2)
    double(6, 2)
    double(5, 1)
    double(6, 1)
    for copy in ds:
        copy.wait_recv()
    sums_ref[...] = tree_sum([sum_t[...]] + [got_d[d] for d in range(ranks_dp - 1)])
    for c in range(chunks):
        double(c, 0)
    for copy in [*started, *core_copies, *y_copies, *rs_copies.values(), *ag_copies.values()]:
        copy.wait_send()


def finish_stage(
    lengths, qkv, grad_heads, heads_out, logs, cosine, sine, attn, weight, tokens, rest, shared, terms, firsts, gains, early
):
    pairs3, length, _ = qkv.shape
    pairs = pairs3 // 3
    block, width = tokens.shape
    blocks = length // block
    ranks_dp = lax.axis_size("dp")
    steps = ranks_dp.bit_length() - 1
    straight = list(range(steps))
    crossed = [1, 0, *straight[2:]]
    orders = [straight, crossed, straight, crossed, straight, crossed, straight]
    assert pairs == 2 and steps >= 3
    cut = (2,) * steps
    local = shared.shape[1]
    shared = shared.reshape(blocks, *cut, local // ranks_dp, width)
    terms = [term.reshape(2, *cut, -1, term.shape[-1]) for term in terms]
    firsts = [first.reshape(*cut[1:], -1, first.shape[-1]) for first in firsts]
    wide = (*cut, width // ranks_dp, 3 * PAIR)
    shapes = [term.shape[1:] for term in terms] * 2 + [shared.shape[1:]] + [wide] * pairs
    far = (*terms, shared, qkv, grad_heads, heads_out, cosine, sine, attn, weight, tokens, rest)
    parts = [shape[k + 1 :] for shape in shapes for k in range(steps)]
    vmem = pl.BlockSpec(memory_space=pltpu.VMEM)
    copies = pltpu.SemaphoreType.DMA
    outs = pl.pallas_call(
        functools.partial(finish_kernel, block, blocks, pairs, orders),
        out_shape=[
            jax.ShapeDtypeStruct((block * width // 128, 128), F32),
            jax.ShapeDtypeStruct((8, width), F32),
            *[jax.ShapeDtypeStruct(term.shape, BF) for term in terms],
            jax.ShapeDtypeStruct(shared.shape[1:], BF),
            jax.ShapeDtypeStruct((pairs, *wide), BF),
        ],
        in_specs=[pl.BlockSpec(memory_space=pltpu.SMEM)] + [vmem] * 5 + [pl.BlockSpec(memory_space=pl.ANY)] * 12,
        out_specs=[vmem] * 6,
        scratch_shapes=[
            *[pltpu.VMEM(array.shape, array.dtype) for array in far],
            pltpu.VMEM((8, length), jnp.int32),
            pltpu.VMEM((length, PAIR), F32),
            pltpu.VMEM((8, length), F32),
            pltpu.VMEM((pairs3, length, PAIR), BF),
            pltpu.VMEM(shared.shape[1:], BF),
            pltpu.VMEM((pairs, *wide), BF),
            pltpu.VMEM((blocks, block, width), BF),
            pltpu.VMEM((blocks // 2, *shared.shape[1:]), BF),
            pltpu.VMEM((blocks // 2 - 1, *shared.shape[1:]), BF),
            pltpu.VMEM((blocks // 2, block, width), BF),
            pltpu.VMEM((blocks // 2 - 1, block, width), BF),
            pltpu.VMEM((8, width), F32),
            pltpu.VMEM((blocks - 1, 8, width), F32),
            pltpu.VMEM((8, width), F32),
            pltpu.VMEM((ranks_dp - 1, 8, width), F32),
            *[pltpu.VMEM(shape, BF) for shape in parts],
            copies((12,)),
            copies((2, len(parts))),
            copies((2, len(parts))),
            copies((2, blocks // 2)),
            copies((2, blocks // 2 - 1)),
            copies((2, blocks // 2)),
            copies((2, blocks // 2 - 1)),
            copies((2, blocks - 1)),
            copies((2, ranks_dp - 1)),
        ],
        compiler_params=pltpu.CompilerParams(vmem_limit_bytes=62 << 20, collective_id=0, has_side_effects=True),
        name="finish_stage",
    )(lengths, *firsts, logs, gains, early, *far)
    input_grad, sums, down, up, own, wides = outs
    return (
        input_grad,
        sums,
        down.reshape(width, width),
        up.reshape(2, width, -1),
        own.reshape(local, width),
        wides.reshape(pairs, width, 3 * PAIR),
    )


def widen_kernel(pairs, down_ref, up_ref, own_ref, wide_ref, out_ref, input_ref, sums_ref, *refs):
    down_out, up_out, own_out, qkv_out, out_out, input_out, gain_out, bias_out = refs
    gain_out[...] = sums_ref[0:4, :]
    bias_out[...] = sums_ref[4:8, :]
    down_out[...] = down_ref[...].astype(F32)
    half = up_ref.shape[2]
    for side in range(2):
        up_out[:, side * half : (side + 1) * half] = up_ref[side].astype(F32)
    own_out[...] = own_ref[...].astype(F32)
    for c in range(3):
        for pair in range(pairs):
            piece = wide_ref[pair, :, c * PAIR : (c + 1) * PAIR]
            qkv_out[c, :, pair * PAIR : (pair + 1) * PAIR] = piece.astype(F32)
    out_out[...] = out_ref[...]
    input_out[...] = input_ref[...]


def widen(down, up, own, wides, block_out, input_grad, sums):
    pairs, width, _ = wides.shape
    steps = 4
    rows = lambda array: pl.BlockSpec((array.shape[0] // steps, *array.shape[1:]), lambda i: (i, 0))
    deep = lambda array: pl.BlockSpec(
        (array.shape[0], array.shape[1] // steps, array.shape[2]), lambda i: (0, i, 0)
    )
    still = lambda array: pl.BlockSpec(array.shape, lambda i: (0, 0))
    norm = jax.ShapeDtypeStruct((sums.shape[0] // 2, width), F32)
    qkv = jax.ShapeDtypeStruct((3, width, pairs * PAIR), F32)
    ups = jax.ShapeDtypeStruct((up.shape[1], 2 * up.shape[2]), F32)
    return pl.pallas_call(
        functools.partial(widen_kernel, pairs),
        grid=(steps,),
        out_shape=[
            jax.ShapeDtypeStruct(down.shape, F32),
            ups,
            jax.ShapeDtypeStruct(own.shape, F32),
            qkv,
            jax.ShapeDtypeStruct(block_out.shape, block_out.dtype),
            jax.ShapeDtypeStruct(input_grad.shape, F32),
            norm,
            norm,
        ],
        in_specs=[rows(down), deep(up), rows(own), deep(wides), rows(block_out), rows(input_grad), still(sums)],
        out_specs=[rows(down), rows(ups), rows(own), deep(qkv), rows(block_out), rows(input_grad), still(norm), still(norm)],
        compiler_params=pltpu.CompilerParams(vmem_limit_bytes=62 << 20),
        name="widen",
    )(down, up, own, wides, block_out, input_grad, sums)


def body(block_in, lengths, qkv_weight, out_weight, up_weight, down_weight, norm_gain, norm_bias, cotangent):
    block, row_count, width = block_in.shape
    assert row_count == 1
    pairs = out_weight.shape[0] // PAIR
    qkv_swapped = jnp.transpose(qkv_weight, (1, 0, 2))

    qkv, attn_full, heads_mixed, logs, heads_parts, cosine, sine, rests = attend_forward(
        lengths,
        block_in.reshape(block, width),
        norm_gain,
        norm_bias,
        qkv_swapped,
        (out_weight, up_weight, down_weight),
    )
    block_out, grad_middle, grad_heads, shared, down_terms, up_terms, down_first, up_first, early = middle_stage(
        heads_parts,
        block_in.reshape(block, width),
        cotangent.reshape(block, width),
        norm_gain,
        norm_bias,
        (out_weight, up_weight, down_weight),
        rests,
    )
    input_grad, sums, down_sum, up_sums, out_sum, qkv_sums = finish_stage(
        lengths,
        qkv,
        grad_heads,
        heads_mixed,
        logs,
        cosine,
        sine,
        attn_full,
        qkv_swapped,
        block_in.reshape(block, width),
        grad_middle,
        shared,
        (down_terms, up_terms),
        (down_first, up_first),
        norm_gain,
        early,
    )
    down_grad, up_grad, out_grad, qkv_grad, block_out, input_grad, gain_grad, bias_grad = widen(
        down_sum, up_sums, out_sum, qkv_sums, block_out, input_grad, sums
    )
    qkv_grad = jnp.transpose(qkv_grad, (1, 0, 2))
    return (
        block_out.reshape(block_in.shape),
        input_grad.reshape(block_in.shape),
        qkv_grad,
        out_grad,
        up_grad,
        down_grad,
        gain_grad,
        bias_grad,
    )


def solution(mesh):
    tokens, rows, columns, copied = P("tensor", "dp", None), P("tensor", None), P(None, "tensor"), P()
    heads = P(None, None, "tensor")
    return jax.shard_map(
        body,
        mesh=mesh,
        in_specs=(tokens, P("dp", None), heads, rows, columns, rows, copied, copied, tokens),
        out_specs=(tokens, tokens, heads, rows, columns, rows, copied, copied),
        check_vma=False,
    )
```

```python
import functools

import jax
import jax.numpy as jnp
import numpy as np
from jax import lax
from jax.experimental import pallas as pl
from jax.experimental.pallas import tpu as pltpu
from jax.sharding import PartitionSpec as P

HD = 64
PAIR = 128
EPSILON = 1e-05
ROPE_BASE = 10000.0
NEG = -1e30
MESH = pl.DeviceIdType.MESH
BF = jnp.bfloat16
F32 = jnp.float32
NT = (((1,), (1,)), ((), ()))
NN = (((1,), (0,)), ((), ()))
TN = (((0,), (0,)), ((), ()))


def dot(a, b, dims=NN):
    return lax.dot_general(a, b, dims, preferred_element_type=F32)


def layer_norm(values, gain, shift):
    centre = values - jnp.mean(values, axis=-1, keepdims=True)
    spread = jnp.mean(centre * centre, axis=-1, keepdims=True)
    return centre * lax.rsqrt(spread + EPSILON) * gain + shift


def flip(index, offset):
    bit = 1
    while bit <= offset:
        if offset & bit:
            index = index + bit - 2 * bit * lax.rem(lax.div(index, bit), 2)
        bit *= 2
    return index


def xor(a, b, size):
    total, bit = 0, 1
    while bit < size:
        total = total + bit * lax.rem(lax.div(a, bit) + lax.div(b, bit), 2)
        bit *= 2
    return total


def greet(axes):
    barrier = pltpu.get_barrier_semaphore()
    count = 0
    for axis in axes:
        index = lax.axis_index(axis)
        for d in range(1, lax.axis_size(axis)):
            pl.semaphore_signal(barrier, inc=1, device_id={axis: flip(index, d)}, device_id_type=MESH)
            count += 1
    pl.semaphore_wait(barrier, count)


def tree_sum(parts):
    parts = [part.astype(F32) for part in parts]
    while len(parts) > 1:
        parts = [parts[i] + parts[i + 1] for i in range(0, len(parts), 2)]
    return parts[0]


def push(src, dst, sems, slot, axis, offset):
    return pltpu.make_async_remote_copy(
        src_ref=src,
        dst_ref=dst,
        send_sem=sems.at[0, slot],
        recv_sem=sems.at[1, slot],
        device_id={axis: flip(lax.axis_index(axis), offset)},
        device_id_type=MESH,
    )


def turn(values, cosine, signed_sine):
    lane = lax.broadcasted_iota(jnp.int32, values.shape, 1)
    other = jnp.where(lane % HD < HD // 2, pltpu.roll(values, PAIR - HD // 2, 1), pltpu.roll(values, HD // 2, 1))
    return values * cosine + other * signed_sine


def head_mask(shape, head):
    lane = lax.broadcasted_iota(jnp.int32, shape, 1)
    return lane // HD == head


def document_start(lengths_ref, spot):
    begin = jnp.zeros_like(spot)
    total = jnp.int32(0)
    for j in range(lengths_ref.shape[1] - 1):
        total = total + lengths_ref[0, j]
        begin = jnp.where(spot >= total, total, begin)
    return begin


def forward_kernel(block, ranks, pairs, chunks, *refs):
    lengths_ref, x_ref, gain_ref, shift_ref, w_ref, freq_ref, *refs = refs
    weights, refs = refs[:3], refs[3:]
    mixed_ref, log_ref, heads_ref, qkv_out, attn_out, cos_out, sin_out, *refs = refs
    rests, refs = refs[:3], refs[3:]
    scores_ref, qkv_ref, attn_ref, cos_ref, sin_ref, query_marks, key_marks, out_sems, attn_sems, head_sems, own_sems, y_sems, z_sems, x_sems, core_sems = refs

    mine = lax.axis_index("tensor")
    rank = lax.axis_index("dp")
    group = lax.axis_size("dp") // 2
    x_bit, z_place = lax.rem(rank, 2), lax.div(rank, 2)
    direct = len(chunks) - 1
    started = []

    def start(copy):
        copy.start()
        started.append(copy)
        return copy

    outward = [
        pltpu.make_async_copy(src, dst, out_sems.at[i])
        for i, (src, dst) in enumerate(
            [(attn_ref, attn_out), (qkv_ref, qkv_out), (cos_ref, cos_out), (sin_ref, sin_out)]
        )
    ]

    def cut(array, c, *lead):
        at, (_, low, size) = array.at, chunks[c]
        return at[(*lead, slice(None), pl.ds(low, size))]

    def every(array, c, *lead):
        at, (_, low, size) = array.at, chunks[c]
        return at[(*lead, slice(None), slice(None), pl.ds(low, size))]

    def rest(c):
        return rests[chunks[c][0]]

    y_copies = [
        push(
            cut(weights[chunks[c][0]], c, x_bit, z_place), cut(rest(c), c, 1, x_bit, z_place), y_sems, c, "tensor", 2
        )
        for c in range(direct)
    ]
    whole = lambda array, c, *lead: array.at[(*lead, slice(None), slice(None), slice(None), pl.ds(*chunks[c][1:]))]
    y_copies.append(
        push(whole(weights[chunks[direct][0]], direct), whole(rest(direct), direct, 1), y_sems, direct, "tensor", 2)
    )
    z_copies = [
        [
            push(
                cut(rest(c), c, 1, x_bit, z_place),
                cut(rest(c), c, 1, x_bit, z_place),
                z_sems,
                c * (group - 1) + d - 1,
                "dp",
                2 * d,
            )
            for d in range(1, group)
        ]
        for c in range(direct)
    ]
    x_copies = [
        push(every(rest(c), c, 1, x_bit), every(rest(c), c, 1, x_bit), x_sems, c, "dp", 1) for c in range(direct - 1)
    ]
    core_copies = {
        c: push(whole(rest(c), c, 1), whole(rest(c), c, 2), core_sems, c, "tensor", 1)
        for c in [*range(direct - 1), direct]
    }
    own_copies = [push(weights[a], rests[a].at[0], own_sems, a, "tensor", 1) for a in range(3)]

    def to_z(c):
        y_copies[c].wait_recv()
        for copy in z_copies[c]:
            copy.start()

    def to_x(c):
        for copy in z_copies[c]:
            copy.wait_recv()
        x_copies[c].start()

    def to_core(c):
        (y_copies if c == direct else x_copies)[c].wait_recv()
        core_copies[c].start()

    greet(("tensor", "dp"))
    for c in range(direct - 1):
        y_copies[c].start()

    strips = 4
    strip = block // strips
    gain, shift = gain_ref[0:1, :], shift_ref[0:1, :]
    across, beside, onward = [], [], []
    for q in range(strips):

        @pl.loop(0, strip // 64)
        def _(r):
            at = pl.ds(pl.multiple_of(q * strip + r * 64, 64), 64)
            attn_ref[0, at, :] = layer_norm(x_ref[at, :].astype(F32), gain, shift).astype(BF)

        at = pl.ds(q * strip, strip)
        across.append(start(push(attn_ref.at[0, at], attn_ref.at[2, at], attn_sems, q, "tensor", 2)))
        beside.append(start(push(attn_ref.at[0, at], attn_ref.at[1, at], attn_sems, strips + q, "tensor", 1)))
        onward.append(push(attn_ref.at[2, at], attn_ref.at[3, at], attn_sems, 2 * strips + q, "tensor", 1))

    y_copies[direct - 1].start()
    to_z(0)

    lane = lax.broadcasted_iota(jnp.int32, (64, PAIR), 1)
    sign = jnp.where(lane % HD < HD // 2, -1.0, 1.0)
    first, past = jnp.zeros_like(lane), jnp.zeros_like(lane)
    total = jnp.int32(0)
    for j in range(lengths_ref.shape[1]):
        first = jnp.where(lane % HD == j, total, first)
        total = total + lengths_ref[0, j]
        past = jnp.where(lane % HD == j, total, past)

    @pl.loop(0, ranks * block // 64)
    def _(r):
        at = pl.ds(pl.multiple_of(r * 64, 64), 64)
        spot = r * 64 + lax.broadcasted_iota(jnp.int32, (64, PAIR), 0)
        begin = document_start(lengths_ref, spot)
        inside = (spot >= first) & (spot < past)
        query_marks[at, :] = jnp.where(inside, 1.0, 0.0).astype(BF)
        key_marks[at, :] = jnp.where(inside, 0.0, NEG).astype(BF)
        angle = (spot - begin).astype(F32) * freq_ref[...]
        cos_ref[at, :] = jnp.cos(angle)
        sin_ref[at, :] = jnp.sin(angle) * sign

    def middle():
        to_x(0)
        to_z(1)
        for q in range(strips - 1):
            across[q].wait_recv()
            onward[q].start()
        to_x(1)
        to_z(2)
        across[strips - 1].wait_recv()
        onward[strips - 1].start()
        y_copies[direct].start()
        for copy in own_copies:
            copy.start()

    def beside_here():
        for copy in beside:
            copy.wait_recv()

    def onward_here():
        for copy in onward:
            copy.wait_recv()

    @pl.loop(0, ranks)
    def _(d):
        pl.when(d == 1)(beside_here)
        pl.when(d == 2)(middle)
        pl.when(d == 3)(onward_here)
        x = attn_ref[d]
        rows = pl.ds(pl.multiple_of(d * block, block), block)
        real = pl.ds(pl.multiple_of(xor(d, mine, ranks) * block, block), block)
        for part in range(3):
            project = dot(x, w_ref[part])
            for pair in range(pairs):
                piece = project[:, pair * PAIR : (pair + 1) * PAIR]
                if part < 2:
                    piece = turn(piece, cos_ref[real, :], sin_ref[real, :])
                qkv_ref[part * pairs + pair, rows, :] = piece.astype(BF)

    sub = block // 2

    def unit(pair, d):
        row_block = xor(d, mine, ranks)
        rows = pl.ds(pl.multiple_of(d * block, block), block)
        queries = qkv_ref[pair, rows, :] * HD**-0.5
        marks = query_marks[pl.ds(pl.multiple_of(row_block * block, block), block), :]
        heads = range(PAIR // HD)
        masks = [head_mask(queries.shape, head) for head in heads]
        parts = [jnp.where(mask, queries, marks) for mask in masks]
        column = lax.broadcasted_iota(jnp.int32, (block, 128), 1)

        def score(j, tops, last):
            at = pl.ds(pl.multiple_of(xor(j, mine, ranks) * block, block), block)
            keys = qkv_ref[pairs + pair, at, :]
            marks = key_marks[pl.ds(pl.multiple_of(j * block, block), block), :]
            keys = [jnp.where(mask, keys, marks) for mask in masks]
            tops = list(tops)
            for low in range(0, block, sub):
                for head in heads:
                    s = dot(parts[head], keys[head][low : low + sub], NT)
                    for c in range(0, sub, 128):
                        piece = s[:, c : c + 128]
                        if last:
                            visible = column + (low + c) <= lax.broadcasted_iota(jnp.int32, (block, 128), 0)
                            piece = jnp.where(visible, piece, NEG)
                        scores_ref[head, j, :, low + c : low + c + 128] = piece
                        tops[head] = jnp.maximum(tops[head], piece)
            return tuple(tops)

        tops = tuple(jnp.full((block, 128), NEG, F32) for _ in heads)
        tops = lax.fori_loop(0, row_block, lambda j, tops: score(j, tops, False), tops)
        tops = score(row_block, tops, True)
        tops = [jnp.broadcast_to(jnp.max(top, axis=1, keepdims=True), (block, 128)) for top in tops]

        def mix(j, accs):
            at = pl.ds(pl.multiple_of(xor(j, mine, ranks) * block, block), block)
            values = qkv_ref[2 * pairs + pair, at, :]
            accs = list(accs)
            for low in range(0, block, sub):
                for head in heads:
                    filled = jnp.where(masks[head], values, jnp.ones_like(values))[low : low + sub]
                    shares = [
                        jnp.exp(scores_ref[head, j, :, low + c : low + c + 128] - tops[head]).astype(BF)
                        for c in range(0, sub, 128)
                    ]
                    accs[head] = accs[head] + dot(jnp.concatenate(shares, axis=1), filled)
            return tuple(accs)

        accs = lax.fori_loop(0, row_block + 1, mix, tuple(jnp.zeros((block, PAIR), F32) for _ in heads))
        totals = [pltpu.roll(acc, HD, 1) for acc in accs]
        mixed_ref[pair, rows, :] = jnp.where(masks[0], accs[0] / totals[0], accs[1] / totals[1]).astype(BF)
        for head in heads:
            logs = tops[head] + jnp.log(jnp.where(masks[head], totals[head], accs[head]))
            log_ref[pair, head : head + 1, rows] = jnp.transpose(logs)[0:1, :]

    def head_copy(pair, d):
        slot = d * pairs + pair
        return pltpu.make_async_remote_copy(
            src_ref=mixed_ref.at[pair, pl.ds(pl.multiple_of(d * block, block), block)],
            dst_ref=heads_ref.at[slot],
            send_sem=head_sems.at[0, slot],
            recv_sem=head_sems.at[1, slot],
            device_id={"tensor": xor(mine, d, ranks)},
            device_id_type=MESH,
        )

    for copy in outward:
        copy.start()
    units = pairs * ranks
    events = {
        0: [lambda: to_x(2), lambda: to_z(3), lambda: to_z(4), lambda: to_core(0)],
        1: [lambda: to_core(1)],
    }
    far = lax.div(mine, 2)

    @pl.loop(0, units)
    def _(u):
        pair, d = lax.rem(u, pairs), ranks - 1 - lax.div(u, pairs)
        unit(pair, d)
        pl.when(d > 0)(lambda: head_copy(pair, d).start())
        pl.when(u == 2 + 3 * far)(lambda: to_x(3))
        pl.when(u == 5 + far)(lambda: to_core(2))
        for when, steps in events.items():

            @pl.when(u == min(when, units - 1))
            def _():
                for step in steps:
                    step()

    for pair in range(pairs):
        heads_ref[pair] = mixed_ref[pair, 0:block, :]
    to_core(3)
    to_core(direct)

    @pl.loop(pairs, units)
    def _(slot):
        copy = head_copy(lax.rem(slot, pairs), lax.div(slot, pairs))
        copy.wait_recv()
        copy.wait_send()

    for copy in [*core_copies.values(), *own_copies, *z_copies[direct - 1]]:
        copy.wait_recv()
    for copy in [*started, *onward, *own_copies, *y_copies, *x_copies, *core_copies.values()]:
        copy.wait_send()
    for copies in z_copies:
        for copy in copies:
            copy.wait_send()
    for copy in outward:
        copy.wait()


def attend_forward(lengths, tokens, gains, shifts, weight, weights):
    block, width = tokens.shape
    ranks = lax.axis_size("tensor")
    assert ranks == 4
    length = block * ranks
    pairs = weight.shape[2] // PAIR
    group = lax.axis_size("dp") // 2
    views = [w.reshape(2, group, w.shape[0] // (2 * group), w.shape[1]) for w in weights]
    chunks = [(0, 0, width)]
    for a in (1, 2):
        columns = weights[a].shape[1] // 2
        chunks += [(a, 0, columns), (a, columns, columns)]
    chunks[3:] = [(2, columns, columns // 2), (2, 0, columns), (2, columns + columns // 2, columns // 2)]
    vmem = pl.BlockSpec(memory_space=pltpu.VMEM)
    hbm = pl.BlockSpec(memory_space=pl.ANY)
    copies = pltpu.SemaphoreType.DMA
    lane = np.arange(PAIR) % (HD // 2)
    frequencies = jnp.asarray((ROPE_BASE ** (-lane * 2.0 / HD))[None, :], F32)
    smem = pl.BlockSpec(memory_space=pltpu.SMEM)
    mixed, logs, heads, qkv, attn, cosine, sine, *rests = pl.pallas_call(
        functools.partial(forward_kernel, block, ranks, pairs, chunks),
        out_shape=[
            jax.ShapeDtypeStruct((pairs, length, PAIR), BF),
            jax.ShapeDtypeStruct((pairs, 8, length), F32),
            jax.ShapeDtypeStruct((ranks * pairs, block, PAIR), BF),
            jax.ShapeDtypeStruct((3 * pairs, length, PAIR), BF),
            jax.ShapeDtypeStruct((ranks, block, width), BF),
            jax.ShapeDtypeStruct((length, PAIR), F32),
            jax.ShapeDtypeStruct((length, PAIR), F32),
            *[jax.ShapeDtypeStruct((ranks - 1, *view.shape), BF) for view in views],
        ],
        in_specs=[smem] + [vmem] * 5 + [hbm] * 3,
        out_specs=[vmem] * 3 + [hbm] * 7,
        scratch_shapes=[
            pltpu.VMEM((PAIR // HD, ranks, block, block), F32),
            pltpu.VMEM((3 * pairs, length, PAIR), BF),
            pltpu.VMEM((ranks, block, width), BF),
            pltpu.VMEM((length, PAIR), F32),
            pltpu.VMEM((length, PAIR), F32),
            pltpu.VMEM((length, PAIR), BF),
            pltpu.VMEM((length, PAIR), BF),
            copies((4,)),
            copies((2, 12)),
            copies((2, ranks * pairs)),
            copies((2, 3)),
            copies((2, len(chunks))),
            copies((2, len(chunks) * (group - 1))),
            copies((2, len(chunks))),
            copies((2, len(chunks))),
        ],
        compiler_params=pltpu.CompilerParams(vmem_limit_bytes=56 << 20, collective_id=2, has_side_effects=True),
        name="attend_forward",
    )(lengths, tokens, gains, shifts, weight, frequencies, *views)
    rests = [r.reshape(ranks - 1, *w.shape) for r, w in zip(rests, weights)]
    return qkv, attn, mixed, logs, heads, cosine, sine, rests


def unit_scale(values):
    centre = values - jnp.mean(values, axis=-1, keepdims=True)
    scale = lax.rsqrt(jnp.mean(centre * centre, axis=-1, keepdims=True) + EPSILON)
    return centre * scale, scale


def norm_pull(grad, unit, scale, gain):
    inside = grad * gain
    first = jnp.mean(inside, axis=-1, keepdims=True)
    second = jnp.mean(inside * unit, axis=-1, keepdims=True)
    return scale * (inside - first - unit * second)


def gelu_both(x):
    bend = 0.7978845608028654
    square = x * x
    t = jnp.tanh(bend * (x + 0.044715 * (square * x)))
    side = 0.5 * (1.0 + t)
    return x * side, side + 0.5 * x * (1.0 - t * t) * (bend * (1.0 + 0.134145 * square))


def middle_kernel(block, ranks, pairs, *refs):
    (heads_ref, x_ref, dy_ref, gains_ref, shifts_ref, *refs) = refs
    sources, refs = refs[:6], refs[6:]
    (down_ref, up_ref, early_ref, do_ref, got_down, got_up, out_far, rest_far, shared_far, *refs) = refs
    (out_ref, rest_ref, shared_ref, leave_sems, out_all, up_all, down_all, work_ref, mlp_ref, gmp_ref, middle_ref, proj_ref, acc_ref, gap_ref, gh_ref, *refs) = refs
    (out_sems, up_sems, down_sems, part_sems, cross_sems, mlp_sems, gmp_sems, head_sems, sum_sems) = refs

    mine = lax.axis_index("tensor")
    width = x_ref.shape[1]
    strips, rows = 4, 64
    strip = block // strips
    columns = width // 2

    def loads(own, rest, array, sems):
        return [
            pltpu.make_async_copy(own if d == 0 else rest.at[d - 1], array.at[d], sems.at[d]) for d in range(ranks)
        ]

    out_loads = loads(sources[0], sources[1], out_all, out_sems)
    up_loads = loads(sources[2], sources[3], up_all, up_sems)
    down_loads = loads(sources[4], sources[5], down_all, down_sems)[:2]
    rank = lax.axis_index("dp")
    near = pl.ds(pl.multiple_of(lax.rem(rank, 2) * columns, columns), columns)
    left, inner = pl.ds(0, columns), pl.ds(columns, columns)
    far_down = sources[5]
    part_loads = [
        pltpu.make_async_copy(far_down.at[1, near, left], down_all.at[2, near, left], part_sems.at[0]),
        pltpu.make_async_copy(far_down.at[1, :, inner], down_all.at[2, :, inner], part_sems.at[1]),
        pltpu.make_async_copy(far_down.at[2, :, inner], down_all.at[3, :, inner], part_sems.at[2]),
    ]
    part_copies = [
        push(far_down.at[1, near, left], down_all.at[2, near, left], cross_sems, 0, "dp", 1),
        push(down_all.at[2, :, left], down_all.at[3, :, left], cross_sems, 1, "tensor", 1),
    ]
    for copy in out_loads:
        copy.start()
    for d in range(ranks):
        up_loads[d].start()
        if d < 2:
            down_loads[d].start()
    for load in part_loads:
        load.start()
    greet(("tensor", "dp"))
    part_copies[0].start()

    def senders(array, sems):
        found = []
        for q in range(strips):
            at = pl.ds(q * strip, strip)
            found.append(
                (
                    push(array.at[0, at], array.at[2, at], sems, q, "tensor", 2),
                    push(array.at[0, at], array.at[1, at], sems, strips + q, "tensor", 1),
                    push(array.at[2, at], array.at[3, at], sems, 2 * strips + q, "tensor", 1),
                )
            )
        return found

    mlp_copies = senders(mlp_ref, mlp_sems)
    gmp_copies = senders(gmp_ref, gmp_sems)

    def send_strip(copies, q):
        copies[q][0].start()
        copies[q][1].start()

    def forward_on(copies):
        for across, _, onward in copies:
            across.wait_recv()
            onward.start()

    for d in range(ranks):
        out_loads[d].wait()
    for c in (0, columns):
        at = pl.ds(c, columns)
        total = None
        for d in range(ranks):
            part = jnp.concatenate([heads_ref[d * pairs + p] for p in range(pairs)], axis=1)
            term = dot(part, out_all[d, :, at])
            total = term if total is None else total + term
        proj_ref[:, at] = total

    gain = [gains_ref[j : j + 1, :] for j in range(4)]
    shift = [shifts_ref[j : j + 1, :] for j in range(4)]

    for q in range(strips):

        @pl.loop(0, strip // rows)
        def _(r):
            at = pl.ds(pl.multiple_of(q * strip + r * rows, rows), rows)
            unit, _ = unit_scale(proj_ref[at, :])
            middle = x_ref[at, :].astype(F32) + (unit * gain[1] + shift[1])
            middle_ref[at, :] = middle
            unit, _ = unit_scale(middle)
            mlp_ref[0, at, :] = (unit * gain[2] + shift[2]).astype(BF)

        send_strip(mlp_copies, q)

    acc_ref[...] = jnp.zeros_like(acc_ref)

    @pl.loop(0, ranks)
    def _(d):
        pltpu.make_async_copy(up_all.at[d], up_all.at[d], up_sems.at[d]).wait()

        @pl.when(d < 2)
        def _():
            pltpu.make_async_copy(down_all.at[d], down_all.at[d], down_sems.at[d]).wait()

        @pl.when(d == 2)
        def _():
            for load in part_loads[:2]:
                load.wait()
            part_copies[0].wait_recv()
            part_copies[1].start()

        @pl.when(d == 3)
        def _():
            part_loads[2].wait()
            part_copies[1].wait_recv()

        for c in (0, columns):
            at = pl.ds(c, columns)
            hidden, slope = gelu_both(dot(mlp_ref[0], up_all[d, :, at]))
            work_ref[d, :, at] = slope
            acc_ref[...] += dot(hidden.astype(BF), down_all[d, at, :])

    zero = jnp.zeros((1, width), F32)
    gain_three, shift_three = zero, zero
    for q in range(strips):

        def last_norm(r, carry):
            gain_term, shift_term = carry
            at = pl.ds(pl.multiple_of(q * strip + r * rows, rows), rows)
            unit, scale = unit_scale(acc_ref[at, :])
            out_ref[at, :] = (middle_ref[at, :] + (unit * gain[3] + shift[3])).astype(BF)
            dy = dy_ref[at, :].astype(F32)
            gmp_ref[0, at, :] = norm_pull(dy, unit, scale, gain[3]).astype(BF)
            return (
                gain_term + jnp.sum(dy * unit, axis=0, keepdims=True),
                shift_term + jnp.sum(dy, axis=0, keepdims=True),
            )

        gain_three, shift_three = lax.fori_loop(0, strip // rows, last_norm, (gain_three, shift_three))
        send_strip(gmp_copies, q)

    acc_ref[...] = jnp.zeros_like(acc_ref)

    @pl.loop(0, ranks)
    def _(d):
        for c in (0, columns):
            at = pl.ds(c, columns)
            grad = dot(gmp_ref[0], down_all[d, at, :], NT)
            grad = (grad * work_ref[d, :, at]).astype(BF)
            acc_ref[...] += dot(grad, up_all[d, :, at], NT)

    forward_on(mlp_copies)

    def inner_norms(r, carry):
        gain_two, shift_two, gain_one, shift_one = carry
        at = pl.ds(pl.multiple_of(r * rows, rows), rows)
        grad = acc_ref[at, :]
        unit, scale = unit_scale(middle_ref[at, :])
        gain_two = gain_two + jnp.sum(grad * unit, axis=0, keepdims=True)
        shift_two = shift_two + jnp.sum(grad, axis=0, keepdims=True)
        grad = dy_ref[at, :].astype(F32) + norm_pull(grad, unit, scale, gain[2])
        rest_ref[at, :] = grad
        unit, scale = unit_scale(proj_ref[at, :])
        gain_one = gain_one + jnp.sum(grad * unit, axis=0, keepdims=True)
        shift_one = shift_one + jnp.sum(grad, axis=0, keepdims=True)
        gap_ref[at, :] = norm_pull(grad, unit, scale, gain[1]).astype(BF)
        return gain_two, shift_two, gain_one, shift_one

    gain_two, shift_two, gain_one, shift_one = lax.fori_loop(0, block // rows, inner_norms, (zero, zero, zero, zero))
    early_ref[...] = jnp.concatenate(
        [zero, gain_one, gain_two, gain_three, zero, shift_one, shift_two, shift_three], axis=0
    )

    head_copies = []
    for d in [*range(1, ranks), 0]:
        grad = dot(gap_ref[...], out_all[d], NT).astype(BF)
        for pair in range(pairs):
            piece = grad[:, pair * PAIR : (pair + 1) * PAIR]
            slot = d * pairs + pair
            gh_ref[slot] = piece
            if d > 0:
                head_copies.append(push(gh_ref.at[slot], do_ref.at[pair, d], head_sems, slot, "tensor", d))
    for d in range(ranks):
        part = jnp.concatenate([heads_ref[d * pairs + p] for p in range(pairs)], axis=1)
        shared_ref[d] = dot(part, gap_ref[...], TN).astype(BF)

    leaving = [
        pltpu.make_async_copy(near_ref, far_ref, leave_sems.at[i])
        for i, (near_ref, far_ref) in enumerate([(out_ref, out_far), (rest_ref, rest_far), (shared_ref, shared_far)])
    ]
    leaving += [
        pltpu.make_async_copy(gh_ref.at[pair], do_ref.at[pair, 0], leave_sems.at[3 + pair]) for pair in range(pairs)
    ]
    for copy in leaving:
        copy.start()

    for copies in (mlp_copies, gmp_copies):
        for _, beside, _ in copies:
            beside.wait_recv()
    work_ref[...] = jnp.zeros_like(work_ref)

    def late():
        forward_on(gmp_copies)
        for copy in head_copies:
            copy.start()

    def latest():
        for copies in (mlp_copies, gmp_copies):
            for _, _, onward in copies:
                onward.wait_recv()

    sums = [
        push(ref.at[0, 1 - lax.rem(lax.div(rank, 1 << o), 2)], got, sum_sems, o, "dp", 1 << o)
        for o, (ref, got) in enumerate([(down_ref, got_down), (up_ref, got_up)])
    ]
    half = columns // 2

    @pl.loop(0, 2 * ranks)
    def _(step):
        part = lax.div(step + 1, 3)
        i = step + 1 - 3 * part
        first, last, up = lax.div(2 - part, 2), lax.div(part, 2), lax.div(i + 1, 2)
        centre = 1 - first - last
        h = centre * (1 - up) + last
        b = first * (i - 1) + centre * (i + up) + last * (i + 1)
        pl.when(step == 3)(late)
        pl.when(step == 4)(latest)
        at = pl.ds(pl.multiple_of(h * columns, columns), columns)
        tokens, grads = mlp_ref[b], gmp_ref[b]
        hidden, slope = gelu_both(dot(tokens, up_all[0, :, at]))
        grad = (dot(grads, down_all[0, at, :], NT) * slope).astype(BF)
        work_ref[2 * h] += dot(hidden.astype(BF), grads, TN)
        work_ref[2 * h + 1, :, 0:columns] += dot(tokens[:, 0:columns], grad, TN)
        work_ref[2 * h + 1, :, columns:] += dot(tokens[:, columns:], grad, TN)

        @pl.when(b == ranks - 1)
        def _():
            for side in range(2):
                down_ref[h, side] = work_ref[2 * h, side * half : (side + 1) * half, :].astype(BF)
                up_ref[h, side] = work_ref[2 * h + 1, :, side * columns : (side + 1) * columns].astype(BF)

        @pl.when(step == 4)
        def _():
            for copy in sums:
                copy.start()

    for copy in sums:
        copy.wait()
    for copy in head_copies:
        copy.wait_recv()
        copy.wait_send()
    for copy in part_copies:
        copy.wait_send()
    for copy in leaving:
        copy.wait()
    for copies in (mlp_copies, gmp_copies):
        for group in copies:
            for copy in group:
                copy.wait_send()


def middle_stage(heads, tokens, cotangent, gains, shifts, weights, rests):
    block, width = tokens.shape
    ranks = lax.axis_size("tensor")
    local = weights[0].shape[0]
    pairs = local // PAIR
    hidden = weights[2].shape[0]
    vmem = pl.BlockSpec(memory_space=pltpu.VMEM)
    hbm = pl.BlockSpec(memory_space=pl.ANY)
    copies = pltpu.SemaphoreType.DMA
    assert block * 2 == width and hidden == width
    early = [
        jax.ShapeDtypeStruct((block, width), BF),
        jax.ShapeDtypeStruct((block, width), F32),
        jax.ShapeDtypeStruct((ranks, local, width), BF),
    ]
    operands = [array for pair in zip(weights, rests) for array in pair]
    done = pl.pallas_call(
        functools.partial(middle_kernel, block, ranks, pairs),
        out_shape=[
            jax.ShapeDtypeStruct((2, 2, block // 2, width), BF),
            jax.ShapeDtypeStruct((2, 2, block, width // 2), BF),
            jax.ShapeDtypeStruct((8, width), F32),
            jax.ShapeDtypeStruct((pairs, ranks, block, PAIR), BF),
            jax.ShapeDtypeStruct((block // 2, width), BF),
            jax.ShapeDtypeStruct((block, width // 2), BF),
            *early,
        ],
        in_specs=[vmem] * 5 + [hbm] * 6,
        out_specs=[vmem] * 3 + [hbm] * 6,
        scratch_shapes=[
            *[pltpu.VMEM(array.shape, array.dtype) for array in early],
            copies((3 + pairs,)),
            pltpu.VMEM((ranks, local, width), BF),
            pltpu.VMEM((ranks, width, hidden), BF),
            pltpu.VMEM((ranks, hidden, width), BF),
            pltpu.VMEM((ranks, block, width), F32),
            pltpu.VMEM((ranks, block, width), BF),
            pltpu.VMEM((ranks, block, width), BF),
            pltpu.VMEM((block, width), F32),
            pltpu.VMEM((block, width), F32),
            pltpu.VMEM((block, width), F32),
            pltpu.VMEM((block, width), BF),
            pltpu.VMEM((ranks * pairs, block, PAIR), BF),
            copies((ranks,)),
            copies((ranks,)),
            copies((2,)),
            copies((3,)),
            copies((2, 2)),
            copies((2, 12)),
            copies((2, 12)),
            copies((2, ranks * pairs)),
            copies((2, 2)),
        ],
        compiler_params=pltpu.CompilerParams(vmem_limit_bytes=62 << 20, collective_id=3, has_side_effects=True),
        name="middle_stage",
    )(heads, tokens, cotangent, gains, shifts, *operands)
    down, up, sums, grad_heads, first_down, first_up, block_out, rest, shared = done
    return block_out, rest, grad_heads, shared, down, up, first_down, first_up, sums


def finish_kernel(block, blocks, pairs, orders, *refs):
    (lengths_ref, first_down, first_up, log_ref, gain_ref, early_ref, *refs) = refs
    far_refs, refs = refs[:12], refs[12:]
    (input_ref, sums_ref, down_out, up_out, own_out, qkv_out, *refs) = refs
    near_refs, refs = refs[:12], refs[12:]
    (down_ref, up_ref, shared_ref, qkv_ref, do_ref, o_ref, cos_ref, sin_ref, attn_ref, w_ref, x_ref, rest_ref) = near_refs
    down_far, up_far, shared_far = far_refs[:3]
    (start_ref, dq_ref, inner_ref, grads_ref, own_ref, wide_ref, token_ref, core_sum, got_y, *refs) = refs
    (token_sum, token_y, norm_ref, got_t, sum_t, got_d, *refs) = refs
    chunks, steps = len(orders), len(orders[0])
    count = chunks * steps
    got, refs = refs[:count], refs[count:]
    (load_sems, rs_sems, ag_sems, core_sems, y_sems, token_core_sems, token_y_sems, t_sems, d_sems) = refs

    mine = lax.axis_index("tensor")
    rank = lax.axis_index("dp")
    ranks_dp = lax.axis_size("dp")
    heads = PAIR // HD
    started = []
    loads = [
        pltpu.make_async_copy(far, near, load_sems.at[i]) for i, (far, near) in enumerate(zip(far_refs, near_refs))
    ]
    for load in loads:
        load.start()

    def start(copy):
        copy.start()
        started.append(copy)
        return copy

    sources = [down_ref.at[0], up_ref.at[0], down_ref.at[1], up_ref.at[1], own_ref] + [wide_ref.at[p] for p in range(pairs)]
    results = [down_out.at[0], up_out.at[0], down_out.at[1], up_out.at[1], own_out] + [qkv_out.at[p] for p in range(pairs)]
    firsts = {0: first_down, 1: first_up}
    bits = [[lax.rem(lax.div(rank, 1 << o), 2) for o in order] for order in orders]
    rs_copies, ag_copies = {}, {}

    def held(c, k):
        return sources[c] if k == 0 else got[c * steps + k - 1]

    for c in range(chunks):
        for k in range(steps):
            far = 1 << orders[c][k]
            if k > 0 or c not in firsts:
                source = {2: down_far.at[1], 3: up_far.at[1]}.get(c, held(c, k)) if k == 0 else held(c, k)
                source = source.at[1 - bits[c][k]]
                rs_copies[c, k] = push(source, got[c * steps + k], rs_sems, c * steps + k, "dp", far)
            region = results[c].at[tuple(bits[c][: k + 1])]
            ag_copies[c, k] = push(region, region, ag_sems, c * steps + k, "dp", far)

    def begin(c):
        rs_copies[c, 0].start()

    def halve(c, k):
        at = c * steps + k
        if (c, k) in rs_copies:
            rs_copies[c, k].wait_recv()
            term = got[at]
        else:
            term = firsts[c]
        mine_half = held(c, k).at[bits[c][k]]
        strip = min(16, got[at].shape[-2])
        lead = (slice(None),) * (len(got[at].shape) - 2)

        @pl.loop(0, got[at].shape[-2] // strip)
        def _(r):
            where = (*lead, pl.ds(pl.multiple_of(r * strip, strip), strip), slice(None))
            total = (mine_half[where].astype(F32) + term[where].astype(F32)).astype(BF)
            got[at][where] = total
            if k + 1 == steps:
                results[c].at[tuple(bits[c])][where] = total

        (rs_copies[c, k + 1] if k + 1 < steps else ag_copies[c, k]).start()

    def double(c, k):
        ag_copies[c, k].wait_recv()
        if k > 0:
            ag_copies[c, k - 1].start()

    core_copies = [
        push(shared_far.at[d + 1], core_sum.at[d // 2], core_sems, d // 2, "tensor", 1) for d in range(0, blocks, 2)
    ]
    y_copies = [
        push(core_sum.at[h], got_y.at[h - 1], y_sems, h - 1, "tensor", 2 * h) for h in range(1, blocks // 2)
    ]

    def pair_up():
        for h in range(blocks // 2):
            core_copies[h].wait_recv()
            core_sum[h] = (shared_ref[2 * h].astype(F32) + core_sum[h].astype(F32)).astype(BF)
        for copy in y_copies:
            copy.start()

    def settle():
        total = core_sum[0].astype(F32)
        for h in range(1, blocks // 2):
            y_copies[h - 1].wait_recv()
            total = total + got_y[h - 1].astype(F32)
        own_ref[...] = total.astype(BF)

    def prepare(pair):
        dq_ref[...] = jnp.zeros_like(dq_ref)
        for b in range(blocks):
            rows = pl.ds(b * block, block)
            product = do_ref[pair, b].astype(F32) * o_ref[pair, rows, :].astype(F32)
            high = product.astype(BF)
            low = (product - high.astype(F32)).astype(BF)
            for head in range(heads):
                ones = head_mask((16, PAIR), head).astype(F32).astype(BF)
                inner = dot(ones, high, NT) + dot(ones, low, NT)
                inner_ref[head : head + 1, rows] = inner[0:1, :]

    def unit(pair, key_block):
        slot = xor(key_block, mine, blocks)
        here = pl.ds(pl.multiple_of(slot * block, block), block)
        keys = qkv_ref[pairs + pair, here, :]
        values = qkv_ref[2 * pairs + pair, here, :]
        dk = jnp.zeros((block, PAIR), F32)
        dv = jnp.zeros((block, PAIR), F32)
        for head in range(heads):
            mask = head_mask(keys.shape, head)
            key = jnp.where(mask, keys * HD**-0.5, jnp.zeros_like(keys))
            value = jnp.where(mask, values, jnp.zeros_like(values))

            def one(i, carry, first):
                dk, dv = carry
                place = xor(i, mine, blocks)
                rows = pl.ds(pl.multiple_of(place * block, block), block)
                real = pl.ds(pl.multiple_of(i * block, block), block)
                query = qkv_ref[pair, rows, :]
                grad = do_ref[pair, place]
                s = dot(key, query, NT)
                row = lax.broadcasted_iota(jnp.int32, s.shape, 0)
                visible = row >= start_ref[0:1, real] - key_block * block
                if first:
                    visible &= row <= lax.broadcasted_iota(jnp.int32, s.shape, 1)
                probs = jnp.where(visible, jnp.exp(s - log_ref[pair, head : head + 1, rows]), 0.0)
                grad_probs = dot(value, grad, NT)
                ds = (probs * (grad_probs - inner_ref[head : head + 1, rows])).astype(BF)
                zero = jnp.zeros_like(query)
                dv = dv + dot(probs.astype(BF), jnp.where(mask, grad, zero))
                dk = dk + dot(ds, jnp.where(mask, query, zero))
                dq_ref[rows, :] += dot(ds, key, TN)
                return dk, dv

            dk, dv = one(key_block, (dk, dv), True)
            dk, dv = lax.fori_loop(key_block + 1, blocks, lambda i, carry: one(i, carry, False), (dk, dv))
        real = pl.ds(pl.multiple_of(key_block * block, block), block)
        grads_ref[pairs + pair, here, :] = turn(dk * HD**-0.5, cos_ref[real, :], -sin_ref[real, :]).astype(BF)
        grads_ref[2 * pairs + pair, here, :] = dv.astype(BF)

    def close(pair):
        for b in range(blocks):
            rows = pl.ds(b * block, block)
            real = pl.ds(pl.multiple_of(flip(mine, b) * block, block), block)
            grads_ref[pair, rows, :] = turn(dq_ref[rows, :], cos_ref[real, :], -sin_ref[real, :]).astype(BF)
        total = None
        for b in range(blocks):
            rows = pl.ds(b * block, block)
            wide = jnp.concatenate([grads_ref[c * pairs + pair, rows, :] for c in range(3)], axis=1)
            term = dot(attn_ref[b], wide, TN)
            total = term if total is None else total + term
        wide_ref[pair] = total.astype(BF).reshape(wide_ref.shape[1:])

    greet(("tensor", "dp"))
    for copy in core_copies:
        copy.start()
    begin(3)
    begin(2)
    for load in loads[:3]:
        load.wait()
    halve(0, 0)
    halve(1, 0)
    start_ref[...] = document_start(lengths_ref, lax.broadcasted_iota(jnp.int32, start_ref.shape, 1))
    for load in loads[3:8]:
        load.wait()
    slots = pairs * blocks
    halving = lambda *steps: [functools.partial(halve, c, k) for c, k in steps]
    doubling = lambda *steps: [functools.partial(double, c, k) for c, k in steps]
    beginning = lambda c: [functools.partial(begin, c)]
    events = {
        0: [pair_up],
        2: [settle] + beginning(4) + halving((0, 1), (3, 0), (1, 1), (2, 0)),
        3: [lambda: [load.wait() for load in loads[8:]]],
        4: beginning(5) + halving((0, 2), (4, 0), (3, 1), (1, 2)),
        5: halving((2, 1)),
        6: halving((4, 1)) + doubling((0, 2)),
        7: halving((3, 2)) + doubling((1, 2)),
    }

    @pl.loop(0, slots)
    def _(u):
        pair, key_block = lax.div(u, blocks), lax.rem(u, blocks)
        for when, todo in events.items():

            @pl.when(u == when)
            def _():
                for step in todo:
                    step()

        for p in range(pairs):
            pl.when(u == p * blocks)(functools.partial(prepare, p))
        unit(pair, key_block)
        for p in range(pairs):
            pl.when(u == p * blocks + blocks - 1)(functools.partial(close, p))

    begin(6)
    halve(4, 2)
    halve(2, 2)

    def token_term(d):
        rows = pl.ds(d * block, block)
        total = None
        for c in range(3):
            wide = jnp.concatenate([grads_ref[c * pairs + p, rows, :] for p in range(pairs)], axis=1)
            term = dot(wide, w_ref[c], NT)
            total = term if total is None else total + term
        token_ref[d] = total.astype(BF)

    token_copies = []
    for d in range(0, blocks, 2):
        token_term(d + 1)
        token_copies.append(start(push(token_ref.at[d + 1], token_sum.at[d // 2], token_core_sems, d // 2, "tensor", 1)))
    double(1, 1)
    for d in range(blocks - 2, -1, -2):
        token_term(d)
        token_copies[d // 2].wait_recv()
        token_sum[d // 2] = (token_ref[d].astype(F32) + token_sum[d // 2].astype(F32)).astype(BF)
        if d > 0:
            across = start(push(token_sum.at[d // 2], token_y.at[d // 2 - 1], token_y_sems, d // 2 - 1, "tensor", d))
    double(3, 2)
    halve(5, 0)
    double(4, 2)
    halve(6, 0)
    double(0, 1)
    double(2, 2)
    double(3, 1)
    halve(5, 1)
    double(4, 1)

    across.wait_recv()
    rows = 64
    lanes = x_ref.shape[1] // 128
    gain = gain_ref[0:1, :]

    def norm(r, carry):
        gain_term, shift_term = carry
        at = pl.ds(pl.multiple_of(r * rows, rows), rows)
        grad = token_sum[0, at, :].astype(F32)
        for h in range(blocks // 2 - 1):
            grad = grad + token_y[h, at, :].astype(F32)
        unit, scale = unit_scale(x_ref[at, :].astype(F32))
        total = rest_ref[at, :] + norm_pull(grad, unit, scale, gain)
        for c in range(lanes):
            there = pl.ds(pl.multiple_of(r * (rows * lanes), rows * lanes) + c, rows, stride=lanes)
            input_ref[there, :] = total[:, c * 128 : (c + 1) * 128]
        return (
            gain_term + jnp.sum(grad * unit, axis=0, keepdims=True),
            shift_term + jnp.sum(grad, axis=0, keepdims=True),
        )

    zero = jnp.zeros(gain.shape, F32)
    gain_term, shift_term = lax.fori_loop(0, block // rows, norm, (zero, zero))
    norm_ref[...] = early_ref[...]
    norm_ref[0:1, :] = gain_term
    norm_ref[4:5, :] = shift_term
    ts = [start(push(norm_ref, got_t.at[d - 1], t_sems, d - 1, "tensor", d)) for d in range(1, blocks)]
    halve(6, 1)
    halve(5, 2)
    for copy in ts:
        copy.wait_recv()
    sum_t[...] = tree_sum([norm_ref[...]] + [got_t[d] for d in range(blocks - 1)])
    ds = [start(push(sum_t, got_d.at[d - 1], d_sems, d - 1, "dp", d)) for d in range(1, ranks_dp)]
    double(2, 1)
    halve(6, 2)
    double(5, 2)
    double(6, 2)
    double(5, 1)
    double(6, 1)
    for copy in ds:
        copy.wait_recv()
    sums_ref[...] = tree_sum([sum_t[...]] + [got_d[d] for d in range(ranks_dp - 1)])
    for c in range(chunks):
        double(c, 0)
    for copy in [*started, *core_copies, *y_copies, *rs_copies.values(), *ag_copies.values()]:
        copy.wait_send()


def finish_stage(
    lengths, qkv, grad_heads, heads_out, logs, cosine, sine, attn, weight, tokens, rest, shared, terms, firsts, gains, early
):
    pairs3, length, _ = qkv.shape
    pairs = pairs3 // 3
    block, width = tokens.shape
    blocks = length // block
    ranks_dp = lax.axis_size("dp")
    steps = ranks_dp.bit_length() - 1
    straight = list(range(steps))
    crossed = [1, 0, *straight[2:]]
    orders = [straight, crossed, straight, crossed, straight, crossed, straight]
    assert pairs == 2 and steps >= 3
    cut = (2,) * steps
    local = shared.shape[1]
    shared = shared.reshape(blocks, *cut, local // ranks_dp, width)
    terms = [term.reshape(2, *cut, -1, term.shape[-1]) for term in terms]
    firsts = [first.reshape(*cut[1:], -1, first.shape[-1]) for first in firsts]
    wide = (*cut, width // ranks_dp, 3 * PAIR)
    shapes = [term.shape[1:] for term in terms] * 2 + [shared.shape[1:]] + [wide] * pairs
    far = (*terms, shared, qkv, grad_heads, heads_out, cosine, sine, attn, weight, tokens, rest)
    parts = [shape[k + 1 :] for shape in shapes for k in range(steps)]
    vmem = pl.BlockSpec(memory_space=pltpu.VMEM)
    copies = pltpu.SemaphoreType.DMA
    outs = pl.pallas_call(
        functools.partial(finish_kernel, block, blocks, pairs, orders),
        out_shape=[
            jax.ShapeDtypeStruct((block * width // 128, 128), F32),
            jax.ShapeDtypeStruct((8, width), F32),
            *[jax.ShapeDtypeStruct(term.shape, BF) for term in terms],
            jax.ShapeDtypeStruct(shared.shape[1:], BF),
            jax.ShapeDtypeStruct((pairs, *wide), BF),
        ],
        in_specs=[pl.BlockSpec(memory_space=pltpu.SMEM)] + [vmem] * 5 + [pl.BlockSpec(memory_space=pl.ANY)] * 12,
        out_specs=[vmem] * 6,
        scratch_shapes=[
            *[pltpu.VMEM(array.shape, array.dtype) for array in far],
            pltpu.VMEM((8, length), jnp.int32),
            pltpu.VMEM((length, PAIR), F32),
            pltpu.VMEM((8, length), F32),
            pltpu.VMEM((pairs3, length, PAIR), BF),
            pltpu.VMEM(shared.shape[1:], BF),
            pltpu.VMEM((pairs, *wide), BF),
            pltpu.VMEM((blocks, block, width), BF),
            pltpu.VMEM((blocks // 2, *shared.shape[1:]), BF),
            pltpu.VMEM((blocks // 2 - 1, *shared.shape[1:]), BF),
            pltpu.VMEM((blocks // 2, block, width), BF),
            pltpu.VMEM((blocks // 2 - 1, block, width), BF),
            pltpu.VMEM((8, width), F32),
            pltpu.VMEM((blocks - 1, 8, width), F32),
            pltpu.VMEM((8, width), F32),
            pltpu.VMEM((ranks_dp - 1, 8, width), F32),
            *[pltpu.VMEM(shape, BF) for shape in parts],
            copies((12,)),
            copies((2, len(parts))),
            copies((2, len(parts))),
            copies((2, blocks // 2)),
            copies((2, blocks // 2 - 1)),
            copies((2, blocks // 2)),
            copies((2, blocks // 2 - 1)),
            copies((2, blocks - 1)),
            copies((2, ranks_dp - 1)),
        ],
        compiler_params=pltpu.CompilerParams(vmem_limit_bytes=62 << 20, collective_id=0, has_side_effects=True),
        name="finish_stage",
    )(lengths, *firsts, logs, gains, early, *far)
    input_grad, sums, down, up, own, wides = outs
    return (
        input_grad,
        sums,
        down.reshape(width, width),
        up.reshape(2, width, -1),
        own.reshape(local, width),
        wides.reshape(pairs, width, 3 * PAIR),
    )


def widen_kernel(pairs, down_ref, up_ref, own_ref, wide_ref, out_ref, input_ref, sums_ref, *refs):
    down_out, up_out, own_out, qkv_out, out_out, input_out, gain_out, bias_out = refs
    gain_out[...] = sums_ref[0:4, :]
    bias_out[...] = sums_ref[4:8, :]
    down_out[...] = down_ref[...].astype(F32)
    half = up_ref.shape[2]
    for side in range(2):
        up_out[:, side * half : (side + 1) * half] = up_ref[side].astype(F32)
    own_out[...] = own_ref[...].astype(F32)
    for c in range(3):
        for pair in range(pairs):
            piece = wide_ref[pair, :, c * PAIR : (c + 1) * PAIR]
            qkv_out[c, :, pair * PAIR : (pair + 1) * PAIR] = piece.astype(F32)
    out_out[...] = out_ref[...]
    input_out[...] = input_ref[...]


def widen(down, up, own, wides, block_out, input_grad, sums):
    pairs, width, _ = wides.shape
    steps = 4
    rows = lambda array: pl.BlockSpec((array.shape[0] // steps, *array.shape[1:]), lambda i: (i, 0))
    deep = lambda array: pl.BlockSpec(
        (array.shape[0], array.shape[1] // steps, array.shape[2]), lambda i: (0, i, 0)
    )
    still = lambda array: pl.BlockSpec(array.shape, lambda i: (0, 0))
    norm = jax.ShapeDtypeStruct((sums.shape[0] // 2, width), F32)
    qkv = jax.ShapeDtypeStruct((3, width, pairs * PAIR), F32)
    ups = jax.ShapeDtypeStruct((up.shape[1], 2 * up.shape[2]), F32)
    return pl.pallas_call(
        functools.partial(widen_kernel, pairs),
        grid=(steps,),
        out_shape=[
            jax.ShapeDtypeStruct(down.shape, F32),
            ups,
            jax.ShapeDtypeStruct(own.shape, F32),
            qkv,
            jax.ShapeDtypeStruct(block_out.shape, block_out.dtype),
            jax.ShapeDtypeStruct(input_grad.shape, F32),
            norm,
            norm,
        ],
        in_specs=[rows(down), deep(up), rows(own), deep(wides), rows(block_out), rows(input_grad), still(sums)],
        out_specs=[rows(down), rows(ups), rows(own), deep(qkv), rows(block_out), rows(input_grad), still(norm), still(norm)],
        compiler_params=pltpu.CompilerParams(vmem_limit_bytes=62 << 20),
        name="widen",
    )(down, up, own, wides, block_out, input_grad, sums)


def body(block_in, lengths, qkv_weight, out_weight, up_weight, down_weight, norm_gain, norm_bias, cotangent):
    block, row_count, width = block_in.shape
    assert row_count == 1
    pairs = out_weight.shape[0] // PAIR
    qkv_swapped = jnp.transpose(qkv_weight, (1, 0, 2))

    qkv, attn_full, heads_mixed, logs, heads_parts, cosine, sine, rests = attend_forward(
        lengths,
        block_in.reshape(block, width),
        norm_gain,
        norm_bias,
        qkv_swapped,
        (out_weight, up_weight, down_weight),
    )
    block_out, grad_middle, grad_heads, shared, down_terms, up_terms, down_first, up_first, early = middle_stage(
        heads_parts,
        block_in.reshape(block, width),
        cotangent.reshape(block, width),
        norm_gain,
        norm_bias,
        (out_weight, up_weight, down_weight),
        rests,
    )
    input_grad, sums, down_sum, up_sums, out_sum, qkv_sums = finish_stage(
        lengths,
        qkv,
        grad_heads,
        heads_mixed,
        logs,
        cosine,
        sine,
        attn_full,
        qkv_swapped,
        block_in.reshape(block, width),
        grad_middle,
        shared,
        (down_terms, up_terms),
        (down_first, up_first),
        norm_gain,
        early,
    )
    down_grad, up_grad, out_grad, qkv_grad, block_out, input_grad, gain_grad, bias_grad = widen(
        down_sum, up_sums, out_sum, qkv_sums, block_out, input_grad, sums
    )
    qkv_grad = jnp.transpose(qkv_grad, (1, 0, 2))
    return (
        block_out.reshape(block_in.shape),
        input_grad.reshape(block_in.shape),
        qkv_grad,
        out_grad,
        up_grad,
        down_grad,
        gain_grad,
        bias_grad,
    )


def solution(mesh):
    tokens, rows, columns, copied = P("tensor", "dp", None), P("tensor", None), P(None, "tensor"), P()
    heads = P(None, None, "tensor")
    return jax.shard_map(
        body,
        mesh=mesh,
        in_specs=(tokens, P("dp", None), heads, rows, columns, rows, copied, copied, tokens),
        out_specs=(tokens, tokens, heads, rows, columns, rows, copied, copied),
        check_vma=False,
    )
```
